32 devices in a mesh: seq: 16 (over z, y, core), tp: 2 (over x).
Axes of the slice: x: 2, y: 2, z: 4, core: 2. Of those that a mesh axis runs over, the one named last changes fastest.
Arguments:
- rollout_rows: bfloat16 [6144, 5120], P('seq', 'tp'), may hold values from -6 to 6
- live_rows: int32 [16], P('seq'), may hold values from 129 to 383, as said below
- doc_lengths: int32 [8], replicated, may hold values from 1 to 769, 4096 in all
- block_owner: int32 [16], replicated, may hold values from 0 to 15, each once
- norm_gain: bfloat16 [5120], replicated, may hold values from 0.099609375 to 1.8984375
- qkv_weight: bfloat16 [5120, 5120], P('seq', 'tp'), may hold values from -1.8168052 to 1.8168052
- out_weight: bfloat16 [5120, 3072], P('seq', 'tp'), may hold values from -0.109375 to 0.109375
Outputs:
- layer_out: bfloat16 [4096, 5120], P('seq', 'tp')
- key_cache: bfloat16 [4096, 1024], P('seq', 'tp')
- value_cache: bfloat16 [4096, 1024], P('seq', 'tp')
The draws below stay inside these ranges and needn't reach their ends.
Inputs may be any that keep to these rules, and one draw needn't show every extreme that they name: Device s's live rows number live_rows[s]; the live rows of the devices before s number at least 256 * s and less than 256 * s + 128; all live rows together number 4096. `block_owner`: a permutation.
All inputs are finite; a program needn't handle non-finite values.
Results may differ from the reference program's by a relative error of at most 0.015.
The reference program's roundings to bfloat16 on the way count: a program that leaves them out, or rounds other values in their place, can miss the bound.
Values may be sent and summed in bfloat16 or wider, within the bound.
No kernel may reach another device: no remote copies, remote signals or barrier semaphores. Data moves between devices by JAX's collectives and lax.ppermute only.
A program may use at most 128 MiB of HBM per device.

```python
import math
import jax
import jax.numpy as jnp
import numpy as np
from jax import lax

D = 5120
KV_HEADS = 8
HD = 128
HEADS = 24
WINDOW = 4
TOK_DEV = 256
CAP = 384
TOKENS = 4096
DOCS = 8
MOST = 769
QKV_COLS = 5120
N_SEQ = 16
N_TP = 2


def draw_live_rows(key, part):
    half_rows = TOK_DEV // 2
    first_key, second_key = jax.random.split(jax.random.fold_in(key, 11))
    spilled = jax.random.randint(first_key, (N_SEQ,), 0, half_rows)
    chosen = jax.random.randint(second_key, (), 1, N_SEQ - 1)
    indices = jnp.arange(N_SEQ)
    spilled = jnp.where(indices == chosen, half_rows - 1, spilled)
    spilled = jnp.where(indices == chosen - 1, 0, spilled)
    spilled = jnp.where(indices == chosen + 1, 0, spilled)
    spilled = jnp.where(indices == N_SEQ - 1, 0, spilled)
    earlier = jnp.concatenate([jnp.zeros((1,), spilled.dtype), spilled[:-1]])
    return (TOK_DEV + spilled - earlier).astype(jnp.int32)


def draw_qkv_weight(key, part):
    base_key = jax.random.fold_in(jax.random.fold_in(key, 21), 0)
    base = jax.random.truncated_normal(base_key, -4.0, 4.0, (D, QKV_COLS), jnp.float32) * D ** (-0.5)
    return base.astype(jnp.bfloat16)


def levels(rng, dims, shards, smallest, largest):
    def one(dim, blocks):
        draws = jax.random.uniform(jax.random.fold_in(jax.random.fold_in(rng, 6), dim), (blocks,), jnp.float32, smallest / len(shards), largest / len(shards))
        return jnp.repeat(jnp.exp(draws), dims[dim] // blocks).reshape((-1,) + (1,) * (len(dims) - dim - 1))

    gain = one(*shards[0])
    for cut in shards[1:]:
        gain = gain * one(*cut)
    return gain


def split_up(number_of, total, most, slope):
    portions = [(1 << 20) // math.isqrt(grade ** slope) + 1 for grade in range(2, number_of + 1)]
    spare, counts = total - most - (number_of - 1), [1] * (number_of - 1)
    while spare > 0:
        free = [i for i in range(number_of - 1) if counts[i] < most]
        whole, left = sum([portions[i] for i in free]), spare
        for i in free:
            addition = min(most - counts[i], max(1, left * portions[i] // whole), spare)
            counts[i] = counts[i] + addition
            spare = spare - addition
    return np.array([most] + counts)


def ragged_sizes(stream_key, amount, total, reach, slope):
    if amount == 2:
        one = jax.random.randint(stream_key, (), max(1, total - reach), min(reach, total - 1) + 1)
        return jnp.stack([one, total - one])
    tallies = jnp.asarray(split_up(amount, total, reach, slope), jnp.int32)
    couples = (amount - 1) // 2
    source_of, sink = tallies[1:1 + 2 * couples:2], tallies[2:2 + 2 * couples:2]
    room = jnp.minimum(source_of - 1, reach - sink)
    passed = jax.random.randint(jax.random.fold_in(stream_key, 1), (couples,), 0, 1 << 20) % (room + 1)
    tallies = tallies.at[1:1 + 2 * couples:2].set(source_of - passed).at[2:2 + 2 * couples:2].set(sink + passed)
    return tallies[jax.random.permutation(jax.random.fold_in(stream_key, 2), amount)]


def noise(rng, extent, scale, limit, pieces=(), held_as=jnp.bfloat16):
    result = jax.random.normal(rng, extent, jnp.float32) * scale
    if len(pieces) > 0:
        result = levels(rng, extent, pieces, -0.22, 0.18) * result
    return jnp.clip(result, min=-limit, max=limit).astype(held_as)


def setup_inputs(seed: int = 0) -> dict:
    arg_keys = jax.random.split(jax.random.key(seed), 8)
    rollout_rows = noise(arg_keys[0], (N_SEQ * CAP, D), 1.0, 6.0, ((0, 16), (1, 2)))
    live_rows = draw_live_rows(jax.random.fold_in(arg_keys[7], 71), 0)
    doc_lengths = ragged_sizes(arg_keys[2], DOCS, TOKENS, MOST, 2).astype(jnp.int32)
    block_owner = jax.random.permutation(arg_keys[3], N_SEQ).astype(jnp.int32)
    norm_gain = jnp.clip(1.0 + 0.18 * jax.random.normal(arg_keys[4], (D,), jnp.float32), 0.099609375, 1.8984375).astype(jnp.bfloat16)
    qkv_weight = draw_qkv_weight(jax.random.fold_in(arg_keys[7], 71), 0)
    out_weight = noise(arg_keys[6], (D, HEADS * HD), (HEADS * HD) ** -0.5, 0.109375, ((0, 16), (1, 2)))
    return {"rollout_rows": rollout_rows, "live_rows": live_rows, "doc_lengths": doc_lengths, "block_owner": block_owner, "norm_gain": norm_gain, "qkv_weight": qkv_weight, "out_weight": out_weight}


EPSILON = 1e-06
NEG_LARGE = -1e+30

def reference(rollout_rows, live_rows, doc_lengths, block_owner, norm_gain, qkv_weight, out_weight):
    offsets = jnp.cumsum(live_rows) - live_rows
    position = jnp.arange(TOKENS, dtype=jnp.int32)
    source = lax.optimization_barrier(jnp.sum((offsets[None, 1:] <= position[:, None]).astype(jnp.int32), axis=1)).astype(jnp.int32)
    local_row = position - offsets[source]
    stream = rollout_rows[source * CAP + local_row]
    values_f = stream.astype(jnp.float32)
    scale = lax.rsqrt(lax.optimization_barrier(jnp.mean(values_f * values_f, axis=-1, keepdims=True)) + EPSILON)
    normed = (values_f * scale * norm_gain.astype(jnp.float32)).astype(jnp.bfloat16)
    block_rows = D // N_SEQ
    permuted = normed.reshape(TOKENS, N_SEQ, block_rows)[:, block_owner, :].reshape(TOKENS, D)
    projected = jnp.dot(permuted, qkv_weight, preferred_element_type=jnp.float32)
    group = HEADS // KV_HEADS
    kv_local = KV_HEADS // N_TP
    width = QKV_COLS // N_TP
    q_width = kv_local * group * HD
    cube = projected.reshape(TOKENS, N_TP, width)
    query = (cube[:, :, :q_width] * HD ** (-0.5)).astype(jnp.bfloat16).reshape(TOKENS, KV_HEADS, group, HD)
    key_all = cube[:, :, q_width:q_width + kv_local * HD].astype(jnp.bfloat16).reshape(TOKENS, KV_HEADS, HD)
    value_all = cube[:, :, q_width + kv_local * HD:].astype(jnp.bfloat16).reshape(TOKENS, KV_HEADS, HD)
    doc_starts = jnp.cumsum(doc_lengths) - doc_lengths
    first_pos = lax.optimization_barrier(jnp.max(jnp.where(doc_starts[None, :] <= position[:, None], doc_starts[None, :], 0), axis=1))
    padding = (WINDOW - 1) * TOK_DEV
    key_pad = jnp.concatenate([jnp.zeros((padding, KV_HEADS, HD), jnp.bfloat16), key_all], 0)
    value_pad = jnp.concatenate([jnp.zeros((padding, KV_HEADS, HD), jnp.bfloat16), value_all], 0)

    def one_block(block):
        begin = (block * TOK_DEV).astype(jnp.int32)
        queries = lax.dynamic_slice_in_dim(query, begin, TOK_DEV, 0)
        keys_block = lax.dynamic_slice_in_dim(key_pad, begin, WINDOW * TOK_DEV, 0)
        values_block = lax.dynamic_slice_in_dim(value_pad, begin, WINDOW * TOK_DEV, 0)
        query_pos = begin + jnp.arange(TOK_DEV, dtype=jnp.int32)
        key_pos = begin - padding + jnp.arange(WINDOW * TOK_DEV, dtype=jnp.int32)
        starts = lax.dynamic_slice_in_dim(first_pos, begin, TOK_DEV, 0)
        allowed = (key_pos[None, :] <= query_pos[:, None]) & (key_pos[None, :] >= starts[:, None])
        scores = jnp.einsum('tgjd,sgd->gjts', queries.astype(jnp.float32), keys_block.astype(jnp.float32))
        masked = jnp.where(allowed, scores, NEG_LARGE)
        highest = lax.optimization_barrier(jnp.max(masked, axis=-1, keepdims=True))
        expo = jnp.where(allowed, jnp.exp(masked - highest), 0.0)
        totals = lax.optimization_barrier(jnp.sum(expo, axis=-1))
        summed = jnp.einsum('gjts,sgd->tgjd', expo.astype(jnp.bfloat16).astype(jnp.float32), values_block.astype(jnp.float32))
        context = summed / jnp.transpose(totals, (2, 0, 1))[..., None]
        return context.astype(jnp.bfloat16).reshape(TOK_DEV, HEADS * HD)
    context_all = lax.map(one_block, jnp.arange(N_SEQ, dtype=jnp.int32)).reshape(TOKENS, HEADS * HD)
    head_width = HEADS * HD // N_TP
    context_groups = context_all.reshape(TOKENS, N_TP, head_width)
    weight_groups = out_weight.reshape(D, N_TP, head_width)
    summed_out = jnp.zeros((TOKENS, D), jnp.float32)
    for group_index in range(N_TP):
        partial_value = lax.dot_general(context_groups[:, group_index, :], weight_groups[:, group_index, :], (((1,), (1,)), ((), ())), preferred_element_type=jnp.float32)
        rounded = lax.optimization_barrier(partial_value.astype(jnp.bfloat16))
        summed_out = summed_out + rounded.astype(jnp.float32)
    placed = jnp.zeros((TOKENS, N_SEQ, block_rows), jnp.float32).at[:, block_owner, :].set(summed_out.reshape(TOKENS, N_SEQ, block_rows))
    layer_out = placed.reshape(TOKENS, D).astype(jnp.bfloat16)
    return (layer_out, key_all.reshape(TOKENS, KV_HEADS * HD), value_all.reshape(TOKENS, KV_HEADS * HD))
```

```python
import jax
import jax.numpy as jnp
from jax import lax
from jax.sharding import PartitionSpec as P

D = 5120
KV_HEADS = 8
HD = 128
HEADS = 24
WINDOW = 4
TOK_DEV = 256


EPSILON = 1e-06
NEG_LARGE = -1e30


def carried_in(value, axis, join, neutral):
    count, mine = (lax.axis_size(axis), lax.axis_index(axis))
    pieces = lax.all_gather(value, axis)
    total = jnp.full_like(value, 0) + jnp.asarray(neutral, value.dtype)

    def turn(position, total):
        longer = join(total, pieces[position])
        return jnp.where(position < mine, longer, total)

    return lax.fori_loop(0, count - 1, turn, total)


def shifted(x, axis, by):
    count = lax.axis_size(axis)
    pairs = [(i, i + by) for i in range(count) if 0 <= i + by < count]
    return lax.ppermute(x, axis, pairs)


def gathered_body(rollout_rows, live_rows, doc_lengths, block_owner, norm_gain, qkv_weight, out_weight):
    half_rows = TOK_DEV // 2
    seq_index = lax.axis_index("seq")

    def combine(earlier, later):
        return earlier + later

    before = carried_in(live_rows, "seq", combine, jnp.zeros_like(live_rows))
    spilled_in = before[0] - seq_index * TOK_DEV
    tail_rows = lax.dynamic_slice_in_dim(rollout_rows, live_rows[0] - half_rows, half_rows, 0)
    arrived = shifted(tail_rows, "seq", 1)
    joined = jnp.concatenate([arrived, rollout_rows], 0)
    owned = lax.dynamic_slice_in_dim(joined, half_rows - spilled_in, TOK_DEV, 0)
    full_rows = lax.all_gather(owned, "tp", axis=1, tiled=True)
    values_f = full_rows.astype(jnp.float32)
    scale = lax.rsqrt(jnp.mean(values_f * values_f, axis=-1, keepdims=True) + EPSILON)
    normed = (values_f * scale * norm_gain.astype(jnp.float32)).astype(jnp.bfloat16)
    block_rows = qkv_weight.shape[0]
    block_count = D // block_rows
    permuted = normed.reshape(TOK_DEV, block_count, block_rows)[:, block_owner, :].reshape(
        TOK_DEV, D
    )
    positions = jnp.arange(block_count, dtype=jnp.int32)
    inverse = jnp.sum(
        jnp.where(block_owner[None, :] == positions[:, None], positions[None, :], 0), axis=1
    )
    projected = jnp.dot(
        permuted,
        lax.all_gather(qkv_weight, "seq", axis=0, tiled=True),
        preferred_element_type=jnp.float32,
    )
    group = HEADS // KV_HEADS
    kv_local = projected.shape[1] // ((group + 2) * HD)
    q_width = kv_local * group * HD
    query_rows = (projected[:, :q_width] * HD ** (-0.5)).astype(jnp.bfloat16)
    key_rows = projected[:, q_width : q_width + kv_local * HD].astype(jnp.bfloat16)
    value_rows = projected[:, q_width + kv_local * HD :].astype(jnp.bfloat16)
    queries = query_rows.reshape(TOK_DEV, kv_local, group, HD)
    query_pos = seq_index * TOK_DEV + jnp.arange(TOK_DEV, dtype=jnp.int32)
    doc_starts = jnp.cumsum(doc_lengths) - doc_lengths
    first_pos = jnp.max(
        jnp.where(doc_starts[None, :] <= query_pos[:, None], doc_starts[None, :], 0), axis=1
    )
    initial = (
        jnp.full((kv_local, group, TOK_DEV), NEG_LARGE, jnp.float32),
        jnp.zeros((kv_local, group, TOK_DEV), jnp.float32),
        jnp.zeros((kv_local, group, TOK_DEV, HD), jnp.float32),
    )
    keys_all, values_all = (key_rows, value_rows)
    for level in range(WINDOW.bit_length() - 1):
        got_keys, got_values = shifted((keys_all, values_all), "seq", 1 << level)
        keys_all = jnp.concatenate([got_keys, keys_all], 0)
        values_all = jnp.concatenate([got_values, values_all], 0)
    state = initial
    for block in range(WINDOW):
        keys_block = keys_all[block * TOK_DEV : (block + 1) * TOK_DEV]
        attend_best, attend_totals, attend_accum = state
        key_count = keys_block.shape[0]
        keys_three = keys_block.reshape(key_count, kv_local, HD)
        values_three = values_all[block * TOK_DEV : (block + 1) * TOK_DEV].reshape(
            key_count, kv_local, HD
        )
        scores = jnp.einsum(
            "tgjd,sgd->gjts", queries, keys_three, preferred_element_type=jnp.float32
        )
        key_pos = (seq_index - WINDOW + 1 + block) * TOK_DEV + jnp.arange(
            key_count, dtype=jnp.int32
        )
        allowed = (key_pos[None, :] <= query_pos[:, None]) & (
            key_pos[None, :] >= first_pos[:, None]
        )
        masked = jnp.where(allowed, scores, NEG_LARGE)
        newest = jnp.maximum(attend_best, jnp.max(masked, axis=-1))
        rescale = jnp.exp(attend_best - newest)
        weights = jnp.where(allowed, jnp.exp(masked - newest[..., None]), 0.0)
        attend_totals = attend_totals * rescale + jnp.sum(weights, axis=-1)
        update = jnp.einsum(
            "gjts,sgd->gjtd",
            weights.astype(jnp.bfloat16),
            values_three,
            preferred_element_type=jnp.float32,
        )
        attend_accum = attend_accum * rescale[..., None] + update
        state = (newest, attend_totals, attend_accum)
    best, totals, accum = state
    context = (
        jnp.transpose(accum / totals[..., None], (2, 0, 1, 3))
        .reshape(TOK_DEV, q_width)
        .astype(jnp.bfloat16)
    )
    delivered = lax.dot_general(
        context,
        lax.all_gather(out_weight, "seq", axis=0, tiled=True),
        (((1,), (1,)), ((), ())),
        preferred_element_type=jnp.float32,
    )
    partial_value = delivered.reshape(TOK_DEV, block_count, block_rows)[:, inverse, :].reshape(
        TOK_DEV, D
    )
    mixed = lax.psum_scatter(
        partial_value.astype(jnp.bfloat16).astype(jnp.float32).astype(jnp.bfloat16),
        "tp",
        scatter_dimension=1,
        tiled=True,
    )
    return (mixed, key_rows, value_rows)


def swapped(x, axis, bit):
    count = lax.axis_size(axis)
    return lax.ppermute(x, axis, [(i, i ^ bit) for i in range(count)])


def turned(x, axis, by):
    count = lax.axis_size(axis)
    return lax.ppermute(x, axis, [(i, (i + by) % count) for i in range(count)])


def pick(stacked, index):
    return lax.dynamic_index_in_dim(stacked, index, 0, keepdims=False)


def plane_body(rollout_rows, live_rows, doc_lengths, block_owner, norm_gain, qkv_weight, out_weight):
    seq_count, seq_index = lax.axis_size("seq"), lax.axis_index("seq")
    tp_index = lax.axis_index("tp")
    block_rows, columns = qkv_weight.shape
    local_features = rollout_rows.shape[1]
    group = HEADS // KV_HEADS
    size = columns // ((group + 2) * HD)
    planes = seq_count // size
    place, plane = seq_index % size, seq_index // size
    head_width = group * HD
    half_rows = TOK_DEV // 2

    q_width = size * head_width
    by_head = jnp.stack(
        [
            jnp.concatenate(
                [
                    qkv_weight[:, k * head_width : (k + 1) * head_width],
                    qkv_weight[:, q_width + k * HD : q_width + (k + 1) * HD],
                    qkv_weight[:, q_width + (size + k) * HD : q_width + (size + k + 1) * HD],
                ],
                1,
            )
            for k in range(size)
        ]
    )
    mine = [pick(by_head, place)]
    for m in range(1, size):
        mine.append(swapped(pick(by_head, place ^ m), "seq", m))
    half = size // 2
    chain_a = [jnp.concatenate(mine[:half], 0)]
    chain_b = [jnp.concatenate(mine[half:], 0)]
    for r in range(1, planes):
        chain_a.append(turned(chain_a[-1], "seq", size))
        chain_b.append(turned(chain_b[-1], "seq", size))
    chain_o = [lax.optimization_barrier((out_weight, chain_a[-1]))[0]]
    for r in range(1, planes):
        chain_o.append(turned(chain_o[-1], "seq", size))

    all_live = lax.all_gather(live_rows, "seq", axis=0, tiled=True)
    before = jnp.sum(jnp.where(jnp.arange(seq_count) < seq_index, all_live, 0))
    spilled_in = before - seq_index * TOK_DEV
    tail_rows = lax.dynamic_slice_in_dim(rollout_rows, live_rows[0] - half_rows, half_rows, 0)
    arrived = shifted(tail_rows, "seq", 1)
    joined = jnp.concatenate([arrived, rollout_rows], 0)
    owned = lax.dynamic_slice_in_dim(joined, half_rows - spilled_in, TOK_DEV, 0)
    values_f = owned.astype(jnp.float32)
    squares = jnp.sum(values_f * values_f, axis=-1)
    squares = squares + swapped(squares, "tp", 1)
    scale = lax.rsqrt(squares[:, None] / D + EPSILON)
    gain = lax.dynamic_slice_in_dim(norm_gain, tp_index * local_features, local_features, 0)
    normed = (values_f * scale * gain.astype(jnp.float32)).astype(jnp.bfloat16)

    cut = local_features // 2
    h1, h2 = normed[:, :cut], normed[:, cut:]
    x1, y2 = swapped(h1, "tp", 1), swapped(h2, "seq", 2)
    x2, y1 = swapped(h2, "tp", 1), swapped(h1, "seq", 2)
    yx2, xy1 = swapped(y2, "tp", 1), swapped(x1, "seq", 2)
    rows_a, rows_c = [h1, h2, x1, x2], [y1, y2, xy1, yx2]
    rows_b = [swapped(v, "seq", 1) for v in rows_a]
    rows_d = [swapped(v, "seq", 1) for v in rows_c]
    full_rows = jnp.concatenate(
        [jnp.concatenate(v, 1) for v in (rows_a, rows_b, rows_c, rows_d)], 0
    )

    numbers = jnp.arange(seq_count, dtype=jnp.int32)
    inverse = jnp.sum(
        jnp.where(block_owner[None, :] == numbers[:, None], numbers[None, :], 0), axis=1
    )
    half_blocks = local_features // block_rows

    def slot(blocks):
        source = inverse[blocks]
        step = (plane - source // size) % planes
        return step * size + ((source % size) ^ place)

    in_order = slot((numbers + tp_index * half_blocks) % seq_count)
    arrived_w = jnp.concatenate(
        [v for r in range(planes) for v in (chain_a[r], chain_b[r])], 0
    ).reshape(seq_count, block_rows, -1)
    true_w = arrived_w[in_order].reshape(D, -1)
    projected = jnp.dot(full_rows, true_w, preferred_element_type=jnp.float32)
    query_rows = (projected[:, :head_width] * HD ** (-0.5)).astype(jnp.bfloat16)
    kv_rows = projected[:, head_width:].astype(jnp.bfloat16).reshape(size, TOK_DEV, 2 * HD)

    kv_true = kv_rows[jnp.arange(size) ^ place].reshape(size * TOK_DEV, 2 * HD)
    back = WINDOW - 1
    halo = lax.ppermute(
        kv_true[(size - back) * TOK_DEV :],
        "seq",
        [(i, i + size) for i in range(seq_count - size)],
    )
    kv_all = jnp.concatenate([halo, kv_true], 0)
    kv_home = jnp.stack([kv_rows[0]] + [swapped(kv_rows[m], "seq", m) for m in range(1, size)])
    kv_home = kv_home[jnp.arange(size) ^ place]
    key_out = jnp.concatenate([kv_home[k][:, :HD] for k in range(size)], 1)
    value_out = jnp.concatenate([kv_home[k][:, HD:] for k in range(size)], 1)

    doc_starts = jnp.cumsum(doc_lengths) - doc_lengths
    contexts = []
    for m in range(size):
        block = place ^ m
        queries = query_rows[m * TOK_DEV : (m + 1) * TOK_DEV].reshape(TOK_DEV, group, HD)
        window = lax.dynamic_slice_in_dim(kv_all, block * TOK_DEV, WINDOW * TOK_DEV, 0)
        query_pos = (plane * size + block) * TOK_DEV + jnp.arange(TOK_DEV, dtype=jnp.int32)
        key_pos = (plane * size + block - back) * TOK_DEV + jnp.arange(
            WINDOW * TOK_DEV, dtype=jnp.int32
        )
        first_pos = jnp.max(
            jnp.where(doc_starts[None, :] <= query_pos[:, None], doc_starts[None, :], 0), axis=1
        )
        allowed = (key_pos[None, :] <= query_pos[:, None]) & (
            key_pos[None, :] >= first_pos[:, None]
        )
        scores = jnp.einsum(
            "tjd,sd->jts", queries, window[:, :HD], preferred_element_type=jnp.float32
        )
        masked = jnp.where(allowed, scores, NEG_LARGE)
        best = jnp.max(masked, axis=-1, keepdims=True)
        weights = jnp.where(allowed, jnp.exp(masked - best), 0.0)
        totals = jnp.sum(weights, axis=-1)
        summed = jnp.einsum(
            "jts,sd->jtd",
            weights.astype(jnp.bfloat16),
            window[:, HD:],
            preferred_element_type=jnp.float32,
        )
        context = summed / totals[..., None]
        contexts.append(
            jnp.transpose(context, (1, 0, 2)).reshape(TOK_DEV, head_width).astype(jnp.bfloat16)
        )
    context = jnp.stack(contexts)

    from_c = swapped(context, "seq", 2)
    from_b, from_d = swapped(context, "seq", 1), swapped(from_c, "seq", 1)
    order = jnp.arange(size)
    full_context = jnp.concatenate(
        [v[order ^ m] for m, v in enumerate((context, from_b, from_c, from_d))], 2
    ).reshape(size * TOK_DEV, size * head_width)

    def delivered(steps):
        rows = jnp.concatenate([chain_o[r] for r in steps], 0)
        rows = jnp.concatenate(
            [
                lax.dynamic_slice_in_dim(rows, (place ^ m) * head_width, head_width, 1)
                for m in range(size)
            ],
            1,
        )
        partial = lax.dot_general(
            rows, full_context, (((1,), (1,)), ((), ())), preferred_element_type=jnp.float32
        ).astype(jnp.bfloat16)
        pieces = [partial[:, m * TOK_DEV : (m + 1) * TOK_DEV] for m in range(size)]
        pieces = [pieces[0]] + [swapped(pieces[m], "seq", m) for m in range(1, size)]
        return jnp.stack(pieces, 0).reshape(size, len(steps), block_rows, TOK_DEV)

    early, late = delivered(range(planes - 1)), delivered([planes - 1])
    shares = jnp.concatenate([early, late], 1)
    shares = jnp.transpose(shares, (1, 0, 2, 3)).reshape(seq_count, block_rows, TOK_DEV)
    here = in_order[:half_blocks]
    there = in_order[half_blocks:]
    other = swapped(shares[there], "tp", 1)
    total = shares[here].astype(jnp.float32) + other.astype(jnp.float32)
    mixed = jnp.transpose(total.astype(jnp.bfloat16).reshape(local_features, TOK_DEV))
    return (mixed, key_out, value_out)


def solution(mesh):
    in_specs = (P("seq", "tp"), P("seq"), P(), P(), P(), P("seq", "tp"), P("seq", "tp"))
    out_specs = (P("seq", "tp"), P("seq", "tp"), P("seq", "tp"))
    size = KV_HEADS // mesh.shape["tp"]
    by_planes = size == WINDOW and mesh.shape["tp"] == 2 and mesh.shape["seq"] % size == 0
    body = plane_body if by_planes else gathered_body
    return jax.shard_map(body, mesh=mesh, in_specs=in_specs, out_specs=out_specs, check_vma=False)
```

```python
import jax
import jax.numpy as jnp
from jax import lax
from jax.experimental import pallas as pl
from jax.experimental.pallas import tpu as pltpu
from jax.sharding import PartitionSpec as P

D = 5120
KV_HEADS = 8
HD = 128
HEADS = 24
WINDOW = 4
TOK_DEV = 256


EPSILON = 1e-06
NEG_LARGE = -1e30


def carried_in(value, axis, join, neutral):
    count, mine = (lax.axis_size(axis), lax.axis_index(axis))
    pieces = lax.all_gather(value, axis)
    total = jnp.full_like(value, 0) + jnp.asarray(neutral, value.dtype)

    def turn(position, total):
        longer = join(total, pieces[position])
        return jnp.where(position < mine, longer, total)

    return lax.fori_loop(0, count - 1, turn, total)


def shifted(x, axis, by):
    count = lax.axis_size(axis)
    pairs = [(i, i + by) for i in range(count) if 0 <= i + by < count]
    return lax.ppermute(x, axis, pairs)


def gathered_body(rollout_rows, live_rows, doc_lengths, block_owner, norm_gain, qkv_weight, out_weight):
    half_rows = TOK_DEV // 2
    seq_index = lax.axis_index("seq")

    def combine(earlier, later):
        return earlier + later

    before = carried_in(live_rows, "seq", combine, jnp.zeros_like(live_rows))
    spilled_in = before[0] - seq_index * TOK_DEV
    tail_rows = lax.dynamic_slice_in_dim(rollout_rows, live_rows[0] - half_rows, half_rows, 0)
    arrived = shifted(tail_rows, "seq", 1)
    joined = jnp.concatenate([arrived, rollout_rows], 0)
    owned = lax.dynamic_slice_in_dim(joined, half_rows - spilled_in, TOK_DEV, 0)
    full_rows = lax.all_gather(owned, "tp", axis=1, tiled=True)
    values_f = full_rows.astype(jnp.float32)
    scale = lax.rsqrt(jnp.mean(values_f * values_f, axis=-1, keepdims=True) + EPSILON)
    normed = (values_f * scale * norm_gain.astype(jnp.float32)).astype(jnp.bfloat16)
    block_rows = qkv_weight.shape[0]
    block_count = D // block_rows
    permuted = normed.reshape(TOK_DEV, block_count, block_rows)[:, block_owner, :].reshape(
        TOK_DEV, D
    )
    positions = jnp.arange(block_count, dtype=jnp.int32)
    inverse = jnp.sum(
        jnp.where(block_owner[None, :] == positions[:, None], positions[None, :], 0), axis=1
    )
    projected = jnp.dot(
        permuted,
        lax.all_gather(qkv_weight, "seq", axis=0, tiled=True),
        preferred_element_type=jnp.float32,
    )
    group = HEADS // KV_HEADS
    kv_local = projected.shape[1] // ((group + 2) * HD)
    q_width = kv_local * group * HD
    query_rows = (projected[:, :q_width] * HD ** (-0.5)).astype(jnp.bfloat16)
    key_rows = projected[:, q_width : q_width + kv_local * HD].astype(jnp.bfloat16)
    value_rows = projected[:, q_width + kv_local * HD :].astype(jnp.bfloat16)
    queries = query_rows.reshape(TOK_DEV, kv_local, group, HD)
    query_pos = seq_index * TOK_DEV + jnp.arange(TOK_DEV, dtype=jnp.int32)
    doc_starts = jnp.cumsum(doc_lengths) - doc_lengths
    first_pos = jnp.max(
        jnp.where(doc_starts[None, :] <= query_pos[:, None], doc_starts[None, :], 0), axis=1
    )
    initial = (
        jnp.full((kv_local, group, TOK_DEV), NEG_LARGE, jnp.float32),
        jnp.zeros((kv_local, group, TOK_DEV), jnp.float32),
        jnp.zeros((kv_local, group, TOK_DEV, HD), jnp.float32),
    )
    keys_all, values_all = (key_rows, value_rows)
    for level in range(WINDOW.bit_length() - 1):
        got_keys, got_values = shifted((keys_all, values_all), "seq", 1 << level)
        keys_all = jnp.concatenate([got_keys, keys_all], 0)
        values_all = jnp.concatenate([got_values, values_all], 0)
    state = initial
    for block in range(WINDOW):
        keys_block = keys_all[block * TOK_DEV : (block + 1) * TOK_DEV]
        attend_best, attend_totals, attend_accum = state
        key_count = keys_block.shape[0]
        keys_three = keys_block.reshape(key_count, kv_local, HD)
        values_three = values_all[block * TOK_DEV : (block + 1) * TOK_DEV].reshape(
            key_count, kv_local, HD
        )
        scores = jnp.einsum(
            "tgjd,sgd->gjts", queries, keys_three, preferred_element_type=jnp.float32
        )
        key_pos = (seq_index - WINDOW + 1 + block) * TOK_DEV + jnp.arange(
            key_count, dtype=jnp.int32
        )
        allowed = (key_pos[None, :] <= query_pos[:, None]) & (
            key_pos[None, :] >= first_pos[:, None]
        )
        masked = jnp.where(allowed, scores, NEG_LARGE)
        newest = jnp.maximum(attend_best, jnp.max(masked, axis=-1))
        rescale = jnp.exp(attend_best - newest)
        weights = jnp.where(allowed, jnp.exp(masked - newest[..., None]), 0.0)
        attend_totals = attend_totals * rescale + jnp.sum(weights, axis=-1)
        update = jnp.einsum(
            "gjts,sgd->gjtd",
            weights.astype(jnp.bfloat16),
            values_three,
            preferred_element_type=jnp.float32,
        )
        attend_accum = attend_accum * rescale[..., None] + update
        state = (newest, attend_totals, attend_accum)
    best, totals, accum = state
    context = (
        jnp.transpose(accum / totals[..., None], (2, 0, 1, 3))
        .reshape(TOK_DEV, q_width)
        .astype(jnp.bfloat16)
    )
    delivered = lax.dot_general(
        context,
        lax.all_gather(out_weight, "seq", axis=0, tiled=True),
        (((1,), (1,)), ((), ())),
        preferred_element_type=jnp.float32,
    )
    partial_value = delivered.reshape(TOK_DEV, block_count, block_rows)[:, inverse, :].reshape(
        TOK_DEV, D
    )
    mixed = lax.psum_scatter(
        partial_value.astype(jnp.bfloat16).astype(jnp.float32).astype(jnp.bfloat16),
        "tp",
        scatter_dimension=1,
        tiled=True,
    )
    return (mixed, key_rows, value_rows)


LANES = 128
VMEM_LIMIT = 60 * 1024 * 1024


def swapped(x, axis, bit):
    count = lax.axis_size(axis)
    return lax.ppermute(x, axis, [(i, i ^ bit) for i in range(count)])


def turned(x, axis, by):
    count = lax.axis_size(axis)
    return lax.ppermute(x, axis, [(i, (i + by) % count) for i in range(count)])


def both_ways(x, size, planes):
    got = {0: x}
    up = down = x
    for step in range(1, planes):
        near = (step + 1) // 2
        if step % 2:
            up = turned(up, "seq", size)
            got[near] = up
        else:
            down = turned(down, "seq", -size)
            got[planes - near] = down
    return got


def project_kernel(layout, table, *refs, count, rows, block_rows, window, first):
    pieces, weights = layout
    groups = len(pieces)
    x_refs, refs = refs[: sum(pieces)], refs[sum(pieces) :]
    w_refs, refs = refs[: len(weights)], refs[len(weights) :]
    if first:
        acc_out, xs, ws, x_sem, w_sem = refs
    else:
        acc_in, q_out, kv_out, xs, ws, x_sem, w_sem = refs
    spots = [(ref, part) for ref, parts in zip(w_refs, weights) for part in range(parts)]
    for i, (ref, part) in enumerate(spots):
        piece, start, offset = table[i, 0], table[i, 1], table[i, 2]
        pltpu.make_async_copy(
            ref.at[pl.ds(part * block_rows, block_rows), :],
            ws.at[pl.ds(pl.multiple_of(i * window + offset, 64), block_rows), :],
            w_sem.at[i],
        ).start()
        for p in range(pieces[0]):

            @pl.when(piece == p)
            def _():
                for m in range(groups):
                    pltpu.make_async_copy(
                        x_refs[m * pieces[0] + p].at[:, pl.ds(pl.multiple_of(start, LANES), window)],
                        xs.at[pl.ds(m * rows, rows), pl.ds(i * window, window)],
                        x_sem.at[i],
                    ).start()

    pad = window - block_rows
    for i, (ref, part) in enumerate(spots):
        offset = table[i, 2]
        area = ws.at[pl.ds(pl.multiple_of(i * window + offset, 64), block_rows), :]
        pltpu.make_async_copy(ref.at[pl.ds(part * block_rows, block_rows), :], area, w_sem.at[i]).wait()
        spare = pl.multiple_of(i * window + jnp.where(offset == 0, block_rows, 0), 64)
        ws[pl.ds(spare, pad), :] = jnp.zeros((pad, ws.shape[1]), ws.dtype)
    for i in range(len(spots)):
        area = xs.at[:, pl.ds(i * window, window)]
        pltpu.make_async_copy(area, area, x_sem.at[i]).wait()

    def one(m, carry):
        at = pl.ds(pl.multiple_of(m * rows, rows), rows)
        total = jnp.dot(xs[at, :], ws[...], preferred_element_type=jnp.float32)
        if first:
            acc_out[at, :] = total
        else:
            total = total + acc_in[at, :]
            width = q_out.shape[1]
            q_out[at, :] = (total[:, :width] * HD ** (-0.5)).astype(q_out.dtype)
            kv_out[at, :] = total[:, width:].astype(kv_out.dtype)
        return carry

    lax.fori_loop(0, groups, one, 0)


def project(table, piece_rows, weights, acc, block_rows, head_width):
    groups, pieces = len(piece_rows), len(piece_rows[0])
    rows = piece_rows[0][0].shape[0]
    parts = [w.shape[0] // block_rows for w in weights]
    count, columns = sum(parts), weights[0].shape[1]
    window = -(-(block_rows + LANES // 2) // LANES) * LANES
    total = groups * rows
    first = acc is None
    kernel = lambda table, *refs: project_kernel(
        ([pieces] * groups, parts),
        table,
        *refs,
        count=count,
        rows=rows,
        block_rows=block_rows,
        window=window,
        first=first,
    )
    anywhere, local = pl.BlockSpec(memory_space=pl.ANY), pl.BlockSpec(memory_space=pltpu.VMEM)
    if first:
        shapes = jax.ShapeDtypeStruct((total, columns), jnp.float32)
        outs = local
    else:
        shapes = (
            jax.ShapeDtypeStruct((total, head_width), jnp.bfloat16),
            jax.ShapeDtypeStruct((total, columns - head_width), jnp.bfloat16),
        )
        outs = (local, local)
    flops = 2 * total * count * window * columns
    moved = count * (total * window + block_rows * columns) * 2 + total * columns * 4
    return pl.pallas_call(
        kernel,
        out_shape=shapes,
        in_specs=[pl.BlockSpec(memory_space=pltpu.SMEM)]
        + [anywhere] * (groups * pieces + len(weights))
        + ([] if first else [local]),
        out_specs=outs,
        scratch_shapes=[
            pltpu.VMEM((total, count * window), jnp.bfloat16),
            pltpu.VMEM((count * window, columns), jnp.bfloat16),
            pltpu.SemaphoreType.DMA((count,)),
            pltpu.SemaphoreType.DMA((count,)),
        ],
        cost_estimate=pl.CostEstimate(flops=flops, bytes_accessed=moved, transcendentals=0),
        compiler_params=pltpu.CompilerParams(vmem_limit_bytes=VMEM_LIMIT),
        name="project_first" if first else "project_last",
    )(table, *[v for row in piece_rows for v in row], *weights, *([] if first else [acc]))


def attend_kernel(place_ref, starts_ref, q_ref, kv_ref, halo_ref, out_ref, keys, best, norm, accum):
    size = kv_ref.shape[0] // TOK_DEV
    back = WINDOW - 1
    heads = q_ref.shape[1] // HD
    place, plane = place_ref[0], place_ref[1]
    keys[pl.ds(0, back * TOK_DEV), :] = halo_ref[...]
    for m in range(size):
        at = pl.multiple_of((back + (place ^ m)) * TOK_DEV, TOK_DEV)
        keys[pl.ds(at, TOK_DEV), :] = kv_ref[pl.ds(m * TOK_DEV, TOK_DEV), :]

    def one(m, carry):
        block = place ^ m
        base = (plane * size + block) * TOK_DEV
        rows = pl.ds(pl.multiple_of(m * TOK_DEV, TOK_DEV), TOK_DEV)
        query_pos = base + lax.broadcasted_iota(jnp.int32, (TOK_DEV, 1), 0)
        first_pos = jnp.zeros((TOK_DEV, 1), jnp.int32)
        lowest = jnp.int32(0)
        for d in range(starts_ref.shape[0]):
            start = starts_ref[d]
            first_pos = jnp.where(start <= query_pos, jnp.maximum(first_pos, start), first_pos)
            lowest = jnp.where(start <= base, jnp.maximum(lowest, start), lowest)
        earliest = lowest // TOK_DEV - (plane * size + block - back)
        best[...] = jnp.full(best.shape, NEG_LARGE, jnp.float32)
        norm[...] = jnp.zeros(norm.shape, jnp.float32)
        accum[...] = jnp.zeros(accum.shape, jnp.float32)

        def step(w, carry):
            at = pl.ds(pl.multiple_of((block + w) * TOK_DEV, TOK_DEV), TOK_DEV)
            key_pos = base + (w - back) * TOK_DEV + lax.broadcasted_iota(
                jnp.int32, (1, TOK_DEV), 1
            )
            allowed = (key_pos <= query_pos) & (key_pos >= first_pos)
            key_block, value_block = keys[at, :HD], keys[at, HD:]
            for h in range(heads):
                scores = lax.dot_general(
                    q_ref[rows, h * HD : (h + 1) * HD],
                    key_block,
                    (((1,), (1,)), ((), ())),
                    preferred_element_type=jnp.float32,
                )
                masked = jnp.where(allowed, scores, NEG_LARGE)
                old = best[h]
                newest = jnp.maximum(old, jnp.max(masked, axis=-1, keepdims=True))
                rescale = jnp.exp(old - newest)
                weights = jnp.where(allowed, jnp.exp(masked - newest), 0.0)
                norm[h] = norm[h] * rescale + jnp.sum(weights, axis=-1, keepdims=True)
                accum[h] = accum[h] * rescale + jnp.dot(
                    weights.astype(jnp.bfloat16), value_block, preferred_element_type=jnp.float32
                )
                best[h] = newest
            return carry

        lax.fori_loop(jnp.clip(earliest, 0, back), WINDOW, step, 0)
        for h in range(heads):
            out_ref[rows, h * HD : (h + 1) * HD] = (accum[h] / norm[h]).astype(out_ref.dtype)
        return carry

    lax.fori_loop(0, size, one, 0)


def attend(where, doc_starts, query_rows, kv_rows, halo):
    heads = query_rows.shape[1] // HD
    scalar, local = pl.BlockSpec(memory_space=pltpu.SMEM), pl.BlockSpec(memory_space=pltpu.VMEM)
    rows = query_rows.shape[0]
    return pl.pallas_call(
        attend_kernel,
        out_shape=jax.ShapeDtypeStruct(query_rows.shape, jnp.bfloat16),
        in_specs=[scalar, scalar, local, local, local],
        out_specs=local,
        scratch_shapes=[
            pltpu.VMEM((halo.shape[0] + kv_rows.shape[0], 2 * HD), jnp.bfloat16),
            pltpu.VMEM((heads, TOK_DEV, 1), jnp.float32),
            pltpu.VMEM((heads, TOK_DEV, 1), jnp.float32),
            pltpu.VMEM((heads, TOK_DEV, HD), jnp.float32),
        ],
        cost_estimate=pl.CostEstimate(
            flops=4 * rows * heads * WINDOW * TOK_DEV * HD,
            bytes_accessed=4 * rows * heads * HD + 2 * rows * 4 * HD,
            transcendentals=rows * heads * WINDOW * TOK_DEV,
        ),
        compiler_params=pltpu.CompilerParams(vmem_limit_bytes=VMEM_LIMIT),
        name="attend",
    )(where, doc_starts, query_rows, kv_rows, halo)


def deliver_kernel(place_ref, *refs, size, steps):
    contexts, weights, outs = refs[:size], refs[size : size + steps], refs[size + steps :]
    width = contexts[0].shape[1]
    block_rows = weights[0].shape[0]
    place = place_ref[0]
    for r in range(steps):
        for m in range(size):
            total = None
            for other in range(size):
                term = lax.dot_general(
                    weights[r][:, pl.ds(pl.multiple_of((place ^ other) * width, LANES), width)],
                    contexts[other][(m ^ other) * TOK_DEV : ((m ^ other) + 1) * TOK_DEV, :],
                    (((1,), (1,)), ((), ())),
                    preferred_element_type=jnp.float32,
                )
                total = term if total is None else total + term
            outs[m][r * block_rows : (r + 1) * block_rows, :] = total.astype(outs[m].dtype)


def deliver(where, contexts, weights):
    size, steps = len(contexts), len(weights)
    block_rows = weights[0].shape[0]
    rows, width = contexts[0].shape
    scalar, local = pl.BlockSpec(memory_space=pltpu.SMEM), pl.BlockSpec(memory_space=pltpu.VMEM)
    shape = jax.ShapeDtypeStruct((steps * block_rows, TOK_DEV), jnp.bfloat16)
    return pl.pallas_call(
        lambda *refs: deliver_kernel(*refs, size=size, steps=steps),
        out_shape=(shape,) * size,
        in_specs=[scalar] + [local] * (size + steps),
        out_specs=(local,) * size,
        cost_estimate=pl.CostEstimate(
            flops=2 * rows * width * size * steps * block_rows,
            bytes_accessed=2 * (rows * width * size + steps * block_rows * (width * size + rows)),
            transcendentals=0,
        ),
        compiler_params=pltpu.CompilerParams(vmem_limit_bytes=VMEM_LIMIT),
        name="deliver",
    )(where, *contexts, *weights)


def plane_body(rollout_rows, live_rows, doc_lengths, block_owner, norm_gain, qkv_weight, out_weight):
    seq_count, seq_index = lax.axis_size("seq"), lax.axis_index("seq")
    tp_index = lax.axis_index("tp")
    block_rows, columns = qkv_weight.shape
    local_features = rollout_rows.shape[1]
    group = HEADS // KV_HEADS
    size = columns // ((group + 2) * HD)
    planes = seq_count // size
    place, plane = seq_index % size, seq_index // size
    where = jnp.stack([place, plane]).astype(jnp.int32)
    head_width = group * HD
    half_rows = TOK_DEV // 2

    q_width = size * head_width

    def columns_of(k):
        cuts = ((k * head_width, head_width), (q_width + k * HD, HD), (q_width + (size + k) * HD, HD))
        return jnp.concatenate(
            [lax.dynamic_slice_in_dim(qkv_weight, at, wide, 1) for at, wide in cuts], 1
        )

    mine = [columns_of(place)]
    for m in range(1, size):
        mine.append(swapped(columns_of(place ^ m), "seq", m))
    half = size // 2
    sent = mine[:half] + [jnp.concatenate(mine[half:], 0)]
    chains = [both_ways(v, size, planes) for v in sent]
    last = planes // 2
    held = lax.optimization_barrier((out_weight, *[c[last] for c in chains[:-1]]))[0]
    chain_o = both_ways(held, size, planes)

    plane_live = [live_rows] + [swapped(live_rows, "seq", m) for m in range(1, size)]
    before = sum(jnp.where((place ^ m) < place, v, 0) for m, v in enumerate(plane_live))
    in_plane = sum(plane_live)
    for k in range(1, planes):
        before = before + shifted(in_plane, "seq", k * size)
    spilled_in = before[0] - seq_index * TOK_DEV
    tail_rows = lax.dynamic_slice_in_dim(rollout_rows, live_rows[0] - half_rows, half_rows, 0)
    arrived = shifted(tail_rows, "seq", 1)
    joined = jnp.concatenate([arrived, rollout_rows], 0)
    owned = lax.dynamic_slice_in_dim(joined, half_rows - spilled_in, TOK_DEV, 0)
    values_f = owned.astype(jnp.float32)
    squares = jnp.sum(values_f * values_f, axis=-1)
    squares = squares + swapped(squares, "tp", 1)
    scale = lax.rsqrt(squares[:, None] / D + EPSILON)
    gain = lax.dynamic_slice_in_dim(norm_gain, tp_index * local_features, local_features, 0)
    normed = (values_f * scale * gain.astype(jnp.float32)).astype(jnp.bfloat16)

    cut = local_features // 2
    h1, h2 = normed[:, :cut], normed[:, cut:]
    x1, y2 = swapped(h1, "tp", 1), swapped(h2, "seq", 2)
    x2, y1 = swapped(h2, "tp", 1), swapped(h1, "seq", 2)
    yx2, xy1 = swapped(y2, "tp", 1), swapped(x1, "seq", 2)
    rows_a, rows_c = [h1, h2, x1, x2], [y1, y2, xy1, yx2]
    rows_b = [swapped(v, "seq", 1) for v in rows_a]
    rows_d = [swapped(v, "seq", 1) for v in rows_c]
    piece_rows = (rows_a, rows_b, rows_c, rows_d)

    numbers = jnp.arange(seq_count, dtype=jnp.int32)
    inverse = jnp.sum(
        jnp.where(block_owner[None, :] == numbers[:, None], numbers[None, :], 0), axis=1
    )
    half_blocks = local_features // block_rows

    def slot(blocks):
        source = inverse[blocks]
        step = (plane - source // size) % planes
        return step * size + ((source % size) ^ place)

    in_order = slot((numbers + tp_index * half_blocks) % seq_count)
    true_of = jnp.sum(
        jnp.where(in_order[None, :] == numbers[:, None], numbers[None, :], 0), axis=1
    )
    per_piece = cut // block_rows
    inside = (true_of % per_piece) * block_rows
    table = jnp.stack([true_of // per_piece, inside // LANES * LANES, inside % LANES], 1)

    steps = [r for r in range(planes) if r != last]
    by_step = lambda some: [c[r] for r in some for c in chains]
    rows_of = lambda some: jnp.concatenate([table[r * size : (r + 1) * size] for r in some], 0)
    acc = project(rows_of(steps), piece_rows, by_step(steps), None, block_rows, head_width)
    query_rows, kv_rows = project(
        rows_of([last]), piece_rows, by_step([last]), acc, block_rows, head_width
    )

    back = WINDOW - 1
    stacked = kv_rows.reshape(size, TOK_DEV, 2 * HD)
    kv_true = stacked[jnp.arange(size - back, size) ^ place].reshape(back * TOK_DEV, 2 * HD)
    halo = shifted(kv_true, "seq", size)
    kv_home = jnp.stack([stacked[0]] + [swapped(stacked[m], "seq", m) for m in range(1, size)])
    kv_home = kv_home[jnp.arange(size) ^ place]
    key_out = jnp.concatenate([kv_home[k][:, :HD] for k in range(size)], 1)
    value_out = jnp.concatenate([kv_home[k][:, HD:] for k in range(size)], 1)

    doc_starts = (jnp.cumsum(doc_lengths) - doc_lengths).astype(jnp.int32)
    context = attend(where, doc_starts, query_rows, kv_rows, halo)

    from_c = swapped(context, "seq", 2)
    from_b, from_d = swapped(context, "seq", 1), swapped(from_c, "seq", 1)
    contexts = (context, from_b, from_c, from_d)

    def delivered(some):
        pieces = deliver(where, contexts, [chain_o[r] for r in some])
        pieces = [pieces[0]] + [swapped(pieces[m], "seq", m) for m in range(1, size)]
        pieces = [v.reshape(len(some), block_rows, TOK_DEV) for v in pieces]
        return jnp.stack([v[i] for i in range(len(some)) for v in pieces])

    early, late = delivered(steps), delivered([last])
    at = in_order // size
    rank_of = jnp.where(at == last, planes - 1, at - (at > last))
    ready = rank_of * size + in_order % size
    here, there = ready[:half_blocks], ready[half_blocks:]
    limit = (planes - 1) * size
    sure = limit - half_blocks

    def ranks(slots):
        soon = slots < limit
        ahead = jnp.cumsum(soon) - 1
        behind = jnp.sum(soon) + jnp.cumsum(~soon) - 1
        return jnp.where(soon, ahead, behind).astype(jnp.int32)

    going = ranks(there)
    among = jnp.arange(half_blocks, dtype=jnp.int32)
    going_order = jnp.sum(jnp.where(going[None, :] == among[:, None], there[None, :], 0), axis=1)
    got_early = swapped(early[going_order[:sure]], "tp", 1)
    shares = jnp.concatenate([early, late], 0)
    got_late = swapped(shares[going_order[sure:]], "tp", 1)
    other = jnp.concatenate([got_early, got_late], 0)[ranks(here)]
    total = shares[here].astype(jnp.float32) + other.astype(jnp.float32)
    mixed = jnp.transpose(total.astype(jnp.bfloat16).reshape(local_features, TOK_DEV))
    return (mixed, key_out, value_out)


def solution(mesh):
    in_specs = (P("seq", "tp"), P("seq"), P(), P(), P(), P("seq", "tp"), P("seq", "tp"))
    out_specs = (P("seq", "tp"), P("seq", "tp"), P("seq", "tp"))
    size = KV_HEADS // mesh.shape["tp"]
    by_planes = size == WINDOW and mesh.shape["tp"] == 2 and mesh.shape["seq"] == WINDOW * size
    body = plane_body if by_planes else gathered_body
    return jax.shard_map(body, mesh=mesh, in_specs=in_specs, out_specs=out_specs, check_vma=False)
```

```python
import jax
import jax.numpy as jnp
from jax import lax
from jax.experimental import pallas as pl
from jax.experimental.pallas import tpu as pltpu
from jax.sharding import PartitionSpec as P

D = 5120
KV_HEADS = 8
HD = 128
HEADS = 24
WINDOW = 4
TOK_DEV = 256


EPSILON = 1e-06
NEG_LARGE = -1e30


def carried_in(value, axis, join, neutral):
    count, mine = (lax.axis_size(axis), lax.axis_index(axis))
    pieces = lax.all_gather(value, axis)
    total = jnp.full_like(value, 0) + jnp.asarray(neutral, value.dtype)

    def turn(position, total):
        longer = join(total, pieces[position])
        return jnp.where(position < mine, longer, total)

    return lax.fori_loop(0, count - 1, turn, total)


def shifted(x, axis, by):
    count = lax.axis_size(axis)
    pairs = [(i, i + by) for i in range(count) if 0 <= i + by < count]
    return lax.ppermute(x, axis, pairs)


def gathered_body(rollout_rows, live_rows, doc_lengths, block_owner, norm_gain, qkv_weight, out_weight):
    half_rows = TOK_DEV // 2
    seq_index = lax.axis_index("seq")

    def combine(earlier, later):
        return earlier + later

    before = carried_in(live_rows, "seq", combine, jnp.zeros_like(live_rows))
    spilled_in = before[0] - seq_index * TOK_DEV
    tail_rows = lax.dynamic_slice_in_dim(rollout_rows, live_rows[0] - half_rows, half_rows, 0)
    arrived = shifted(tail_rows, "seq", 1)
    joined = jnp.concatenate([arrived, rollout_rows], 0)
    owned = lax.dynamic_slice_in_dim(joined, half_rows - spilled_in, TOK_DEV, 0)
    full_rows = lax.all_gather(owned, "tp", axis=1, tiled=True)
    values_f = full_rows.astype(jnp.float32)
    scale = lax.rsqrt(jnp.mean(values_f * values_f, axis=-1, keepdims=True) + EPSILON)
    normed = (values_f * scale * norm_gain.astype(jnp.float32)).astype(jnp.bfloat16)
    block_rows = qkv_weight.shape[0]
    block_count = D // block_rows
    permuted = normed.reshape(TOK_DEV, block_count, block_rows)[:, block_owner, :].reshape(
        TOK_DEV, D
    )
    positions = jnp.arange(block_count, dtype=jnp.int32)
    inverse = jnp.sum(
        jnp.where(block_owner[None, :] == positions[:, None], positions[None, :], 0), axis=1
    )
    projected = jnp.dot(
        permuted,
        lax.all_gather(qkv_weight, "seq", axis=0, tiled=True),
        preferred_element_type=jnp.float32,
    )
    group = HEADS // KV_HEADS
    kv_local = projected.shape[1] // ((group + 2) * HD)
    q_width = kv_local * group * HD
    query_rows = (projected[:, :q_width] * HD ** (-0.5)).astype(jnp.bfloat16)
    key_rows = projected[:, q_width : q_width + kv_local * HD].astype(jnp.bfloat16)
    value_rows = projected[:, q_width + kv_local * HD :].astype(jnp.bfloat16)
    queries = query_rows.reshape(TOK_DEV, kv_local, group, HD)
    query_pos = seq_index * TOK_DEV + jnp.arange(TOK_DEV, dtype=jnp.int32)
    doc_starts = jnp.cumsum(doc_lengths) - doc_lengths
    first_pos = jnp.max(
        jnp.where(doc_starts[None, :] <= query_pos[:, None], doc_starts[None, :], 0), axis=1
    )
    initial = (
        jnp.full((kv_local, group, TOK_DEV), NEG_LARGE, jnp.float32),
        jnp.zeros((kv_local, group, TOK_DEV), jnp.float32),
        jnp.zeros((kv_local, group, TOK_DEV, HD), jnp.float32),
    )
    keys_all, values_all = (key_rows, value_rows)
    for level in range(WINDOW.bit_length() - 1):
        got_keys, got_values = shifted((keys_all, values_all), "seq", 1 << level)
        keys_all = jnp.concatenate([got_keys, keys_all], 0)
        values_all = jnp.concatenate([got_values, values_all], 0)
    state = initial
    for block in range(WINDOW):
        keys_block = keys_all[block * TOK_DEV : (block + 1) * TOK_DEV]
        attend_best, attend_totals, attend_accum = state
        key_count = keys_block.shape[0]
        keys_three = keys_block.reshape(key_count, kv_local, HD)
        values_three = values_all[block * TOK_DEV : (block + 1) * TOK_DEV].reshape(
            key_count, kv_local, HD
        )
        scores = jnp.einsum(
            "tgjd,sgd->gjts", queries, keys_three, preferred_element_type=jnp.float32
        )
        key_pos = (seq_index - WINDOW + 1 + block) * TOK_DEV + jnp.arange(
            key_count, dtype=jnp.int32
        )
        allowed = (key_pos[None, :] <= query_pos[:, None]) & (
            key_pos[None, :] >= first_pos[:, None]
        )
        masked = jnp.where(allowed, scores, NEG_LARGE)
        newest = jnp.maximum(attend_best, jnp.max(masked, axis=-1))
        rescale = jnp.exp(attend_best - newest)
        weights = jnp.where(allowed, jnp.exp(masked - newest[..., None]), 0.0)
        attend_totals = attend_totals * rescale + jnp.sum(weights, axis=-1)
        update = jnp.einsum(
            "gjts,sgd->gjtd",
            weights.astype(jnp.bfloat16),
            values_three,
            preferred_element_type=jnp.float32,
        )
        attend_accum = attend_accum * rescale[..., None] + update
        state = (newest, attend_totals, attend_accum)
    _, totals, accum = state
    context = (
        jnp.transpose(accum / totals[..., None], (2, 0, 1, 3))
        .reshape(TOK_DEV, q_width)
        .astype(jnp.bfloat16)
    )
    delivered = lax.dot_general(
        context,
        lax.all_gather(out_weight, "seq", axis=0, tiled=True),
        (((1,), (1,)), ((), ())),
        preferred_element_type=jnp.float32,
    )
    partial_value = delivered.reshape(TOK_DEV, block_count, block_rows)[:, inverse, :].reshape(
        TOK_DEV, D
    )
    mixed = lax.psum_scatter(
        partial_value.astype(jnp.bfloat16).astype(jnp.float32).astype(jnp.bfloat16),
        "tp",
        scatter_dimension=1,
        tiled=True,
    )
    return (mixed, key_rows, value_rows)


LANES = 128


def swapped(x, axis, bit):
    count = lax.axis_size(axis)
    return lax.ppermute(x, axis, [(i, i ^ bit) for i in range(count)])


def turned(x, axis, by):
    count = lax.axis_size(axis)
    return lax.ppermute(x, axis, [(i, (i + by) % count) for i in range(count)])


def pick(stacked, index):
    return lax.dynamic_index_in_dim(stacked, index, 0, keepdims=False)


def three_away(x, size):
    up = turned(x, "seq", size)
    down = turned(x, "seq", -size)
    return {0: x, 1: up, 3: down, 2: turned(up, "seq", size)}


def scratch_limit(*arrays):
    total = sum(v.size * v.dtype.itemsize for v in arrays)
    return total + total // 8 + 6 * 1024 * 1024


def project_kernel(layout, table, place_ref, *refs, rows, block_rows, window, first):
    pieces, weights = layout
    groups = len(pieces)
    x_refs, refs = refs[: sum(pieces)], refs[sum(pieces) :]
    w_refs, refs = refs[: len(weights)], refs[len(weights) :]
    if first:
        acc_out, xs, ws, x_sem, w_sem = refs
    else:
        acc_in, q_out, kv_out, halo_out, xs, ws, x_sem, w_sem = refs
    spots = [(ref, part) for ref, parts in zip(w_refs, weights) for part in range(parts)]

    def weight_copy(i, ref, part):
        at = pl.multiple_of(i * window + table[i, 2], 64)
        return pltpu.make_async_copy(
            ref.at[pl.ds(part * block_rows, block_rows), :],
            ws.at[pl.ds(at, block_rows), :],
            w_sem.at[i],
        )

    for i, (ref, part) in enumerate(spots):
        weight_copy(i, ref, part).start()
    for m in range(groups):
        for i in range(len(spots)):
            piece, start = table[i, 0], pl.multiple_of(table[i, 1], LANES)
            for p in range(pieces[0]):

                @pl.when(piece == p)
                def _():
                    pltpu.make_async_copy(
                        x_refs[m * pieces[0] + p].at[:, pl.ds(start, window)],
                        xs.at[pl.ds(m * rows, rows), pl.ds(i * window, window)],
                        x_sem.at[m],
                    ).start()

    pad = window - block_rows
    for i, (ref, part) in enumerate(spots):
        weight_copy(i, ref, part).wait()
        spare = pl.multiple_of(i * window + jnp.where(table[i, 2] == 0, block_rows, 0), 64)
        ws[pl.ds(spare, pad), :] = jnp.zeros((pad, ws.shape[1]), ws.dtype)

    def one(m, carry):
        at = pl.ds(pl.multiple_of(m * rows, rows), rows)
        pltpu.make_async_copy(xs.at[at, :], xs.at[at, :], x_sem.at[m]).wait()
        total = jnp.dot(xs[at, :], ws[...], preferred_element_type=jnp.float32)
        if first:
            acc_out[at, :] = total
        else:
            total = total + acc_in[at, :]
            width = q_out.shape[1]
            q_out[at, :] = (total[:, :width] * HD ** (-0.5)).astype(q_out.dtype)
            kv = total[:, width:].astype(kv_out.dtype)
            block = place_ref[0] ^ m
            kv_out[pl.ds(pl.multiple_of(block * rows, rows), rows), :] = kv
            skipped = groups - halo_out.shape[0] // rows

            @pl.when(block >= skipped)
            def _():
                halo_out[pl.ds(pl.multiple_of((block - skipped) * rows, rows), rows), :] = kv

        return carry

    lax.fori_loop(0, groups, one, 0)


def project(table, where, piece_rows, weights, acc, block_rows, head_width):
    groups, pieces = len(piece_rows), len(piece_rows[0])
    rows = piece_rows[0][0].shape[0]
    parts = [w.shape[0] // block_rows for w in weights]
    count, columns = sum(parts), weights[0].shape[1]
    window = -(-(block_rows + LANES // 2) // LANES) * LANES
    total = groups * rows
    first = acc is None
    kernel = lambda table, place, *refs: project_kernel(
        ([pieces] * groups, parts),
        table,
        place,
        *refs,
        rows=rows,
        block_rows=block_rows,
        window=window,
        first=first,
    )
    scalar = pl.BlockSpec(memory_space=pltpu.SMEM)
    anywhere, local = pl.BlockSpec(memory_space=pl.ANY), pl.BlockSpec(memory_space=pltpu.VMEM)
    acc_shape = jax.ShapeDtypeStruct((total, columns), jnp.float32)
    x_shape = jax.ShapeDtypeStruct((total, count * window), jnp.bfloat16)
    w_shape = jax.ShapeDtypeStruct((count * window, columns), jnp.bfloat16)
    if first:
        shapes, outs = acc_shape, local
    else:
        side = columns - head_width
        shapes = (
            jax.ShapeDtypeStruct((total, head_width), jnp.bfloat16),
            jax.ShapeDtypeStruct((total, side), jnp.bfloat16),
            jax.ShapeDtypeStruct(((WINDOW - 1) * TOK_DEV, side), jnp.bfloat16),
        )
        outs = (local,) * 3
    flops = 2 * total * count * window * columns
    moved = count * (total * window + block_rows * columns) * 2 + total * columns * 4
    return pl.pallas_call(
        kernel,
        out_shape=shapes,
        in_specs=[scalar, scalar]
        + [anywhere] * (groups * pieces + len(weights))
        + ([] if first else [local]),
        out_specs=outs,
        scratch_shapes=[
            pltpu.VMEM(x_shape.shape, jnp.bfloat16),
            pltpu.VMEM(w_shape.shape, jnp.bfloat16),
            pltpu.SemaphoreType.DMA((groups,)),
            pltpu.SemaphoreType.DMA((count,)),
        ],
        cost_estimate=pl.CostEstimate(flops=flops, bytes_accessed=moved, transcendentals=0),
        compiler_params=pltpu.CompilerParams(
            vmem_limit_bytes=scratch_limit(x_shape, w_shape, acc_shape, acc_shape)
        ),
        name="project_first" if first else "project_last",
    )(table, where, *[v for row in piece_rows for v in row], *weights, *([] if first else [acc]))


def attend_kernel(place_ref, starts_ref, q_ref, keys_ref, *refs, own):
    if own:
        stat_ref, acc_ref = refs
    else:
        stat_in, acc_in, out_ref = refs
    size = q_ref.shape[0] // TOK_DEV
    back = WINDOW - 1
    heads = q_ref.shape[1] // HD
    place, plane = place_ref[0], place_ref[1]

    def one(m, carry):
        block = place ^ m
        base = (plane * size + block) * TOK_DEV
        rows = pl.ds(pl.multiple_of(m * TOK_DEV, TOK_DEV), TOK_DEV)
        query_pos = base + lax.broadcasted_iota(jnp.int32, (TOK_DEV, 1), 0)
        first_pos = jnp.zeros((TOK_DEV, 1), jnp.int32)
        lowest = jnp.int32(0)
        for d in range(starts_ref.shape[0]):
            start = starts_ref[d]
            first_pos = jnp.where(start <= query_pos, jnp.maximum(first_pos, start), first_pos)
            lowest = jnp.where(start <= base, jnp.maximum(lowest, start), lowest)
        earliest = jnp.clip(lowest // TOK_DEV - (plane * size + block - back), 0, back)
        middle = jnp.maximum(back - block, 0)

        def step(w, state):
            at = (block + w) * TOK_DEV - (back * TOK_DEV if own else 0)
            at = pl.ds(pl.multiple_of(at, TOK_DEV), TOK_DEV)
            key_pos = base + (w - back) * TOK_DEV + lax.broadcasted_iota(
                jnp.int32, (1, TOK_DEV), 1
            )
            allowed = (key_pos <= query_pos) & (key_pos >= first_pos)
            key_block, value_block = keys_ref[at, :HD], keys_ref[at, HD:]
            after = []
            for h in range(heads):
                best, norm, accum = state[h]
                scores = lax.dot_general(
                    q_ref[rows, h * HD : (h + 1) * HD],
                    key_block,
                    (((1,), (1,)), ((), ())),
                    preferred_element_type=jnp.float32,
                )
                masked = jnp.where(allowed, scores, NEG_LARGE)
                newest = jnp.maximum(best, jnp.max(masked, axis=-1, keepdims=True))
                rescale = jnp.exp(best - newest)
                weights = jnp.where(allowed, jnp.exp(masked - newest), 0.0)
                norm = norm * rescale + jnp.sum(weights, axis=-1, keepdims=True)
                accum = accum * rescale + jnp.dot(
                    weights.astype(jnp.bfloat16), value_block, preferred_element_type=jnp.float32
                )
                after.append((newest, norm, accum))
            return tuple(after)

        if own:
            begin, end = jnp.maximum(earliest, middle), WINDOW
            state = tuple(
                (
                    jnp.full((TOK_DEV, 1), NEG_LARGE, jnp.float32),
                    jnp.zeros((TOK_DEV, 1), jnp.float32),
                    jnp.zeros((TOK_DEV, HD), jnp.float32),
                )
                for _ in range(heads)
            )
        else:
            begin, end = jnp.minimum(earliest, middle), middle
            state = tuple(
                (
                    stat_in[rows, 2 * h : 2 * h + 1],
                    stat_in[rows, 2 * h + 1 : 2 * h + 2],
                    acc_in[rows, h * HD : (h + 1) * HD],
                )
                for h in range(heads)
            )
        state = lax.fori_loop(begin, end, step, state)
        for h in range(heads):
            best, norm, accum = state[h]
            cols = pl.ds(h * HD, HD)
            if own:
                stat_ref[rows, 2 * h : 2 * h + 1] = best
                stat_ref[rows, 2 * h + 1 : 2 * h + 2] = norm
                acc_ref[rows, cols] = accum
            else:
                out_ref[rows, cols] = (accum / norm).astype(out_ref.dtype)
        return carry

    lax.fori_loop(0, size, one, 0)


def attend(where, doc_starts, query_rows, keys, state):
    rows, width = query_rows.shape
    own = state is None
    scalar, local = pl.BlockSpec(memory_space=pltpu.SMEM), pl.BlockSpec(memory_space=pltpu.VMEM)
    stat = jax.ShapeDtypeStruct((rows, LANES), jnp.float32)
    accum = jax.ShapeDtypeStruct((rows, width), jnp.float32)
    out = jax.ShapeDtypeStruct((rows, width), jnp.bfloat16)
    blocks = WINDOW * WINDOW // 2
    return pl.pallas_call(
        lambda *refs: attend_kernel(*refs, own=own),
        out_shape=(stat, accum) if own else out,
        in_specs=[scalar, scalar, local, local] + ([] if own else [local, local]),
        out_specs=(local, local) if own else local,
        cost_estimate=pl.CostEstimate(
            flops=4 * blocks * TOK_DEV * width * TOK_DEV,
            bytes_accessed=8 * rows * width,
            transcendentals=blocks * TOK_DEV * TOK_DEV * width // HD,
        ),
        compiler_params=pltpu.CompilerParams(
            vmem_limit_bytes=scratch_limit(query_rows, keys, stat, accum, out, accum)
        ),
        name="attend_own" if own else "attend_halo",
    )(where, doc_starts, query_rows, keys, *([] if own else state))


def deliver_kernel(place_ref, *refs, size, steps, whole):
    if whole:
        (context_ref,), refs = refs[:1], refs[1:]
    else:
        contexts, refs = refs[:size], refs[size:]
    weights, refs = refs[:steps], refs[steps:]
    outs, refs = refs[:size], refs[size:]
    if whole:
        ws, w_sem = refs
    else:
        context_ref, ws, w_sem, c_sem = refs
    rows = weights[0].shape[0]
    copies = [
        pltpu.make_async_copy(weights[i], ws.at[pl.ds(i * rows, rows), :], w_sem.at[i])
        for i in range(steps)
    ]
    if not whole:
        width = contexts[0].shape[1]
        for m in range(size):
            for other in range(size):
                at = pl.multiple_of((place_ref[0] ^ other) * width, LANES)
                copies.append(
                    pltpu.make_async_copy(
                        contexts[other].at[pl.ds((m ^ other) * TOK_DEV, TOK_DEV), :],
                        context_ref.at[pl.ds(m * TOK_DEV, TOK_DEV), pl.ds(at, width)],
                        c_sem.at[m * size + other],
                    )
                )
    for copy in copies:
        copy.start()
    for copy in copies:
        copy.wait()
    for m in range(size):
        outs[m][...] = lax.dot_general(
            ws[...],
            context_ref[m * TOK_DEV : (m + 1) * TOK_DEV, :],
            (((1,), (1,)), ((), ())),
            preferred_element_type=jnp.float32,
        ).astype(outs[m].dtype)


def deliver(where, contexts, weights):
    steps, (rows, columns) = len(weights), weights[0].shape
    whole = len(contexts) == 1
    size = WINDOW
    total = contexts[0].shape[0]
    scalar = pl.BlockSpec(memory_space=pltpu.SMEM)
    anywhere, local = pl.BlockSpec(memory_space=pl.ANY), pl.BlockSpec(memory_space=pltpu.VMEM)
    part = jax.ShapeDtypeStruct((steps * rows, TOK_DEV), jnp.bfloat16)
    context = jax.ShapeDtypeStruct((total, columns), jnp.bfloat16)
    w_shape = jax.ShapeDtypeStruct((steps * rows, columns), jnp.bfloat16)
    scratch = [pltpu.VMEM(w_shape.shape, jnp.bfloat16), pltpu.SemaphoreType.DMA((steps,))]
    if not whole:
        scratch.append(pltpu.SemaphoreType.DMA((size * size,)))
    return pl.pallas_call(
        lambda *refs: deliver_kernel(*refs, size=size, steps=steps, whole=whole),
        out_shape=(part,) * size + (() if whole else (context,)),
        in_specs=[scalar] + [local if whole else anywhere] * len(contexts) + [anywhere] * steps,
        out_specs=(local,) * (size if whole else size + 1),
        scratch_shapes=scratch,
        cost_estimate=pl.CostEstimate(
            flops=2 * total * columns * steps * rows,
            bytes_accessed=2 * (total * columns + steps * rows * (columns + total)),
            transcendentals=0,
        ),
        compiler_params=pltpu.CompilerParams(
            vmem_limit_bytes=scratch_limit(context, w_shape, *[part] * (3 * size))
        ),
    )(where, *contexts, *weights)


def fetch(table, k, sources, target, sem):
    rows = target.shape[0]
    low = 0
    for group in sources:
        units = group[0].shape[0] // rows
        for m, ref in enumerate(group):
            inside = (table[k, 0] == m) & (table[k, 1] >= low) & (table[k, 1] < low + units)

            @pl.when(inside)
            def _():
                at = pl.multiple_of((table[k, 1] - low) * rows, 32)
                pltpu.make_async_copy(ref.at[pl.ds(at, rows), :], target, sem).start()

        low += units


def choose(table, sources, rows):
    count = table.shape[0]
    groups = [len(group) for group in sources]

    def kernel(table_ref, *refs):
        refs, (out, sem) = list(refs[:-2]), refs[-2:]
        split = [[refs.pop(0) for _ in range(n)] for n in groups]
        for k in range(count):
            fetch(table_ref, k, split, out.at[k], sem.at[k])
        for k in range(count):
            pltpu.make_async_copy(out.at[k], out.at[k], sem.at[k]).wait()

    shape = jax.ShapeDtypeStruct((count, rows, TOK_DEV), jnp.bfloat16)
    flat = [v for group in sources for v in group]
    return pl.pallas_call(
        kernel,
        out_shape=shape,
        in_specs=[pl.BlockSpec(memory_space=pltpu.SMEM)]
        + [pl.BlockSpec(memory_space=pl.ANY)] * len(flat),
        out_specs=pl.BlockSpec(memory_space=pltpu.VMEM),
        scratch_shapes=[pltpu.SemaphoreType.DMA((count,))],
        cost_estimate=pl.CostEstimate(flops=0, bytes_accessed=4 * shape.size, transcendentals=0),
        compiler_params=pltpu.CompilerParams(vmem_limit_bytes=scratch_limit(shape, shape)),
    )(table, *flat)


def combine(table, ranks, sources, received, rows):
    count = table.shape[0]
    groups = [len(group) for group in sources]
    step = 640 // rows

    def kernel(table_ref, rank_ref, *refs):
        refs, (out, mine, theirs, sem, other_sem) = list(refs[:-5]), refs[-5:]
        split = [[refs.pop(0) for _ in range(n)] for n in groups]
        for k in range(count):
            fetch(table_ref, k, split, mine.at[k], sem.at[k])
            low = 0
            for ref in refs:
                units = ref.shape[0]
                inside = (rank_ref[k] >= low) & (rank_ref[k] < low + units)

                @pl.when(inside)
                def _():
                    pltpu.make_async_copy(
                        ref.at[rank_ref[k] - low], theirs.at[k], other_sem.at[k]
                    ).start()

                low += units
        for k in range(count):
            pltpu.make_async_copy(mine.at[k], mine.at[k], sem.at[k]).wait()
            pltpu.make_async_copy(theirs.at[k], theirs.at[k], other_sem.at[k]).wait()
        for k in range(0, count, step):
            some = [
                mine[k + i].astype(jnp.float32) + theirs[k + i].astype(jnp.float32)
                for i in range(step)
            ]
            total = jnp.concatenate(some, 0)
            out[:, k * rows : (k + step) * rows] = jnp.transpose(total).astype(out.dtype)

    shape = jax.ShapeDtypeStruct((TOK_DEV, count * rows), jnp.bfloat16)
    flat = [v for group in sources for v in group]
    return pl.pallas_call(
        kernel,
        out_shape=shape,
        in_specs=[pl.BlockSpec(memory_space=pltpu.SMEM)] * 2
        + [pl.BlockSpec(memory_space=pl.ANY)] * (len(flat) + len(received)),
        out_specs=pl.BlockSpec(memory_space=pltpu.VMEM),
        scratch_shapes=[
            pltpu.VMEM((count, rows, TOK_DEV), jnp.bfloat16),
            pltpu.VMEM((count, rows, TOK_DEV), jnp.bfloat16),
            pltpu.SemaphoreType.DMA((count,)),
            pltpu.SemaphoreType.DMA((count,)),
        ],
        cost_estimate=pl.CostEstimate(
            flops=shape.size, bytes_accessed=6 * shape.size, transcendentals=0
        ),
        compiler_params=pltpu.CompilerParams(vmem_limit_bytes=scratch_limit(shape, shape, shape, shape)),
        name="combine",
    )(table, ranks, *flat, *received)


def plane_body(*args):
    return plane_steps(*args)


def plane_steps(rollout_rows, live_rows, doc_lengths, block_owner, norm_gain, qkv_weight, out_weight):
    seq_count, seq_index = lax.axis_size("seq"), lax.axis_index("seq")
    tp_index = lax.axis_index("tp")
    block_rows, columns = qkv_weight.shape
    local_features = rollout_rows.shape[1]
    group = HEADS // KV_HEADS
    size = columns // ((group + 2) * HD)
    planes = seq_count // size
    place, plane = seq_index % size, seq_index // size
    where = jnp.stack([place, plane]).astype(jnp.int32)
    head_width = group * HD
    half_rows = TOK_DEV // 2

    q_width = size * head_width

    def columns_of(k):
        cuts = ((k * head_width, head_width), (q_width + k * HD, HD), (q_width + (size + k) * HD, HD))
        return jnp.concatenate(
            [lax.dynamic_slice_in_dim(qkv_weight, at, wide, 1) for at, wide in cuts], 1
        )

    below = sum(shifted(live_rows, "seq", k * size) for k in range(1, planes))
    own_columns = columns_of(place)
    chains = [three_away(own_columns, size)]
    pair = jnp.concatenate([below, live_rows])
    plane_pairs = [pair] + [swapped(pair, "seq", m) for m in range(1, size)]
    for m in (2, 3, 1):
        chains.append(swapped(columns_of(place ^ m), "seq", m))
    chains = [chains[0]] + [three_away(chains[k], size) for k in (3, 1, 2)]
    last = 2
    top = out_weight.shape[0] // 2
    chain_o = [three_away(out_weight[:top], size), three_away(out_weight[top:], size)]

    before = sum(
        v[0] + jnp.where((place ^ m) < place, v[1], 0) for m, v in enumerate(plane_pairs)
    )
    spilled_in = before - seq_index * TOK_DEV
    tail_rows = lax.dynamic_slice_in_dim(rollout_rows, live_rows[0] - half_rows, half_rows, 0)
    arrived = shifted(tail_rows, "seq", 1)
    joined = jnp.concatenate([arrived, rollout_rows], 0)
    values_f = joined.astype(jnp.float32)
    squares = jnp.sum(values_f * values_f, axis=-1)
    squares = squares + swapped(squares, "tp", 1)
    scale = lax.rsqrt(squares[:, None] / D + EPSILON)
    gain = lax.dynamic_slice_in_dim(norm_gain, tp_index * local_features, local_features, 0)
    at = half_rows - spilled_in
    values_f = lax.dynamic_slice_in_dim(joined, at, TOK_DEV, 0).astype(jnp.float32)
    scale = lax.dynamic_slice_in_dim(scale, at, TOK_DEV, 0)
    normed = (values_f * scale * gain.astype(jnp.float32)).astype(jnp.bfloat16)

    cut = local_features // 2
    h1, h2 = normed[:, :cut], normed[:, cut:]
    x1, y2 = swapped(h1, "tp", 1), swapped(h2, "seq", 2)
    x2, y1 = swapped(h2, "tp", 1), swapped(h1, "seq", 2)
    yx2, xy1 = swapped(y2, "tp", 1), swapped(x1, "seq", 2)
    rows_a, rows_c = [h1, h2, x1, x2], [y1, y2, xy1, yx2]
    rows_b = [swapped(v, "seq", 1) for v in rows_a]
    rows_d = [swapped(v, "seq", 1) for v in rows_c]
    piece_rows = (rows_a, rows_b, rows_c, rows_d)

    numbers = jnp.arange(seq_count, dtype=jnp.int32)
    inverse = jnp.sum(
        jnp.where(block_owner[None, :] == numbers[:, None], numbers[None, :], 0), axis=1
    )
    half_blocks = local_features // block_rows

    def slot(blocks):
        source = inverse[blocks]
        step = (plane - source // size) % planes
        return step * size + ((source % size) ^ place)

    in_order = slot((numbers + tp_index * half_blocks) % seq_count)
    true_of = jnp.sum(
        jnp.where(in_order[None, :] == numbers[:, None], numbers[None, :], 0), axis=1
    )
    per_piece = cut // block_rows
    inside = (true_of % per_piece) * block_rows
    table = jnp.stack([true_of // per_piece, inside // LANES * LANES, inside % LANES], 1)

    steps = [r for r in range(planes) if r != last]
    by_step = lambda some: [c[r] for r in some for c in chains]
    rows_of = lambda some: jnp.concatenate([table[r * size : (r + 1) * size] for r in some], 0)
    acc = project(rows_of(steps), where, piece_rows, by_step(steps), None, block_rows, head_width)
    query_rows, kv_rows, kv_last = project(
        rows_of([last]), where, piece_rows, by_step([last]), acc, block_rows, head_width
    )

    halo = shifted(kv_last, "seq", size)
    stacked = kv_rows.reshape(size, TOK_DEV, 2 * HD)
    kv_home = jnp.stack(
        [pick(stacked, place)]
        + [swapped(pick(stacked, place ^ m), "seq", m) for m in range(1, size)]
    )
    kv_home = kv_home[jnp.arange(size) ^ place]
    key_out = jnp.concatenate([kv_home[k][:, :HD] for k in range(size)], 1)
    value_out = jnp.concatenate([kv_home[k][:, HD:] for k in range(size)], 1)

    doc_starts = (jnp.cumsum(doc_lengths) - doc_lengths).astype(jnp.int32)
    state = attend(where, doc_starts, query_rows, kv_rows, None)
    context = attend(where, doc_starts, query_rows, halo, state)

    from_c = swapped(context, "seq", 2)
    from_b = swapped(context, "seq", 1)
    from_d = swapped(from_c, "seq", 1)
    contexts = (context, from_b, from_c, from_d)

    def delivered(given, weights):
        pieces = deliver(where, given, weights)
        home = [pieces[0]] + [swapped(pieces[m], "seq", m) for m in range(1, size)]
        return home, pieces[size:]

    early, whole = delivered(contexts, [c[r] for r in steps for c in chain_o])
    mid, _ = delivered(whole, [chain_o[0][last]])
    late, _ = delivered(whole, [chain_o[1][last]])

    rows = block_rows // 2
    step, spot = in_order // size, in_order % size
    step = jnp.where(step == last, planes - 1, step - (step > last))
    units = jnp.stack([jnp.repeat(spot, 2), (2 * step[:, None] + jnp.arange(2)).reshape(-1)], 1)
    count = 2 * half_blocks
    here, there = units[:count], units[count:]
    among = jnp.arange(count, dtype=jnp.int32)
    early_units = 2 * (planes - 1)

    def ranks(part):
        key = jnp.maximum(part[:, 1] - early_units + 1, 0) * count + among
        return jnp.sum((key[None, :] < key[:, None]).astype(jnp.int32), axis=1)

    hit = ranks(there)[None, :] == among[:, None]
    going = jnp.sum(jnp.where(hit[:, :, None], there[None, :, :], 0), axis=1).astype(jnp.int32)
    first, second = count - 2 * size, count - size
    cuts = (
        (going[:first], (early,)),
        (going[first:second], (early, mid)),
        (going[second:], (early, mid, late)),
    )
    received = [swapped(choose(part, sources, rows), "tp", 1) for part, sources in cuts]
    mixed = combine(here.astype(jnp.int32), ranks(here), (early, mid, late), received, rows)
    return (mixed, key_out, value_out)


def solution(mesh):
    in_specs = (P("seq", "tp"), P("seq"), P(), P(), P(), P("seq", "tp"), P("seq", "tp"))
    out_specs = (P("seq", "tp"), P("seq", "tp"), P("seq", "tp"))
    size = KV_HEADS // mesh.shape["tp"]
    by_planes = size == WINDOW and mesh.shape["tp"] == 2 and mesh.shape["seq"] == WINDOW * size
    body = plane_body if by_planes else gathered_body
    return jax.shard_map(body, mesh=mesh, in_specs=in_specs, out_specs=out_specs, check_vma=False)
```

```python
import jax
import jax.numpy as jnp
from jax import lax
from jax.experimental import pallas as pl
from jax.experimental.pallas import tpu as pltpu
from jax.sharding import PartitionSpec as P

D = 5120
KV_HEADS = 8
HD = 128
HEADS = 24
WINDOW = 4
TOK_DEV = 256


EPSILON = 1e-06
NEG_LARGE = -1e30


def carried_in(value, axis, join, neutral):
    count, mine = (lax.axis_size(axis), lax.axis_index(axis))
    pieces = lax.all_gather(value, axis)
    total = jnp.full_like(value, 0) + jnp.asarray(neutral, value.dtype)

    def turn(position, total):
        longer = join(total, pieces[position])
        return jnp.where(position < mine, longer, total)

    return lax.fori_loop(0, count - 1, turn, total)


def shifted(x, axis, by):
    count = lax.axis_size(axis)
    pairs = [(i, i + by) for i in range(count) if 0 <= i + by < count]
    return lax.ppermute(x, axis, pairs)


def gathered_body(rollout_rows, live_rows, doc_lengths, block_owner, norm_gain, qkv_weight, out_weight):
    half_rows = TOK_DEV // 2
    seq_index = lax.axis_index("seq")

    def combine(earlier, later):
        return earlier + later

    before = carried_in(live_rows, "seq", combine, jnp.zeros_like(live_rows))
    spilled_in = before[0] - seq_index * TOK_DEV
    tail_rows = lax.dynamic_slice_in_dim(rollout_rows, live_rows[0] - half_rows, half_rows, 0)
    arrived = shifted(tail_rows, "seq", 1)
    joined = jnp.concatenate([arrived, rollout_rows], 0)
    owned = lax.dynamic_slice_in_dim(joined, half_rows - spilled_in, TOK_DEV, 0)
    full_rows = lax.all_gather(owned, "tp", axis=1, tiled=True)
    values_f = full_rows.astype(jnp.float32)
    scale = lax.rsqrt(jnp.mean(values_f * values_f, axis=-1, keepdims=True) + EPSILON)
    normed = (values_f * scale * norm_gain.astype(jnp.float32)).astype(jnp.bfloat16)
    block_rows = qkv_weight.shape[0]
    block_count = D // block_rows
    permuted = normed.reshape(TOK_DEV, block_count, block_rows)[:, block_owner, :].reshape(
        TOK_DEV, D
    )
    positions = jnp.arange(block_count, dtype=jnp.int32)
    inverse = jnp.sum(
        jnp.where(block_owner[None, :] == positions[:, None], positions[None, :], 0), axis=1
    )
    projected = jnp.dot(
        permuted,
        lax.all_gather(qkv_weight, "seq", axis=0, tiled=True),
        preferred_element_type=jnp.float32,
    )
    group = HEADS // KV_HEADS
    kv_local = projected.shape[1] // ((group + 2) * HD)
    q_width = kv_local * group * HD
    query_rows = (projected[:, :q_width] * HD ** (-0.5)).astype(jnp.bfloat16)
    key_rows = projected[:, q_width : q_width + kv_local * HD].astype(jnp.bfloat16)
    value_rows = projected[:, q_width + kv_local * HD :].astype(jnp.bfloat16)
    queries = query_rows.reshape(TOK_DEV, kv_local, group, HD)
    query_pos = seq_index * TOK_DEV + jnp.arange(TOK_DEV, dtype=jnp.int32)
    doc_starts = jnp.cumsum(doc_lengths) - doc_lengths
    first_pos = jnp.max(
        jnp.where(doc_starts[None, :] <= query_pos[:, None], doc_starts[None, :], 0), axis=1
    )
    initial = (
        jnp.full((kv_local, group, TOK_DEV), NEG_LARGE, jnp.float32),
        jnp.zeros((kv_local, group, TOK_DEV), jnp.float32),
        jnp.zeros((kv_local, group, TOK_DEV, HD), jnp.float32),
    )
    keys_all, values_all = (key_rows, value_rows)
    for level in range(WINDOW.bit_length() - 1):
        got_keys, got_values = shifted((keys_all, values_all), "seq", 1 << level)
        keys_all = jnp.concatenate([got_keys, keys_all], 0)
        values_all = jnp.concatenate([got_values, values_all], 0)
    state = initial
    for block in range(WINDOW):
        keys_block = keys_all[block * TOK_DEV : (block + 1) * TOK_DEV]
        attend_best, attend_totals, attend_accum = state
        key_count = keys_block.shape[0]
        keys_three = keys_block.reshape(key_count, kv_local, HD)
        values_three = values_all[block * TOK_DEV : (block + 1) * TOK_DEV].reshape(
            key_count, kv_local, HD
        )
        scores = jnp.einsum(
            "tgjd,sgd->gjts", queries, keys_three, preferred_element_type=jnp.float32
        )
        key_pos = (seq_index - WINDOW + 1 + block) * TOK_DEV + jnp.arange(
            key_count, dtype=jnp.int32
        )
        allowed = (key_pos[None, :] <= query_pos[:, None]) & (
            key_pos[None, :] >= first_pos[:, None]
        )
        masked = jnp.where(allowed, scores, NEG_LARGE)
        newest = jnp.maximum(attend_best, jnp.max(masked, axis=-1))
        rescale = jnp.exp(attend_best - newest)
        weights = jnp.where(allowed, jnp.exp(masked - newest[..., None]), 0.0)
        attend_totals = attend_totals * rescale + jnp.sum(weights, axis=-1)
        update = jnp.einsum(
            "gjts,sgd->gjtd",
            weights.astype(jnp.bfloat16),
            values_three,
            preferred_element_type=jnp.float32,
        )
        attend_accum = attend_accum * rescale[..., None] + update
        state = (newest, attend_totals, attend_accum)
    _, totals, accum = state
    context = (
        jnp.transpose(accum / totals[..., None], (2, 0, 1, 3))
        .reshape(TOK_DEV, q_width)
        .astype(jnp.bfloat16)
    )
    delivered = lax.dot_general(
        context,
        lax.all_gather(out_weight, "seq", axis=0, tiled=True),
        (((1,), (1,)), ((), ())),
        preferred_element_type=jnp.float32,
    )
    partial_value = delivered.reshape(TOK_DEV, block_count, block_rows)[:, inverse, :].reshape(
        TOK_DEV, D
    )
    mixed = lax.psum_scatter(
        partial_value.astype(jnp.bfloat16).astype(jnp.float32).astype(jnp.bfloat16),
        "tp",
        scatter_dimension=1,
        tiled=True,
    )
    return (mixed, key_rows, value_rows)


LANES = 128


def swapped(x, axis, bit):
    count = lax.axis_size(axis)
    return lax.ppermute(x, axis, [(i, i ^ bit) for i in range(count)])


def turned(x, axis, by):
    count = lax.axis_size(axis)
    return lax.ppermute(x, axis, [(i, (i + by) % count) for i in range(count)])


def three_away(x, size):
    up = turned(x, "seq", size)
    down = turned(x, "seq", -size)
    return {0: x, 1: up, 3: down, 2: turned(up, "seq", size)}


def scratch_limit(*arrays):
    total = sum(v.size * v.dtype.itemsize for v in arrays)
    return total + total // 8 + 6 * 1024 * 1024


def project_kernel(layout, table, place_ref, *refs, rows, block_rows, window, first):
    pieces, weights = layout
    groups = len(pieces)
    x_refs, refs = refs[: sum(pieces)], refs[sum(pieces) :]
    w_refs, refs = refs[: len(weights)], refs[len(weights) :]
    if first:
        acc_out, xs, ws, x_sem, w_sem = refs
    else:
        acc_in, q_out, kv_out, halo_out, *homes, xs, ws, x_sem, w_sem = refs
    spots = [(ref, part) for ref, parts in zip(w_refs, weights) for part in range(parts)]

    def weight_copy(i, ref, part):
        at = pl.multiple_of(i * window + table[i, 2], 64)
        return pltpu.make_async_copy(
            ref.at[pl.ds(part * block_rows, block_rows), :],
            ws.at[pl.ds(at, block_rows), :],
            w_sem.at[i],
        )

    for i, (ref, part) in enumerate(spots):
        weight_copy(i, ref, part).start()
    for m in range(groups):
        for i in range(len(spots)):
            piece, start = table[i, 0], pl.multiple_of(table[i, 1], LANES)
            for p in range(pieces[0]):

                @pl.when(piece == p)
                def _():
                    pltpu.make_async_copy(
                        x_refs[m * pieces[0] + p].at[:, pl.ds(start, window)],
                        xs.at[pl.ds(m * rows, rows), pl.ds(i * window, window)],
                        x_sem.at[m],
                    ).start()

    pad = window - block_rows
    for i, (ref, part) in enumerate(spots):
        weight_copy(i, ref, part).wait()
        spare = pl.multiple_of(i * window + jnp.where(table[i, 2] == 0, block_rows, 0), 64)
        ws[pl.ds(spare, pad), :] = jnp.zeros((pad, ws.shape[1]), ws.dtype)

    def one(m, carry):
        at = pl.ds(pl.multiple_of(m * rows, rows), rows)
        pltpu.make_async_copy(xs.at[at, :], xs.at[at, :], x_sem.at[m]).wait()
        total = jnp.dot(xs[at, :], ws[...], preferred_element_type=jnp.float32)
        if first:
            acc_out[at, :] = total
        else:
            total = total + acc_in[at, :]
            width = q_out.shape[1]
            q_out[at, :] = (total[:, :width] * HD ** (-0.5)).astype(q_out.dtype)
            kv = total[:, width:].astype(kv_out.dtype)
            for other, home in enumerate(homes):

                @pl.when(m == other)
                def _():
                    home[...] = kv

            block = place_ref[0] ^ m
            kv_out[pl.ds(pl.multiple_of(block * rows, rows), rows), :] = kv
            skipped = groups - halo_out.shape[0] // rows

            @pl.when(block >= skipped)
            def _():
                halo_out[pl.ds(pl.multiple_of((block - skipped) * rows, rows), rows), :] = kv

        return carry

    lax.fori_loop(0, groups, one, 0)


def project(table, where, piece_rows, weights, acc, block_rows, head_width):
    groups, pieces = len(piece_rows), len(piece_rows[0])
    rows = piece_rows[0][0].shape[0]
    parts = [w.shape[0] // block_rows for w in weights]
    count, columns = sum(parts), weights[0].shape[1]
    window = -(-(block_rows + LANES // 2) // LANES) * LANES
    total = groups * rows
    first = acc is None
    kernel = lambda table, place, *refs: project_kernel(
        ([pieces] * groups, parts),
        table,
        place,
        *refs,
        rows=rows,
        block_rows=block_rows,
        window=window,
        first=first,
    )
    scalar = pl.BlockSpec(memory_space=pltpu.SMEM)
    anywhere, local = pl.BlockSpec(memory_space=pltpu.HBM), pl.BlockSpec(memory_space=pltpu.VMEM)
    acc_shape = jax.ShapeDtypeStruct((total, columns), jnp.float32)
    x_shape = jax.ShapeDtypeStruct((total, count * window), jnp.bfloat16)
    w_shape = jax.ShapeDtypeStruct((count * window, columns), jnp.bfloat16)
    if first:
        shapes, outs = acc_shape, local
    else:
        side = columns - head_width
        shapes = (
            jax.ShapeDtypeStruct((total, head_width), jnp.bfloat16),
            jax.ShapeDtypeStruct((total, side), jnp.bfloat16),
            jax.ShapeDtypeStruct(((WINDOW - 1) * TOK_DEV, side), jnp.bfloat16),
        ) + (jax.ShapeDtypeStruct((rows, side), jnp.bfloat16),) * groups
        outs = (local,) * (3 + groups)
    flops = 2 * total * count * window * columns
    moved = count * (total * window + block_rows * columns) * 2 + total * columns * 4
    return pl.pallas_call(
        kernel,
        out_shape=shapes,
        in_specs=[scalar, scalar]
        + [anywhere] * (groups * pieces + len(weights))
        + ([] if first else [local]),
        out_specs=outs,
        scratch_shapes=[
            pltpu.VMEM(x_shape.shape, jnp.bfloat16),
            pltpu.VMEM(w_shape.shape, jnp.bfloat16),
            pltpu.SemaphoreType.DMA((groups,)),
            pltpu.SemaphoreType.DMA((count,)),
        ],
        cost_estimate=pl.CostEstimate(flops=flops, bytes_accessed=moved, transcendentals=0),
        compiler_params=pltpu.CompilerParams(
            vmem_limit_bytes=scratch_limit(x_shape, w_shape, acc_shape, acc_shape)
        ),
        name="project_first" if first else "project_last",
    )(table, where, *[v for row in piece_rows for v in row], *weights, *([] if first else [acc]))


def attend_kernel(place_ref, starts_ref, q_ref, keys_ref, *refs, own):
    if own:
        stat_ref, acc_ref = refs
    else:
        stat_in, acc_in, out_ref = refs
    size = q_ref.shape[0] // TOK_DEV
    back = WINDOW - 1
    heads = q_ref.shape[1] // HD
    place, plane = place_ref[0], place_ref[1]

    def one(m, carry):
        block = place ^ m
        base = (plane * size + block) * TOK_DEV
        rows = pl.ds(pl.multiple_of(m * TOK_DEV, TOK_DEV), TOK_DEV)
        query_pos = base + lax.broadcasted_iota(jnp.int32, (1, TOK_DEV), 1)
        first_pos = jnp.zeros((1, TOK_DEV), jnp.int32)
        lowest = jnp.int32(0)
        for d in range(starts_ref.shape[0]):
            start = starts_ref[d]
            first_pos = jnp.where(start <= query_pos, jnp.maximum(first_pos, start), first_pos)
            lowest = jnp.where(start <= base, jnp.maximum(lowest, start), lowest)
        earliest = jnp.clip(lowest // TOK_DEV - (plane * size + block - back), 0, back)
        middle = jnp.maximum(back - block, 0)
        top = WINDOW - 1 if own else middle - 1

        def step(i, state):
            w = top - i
            at = (block + w) * TOK_DEV - (back * TOK_DEV if own else 0)
            at = pl.ds(pl.multiple_of(at, TOK_DEV), TOK_DEV)
            key_pos = base + (w - back) * TOK_DEV + lax.broadcasted_iota(
                jnp.int32, (TOK_DEV, 1), 0
            )
            allowed = (key_pos <= query_pos) & (key_pos >= first_pos)
            key_block, value_block = keys_ref[at, :HD], keys_ref[at, HD:]
            after = []
            for h in range(heads):
                best, norm, accum = state[h]
                scores = lax.dot_general(
                    key_block,
                    q_ref[rows, h * HD : (h + 1) * HD],
                    (((1,), (1,)), ((), ())),
                    preferred_element_type=jnp.float32,
                )
                masked = jnp.where(allowed, scores, NEG_LARGE)
                newest = jnp.maximum(best, jnp.max(masked, axis=0, keepdims=True))
                rescale = jnp.exp(best - newest)
                weights = jnp.exp(masked - newest)
                norm = norm * rescale + jnp.sum(weights, axis=0, keepdims=True)
                accum = accum * rescale + lax.dot_general(
                    value_block,
                    weights.astype(jnp.bfloat16),
                    (((0,), (0,)), ((), ())),
                    preferred_element_type=jnp.float32,
                )
                after.append((newest, norm, accum))
            return tuple(after)

        if own:
            count = WINDOW - jnp.maximum(earliest, middle)
            state = tuple(
                (
                    jnp.full((1, TOK_DEV), NEG_LARGE, jnp.float32),
                    jnp.zeros((1, TOK_DEV), jnp.float32),
                    jnp.zeros((HD, TOK_DEV), jnp.float32),
                )
                for _ in range(heads)
            )
        else:
            count = jnp.maximum(middle - earliest, 0)
            state = tuple(
                (
                    stat_in[2 * h : 2 * h + 1, rows],
                    stat_in[2 * h + 1 : 2 * h + 2, rows],
                    acc_in[h * HD : (h + 1) * HD, rows],
                )
                for h in range(heads)
            )
        state = lax.fori_loop(0, count, step, state)
        for h in range(heads):
            best, norm, accum = state[h]
            some = pl.ds(h * HD, HD)
            if own:
                stat_ref[2 * h : 2 * h + 1, rows] = best
                stat_ref[2 * h + 1 : 2 * h + 2, rows] = norm
                acc_ref[some, rows] = accum
            else:
                out_ref[some, rows] = (accum / norm).astype(out_ref.dtype)
        return carry

    lax.fori_loop(0, size, one, 0)


def attend(where, doc_starts, query_rows, keys, state):
    rows, width = query_rows.shape
    own = state is None
    scalar, local = pl.BlockSpec(memory_space=pltpu.SMEM), pl.BlockSpec(memory_space=pltpu.VMEM)
    stat = jax.ShapeDtypeStruct((2 * width // HD, rows), jnp.float32)
    accum = jax.ShapeDtypeStruct((width, rows), jnp.float32)
    out = jax.ShapeDtypeStruct((width, rows), jnp.bfloat16)
    blocks = WINDOW * WINDOW // 2
    return pl.pallas_call(
        lambda *refs: attend_kernel(*refs, own=own),
        out_shape=(stat, accum) if own else out,
        in_specs=[scalar, scalar, local, local] + ([] if own else [local, local]),
        out_specs=(local, local) if own else local,
        cost_estimate=pl.CostEstimate(
            flops=4 * blocks * TOK_DEV * width * TOK_DEV,
            bytes_accessed=8 * rows * width,
            transcendentals=blocks * TOK_DEV * TOK_DEV * width // HD,
        ),
        compiler_params=pltpu.CompilerParams(
            vmem_limit_bytes=scratch_limit(query_rows, keys, stat, accum, out, accum)
        ),
        name="attend_own" if own else "attend_halo",
    )(where, doc_starts, query_rows, keys, *([] if own else state))


def deliver_kernel(place_ref, *refs, size, steps, whole):
    if whole:
        (context_ref,), refs = refs[:1], refs[1:]
    else:
        contexts, refs = refs[:size], refs[size:]
    weights, refs = refs[:steps], refs[steps:]
    outs, refs = refs[:size], refs[size:]
    if whole:
        ws, w_sem = refs
    else:
        context_ref, ws, w_sem, c_sem = refs
    rows = weights[0].shape[0]
    copies = [
        pltpu.make_async_copy(weights[i], ws.at[pl.ds(i * rows, rows), :], w_sem.at[i])
        for i in range(steps)
    ]
    if not whole:
        width = contexts[0].shape[0]
        for m in range(size):
            for other in range(size):
                at = pl.multiple_of((place_ref[0] ^ other) * width, LANES)
                copies.append(
                    pltpu.make_async_copy(
                        contexts[other].at[:, pl.ds((m ^ other) * TOK_DEV, TOK_DEV)],
                        context_ref.at[pl.ds(at, width), pl.ds(m * TOK_DEV, TOK_DEV)],
                        c_sem.at[m * size + other],
                    )
                )
    for copy in copies:
        copy.start()
    for copy in copies:
        copy.wait()
    for m in range(size):
        outs[m][...] = jnp.dot(
            ws[...],
            context_ref[:, m * TOK_DEV : (m + 1) * TOK_DEV],
            preferred_element_type=jnp.float32,
        ).astype(outs[m].dtype)


def deliver(where, contexts, weights):
    steps, (rows, columns) = len(weights), weights[0].shape
    whole = len(contexts) == 1
    size = WINDOW
    total = contexts[0].shape[1]
    scalar = pl.BlockSpec(memory_space=pltpu.SMEM)
    anywhere, local = pl.BlockSpec(memory_space=pltpu.HBM), pl.BlockSpec(memory_space=pltpu.VMEM)
    part = jax.ShapeDtypeStruct((steps * rows, TOK_DEV), jnp.bfloat16)
    context = jax.ShapeDtypeStruct((columns, total), jnp.bfloat16)
    w_shape = jax.ShapeDtypeStruct((steps * rows, columns), jnp.bfloat16)
    scratch = [pltpu.VMEM(w_shape.shape, jnp.bfloat16), pltpu.SemaphoreType.DMA((steps,))]
    if not whole:
        scratch.append(pltpu.SemaphoreType.DMA((size * size,)))
    return pl.pallas_call(
        lambda *refs: deliver_kernel(*refs, size=size, steps=steps, whole=whole),
        out_shape=(part,) * size + (() if whole else (context,)),
        in_specs=[scalar] + [local if whole else anywhere] * len(contexts) + [anywhere] * steps,
        out_specs=(local,) * (size if whole else size + 1),
        scratch_shapes=scratch,
        cost_estimate=pl.CostEstimate(
            flops=2 * total * columns * steps * rows,
            bytes_accessed=2 * (total * columns + steps * rows * (columns + total)),
            transcendentals=0,
        ),
        compiler_params=pltpu.CompilerParams(
            vmem_limit_bytes=scratch_limit(context, w_shape, *[part] * (3 * size))
        ),
    )(where, *contexts, *weights)


def fetch(table, k, sources, target, sem):
    rows = target.shape[0]
    low = 0
    for group in sources:
        units = group[0].shape[0] // rows
        for m, ref in enumerate(group):
            inside = (table[k, 0] == m) & (table[k, 1] >= low) & (table[k, 1] < low + units)

            @pl.when(inside)
            def _():
                at = pl.multiple_of((table[k, 1] - low) * rows, 32)
                pltpu.make_async_copy(ref.at[pl.ds(at, rows), :], target, sem).start()

        low += units


def choose(table, sources, rows):
    count = table.shape[0]
    groups = [len(group) for group in sources]

    def kernel(table_ref, *refs):
        refs, (out, sem) = list(refs[:-2]), refs[-2:]
        split = [[refs.pop(0) for _ in range(n)] for n in groups]
        for k in range(count):
            fetch(table_ref, k, split, out.at[k], sem.at[k])
        for k in range(count):
            pltpu.make_async_copy(out.at[k], out.at[k], sem.at[k]).wait()

    shape = jax.ShapeDtypeStruct((count, rows, TOK_DEV), jnp.bfloat16)
    flat = [v for group in sources for v in group]
    return pl.pallas_call(
        kernel,
        out_shape=shape,
        in_specs=[pl.BlockSpec(memory_space=pltpu.SMEM)]
        + [pl.BlockSpec(memory_space=pltpu.HBM)] * len(flat),
        out_specs=pl.BlockSpec(memory_space=pltpu.VMEM),
        scratch_shapes=[pltpu.SemaphoreType.DMA((count,))],
        cost_estimate=pl.CostEstimate(flops=0, bytes_accessed=4 * shape.size, transcendentals=0),
        compiler_params=pltpu.CompilerParams(vmem_limit_bytes=scratch_limit(shape, shape)),
    )(table, *flat)


def combine(ranks, mine, received):
    count, rows = mine.shape[:2]
    step = 640 // rows

    def kernel(rank_ref, mine_ref, *refs):
        theirs, sem = refs[-2:]
        out, refs = refs[-3], refs[:-3]
        low = 0
        copies = []
        for i, ref in enumerate(refs):
            units = ref.shape[0]
            copies.append(pltpu.make_async_copy(ref, theirs.at[pl.ds(low, units)], sem.at[i]))
            low += units
        for copy in copies:
            copy.start()
        for copy in copies:
            copy.wait()
        for k in range(0, count, step):
            some = [
                mine_ref[k + i].astype(jnp.float32) + theirs[rank_ref[k + i]].astype(jnp.float32)
                for i in range(step)
            ]
            total = jnp.concatenate(some, 0)
            out[:, k * rows : (k + step) * rows] = jnp.transpose(total).astype(out.dtype)

    shape = jax.ShapeDtypeStruct((TOK_DEV, count * rows), jnp.bfloat16)
    local = pl.BlockSpec(memory_space=pltpu.VMEM)
    return pl.pallas_call(
        kernel,
        out_shape=shape,
        in_specs=[pl.BlockSpec(memory_space=pltpu.SMEM), local]
        + [pl.BlockSpec(memory_space=pltpu.HBM)] * len(received),
        out_specs=local,
        scratch_shapes=[
            pltpu.VMEM((count, rows, TOK_DEV), jnp.bfloat16),
            pltpu.SemaphoreType.DMA((len(received),)),
        ],
        cost_estimate=pl.CostEstimate(
            flops=shape.size, bytes_accessed=6 * shape.size, transcendentals=0
        ),
        compiler_params=pltpu.CompilerParams(vmem_limit_bytes=scratch_limit(shape, shape, shape)),
        name="combine",
    )(ranks, mine, *received)


def settle(where, pieces):
    size, rows = len(pieces), pieces[0].shape[0]

    def kernel(place_ref, *refs):
        key_out, value_out = refs[-2:]
        for m, ref in enumerate(refs[:-2]):
            at = pl.ds(pl.multiple_of((place_ref[0] ^ m) * HD, HD), HD)
            key_out[:, at] = ref[:, :HD]
            value_out[:, at] = ref[:, HD:]

    shape = jax.ShapeDtypeStruct((rows, size * HD), jnp.bfloat16)
    local = pl.BlockSpec(memory_space=pltpu.VMEM)
    return pl.pallas_call(
        kernel,
        out_shape=(shape, shape),
        in_specs=[pl.BlockSpec(memory_space=pltpu.SMEM)] + [local] * size,
        out_specs=(local, local),
        cost_estimate=pl.CostEstimate(flops=0, bytes_accessed=8 * shape.size, transcendentals=0),
        compiler_params=pltpu.CompilerParams(vmem_limit_bytes=scratch_limit(*[shape] * 6)),
        name="settle",
    )(where, *pieces)


def plane_body(*args):
    return plane_steps(*args)


def plane_steps(rollout_rows, live_rows, doc_lengths, block_owner, norm_gain, qkv_weight, out_weight):
    seq_count, seq_index = lax.axis_size("seq"), lax.axis_index("seq")
    tp_index = lax.axis_index("tp")
    block_rows, columns = qkv_weight.shape
    local_features = rollout_rows.shape[1]
    group = HEADS // KV_HEADS
    size = columns // ((group + 2) * HD)
    planes = seq_count // size
    place, plane = seq_index % size, seq_index // size
    where = jnp.stack([place, plane]).astype(jnp.int32)
    head_width = group * HD
    half_rows = TOK_DEV // 2

    q_width = size * head_width

    def columns_of(k):
        cuts = ((k * head_width, head_width), (q_width + k * HD, HD), (q_width + (size + k) * HD, HD))
        return jnp.concatenate(
            [lax.dynamic_slice_in_dim(qkv_weight, at, wide, 1) for at, wide in cuts], 1
        )

    live = jnp.broadcast_to(live_rows[None], (8, LANES))
    below = jnp.zeros_like(live)
    for k in range(1, planes):
        below = below + jnp.where(plane >= k, turned(live, "seq", k * size), 0)
    chains = [three_away(columns_of(place), size)]
    pair = jnp.where(lax.broadcasted_iota(jnp.int32, live.shape, 0) == 0, below, live)
    plane_pairs = [pair] + [swapped(pair, "seq", m) for m in range(1, size)]
    for m in (2, 3, 1):
        chains.append(swapped(columns_of(place ^ m), "seq", m))
    chains = [chains[0]] + [three_away(chains[k], size) for k in (3, 1, 2)]
    last = 2
    top = out_weight.shape[0] // 2
    chain_o = [three_away(out_weight[:top], size), three_away(out_weight[top:], size)]

    before = sum(
        v[0, 0] + jnp.where((place ^ m) < place, v[1, 0], 0) for m, v in enumerate(plane_pairs)
    )
    spilled_in = before - seq_index * TOK_DEV
    tail_rows = lax.dynamic_slice_in_dim(rollout_rows, live_rows[0] - half_rows, half_rows, 0)
    arrived = shifted(tail_rows, "seq", 1)
    joined = jnp.concatenate([arrived, rollout_rows], 0)
    values_f = joined.astype(jnp.float32)
    squares = jnp.sum(values_f * values_f, axis=-1)
    squares = squares + swapped(squares, "tp", 1)
    scale = lax.rsqrt(squares[:, None] / D + EPSILON)
    gain = lax.dynamic_slice_in_dim(norm_gain, tp_index * local_features, local_features, 0)
    at = half_rows - spilled_in
    values_f = lax.dynamic_slice_in_dim(joined, at, TOK_DEV, 0).astype(jnp.float32)
    scale = lax.dynamic_slice_in_dim(scale, at, TOK_DEV, 0)
    normed = (values_f * scale * gain.astype(jnp.float32)).astype(jnp.bfloat16)

    cut = local_features // 2
    h1, h2 = normed[:, :cut], normed[:, cut:]
    x1, y2 = swapped(h1, "tp", 1), swapped(h2, "seq", 2)
    x2, y1 = swapped(h2, "tp", 1), swapped(h1, "seq", 2)
    yx2, xy1 = swapped(y2, "tp", 1), swapped(x1, "seq", 2)
    rows_a, rows_c = [h1, h2, x1, x2], [y1, y2, xy1, yx2]
    rows_b = [swapped(v, "seq", 1) for v in rows_a]
    rows_d = [swapped(v, "seq", 1) for v in rows_c]
    piece_rows = (rows_a, rows_b, rows_c, rows_d)

    numbers = jnp.arange(seq_count, dtype=jnp.int32)
    inverse = jnp.sum(
        jnp.where(block_owner[None, :] == numbers[:, None], numbers[None, :], 0), axis=1
    )
    half_blocks = local_features // block_rows

    def slot(blocks):
        source = inverse[blocks]
        step = (plane - source // size) % planes
        return step * size + ((source % size) ^ place)

    in_order = slot((numbers + tp_index * half_blocks) % seq_count)
    true_of = jnp.sum(
        jnp.where(in_order[None, :] == numbers[:, None], numbers[None, :], 0), axis=1
    )
    per_piece = cut // block_rows
    inside = (true_of % per_piece) * block_rows
    table = jnp.stack([true_of // per_piece, inside // LANES * LANES, inside % LANES], 1)

    steps = [r for r in range(planes) if r != last]
    by_step = lambda some: [c[r] for r in some for c in chains]
    rows_of = lambda some: jnp.concatenate([table[r * size : (r + 1) * size] for r in some], 0)
    acc = project(rows_of(steps), where, piece_rows, by_step(steps), None, block_rows, head_width)
    query_rows, kv_rows, kv_last, *kv_home = project(
        rows_of([last]), where, piece_rows, by_step([last]), acc, block_rows, head_width
    )

    halo = shifted(kv_last, "seq", size)
    kv_home = [kv_home[0]] + [swapped(kv_home[m], "seq", m) for m in range(1, size)]
    key_out, value_out = settle(where, kv_home)

    doc_starts = (jnp.cumsum(doc_lengths) - doc_lengths).astype(jnp.int32)
    state = attend(where, doc_starts, query_rows, kv_rows, None)
    context = attend(where, doc_starts, query_rows, halo, state)

    from_c = swapped(context, "seq", 2)
    from_b = swapped(context, "seq", 1)
    from_d = swapped(from_c, "seq", 1)
    contexts = (context, from_b, from_c, from_d)

    def delivered(given, weights):
        pieces = deliver(where, given, weights)
        home = [pieces[0]] + [swapped(pieces[m], "seq", m) for m in range(1, size)]
        return home, pieces[size:]

    near, whole = delivered(contexts, [c[r] for r in (0, 1) for c in chain_o])
    far, _ = delivered(whole, [c[3] for c in chain_o])
    mid, _ = delivered(whole, [chain_o[0][last]])
    late, _ = delivered(whole, [chain_o[1][last]])

    rows = block_rows // 2
    step, spot = in_order // size, in_order % size
    step = jnp.where(step == last, planes - 1, step - (step > last))
    units = jnp.stack([jnp.repeat(spot, 2), (2 * step[:, None] + jnp.arange(2)).reshape(-1)], 1)
    count = 2 * half_blocks
    here, there = units[:count], units[count:]
    among = jnp.arange(count, dtype=jnp.int32)
    early_units = 2 * (planes - 1)

    def ranks(part):
        key = jnp.maximum(part[:, 1] - early_units + 1, 0) * count + among
        return jnp.sum((key[None, :] < key[:, None]).astype(jnp.int32), axis=1)

    hit = ranks(there)[None, :] == among[:, None]
    going = jnp.sum(jnp.where(hit[:, :, None], there[None, :, :], 0), axis=1).astype(jnp.int32)
    first, second = count - 2 * size, count - size
    cuts = (
        (going[:first], (near, far)),
        (going[first:second], (near, far, mid)),
        (going[second:], (near, far, mid, late)),
    )
    received = [swapped(choose(part, sources, rows), "tp", 1) for part, sources in cuts]
    mine = choose(here.astype(jnp.int32), (near, far, mid, late), rows)
    mixed = combine(ranks(here), mine, received)
    return (mixed, key_out, value_out)


def solution(mesh):
    in_specs = (P("seq", "tp"), P("seq"), P(), P(), P(), P("seq", "tp"), P("seq", "tp"))
    out_specs = (P("seq", "tp"), P("seq", "tp"), P("seq", "tp"))
    size = KV_HEADS // mesh.shape["tp"]
    by_planes = size == WINDOW and mesh.shape["tp"] == 2 and mesh.shape["seq"] == WINDOW * size
    body = plane_body if by_planes else gathered_body
    return jax.shard_map(body, mesh=mesh, in_specs=in_specs, out_specs=out_specs, check_vma=False)
```

```python
import jax
import jax.numpy as jnp
from jax import lax
from jax.experimental import pallas as pl
from jax.experimental.pallas import tpu as pltpu
from jax.sharding import PartitionSpec as P

D = 5120
KV_HEADS = 8
HD = 128
HEADS = 24
WINDOW = 4
TOK_DEV = 256


EPSILON = 1e-06
NEG_LARGE = -1e30


def carried_in(value, axis, join, neutral):
    count, mine = (lax.axis_size(axis), lax.axis_index(axis))
    pieces = lax.all_gather(value, axis)
    total = jnp.full_like(value, 0) + jnp.asarray(neutral, value.dtype)

    def turn(position, total):
        longer = join(total, pieces[position])
        return jnp.where(position < mine, longer, total)

    return lax.fori_loop(0, count - 1, turn, total)


def shifted(x, axis, by):
    count = lax.axis_size(axis)
    pairs = [(i, i + by) for i in range(count) if 0 <= i + by < count]
    return lax.ppermute(x, axis, pairs)


def gathered_body(rollout_rows, live_rows, doc_lengths, block_owner, norm_gain, qkv_weight, out_weight):
    half_rows = TOK_DEV // 2
    seq_index = lax.axis_index("seq")

    def combine(earlier, later):
        return earlier + later

    before = carried_in(live_rows, "seq", combine, jnp.zeros_like(live_rows))
    spilled_in = before[0] - seq_index * TOK_DEV
    tail_rows = lax.dynamic_slice_in_dim(rollout_rows, live_rows[0] - half_rows, half_rows, 0)
    arrived = shifted(tail_rows, "seq", 1)
    joined = jnp.concatenate([arrived, rollout_rows], 0)
    owned = lax.dynamic_slice_in_dim(joined, half_rows - spilled_in, TOK_DEV, 0)
    full_rows = lax.all_gather(owned, "tp", axis=1, tiled=True)
    values_f = full_rows.astype(jnp.float32)
    scale = lax.rsqrt(jnp.mean(values_f * values_f, axis=-1, keepdims=True) + EPSILON)
    normed = (values_f * scale * norm_gain.astype(jnp.float32)).astype(jnp.bfloat16)
    block_rows = qkv_weight.shape[0]
    block_count = D // block_rows
    permuted = normed.reshape(TOK_DEV, block_count, block_rows)[:, block_owner, :].reshape(
        TOK_DEV, D
    )
    positions = jnp.arange(block_count, dtype=jnp.int32)
    inverse = jnp.sum(
        jnp.where(block_owner[None, :] == positions[:, None], positions[None, :], 0), axis=1
    )
    projected = jnp.dot(
        permuted,
        lax.all_gather(qkv_weight, "seq", axis=0, tiled=True),
        preferred_element_type=jnp.float32,
    )
    group = HEADS // KV_HEADS
    kv_local = projected.shape[1] // ((group + 2) * HD)
    q_width = kv_local * group * HD
    query_rows = (projected[:, :q_width] * HD ** (-0.5)).astype(jnp.bfloat16)
    key_rows = projected[:, q_width : q_width + kv_local * HD].astype(jnp.bfloat16)
    value_rows = projected[:, q_width + kv_local * HD :].astype(jnp.bfloat16)
    queries = query_rows.reshape(TOK_DEV, kv_local, group, HD)
    query_pos = seq_index * TOK_DEV + jnp.arange(TOK_DEV, dtype=jnp.int32)
    doc_starts = jnp.cumsum(doc_lengths) - doc_lengths
    first_pos = jnp.max(
        jnp.where(doc_starts[None, :] <= query_pos[:, None], doc_starts[None, :], 0), axis=1
    )
    initial = (
        jnp.full((kv_local, group, TOK_DEV), NEG_LARGE, jnp.float32),
        jnp.zeros((kv_local, group, TOK_DEV), jnp.float32),
        jnp.zeros((kv_local, group, TOK_DEV, HD), jnp.float32),
    )
    keys_all, values_all = (key_rows, value_rows)
    for level in range(WINDOW.bit_length() - 1):
        got_keys, got_values = shifted((keys_all, values_all), "seq", 1 << level)
        keys_all = jnp.concatenate([got_keys, keys_all], 0)
        values_all = jnp.concatenate([got_values, values_all], 0)
    state = initial
    for block in range(WINDOW):
        keys_block = keys_all[block * TOK_DEV : (block + 1) * TOK_DEV]
        attend_best, attend_totals, attend_accum = state
        key_count = keys_block.shape[0]
        keys_three = keys_block.reshape(key_count, kv_local, HD)
        values_three = values_all[block * TOK_DEV : (block + 1) * TOK_DEV].reshape(
            key_count, kv_local, HD
        )
        scores = jnp.einsum(
            "tgjd,sgd->gjts", queries, keys_three, preferred_element_type=jnp.float32
        )
        key_pos = (seq_index - WINDOW + 1 + block) * TOK_DEV + jnp.arange(
            key_count, dtype=jnp.int32
        )
        allowed = (key_pos[None, :] <= query_pos[:, None]) & (
            key_pos[None, :] >= first_pos[:, None]
        )
        masked = jnp.where(allowed, scores, NEG_LARGE)
        newest = jnp.maximum(attend_best, jnp.max(masked, axis=-1))
        rescale = jnp.exp(attend_best - newest)
        weights = jnp.where(allowed, jnp.exp(masked - newest[..., None]), 0.0)
        attend_totals = attend_totals * rescale + jnp.sum(weights, axis=-1)
        update = jnp.einsum(
            "gjts,sgd->gjtd",
            weights.astype(jnp.bfloat16),
            values_three,
            preferred_element_type=jnp.float32,
        )
        attend_accum = attend_accum * rescale[..., None] + update
        state = (newest, attend_totals, attend_accum)
    _, totals, accum = state
    context = (
        jnp.transpose(accum / totals[..., None], (2, 0, 1, 3))
        .reshape(TOK_DEV, q_width)
        .astype(jnp.bfloat16)
    )
    delivered = lax.dot_general(
        context,
        lax.all_gather(out_weight, "seq", axis=0, tiled=True),
        (((1,), (1,)), ((), ())),
        preferred_element_type=jnp.float32,
    )
    partial_value = delivered.reshape(TOK_DEV, block_count, block_rows)[:, inverse, :].reshape(
        TOK_DEV, D
    )
    mixed = lax.psum_scatter(
        partial_value.astype(jnp.bfloat16).astype(jnp.float32).astype(jnp.bfloat16),
        "tp",
        scatter_dimension=1,
        tiled=True,
    )
    return (mixed, key_rows, value_rows)


LANES = 128


def swapped(x, axis, bit):
    count = lax.axis_size(axis)
    return lax.ppermute(x, axis, [(i, i ^ bit) for i in range(count)])


def turned(x, axis, by):
    count = lax.axis_size(axis)
    return lax.ppermute(x, axis, [(i, (i + by) % count) for i in range(count)])


def three_away(x, size):
    up = turned(x, "seq", size)
    down = turned(x, "seq", -size)
    return {0: x, 1: up, 3: down, 2: turned(up, "seq", size)}


VMEM_LIMIT = 60 * 1024 * 1024


def placed(arrays):
    return [pltpu.with_memory_space_constraint(v, pltpu.HBM) for v in arrays]


def project_kernel(layout, order, table, place_ref, *refs, rows, block_rows, window, first):
    pieces, weights = layout
    groups = len(pieces)
    x_refs, refs = refs[: sum(pieces)], refs[sum(pieces) :]
    w_refs, refs = refs[: len(weights)], refs[len(weights) :]
    if first:
        acc_out, xs, ws, x_sem, w_sem = refs
    else:
        acc_in, q_out, kv_out, halo_out, *homes, xs, ws, x_sem, w_sem = refs
    spots = [(ref, part) for ref, parts in zip(w_refs, weights) for part in range(parts)]

    def weight_copy(i, ref, part):
        at = pl.multiple_of(i * window + table[3 * order[i] + 2], 64)
        return pltpu.make_async_copy(
            ref.at[pl.ds(part * block_rows, block_rows), :],
            ws.at[pl.ds(at, block_rows), :],
            w_sem.at[i],
        )

    for i, (ref, part) in enumerate(spots):
        weight_copy(i, ref, part).start()
    for m in range(groups):
        for i in range(len(spots)):
            piece = table[3 * order[i]]
            start = pl.multiple_of(table[3 * order[i] + 1], LANES)
            for p in range(pieces[0]):

                @pl.when(piece == p)
                def _():
                    pltpu.make_async_copy(
                        x_refs[m * pieces[0] + p].at[:, pl.ds(start, window)],
                        xs.at[pl.ds(m * rows, rows), pl.ds(i * window, window)],
                        x_sem.at[m],
                    ).start()

    pad = window - block_rows
    for i, (ref, part) in enumerate(spots):
        weight_copy(i, ref, part).wait()
        spare = pl.multiple_of(i * window + jnp.where(table[3 * order[i] + 2] == 0, block_rows, 0), 64)
        ws[pl.ds(spare, pad), :] = jnp.zeros((pad, ws.shape[1]), ws.dtype)

    def one(m, carry):
        at = pl.ds(pl.multiple_of(m * rows, rows), rows)
        pltpu.make_async_copy(xs.at[at, :], xs.at[at, :], x_sem.at[m]).wait()
        total = jnp.dot(xs[at, :], ws[...], preferred_element_type=jnp.float32)
        if first:
            acc_out[at, :] = total
        else:
            total = total + acc_in[at, :]
            width = q_out.shape[1]
            q_out[at, :] = (total[:, :width] * HD ** (-0.5)).astype(q_out.dtype)
            kv = total[:, width:].astype(kv_out.dtype)
            for other, home in enumerate(homes):

                @pl.when(m == other)
                def _():
                    home[...] = kv

            block = place_ref[0] ^ m
            kv_out[pl.ds(pl.multiple_of(block * rows, rows), rows), :] = kv
            skipped = groups - halo_out.shape[0] // rows

            @pl.when(block >= skipped)
            def _():
                halo_out[pl.ds(pl.multiple_of((block - skipped) * rows, rows), rows), :] = kv

        return carry

    lax.fori_loop(0, groups, one, 0)


def project(table, order, where, piece_rows, weights, acc, block_rows, head_width):
    groups, pieces = len(piece_rows), len(piece_rows[0])
    rows = piece_rows[0][0].shape[0]
    parts = [w.shape[0] // block_rows for w in weights]
    count, columns = sum(parts), weights[0].shape[1]
    window = -(-(block_rows + LANES // 2) // LANES) * LANES
    total = groups * rows
    first = acc is None
    kernel = lambda table, place, *refs: project_kernel(
        ([pieces] * groups, parts),
        order,
        table,
        place,
        *refs,
        rows=rows,
        block_rows=block_rows,
        window=window,
        first=first,
    )
    scalar = pl.BlockSpec(memory_space=pltpu.SMEM)
    anywhere, local = pl.BlockSpec(memory_space=pltpu.HBM), pl.BlockSpec(memory_space=pltpu.VMEM)
    acc_shape = jax.ShapeDtypeStruct((total, columns), jnp.float32)
    x_shape = jax.ShapeDtypeStruct((total, count * window), jnp.bfloat16)
    w_shape = jax.ShapeDtypeStruct((count * window, columns), jnp.bfloat16)
    if first:
        shapes, outs = acc_shape, local
    else:
        side = columns - head_width
        shapes = (
            jax.ShapeDtypeStruct((total, head_width), jnp.bfloat16),
            jax.ShapeDtypeStruct((total, side), jnp.bfloat16),
            jax.ShapeDtypeStruct(((WINDOW - 1) * TOK_DEV, side), jnp.bfloat16),
        ) + (jax.ShapeDtypeStruct((rows, side), jnp.bfloat16),) * groups
        outs = (local,) * (3 + groups)
    flops = 2 * total * count * window * columns
    moved = count * (total * window + block_rows * columns) * 2 + total * columns * 4
    return pl.pallas_call(
        kernel,
        out_shape=shapes,
        in_specs=[scalar, scalar]
        + [anywhere] * (groups * pieces + len(weights))
        + ([] if first else [local]),
        out_specs=outs,
        scratch_shapes=[
            pltpu.VMEM(x_shape.shape, jnp.bfloat16),
            pltpu.VMEM(w_shape.shape, jnp.bfloat16),
            pltpu.SemaphoreType.DMA((groups,)),
            pltpu.SemaphoreType.DMA((count,)),
        ],
        cost_estimate=pl.CostEstimate(flops=flops, bytes_accessed=moved, transcendentals=0),
        compiler_params=pltpu.CompilerParams(
            vmem_limit_bytes=VMEM_LIMIT
        ),
        name="project_first" if first else "project_last",
    )(
        table,
        where,
        *placed([v for row in piece_rows for v in row]),
        *placed(weights),
        *([] if first else placed([acc])),
    )


def attend_kernel(place_ref, starts_ref, q_ref, keys_ref, *refs, own):
    if own:
        stat_ref, acc_ref = refs
    else:
        stat_in, acc_in, out_ref = refs
    size = q_ref.shape[0] // TOK_DEV
    back = WINDOW - 1
    heads = q_ref.shape[1] // HD
    place, plane = place_ref[0], place_ref[1]

    def one(m, carry):
        block = place ^ m
        base = (plane * size + block) * TOK_DEV
        rows = pl.ds(pl.multiple_of(m * TOK_DEV, TOK_DEV), TOK_DEV)
        query_pos = base + lax.broadcasted_iota(jnp.int32, (1, TOK_DEV), 1)
        first_pos = jnp.zeros((1, TOK_DEV), jnp.int32)
        lowest = jnp.int32(0)
        for d in range(starts_ref.shape[0]):
            start = starts_ref[d]
            first_pos = jnp.where(start <= query_pos, jnp.maximum(first_pos, start), first_pos)
            lowest = jnp.where(start <= base, jnp.maximum(lowest, start), lowest)
        earliest = jnp.clip(lowest // TOK_DEV - (plane * size + block - back), 0, back)
        middle = jnp.maximum(back - block, 0)
        top = WINDOW - 1 if own else middle - 1

        def step(i, state):
            w = top - i
            at = (block + w) * TOK_DEV - (back * TOK_DEV if own else 0)
            at = pl.ds(pl.multiple_of(at, TOK_DEV), TOK_DEV)
            key_pos = base + (w - back) * TOK_DEV + lax.broadcasted_iota(
                jnp.int32, (TOK_DEV, 1), 0
            )
            allowed = (key_pos <= query_pos) & (key_pos >= first_pos)
            key_block, value_block = keys_ref[at, :HD], keys_ref[at, HD:]
            after = []
            for h in range(heads):
                best, norm, accum = state[h]
                scores = lax.dot_general(
                    key_block,
                    q_ref[rows, h * HD : (h + 1) * HD],
                    (((1,), (1,)), ((), ())),
                    preferred_element_type=jnp.float32,
                )
                masked = jnp.where(allowed, scores, NEG_LARGE)
                newest = jnp.maximum(best, jnp.max(masked, axis=0, keepdims=True))
                rescale = jnp.exp(best - newest)
                weights = jnp.exp(masked - newest)
                norm = norm * rescale + jnp.sum(weights, axis=0, keepdims=True)
                accum = accum * rescale + lax.dot_general(
                    value_block,
                    weights.astype(jnp.bfloat16),
                    (((0,), (0,)), ((), ())),
                    preferred_element_type=jnp.float32,
                )
                after.append((newest, norm, accum))
            return tuple(after)

        if own:
            count = WINDOW - jnp.maximum(earliest, middle)
            state = tuple(
                (
                    jnp.full((1, TOK_DEV), NEG_LARGE, jnp.float32),
                    jnp.zeros((1, TOK_DEV), jnp.float32),
                    jnp.zeros((HD, TOK_DEV), jnp.float32),
                )
                for _ in range(heads)
            )
        else:
            count = jnp.maximum(middle - earliest, 0)
            state = tuple(
                (
                    stat_in[2 * h : 2 * h + 1, rows],
                    stat_in[2 * h + 1 : 2 * h + 2, rows],
                    acc_in[h * HD : (h + 1) * HD, rows],
                )
                for h in range(heads)
            )
        state = lax.fori_loop(0, count, step, state)
        for h in range(heads):
            best, norm, accum = state[h]
            some = pl.ds(h * HD, HD)
            if own:
                stat_ref[2 * h : 2 * h + 1, rows] = best
                stat_ref[2 * h + 1 : 2 * h + 2, rows] = norm
                acc_ref[some, rows] = accum
            else:
                out_ref[some, rows] = (accum / norm).astype(out_ref.dtype)
        return carry

    lax.fori_loop(0, size, one, 0)


def attend(where, doc_starts, query_rows, keys, state):
    rows, width = query_rows.shape
    own = state is None
    scalar, local = pl.BlockSpec(memory_space=pltpu.SMEM), pl.BlockSpec(memory_space=pltpu.VMEM)
    stat = jax.ShapeDtypeStruct((2 * width // HD, rows), jnp.float32)
    accum = jax.ShapeDtypeStruct((width, rows), jnp.float32)
    out = jax.ShapeDtypeStruct((width, rows), jnp.bfloat16)
    blocks = WINDOW * WINDOW // 2
    return pl.pallas_call(
        lambda *refs: attend_kernel(*refs, own=own),
        out_shape=(stat, accum) if own else out,
        in_specs=[scalar, scalar, local, local] + ([] if own else [local, local]),
        out_specs=(local, local) if own else local,
        cost_estimate=pl.CostEstimate(
            flops=4 * blocks * TOK_DEV * width * TOK_DEV,
            bytes_accessed=8 * rows * width,
            transcendentals=blocks * TOK_DEV * TOK_DEV * width // HD,
        ),
        compiler_params=pltpu.CompilerParams(
            vmem_limit_bytes=VMEM_LIMIT
        ),
        name="attend_own" if own else "attend_halo",
    )(where, doc_starts, *placed([query_rows, keys]), *([] if own else placed(state)))


def deliver_kernel(place_ref, *refs, size, steps, whole):
    if whole:
        (context_ref,), refs = refs[:1], refs[1:]
    else:
        contexts, refs = refs[:size], refs[size:]
    weights, refs = refs[:steps], refs[steps:]
    outs, refs = refs[:size], refs[size:]
    if whole:
        ws, w_sem = refs
    else:
        context_ref, ws, w_sem, c_sem = refs
    rows = weights[0].shape[0]
    copies = [
        pltpu.make_async_copy(weights[i], ws.at[pl.ds(i * rows, rows), :], w_sem.at[i])
        for i in range(steps)
    ]
    if not whole:
        width = contexts[0].shape[0]
        for m in range(size):
            for other in range(size):
                at = pl.multiple_of((place_ref[0] ^ other) * width, LANES)
                copies.append(
                    pltpu.make_async_copy(
                        contexts[other].at[:, pl.ds((m ^ other) * TOK_DEV, TOK_DEV)],
                        context_ref.at[pl.ds(at, width), pl.ds(m * TOK_DEV, TOK_DEV)],
                        c_sem.at[m * size + other],
                    )
                )
    for copy in copies:
        copy.start()
    for copy in copies:
        copy.wait()
    for m in range(size):
        outs[m][...] = jnp.dot(
            ws[...],
            context_ref[:, m * TOK_DEV : (m + 1) * TOK_DEV],
            preferred_element_type=jnp.float32,
        ).astype(outs[m].dtype)


def deliver(where, contexts, weights):
    steps, (rows, columns) = len(weights), weights[0].shape
    whole = len(contexts) == 1
    size = WINDOW
    total = contexts[0].shape[1]
    scalar = pl.BlockSpec(memory_space=pltpu.SMEM)
    anywhere, local = pl.BlockSpec(memory_space=pltpu.HBM), pl.BlockSpec(memory_space=pltpu.VMEM)
    part = jax.ShapeDtypeStruct((steps * rows, TOK_DEV), jnp.bfloat16)
    context = jax.ShapeDtypeStruct((columns, total), jnp.bfloat16)
    w_shape = jax.ShapeDtypeStruct((steps * rows, columns), jnp.bfloat16)
    scratch = [pltpu.VMEM(w_shape.shape, jnp.bfloat16), pltpu.SemaphoreType.DMA((steps,))]
    if not whole:
        scratch.append(pltpu.SemaphoreType.DMA((size * size,)))
    return pl.pallas_call(
        lambda *refs: deliver_kernel(*refs, size=size, steps=steps, whole=whole),
        out_shape=(part,) * size + (() if whole else (context,)),
        in_specs=[scalar] + [local if whole else anywhere] * len(contexts) + [anywhere] * steps,
        out_specs=(local,) * (size if whole else size + 1),
        scratch_shapes=scratch,
        cost_estimate=pl.CostEstimate(
            flops=2 * total * columns * steps * rows,
            bytes_accessed=2 * (total * columns + steps * rows * (columns + total)),
            transcendentals=0,
        ),
        compiler_params=pltpu.CompilerParams(
            vmem_limit_bytes=VMEM_LIMIT
        ),
    )(where, *placed(contexts), *placed(weights))


def fetch(table, k, sources, target, sem):
    rows = target.shape[0]
    low = 0
    for group in sources:
        units = group[0].shape[0] // rows
        for m, ref in enumerate(group):
            inside = (table[2 * k] == m) & (table[2 * k + 1] >= low) & (table[2 * k + 1] < low + units)

            @pl.when(inside)
            def _():
                at = pl.multiple_of((table[2 * k + 1] - low) * rows, 32)
                pltpu.make_async_copy(ref.at[pl.ds(at, rows), :], target, sem).start()

        low += units


def choose(table, part, sources, rows):
    begin, end = part
    count = end - begin
    groups = [len(group) for group in sources]

    def kernel(table_ref, *refs):
        refs, (out, sem) = list(refs[:-2]), refs[-2:]
        split = [[refs.pop(0) for _ in range(n)] for n in groups]
        for k in range(count):
            fetch(table_ref, begin + k, split, out.at[k], sem.at[k])
        for k in range(count):
            pltpu.make_async_copy(out.at[k], out.at[k], sem.at[k]).wait()

    shape = jax.ShapeDtypeStruct((count, rows, TOK_DEV), jnp.bfloat16)
    flat = [v for group in sources for v in group]
    return pl.pallas_call(
        kernel,
        out_shape=shape,
        in_specs=[pl.BlockSpec(memory_space=pltpu.SMEM)]
        + [pl.BlockSpec(memory_space=pltpu.HBM)] * len(flat),
        out_specs=pl.BlockSpec(memory_space=pltpu.VMEM),
        scratch_shapes=[pltpu.SemaphoreType.DMA((count,))],
        cost_estimate=pl.CostEstimate(flops=0, bytes_accessed=4 * shape.size, transcendentals=0),
        compiler_params=pltpu.CompilerParams(vmem_limit_bytes=VMEM_LIMIT),
    )(table, *placed(flat))


def combine(ranks, mine, received):
    count, rows = mine.shape[:2]
    step = 640 // rows

    def kernel(rank_ref, mine_ref, *refs):
        theirs, sem = refs[-2:]
        out, refs = refs[-3], refs[:-3]
        low = 0
        copies = []
        for i, ref in enumerate(refs):
            units = ref.shape[0]
            copies.append(pltpu.make_async_copy(ref, theirs.at[pl.ds(low, units)], sem.at[i]))
            low += units
        for copy in copies:
            copy.start()
        for copy in copies:
            copy.wait()
        for k in range(0, count, step):
            some = [
                mine_ref[k + i].astype(jnp.float32) + theirs[rank_ref[k + i]].astype(jnp.float32)
                for i in range(step)
            ]
            total = jnp.concatenate(some, 0)
            out[:, k * rows : (k + step) * rows] = jnp.transpose(total).astype(out.dtype)

    shape = jax.ShapeDtypeStruct((TOK_DEV, count * rows), jnp.bfloat16)
    local = pl.BlockSpec(memory_space=pltpu.VMEM)
    return pl.pallas_call(
        kernel,
        out_shape=shape,
        in_specs=[pl.BlockSpec(memory_space=pltpu.SMEM), local]
        + [pl.BlockSpec(memory_space=pltpu.HBM)] * len(received),
        out_specs=local,
        scratch_shapes=[
            pltpu.VMEM((count, rows, TOK_DEV), jnp.bfloat16),
            pltpu.SemaphoreType.DMA((len(received),)),
        ],
        cost_estimate=pl.CostEstimate(
            flops=shape.size, bytes_accessed=6 * shape.size, transcendentals=0
        ),
        compiler_params=pltpu.CompilerParams(vmem_limit_bytes=VMEM_LIMIT),
        name="combine",
    )(ranks, *placed([mine]), *placed(received))


def settle(where, pieces):
    size, rows = len(pieces), pieces[0].shape[0]

    def kernel(place_ref, *refs):
        key_out, value_out = refs[-2:]
        for m, ref in enumerate(refs[:-2]):
            at = pl.ds(pl.multiple_of((place_ref[0] ^ m) * HD, HD), HD)
            key_out[:, at] = ref[:, :HD]
            value_out[:, at] = ref[:, HD:]

    shape = jax.ShapeDtypeStruct((rows, size * HD), jnp.bfloat16)
    local = pl.BlockSpec(memory_space=pltpu.VMEM)
    return pl.pallas_call(
        kernel,
        out_shape=(shape, shape),
        in_specs=[pl.BlockSpec(memory_space=pltpu.SMEM)] + [local] * size,
        out_specs=(local, local),
        cost_estimate=pl.CostEstimate(flops=0, bytes_accessed=8 * shape.size, transcendentals=0),
        compiler_params=pltpu.CompilerParams(vmem_limit_bytes=VMEM_LIMIT),
        name="settle",
    )(where, *placed(pieces))


def plane_body(*args):
    return plane_steps(*args)


def plane_steps(rollout_rows, live_rows, doc_lengths, block_owner, norm_gain, qkv_weight, out_weight):
    seq_count, seq_index = lax.axis_size("seq"), lax.axis_index("seq")
    tp_index = lax.axis_index("tp")
    block_rows, columns = qkv_weight.shape
    local_features = rollout_rows.shape[1]
    group = HEADS // KV_HEADS
    size = columns // ((group + 2) * HD)
    planes = seq_count // size
    place, plane = seq_index % size, seq_index // size
    where = jnp.stack([place, plane]).astype(jnp.int32)
    head_width = group * HD
    half_rows = TOK_DEV // 2

    q_width = size * head_width

    def columns_of(k):
        cuts = ((k * head_width, head_width), (q_width + k * HD, HD), (q_width + (size + k) * HD, HD))
        return jnp.concatenate(
            [lax.dynamic_slice_in_dim(qkv_weight, at, wide, 1) for at, wide in cuts], 1
        )

    live = jnp.broadcast_to(live_rows[None], (8, LANES))
    below = jnp.zeros_like(live)
    for k in range(1, planes):
        below = below + jnp.where(plane >= k, turned(live, "seq", k * size), 0)
    chains = [three_away(columns_of(place), size)]
    pair = jnp.where(lax.broadcasted_iota(jnp.int32, live.shape, 0) == 0, below, live)
    plane_pairs = [pair] + [swapped(pair, "seq", m) for m in range(1, size)]
    for m in (2, 3, 1):
        chains.append(swapped(columns_of(place ^ m), "seq", m))
    chains = [chains[0]] + [three_away(chains[k], size) for k in (3, 1, 2)]
    last = 2
    top = out_weight.shape[0] // 2
    chain_o = [three_away(out_weight[:top], size), three_away(out_weight[top:], size)]

    before = sum(
        v[0, 0] + jnp.where((place ^ m) < place, v[1, 0], 0) for m, v in enumerate(plane_pairs)
    )
    spilled_in = before - seq_index * TOK_DEV
    tail_rows = lax.dynamic_slice_in_dim(rollout_rows, live_rows[0] - half_rows, half_rows, 0)
    arrived = shifted(tail_rows, "seq", 1)
    joined = jnp.concatenate([arrived, rollout_rows], 0)
    values_f = joined.astype(jnp.float32)
    squares = jnp.sum(values_f * values_f, axis=-1)
    squares = squares + swapped(squares, "tp", 1)
    scale = lax.rsqrt(squares[:, None] / D + EPSILON)
    gain = lax.dynamic_slice_in_dim(norm_gain, tp_index * local_features, local_features, 0)
    at = half_rows - spilled_in
    values_f = lax.dynamic_slice_in_dim(joined, at, TOK_DEV, 0).astype(jnp.float32)
    scale = lax.dynamic_slice_in_dim(scale, at, TOK_DEV, 0)
    normed = (values_f * scale * gain.astype(jnp.float32)).astype(jnp.bfloat16)

    cut = local_features // 2
    h1, h2 = normed[:, :cut], normed[:, cut:]
    x1, y2 = swapped(h1, "tp", 1), swapped(h2, "seq", 2)
    x2, y1 = swapped(h2, "tp", 1), swapped(h1, "seq", 2)
    yx2, xy1 = swapped(y2, "tp", 1), swapped(x1, "seq", 2)
    rows_a, rows_c = [h1, h2, x1, x2], [y1, y2, xy1, yx2]
    rows_b = [swapped(v, "seq", 1) for v in rows_a]
    rows_d = [swapped(v, "seq", 1) for v in rows_c]
    piece_rows = (rows_a, rows_b, rows_c, rows_d)

    numbers = jnp.arange(seq_count, dtype=jnp.int32)
    inverse = jnp.sum(
        jnp.where(block_owner[None, :] == numbers[:, None], numbers[None, :], 0), axis=1
    )
    half_blocks = local_features // block_rows

    def slot(blocks):
        source = inverse[blocks]
        step = (plane - source // size) % planes
        return step * size + ((source % size) ^ place)

    in_order = slot((numbers + tp_index * half_blocks) % seq_count)
    true_of = jnp.sum(
        jnp.where(in_order[None, :] == numbers[:, None], numbers[None, :], 0), axis=1
    )
    per_piece = cut // block_rows
    inside = (true_of % per_piece) * block_rows
    table = jnp.stack([true_of // per_piece, inside // LANES * LANES, inside % LANES], 1)
    doc_starts = (jnp.cumsum(doc_lengths) - doc_lengths).astype(jnp.int32)

    last = 2
    steps = [r for r in range(planes) if r != last]
    rows = block_rows // 2
    step, spot = in_order // size, in_order % size
    step = jnp.where(step == last, planes - 1, step - (step > last))
    units = jnp.stack([jnp.repeat(spot, 2), (2 * step[:, None] + jnp.arange(2)).reshape(-1)], 1)
    count = 2 * half_blocks
    here, there = units[:count], units[count:]
    among = jnp.arange(count, dtype=jnp.int32)
    early_units = 2 * (planes - 1)

    def ranks(part):
        key = jnp.maximum(part[:, 1] - early_units + 1, 0) * count + among
        return jnp.sum((key[None, :] < key[:, None]).astype(jnp.int32), axis=1)

    hit = ranks(there)[None, :] == among[:, None]
    going = jnp.sum(jnp.where(hit[:, :, None], there[None, :, :], 0), axis=1).astype(jnp.int32)
    where, table, doc_starts, going, here, here_ranks = lax.optimization_barrier(
        (
            where,
            table.astype(jnp.int32).reshape(-1),
            doc_starts,
            going.reshape(-1),
            here.astype(jnp.int32).reshape(-1),
            ranks(here),
        )
    )

    by_step = lambda some: [c[r] for r in some for c in chains]
    slots_of = lambda some: [r * size + m for r in some for m in range(size)]
    acc = project(
        table, slots_of(steps), where, piece_rows, by_step(steps), None, block_rows, head_width
    )
    query_rows, kv_rows, kv_last, *kv_home = project(
        table, slots_of([last]), where, piece_rows, by_step([last]), acc, block_rows, head_width
    )

    halo = shifted(kv_last, "seq", size)
    kv_home = [kv_home[0]] + [swapped(kv_home[m], "seq", m) for m in range(1, size)]
    key_out, value_out = settle(where, kv_home)

    state = attend(where, doc_starts, query_rows, kv_rows, None)
    context = attend(where, doc_starts, query_rows, halo, state)

    from_c = swapped(context, "seq", 2)
    from_b = swapped(context, "seq", 1)
    from_d = swapped(from_c, "seq", 1)
    contexts = (context, from_b, from_c, from_d)

    def delivered(given, weights):
        pieces = deliver(where, given, weights)
        home = [pieces[0]] + [swapped(pieces[m], "seq", m) for m in range(1, size)]
        return home, pieces[size:]

    near, whole = delivered(contexts, [c[r] for r in (0, 1) for c in chain_o])
    far, _ = delivered(whole, [c[3] for c in chain_o])
    mid, _ = delivered(whole, [chain_o[0][last]])
    late, _ = delivered(whole, [chain_o[1][last]])

    first, second = count - 2 * size, count - size
    cuts = (
        ((0, first), (near, far)),
        ((first, second), (near, far, mid)),
        ((second, count), (near, far, mid, late)),
    )
    received = [swapped(choose(going, part, sources, rows), "tp", 1) for part, sources in cuts]
    mine = choose(here, (0, count), (near, far, mid, late), rows)
    mixed = combine(here_ranks, mine, received)
    return (mixed, key_out, value_out)


def solution(mesh):
    in_specs = (P("seq", "tp"), P("seq"), P(), P(), P(), P("seq", "tp"), P("seq", "tp"))
    out_specs = (P("seq", "tp"), P("seq", "tp"), P("seq", "tp"))
    size = KV_HEADS // mesh.shape["tp"]
    by_planes = size == WINDOW and mesh.shape["tp"] == 2 and mesh.shape["seq"] == WINDOW * size
    body = plane_body if by_planes else gathered_body
    return jax.shard_map(body, mesh=mesh, in_specs=in_specs, out_specs=out_specs, check_vma=False)
```

```python
import jax
import jax.numpy as jnp
from jax import lax
from jax.experimental import pallas as pl
from jax.experimental.pallas import tpu as pltpu
from jax.sharding import PartitionSpec as P

D = 5120
KV_HEADS = 8
HD = 128
HEADS = 24
WINDOW = 4
TOK_DEV = 256


EPSILON = 1e-06
NEG_LARGE = -1e30


def carried_in(value, axis, join, neutral):
    count, mine = (lax.axis_size(axis), lax.axis_index(axis))
    pieces = lax.all_gather(value, axis)
    total = jnp.full_like(value, 0) + jnp.asarray(neutral, value.dtype)

    def turn(position, total):
        longer = join(total, pieces[position])
        return jnp.where(position < mine, longer, total)

    return lax.fori_loop(0, count - 1, turn, total)


def shifted(x, axis, by):
    count = lax.axis_size(axis)
    pairs = [(i, i + by) for i in range(count) if 0 <= i + by < count]
    return lax.ppermute(x, axis, pairs)


def gathered_body(rollout_rows, live_rows, doc_lengths, block_owner, norm_gain, qkv_weight, out_weight):
    half_rows = TOK_DEV // 2
    seq_index = lax.axis_index("seq")

    def combine(earlier, later):
        return earlier + later

    before = carried_in(live_rows, "seq", combine, jnp.zeros_like(live_rows))
    spilled_in = before[0] - seq_index * TOK_DEV
    tail_rows = lax.dynamic_slice_in_dim(rollout_rows, live_rows[0] - half_rows, half_rows, 0)
    arrived = shifted(tail_rows, "seq", 1)
    joined = jnp.concatenate([arrived, rollout_rows], 0)
    owned = lax.dynamic_slice_in_dim(joined, half_rows - spilled_in, TOK_DEV, 0)
    full_rows = lax.all_gather(owned, "tp", axis=1, tiled=True)
    values_f = full_rows.astype(jnp.float32)
    scale = lax.rsqrt(jnp.mean(values_f * values_f, axis=-1, keepdims=True) + EPSILON)
    normed = (values_f * scale * norm_gain.astype(jnp.float32)).astype(jnp.bfloat16)
    block_rows = qkv_weight.shape[0]
    block_count = D // block_rows
    permuted = normed.reshape(TOK_DEV, block_count, block_rows)[:, block_owner, :].reshape(
        TOK_DEV, D
    )
    positions = jnp.arange(block_count, dtype=jnp.int32)
    inverse = jnp.sum(
        jnp.where(block_owner[None, :] == positions[:, None], positions[None, :], 0), axis=1
    )
    projected = jnp.dot(
        permuted,
        lax.all_gather(qkv_weight, "seq", axis=0, tiled=True),
        preferred_element_type=jnp.float32,
    )
    group = HEADS // KV_HEADS
    kv_local = projected.shape[1] // ((group + 2) * HD)
    q_width = kv_local * group * HD
    query_rows = (projected[:, :q_width] * HD ** (-0.5)).astype(jnp.bfloat16)
    key_rows = projected[:, q_width : q_width + kv_local * HD].astype(jnp.bfloat16)
    value_rows = projected[:, q_width + kv_local * HD :].astype(jnp.bfloat16)
    queries = query_rows.reshape(TOK_DEV, kv_local, group, HD)
    query_pos = seq_index * TOK_DEV + jnp.arange(TOK_DEV, dtype=jnp.int32)
    doc_starts = jnp.cumsum(doc_lengths) - doc_lengths
    first_pos = jnp.max(
        jnp.where(doc_starts[None, :] <= query_pos[:, None], doc_starts[None, :], 0), axis=1
    )
    initial = (
        jnp.full((kv_local, group, TOK_DEV), NEG_LARGE, jnp.float32),
        jnp.zeros((kv_local, group, TOK_DEV), jnp.float32),
        jnp.zeros((kv_local, group, TOK_DEV, HD), jnp.float32),
    )
    keys_all, values_all = (key_rows, value_rows)
    for level in range(WINDOW.bit_length() - 1):
        got_keys, got_values = shifted((keys_all, values_all), "seq", 1 << level)
        keys_all = jnp.concatenate([got_keys, keys_all], 0)
        values_all = jnp.concatenate([got_values, values_all], 0)
    state = initial
    for block in range(WINDOW):
        keys_block = keys_all[block * TOK_DEV : (block + 1) * TOK_DEV]
        attend_best, attend_totals, attend_accum = state
        key_count = keys_block.shape[0]
        keys_three = keys_block.reshape(key_count, kv_local, HD)
        values_three = values_all[block * TOK_DEV : (block + 1) * TOK_DEV].reshape(
            key_count, kv_local, HD
        )
        scores = jnp.einsum(
            "tgjd,sgd->gjts", queries, keys_three, preferred_element_type=jnp.float32
        )
        key_pos = (seq_index - WINDOW + 1 + block) * TOK_DEV + jnp.arange(
            key_count, dtype=jnp.int32
        )
        allowed = (key_pos[None, :] <= query_pos[:, None]) & (
            key_pos[None, :] >= first_pos[:, None]
        )
        masked = jnp.where(allowed, scores, NEG_LARGE)
        newest = jnp.maximum(attend_best, jnp.max(masked, axis=-1))
        rescale = jnp.exp(attend_best - newest)
        weights = jnp.where(allowed, jnp.exp(masked - newest[..., None]), 0.0)
        attend_totals = attend_totals * rescale + jnp.sum(weights, axis=-1)
        update = jnp.einsum(
            "gjts,sgd->gjtd",
            weights.astype(jnp.bfloat16),
            values_three,
            preferred_element_type=jnp.float32,
        )
        attend_accum = attend_accum * rescale[..., None] + update
        state = (newest, attend_totals, attend_accum)
    _, totals, accum = state
    context = (
        jnp.transpose(accum / totals[..., None], (2, 0, 1, 3))
        .reshape(TOK_DEV, q_width)
        .astype(jnp.bfloat16)
    )
    delivered = lax.dot_general(
        context,
        lax.all_gather(out_weight, "seq", axis=0, tiled=True),
        (((1,), (1,)), ((), ())),
        preferred_element_type=jnp.float32,
    )
    partial_value = delivered.reshape(TOK_DEV, block_count, block_rows)[:, inverse, :].reshape(
        TOK_DEV, D
    )
    mixed = lax.psum_scatter(
        partial_value.astype(jnp.bfloat16).astype(jnp.float32).astype(jnp.bfloat16),
        "tp",
        scatter_dimension=1,
        tiled=True,
    )
    return (mixed, key_rows, value_rows)


LANES = 128


def swapped(x, axis, bit):
    count = lax.axis_size(axis)
    return lax.ppermute(x, axis, [(i, i ^ bit) for i in range(count)])


def turned(x, axis, by):
    count = lax.axis_size(axis)
    return lax.ppermute(x, axis, [(i, (i + by) % count) for i in range(count)])


def three_away(x, size):
    up = turned(x, "seq", size)
    down = turned(x, "seq", -size)
    return {0: x, 1: up, 3: down, 2: turned(up, "seq", size)}


def scratch_limit(*arrays):
    total = sum(v.size * v.dtype.itemsize for v in arrays)
    return total + total // 8 + 6 * 1024 * 1024


def project_kernel(layout, order, table, place_ref, *refs, rows, block_rows, window, first, final):
    pieces, weights = layout
    groups = len(pieces)
    x_refs, refs = refs[: sum(pieces)], refs[sum(pieces) :]
    w_refs, refs = refs[: len(weights)], refs[len(weights) :]
    if first:
        acc_out, xs, ws, x_sem, w_sem = refs
    elif not final:
        acc_in, acc_out, xs, ws, x_sem, w_sem = refs
    else:
        acc_in, q_out, kv_out, halo_out, *homes, xs, ws, x_sem, w_sem = refs
    spots = [(ref, part) for ref, parts in zip(w_refs, weights) for part in range(parts)]

    def weight_copy(i, ref, part):
        at = pl.multiple_of(i * window + table[3 * order[i] + 2], 64)
        return pltpu.make_async_copy(
            ref.at[pl.ds(part * block_rows, block_rows), :],
            ws.at[pl.ds(at, block_rows), :],
            w_sem.at[i],
        )

    for i, (ref, part) in enumerate(spots):
        weight_copy(i, ref, part).start()
    for m in range(groups):
        for i in range(len(spots)):
            piece = table[3 * order[i]]
            start = pl.multiple_of(table[3 * order[i] + 1], LANES)
            for p in range(pieces[0]):

                @pl.when(piece == p)
                def _():
                    pltpu.make_async_copy(
                        x_refs[m * pieces[0] + p].at[:, pl.ds(start, window)],
                        xs.at[pl.ds(m * rows, rows), pl.ds(i * window, window)],
                        x_sem.at[m],
                    ).start()

    pad = window - block_rows
    for i, (ref, part) in enumerate(spots):
        weight_copy(i, ref, part).wait()
        spare = pl.multiple_of(i * window + jnp.where(table[3 * order[i] + 2] == 0, block_rows, 0), 64)
        ws[pl.ds(spare, pad), :] = jnp.zeros((pad, ws.shape[1]), ws.dtype)

    def one(m, carry):
        at = pl.ds(pl.multiple_of(m * rows, rows), rows)
        pltpu.make_async_copy(xs.at[at, :], xs.at[at, :], x_sem.at[m]).wait()
        total = jnp.dot(xs[at, :], ws[...], preferred_element_type=jnp.float32)
        if not first:
            total = total + acc_in[at, :]
        if not final:
            acc_out[at, :] = total
        else:
            width = q_out.shape[1]
            q_out[at, :] = (total[:, :width] * HD ** (-0.5)).astype(q_out.dtype)
            kv = total[:, width:].astype(kv_out.dtype)
            for other, home in enumerate(homes):

                @pl.when(m == other)
                def _():
                    home[...] = kv

            block = place_ref[0] ^ m
            kv_out[pl.ds(pl.multiple_of(block * rows, rows), rows), :] = kv
            skipped = groups - halo_out.shape[0] // rows

            @pl.when(block >= skipped)
            def _():
                halo_out[pl.ds(pl.multiple_of((block - skipped) * rows, rows), rows), :] = kv

        return carry

    lax.fori_loop(0, groups, one, 0)


def project(table, order, where, piece_rows, weights, acc, block_rows, head_width, name):
    groups, pieces = len(piece_rows), len(piece_rows[0])
    rows = piece_rows[0][0].shape[0]
    parts = [w.shape[0] // block_rows for w in weights]
    count, columns = sum(parts), weights[0].shape[1]
    window = -(-(block_rows + LANES // 2) // LANES) * LANES
    total = groups * rows
    first, final = acc is None, name == "project_last"
    kernel = lambda table, place, *refs: project_kernel(
        ([pieces] * groups, parts),
        order,
        table,
        place,
        *refs,
        rows=rows,
        block_rows=block_rows,
        window=window,
        first=first,
        final=final,
    )
    scalar = pl.BlockSpec(memory_space=pltpu.SMEM)
    anywhere, local = pl.BlockSpec(memory_space=pltpu.HBM), pl.BlockSpec(memory_space=pltpu.VMEM)
    acc_shape = jax.ShapeDtypeStruct((total, columns), jnp.float32)
    x_shape = jax.ShapeDtypeStruct((total, count * window), jnp.bfloat16)
    w_shape = jax.ShapeDtypeStruct((count * window, columns), jnp.bfloat16)
    if not final:
        shapes, outs = acc_shape, local
    else:
        side = columns - head_width
        shapes = (
            jax.ShapeDtypeStruct((total, head_width), jnp.bfloat16),
            jax.ShapeDtypeStruct((total, side), jnp.bfloat16),
            jax.ShapeDtypeStruct(((WINDOW - 1) * TOK_DEV, side), jnp.bfloat16),
        ) + (jax.ShapeDtypeStruct((rows, side), jnp.bfloat16),) * groups
        outs = (local,) * (3 + groups)
    flops = 2 * total * count * window * columns
    moved = count * (total * window + block_rows * columns) * 2 + total * columns * 4
    return pl.pallas_call(
        kernel,
        out_shape=shapes,
        in_specs=[scalar, scalar]
        + [anywhere] * (groups * pieces + len(weights))
        + ([] if first else [local]),
        out_specs=outs,
        scratch_shapes=[
            pltpu.VMEM(x_shape.shape, jnp.bfloat16),
            pltpu.VMEM(w_shape.shape, jnp.bfloat16),
            pltpu.SemaphoreType.DMA((groups,)),
            pltpu.SemaphoreType.DMA((count,)),
        ],
        cost_estimate=pl.CostEstimate(flops=flops, bytes_accessed=moved, transcendentals=0),
        compiler_params=pltpu.CompilerParams(
            vmem_limit_bytes=scratch_limit(x_shape, w_shape, acc_shape, acc_shape)
        ),
    )(table, where, *[v for row in piece_rows for v in row], *weights, *([] if first else [acc]))


def attend_kernel(place_ref, starts_ref, q_ref, keys_ref, *refs, own):
    if own:
        stat_ref, acc_ref = refs
    else:
        stat_in, acc_in, out_ref = refs
    size = q_ref.shape[0] // TOK_DEV
    back = WINDOW - 1
    heads = q_ref.shape[1] // HD
    place, plane = place_ref[0], place_ref[1]

    def one(m, carry):
        block = place ^ m
        base = (plane * size + block) * TOK_DEV
        rows = pl.ds(pl.multiple_of(m * TOK_DEV, TOK_DEV), TOK_DEV)
        query_pos = base + lax.broadcasted_iota(jnp.int32, (1, TOK_DEV), 1)
        first_pos = jnp.zeros((1, TOK_DEV), jnp.int32)
        lowest = jnp.int32(0)
        for d in range(starts_ref.shape[0]):
            start = starts_ref[d]
            first_pos = jnp.where(start <= query_pos, jnp.maximum(first_pos, start), first_pos)
            lowest = jnp.where(start <= base, jnp.maximum(lowest, start), lowest)
        earliest = jnp.clip(lowest // TOK_DEV - (plane * size + block - back), 0, back)
        middle = jnp.maximum(back - block, 0)
        top = WINDOW - 1 if own else middle - 1

        def step(i, state):
            w = top - i
            at = (block + w) * TOK_DEV - (back * TOK_DEV if own else 0)
            at = pl.ds(pl.multiple_of(at, TOK_DEV), TOK_DEV)
            key_pos = base + (w - back) * TOK_DEV + lax.broadcasted_iota(
                jnp.int32, (TOK_DEV, 1), 0
            )
            allowed = (key_pos <= query_pos) & (key_pos >= first_pos)
            key_block, value_block = keys_ref[at, :HD], keys_ref[at, HD:]
            after = []
            for h in range(heads):
                best, norm, accum = state[h]
                scores = lax.dot_general(
                    key_block,
                    q_ref[rows, h * HD : (h + 1) * HD],
                    (((1,), (1,)), ((), ())),
                    preferred_element_type=jnp.float32,
                )
                masked = jnp.where(allowed, scores, NEG_LARGE)
                newest = jnp.maximum(best, jnp.max(masked, axis=0, keepdims=True))
                rescale = jnp.exp(best - newest)
                weights = jnp.exp(masked - newest)
                norm = norm * rescale + jnp.sum(weights, axis=0, keepdims=True)
                accum = accum * rescale + lax.dot_general(
                    value_block,
                    weights.astype(jnp.bfloat16),
                    (((0,), (0,)), ((), ())),
                    preferred_element_type=jnp.float32,
                )
                after.append((newest, norm, accum))
            return tuple(after)

        if own:
            count = WINDOW - jnp.maximum(earliest, middle)
            state = tuple(
                (
                    jnp.full((1, TOK_DEV), NEG_LARGE, jnp.float32),
                    jnp.zeros((1, TOK_DEV), jnp.float32),
                    jnp.zeros((HD, TOK_DEV), jnp.float32),
                )
                for _ in range(heads)
            )
        else:
            count = jnp.maximum(middle - earliest, 0)
            state = tuple(
                (
                    stat_in[2 * h : 2 * h + 1, rows],
                    stat_in[2 * h + 1 : 2 * h + 2, rows],
                    acc_in[h * HD : (h + 1) * HD, rows],
                )
                for h in range(heads)
            )
        state = lax.fori_loop(0, count, step, state)
        for h in range(heads):
            best, norm, accum = state[h]
            some = pl.ds(h * HD, HD)
            if own:
                stat_ref[2 * h : 2 * h + 1, rows] = best
                stat_ref[2 * h + 1 : 2 * h + 2, rows] = norm
                acc_ref[some, rows] = accum
            else:
                out_ref[some, rows] = (accum / norm).astype(out_ref.dtype)
        return carry

    lax.fori_loop(0, size, one, 0)


def attend(where, doc_starts, query_rows, keys, state):
    rows, width = query_rows.shape
    own = state is None
    scalar, local = pl.BlockSpec(memory_space=pltpu.SMEM), pl.BlockSpec(memory_space=pltpu.VMEM)
    stat = jax.ShapeDtypeStruct((2 * width // HD, rows), jnp.float32)
    accum = jax.ShapeDtypeStruct((width, rows), jnp.float32)
    out = jax.ShapeDtypeStruct((width, rows), jnp.bfloat16)
    blocks = WINDOW * WINDOW // 2
    return pl.pallas_call(
        lambda *refs: attend_kernel(*refs, own=own),
        out_shape=(stat, accum) if own else out,
        in_specs=[scalar, scalar, local, local] + ([] if own else [local, local]),
        out_specs=(local, local) if own else local,
        cost_estimate=pl.CostEstimate(
            flops=4 * blocks * TOK_DEV * width * TOK_DEV,
            bytes_accessed=8 * rows * width,
            transcendentals=blocks * TOK_DEV * TOK_DEV * width // HD,
        ),
        compiler_params=pltpu.CompilerParams(
            vmem_limit_bytes=scratch_limit(query_rows, keys, stat, accum, out, accum)
        ),
        name="attend_own" if own else "attend_halo",
    )(where, doc_starts, query_rows, keys, *([] if own else state))


def deliver_kernel(place_ref, *refs, size, steps, whole):
    if whole:
        (context_ref,), refs = refs[:1], refs[1:]
    else:
        contexts, refs = refs[:size], refs[size:]
    weights, refs = refs[:steps], refs[steps:]
    outs, refs = refs[:size], refs[size:]
    if whole:
        ws, w_sem = refs
    else:
        context_ref, ws, w_sem, c_sem = refs
    rows = weights[0].shape[0]
    copies = [
        pltpu.make_async_copy(weights[i], ws.at[pl.ds(i * rows, rows), :], w_sem.at[i])
        for i in range(steps)
    ]
    if not whole:
        width = contexts[0].shape[0]
        for m in range(size):
            for other in range(size):
                at = pl.multiple_of((place_ref[0] ^ other) * width, LANES)
                copies.append(
                    pltpu.make_async_copy(
                        contexts[other].at[:, pl.ds((m ^ other) * TOK_DEV, TOK_DEV)],
                        context_ref.at[pl.ds(at, width), pl.ds(m * TOK_DEV, TOK_DEV)],
                        c_sem.at[m * size + other],
                    )
                )
    for copy in copies:
        copy.start()
    for copy in copies:
        copy.wait()
    for m in range(size):
        outs[m][...] = jnp.dot(
            ws[...],
            context_ref[:, m * TOK_DEV : (m + 1) * TOK_DEV],
            preferred_element_type=jnp.float32,
        ).astype(outs[m].dtype)


def deliver(where, contexts, weights):
    steps, (rows, columns) = len(weights), weights[0].shape
    whole = len(contexts) == 1
    size = WINDOW
    total = contexts[0].shape[1]
    scalar = pl.BlockSpec(memory_space=pltpu.SMEM)
    anywhere, local = pl.BlockSpec(memory_space=pltpu.HBM), pl.BlockSpec(memory_space=pltpu.VMEM)
    part = jax.ShapeDtypeStruct((steps * rows, TOK_DEV), jnp.bfloat16)
    context = jax.ShapeDtypeStruct((columns, total), jnp.bfloat16)
    w_shape = jax.ShapeDtypeStruct((steps * rows, columns), jnp.bfloat16)
    scratch = [pltpu.VMEM(w_shape.shape, jnp.bfloat16), pltpu.SemaphoreType.DMA((steps,))]
    if not whole:
        scratch.append(pltpu.SemaphoreType.DMA((size * size,)))
    return pl.pallas_call(
        lambda *refs: deliver_kernel(*refs, size=size, steps=steps, whole=whole),
        out_shape=(part,) * size + (() if whole else (context,)),
        in_specs=[scalar] + [local if whole else anywhere] * len(contexts) + [anywhere] * steps,
        out_specs=(local,) * (size if whole else size + 1),
        scratch_shapes=scratch,
        cost_estimate=pl.CostEstimate(
            flops=2 * total * columns * steps * rows,
            bytes_accessed=2 * (total * columns + steps * rows * (columns + total)),
            transcendentals=0,
        ),
        compiler_params=pltpu.CompilerParams(
            vmem_limit_bytes=scratch_limit(context, w_shape, *[part] * (3 * size))
        ),
    )(where, *contexts, *weights)


def fetch(table, k, sources, target, sem):
    rows = target.shape[0]
    low = 0
    for group in sources:
        units = group[0].shape[0] // rows
        for m, ref in enumerate(group):
            inside = (table[2 * k] == m) & (table[2 * k + 1] >= low) & (table[2 * k + 1] < low + units)

            @pl.when(inside)
            def _():
                at = pl.multiple_of((table[2 * k + 1] - low) * rows, 32)
                pltpu.make_async_copy(ref.at[pl.ds(at, rows), :], target, sem).start()

        low += units


def choose(table, part, sources, rows):
    begin, end = part
    count = end - begin
    groups = [len(group) for group in sources]

    def kernel(table_ref, *refs):
        refs, (out, sem) = list(refs[:-2]), refs[-2:]
        split = [[refs.pop(0) for _ in range(n)] for n in groups]
        for k in range(count):
            fetch(table_ref, begin + k, split, out.at[k], sem.at[k])
        for k in range(count):
            pltpu.make_async_copy(out.at[k], out.at[k], sem.at[k]).wait()

    shape = jax.ShapeDtypeStruct((count, rows, TOK_DEV), jnp.bfloat16)
    flat = [v for group in sources for v in group]
    return pl.pallas_call(
        kernel,
        out_shape=shape,
        in_specs=[pl.BlockSpec(memory_space=pltpu.SMEM)]
        + [pl.BlockSpec(memory_space=pltpu.HBM)] * len(flat),
        out_specs=pl.BlockSpec(memory_space=pltpu.VMEM),
        scratch_shapes=[pltpu.SemaphoreType.DMA((count,))],
        cost_estimate=pl.CostEstimate(flops=0, bytes_accessed=4 * shape.size, transcendentals=0),
        compiler_params=pltpu.CompilerParams(vmem_limit_bytes=scratch_limit(shape, shape)),
    )(table, *flat)


def combine(ranks, mine, received):
    count, rows = mine.shape[:2]
    step = 640 // rows

    def kernel(rank_ref, mine_ref, *refs):
        theirs, sem = refs[-2:]
        out, refs = refs[-3], refs[:-3]
        low = 0
        copies = []
        for i, ref in enumerate(refs):
            units = ref.shape[0]
            copies.append(pltpu.make_async_copy(ref, theirs.at[pl.ds(low, units)], sem.at[i]))
            low += units
        for copy in copies:
            copy.start()
        for copy in copies:
            copy.wait()
        for k in range(0, count, step):
            some = [
                mine_ref[k + i].astype(jnp.float32) + theirs[rank_ref[k + i]].astype(jnp.float32)
                for i in range(step)
            ]
            total = jnp.concatenate(some, 0)
            out[:, k * rows : (k + step) * rows] = jnp.transpose(total).astype(out.dtype)

    shape = jax.ShapeDtypeStruct((TOK_DEV, count * rows), jnp.bfloat16)
    local = pl.BlockSpec(memory_space=pltpu.VMEM)
    return pl.pallas_call(
        kernel,
        out_shape=shape,
        in_specs=[pl.BlockSpec(memory_space=pltpu.SMEM), local]
        + [pl.BlockSpec(memory_space=pltpu.HBM)] * len(received),
        out_specs=local,
        scratch_shapes=[
            pltpu.VMEM((count, rows, TOK_DEV), jnp.bfloat16),
            pltpu.SemaphoreType.DMA((len(received),)),
        ],
        cost_estimate=pl.CostEstimate(
            flops=shape.size, bytes_accessed=6 * shape.size, transcendentals=0
        ),
        compiler_params=pltpu.CompilerParams(vmem_limit_bytes=scratch_limit(shape, shape, shape)),
        name="combine",
    )(ranks, mine, *received)


def settle(where, pieces):
    size, rows = len(pieces), pieces[0].shape[0]

    def kernel(place_ref, *refs):
        key_out, value_out = refs[-2:]
        for m, ref in enumerate(refs[:-2]):
            at = pl.ds(pl.multiple_of((place_ref[0] ^ m) * HD, HD), HD)
            key_out[:, at] = ref[:, :HD]
            value_out[:, at] = ref[:, HD:]

    shape = jax.ShapeDtypeStruct((rows, size * HD), jnp.bfloat16)
    local = pl.BlockSpec(memory_space=pltpu.VMEM)
    return pl.pallas_call(
        kernel,
        out_shape=(shape, shape),
        in_specs=[pl.BlockSpec(memory_space=pltpu.SMEM)] + [local] * size,
        out_specs=(local, local),
        cost_estimate=pl.CostEstimate(flops=0, bytes_accessed=8 * shape.size, transcendentals=0),
        compiler_params=pltpu.CompilerParams(vmem_limit_bytes=scratch_limit(*[shape] * 6)),
        name="settle",
    )(where, *pieces)


def plane_body(*args):
    return plane_steps(*args)


def plane_steps(rollout_rows, live_rows, doc_lengths, block_owner, norm_gain, qkv_weight, out_weight):
    seq_count, seq_index = lax.axis_size("seq"), lax.axis_index("seq")
    tp_index = lax.axis_index("tp")
    block_rows, columns = qkv_weight.shape
    local_features = rollout_rows.shape[1]
    group = HEADS // KV_HEADS
    size = columns // ((group + 2) * HD)
    planes = seq_count // size
    place, plane = seq_index % size, seq_index // size
    where = jnp.stack([place, plane]).astype(jnp.int32)
    head_width = group * HD
    half_rows = TOK_DEV // 2

    q_width = size * head_width

    def columns_of(k):
        cuts = ((k * head_width, head_width), (q_width + k * HD, HD), (q_width + (size + k) * HD, HD))
        return jnp.concatenate(
            [lax.dynamic_slice_in_dim(qkv_weight, at, wide, 1) for at, wide in cuts], 1
        )

    live = jnp.broadcast_to(live_rows[None], (8, LANES))
    below = jnp.zeros_like(live)
    for k in range(1, planes):
        below = below + jnp.where(plane >= k, turned(live, "seq", k * size), 0)
    chains = [three_away(columns_of(place), size)]
    pair = jnp.where(lax.broadcasted_iota(jnp.int32, live.shape, 0) == 0, below, live)
    plane_pairs = [pair] + [swapped(pair, "seq", m) for m in range(1, size)]
    for m in (2, 3, 1):
        chains.append(swapped(columns_of(place ^ m), "seq", m))
    chains = [chains[0]] + [three_away(chains[k], size) for k in (3, 1, 2)]
    last = 2
    top = out_weight.shape[0] // 2
    chain_o = [three_away(out_weight[:top], size), three_away(out_weight[top:], size)]

    before = sum(
        v[0, 0] + jnp.where((place ^ m) < place, v[1, 0], 0) for m, v in enumerate(plane_pairs)
    )
    spilled_in = before - seq_index * TOK_DEV
    tail_rows = lax.dynamic_slice_in_dim(rollout_rows, live_rows[0] - half_rows, half_rows, 0)
    arrived = shifted(tail_rows, "seq", 1)
    joined = jnp.concatenate([arrived, rollout_rows], 0)
    values_f = joined.astype(jnp.float32)
    squares = jnp.sum(values_f * values_f, axis=-1)
    squares = squares + swapped(squares, "tp", 1)
    scale = lax.rsqrt(squares[:, None] / D + EPSILON)
    gain = lax.dynamic_slice_in_dim(norm_gain, tp_index * local_features, local_features, 0)
    at = half_rows - spilled_in
    values_f = lax.dynamic_slice_in_dim(joined, at, TOK_DEV, 0).astype(jnp.float32)
    scale = lax.dynamic_slice_in_dim(scale, at, TOK_DEV, 0)
    normed = (values_f * scale * gain.astype(jnp.float32)).astype(jnp.bfloat16)

    cut = local_features // 2
    h1, h2 = normed[:, :cut], normed[:, cut:]
    x1, y2 = swapped(h1, "tp", 1), swapped(h2, "seq", 2)
    x2, y1 = swapped(h2, "tp", 1), swapped(h1, "seq", 2)
    yx2, xy1 = swapped(y2, "tp", 1), swapped(x1, "seq", 2)
    rows_a, rows_c = [h1, h2, x1, x2], [y1, y2, xy1, yx2]
    rows_b = [swapped(v, "seq", 1) for v in rows_a]
    rows_d = [swapped(v, "seq", 1) for v in rows_c]
    piece_rows = (rows_a, rows_b, rows_c, rows_d)

    numbers = jnp.arange(seq_count, dtype=jnp.int32)
    inverse = jnp.sum(
        jnp.where(block_owner[None, :] == numbers[:, None], numbers[None, :], 0), axis=1
    )
    half_blocks = local_features // block_rows

    def slot(blocks):
        source = inverse[blocks]
        step = (plane - source // size) % planes
        return step * size + ((source % size) ^ place)

    in_order = slot((numbers + tp_index * half_blocks) % seq_count)
    true_of = jnp.sum(
        jnp.where(in_order[None, :] == numbers[:, None], numbers[None, :], 0), axis=1
    )
    per_piece = cut // block_rows
    inside = (true_of % per_piece) * block_rows
    table = jnp.stack([true_of // per_piece, inside // LANES * LANES, inside % LANES], 1)
    doc_starts = (jnp.cumsum(doc_lengths) - doc_lengths).astype(jnp.int32)

    last = 2
    steps = [r for r in range(planes) if r != last]
    rows = block_rows // 2
    step, spot = in_order // size, in_order % size
    step = jnp.where(step == last, planes - 1, step - (step > last))
    units = jnp.stack([jnp.repeat(spot, 2), (2 * step[:, None] + jnp.arange(2)).reshape(-1)], 1)
    count = 2 * half_blocks
    here, there = units[:count], units[count:]
    among = jnp.arange(count, dtype=jnp.int32)
    early_units = 2 * (planes - 1)

    def ranks(part):
        key = jnp.maximum(part[:, 1] - early_units + 1, 0) * count + among
        return jnp.sum((key[None, :] < key[:, None]).astype(jnp.int32), axis=1)

    hit = ranks(there)[None, :] == among[:, None]
    going = jnp.sum(jnp.where(hit[:, :, None], there[None, :, :], 0), axis=1).astype(jnp.int32)
    where, table, doc_starts, going, here, here_ranks = lax.optimization_barrier(
        (
            where,
            table.astype(jnp.int32).reshape(-1),
            doc_starts,
            going.reshape(-1),
            here.astype(jnp.int32).reshape(-1),
            ranks(here),
        )
    )

    by_step = lambda some: [c[r] for r in some for c in chains]
    slots_of = lambda some: [r * size + m for r in some for m in range(size)]

    def projected(slots, weights, acc, name):
        return project(
            table, slots, where, piece_rows, weights, acc, block_rows, head_width, name
        )

    end = size - 1
    acc = projected(slots_of(steps), by_step(steps), None, "project_first")
    acc = projected(slots_of([last])[:end], by_step([last])[:end], acc, "project_mid")
    query_rows, kv_rows, kv_last, *kv_home = projected(
        slots_of([last])[end:], by_step([last])[end:], acc, "project_last"
    )

    halo = shifted(kv_last, "seq", size)
    kv_home = [kv_home[0]] + [swapped(kv_home[m], "seq", m) for m in range(1, size)]
    key_out, value_out = settle(where, kv_home)

    state = attend(where, doc_starts, query_rows, kv_rows, None)
    context = attend(where, doc_starts, query_rows, halo, state)

    from_c = swapped(context, "seq", 2)
    from_b = swapped(context, "seq", 1)
    from_d = swapped(from_c, "seq", 1)
    contexts = (context, from_b, from_c, from_d)

    def delivered(given, weights):
        pieces = deliver(where, given, weights)
        home = [pieces[0]] + [swapped(pieces[m], "seq", m) for m in range(1, size)]
        return home, pieces[size:]

    near, whole = delivered(contexts, [c[r] for r in (0, 1) for c in chain_o])
    far, _ = delivered(whole, [c[3] for c in chain_o])
    mid, _ = delivered(whole, [chain_o[0][last]])
    late, _ = delivered(whole, [chain_o[1][last]])

    first, second = count - 2 * size, count - size
    cuts = (
        ((0, first), (near, far)),
        ((first, second), (near, far, mid)),
        ((second, count), (near, far, mid, late)),
    )
    received = [swapped(choose(going, part, sources, rows), "tp", 1) for part, sources in cuts]
    mine = choose(here, (0, count), (near, far, mid, late), rows)
    mixed = combine(here_ranks, mine, received)
    return (mixed, key_out, value_out)


def solution(mesh):
    in_specs = (P("seq", "tp"), P("seq"), P(), P(), P(), P("seq", "tp"), P("seq", "tp"))
    out_specs = (P("seq", "tp"), P("seq", "tp"), P("seq", "tp"))
    size = KV_HEADS // mesh.shape["tp"]
    by_planes = size == WINDOW and mesh.shape["tp"] == 2 and mesh.shape["seq"] == WINDOW * size
    body = plane_body if by_planes else gathered_body
    return jax.shard_map(body, mesh=mesh, in_specs=in_specs, out_specs=out_specs, check_vma=False)
```

```python
import jax
import jax.numpy as jnp
from jax import lax
from jax.experimental import pallas as pl
from jax.experimental.pallas import tpu as pltpu
from jax.sharding import PartitionSpec as P

D = 5120
KV_HEADS = 8
HD = 128
HEADS = 24
WINDOW = 4
TOK_DEV = 256


EPSILON = 1e-06
NEG_LARGE = -1e30


def carried_in(value, axis, join, neutral):
    count, mine = (lax.axis_size(axis), lax.axis_index(axis))
    pieces = lax.all_gather(value, axis)
    total = jnp.full_like(value, 0) + jnp.asarray(neutral, value.dtype)

    def turn(position, total):
        longer = join(total, pieces[position])
        return jnp.where(position < mine, longer, total)

    return lax.fori_loop(0, count - 1, turn, total)


def shifted(x, axis, by):
    count = lax.axis_size(axis)
    pairs = [(i, i + by) for i in range(count) if 0 <= i + by < count]
    return lax.ppermute(x, axis, pairs)


def gathered_body(rollout_rows, live_rows, doc_lengths, block_owner, norm_gain, qkv_weight, out_weight):
    half_rows = TOK_DEV // 2
    seq_index = lax.axis_index("seq")

    def combine(earlier, later):
        return earlier + later

    before = carried_in(live_rows, "seq", combine, jnp.zeros_like(live_rows))
    spilled_in = before[0] - seq_index * TOK_DEV
    tail_rows = lax.dynamic_slice_in_dim(rollout_rows, live_rows[0] - half_rows, half_rows, 0)
    arrived = shifted(tail_rows, "seq", 1)
    joined = jnp.concatenate([arrived, rollout_rows], 0)
    owned = lax.dynamic_slice_in_dim(joined, half_rows - spilled_in, TOK_DEV, 0)
    full_rows = lax.all_gather(owned, "tp", axis=1, tiled=True)
    values_f = full_rows.astype(jnp.float32)
    scale = lax.rsqrt(jnp.mean(values_f * values_f, axis=-1, keepdims=True) + EPSILON)
    normed = (values_f * scale * norm_gain.astype(jnp.float32)).astype(jnp.bfloat16)
    block_rows = qkv_weight.shape[0]
    block_count = D // block_rows
    permuted = normed.reshape(TOK_DEV, block_count, block_rows)[:, block_owner, :].reshape(
        TOK_DEV, D
    )
    positions = jnp.arange(block_count, dtype=jnp.int32)
    inverse = jnp.sum(
        jnp.where(block_owner[None, :] == positions[:, None], positions[None, :], 0), axis=1
    )
    projected = jnp.dot(
        permuted,
        lax.all_gather(qkv_weight, "seq", axis=0, tiled=True),
        preferred_element_type=jnp.float32,
    )
    group = HEADS // KV_HEADS
    kv_local = projected.shape[1] // ((group + 2) * HD)
    q_width = kv_local * group * HD
    query_rows = (projected[:, :q_width] * HD ** (-0.5)).astype(jnp.bfloat16)
    key_rows = projected[:, q_width : q_width + kv_local * HD].astype(jnp.bfloat16)
    value_rows = projected[:, q_width + kv_local * HD :].astype(jnp.bfloat16)
    queries = query_rows.reshape(TOK_DEV, kv_local, group, HD)
    query_pos = seq_index * TOK_DEV + jnp.arange(TOK_DEV, dtype=jnp.int32)
    doc_starts = jnp.cumsum(doc_lengths) - doc_lengths
    first_pos = jnp.max(
        jnp.where(doc_starts[None, :] <= query_pos[:, None], doc_starts[None, :], 0), axis=1
    )
    initial = (
        jnp.full((kv_local, group, TOK_DEV), NEG_LARGE, jnp.float32),
        jnp.zeros((kv_local, group, TOK_DEV), jnp.float32),
        jnp.zeros((kv_local, group, TOK_DEV, HD), jnp.float32),
    )
    keys_all, values_all = (key_rows, value_rows)
    for level in range(WINDOW.bit_length() - 1):
        got_keys, got_values = shifted((keys_all, values_all), "seq", 1 << level)
        keys_all = jnp.concatenate([got_keys, keys_all], 0)
        values_all = jnp.concatenate([got_values, values_all], 0)
    state = initial
    for block in range(WINDOW):
        keys_block = keys_all[block * TOK_DEV : (block + 1) * TOK_DEV]
        attend_best, attend_totals, attend_accum = state
        key_count = keys_block.shape[0]
        keys_three = keys_block.reshape(key_count, kv_local, HD)
        values_three = values_all[block * TOK_DEV : (block + 1) * TOK_DEV].reshape(
            key_count, kv_local, HD
        )
        scores = jnp.einsum(
            "tgjd,sgd->gjts", queries, keys_three, preferred_element_type=jnp.float32
        )
        key_pos = (seq_index - WINDOW + 1 + block) * TOK_DEV + jnp.arange(
            key_count, dtype=jnp.int32
        )
        allowed = (key_pos[None, :] <= query_pos[:, None]) & (
            key_pos[None, :] >= first_pos[:, None]
        )
        masked = jnp.where(allowed, scores, NEG_LARGE)
        newest = jnp.maximum(attend_best, jnp.max(masked, axis=-1))
        rescale = jnp.exp(attend_best - newest)
        weights = jnp.where(allowed, jnp.exp(masked - newest[..., None]), 0.0)
        attend_totals = attend_totals * rescale + jnp.sum(weights, axis=-1)
        update = jnp.einsum(
            "gjts,sgd->gjtd",
            weights.astype(jnp.bfloat16),
            values_three,
            preferred_element_type=jnp.float32,
        )
        attend_accum = attend_accum * rescale[..., None] + update
        state = (newest, attend_totals, attend_accum)
    _, totals, accum = state
    context = (
        jnp.transpose(accum / totals[..., None], (2, 0, 1, 3))
        .reshape(TOK_DEV, q_width)
        .astype(jnp.bfloat16)
    )
    delivered = lax.dot_general(
        context,
        lax.all_gather(out_weight, "seq", axis=0, tiled=True),
        (((1,), (1,)), ((), ())),
        preferred_element_type=jnp.float32,
    )
    partial_value = delivered.reshape(TOK_DEV, block_count, block_rows)[:, inverse, :].reshape(
        TOK_DEV, D
    )
    mixed = lax.psum_scatter(
        partial_value.astype(jnp.bfloat16).astype(jnp.float32).astype(jnp.bfloat16),
        "tp",
        scatter_dimension=1,
        tiled=True,
    )
    return (mixed, key_rows, value_rows)


LANES = 128


def swapped(x, axis, bit):
    count = lax.axis_size(axis)
    return lax.ppermute(x, axis, [(i, i ^ bit) for i in range(count)])


def turned(x, axis, by):
    count = lax.axis_size(axis)
    return lax.ppermute(x, axis, [(i, (i + by) % count) for i in range(count)])


def three_away(x, size):
    up = turned(x, "seq", size)
    down = turned(x, "seq", -size)
    return {0: x, 1: up, 3: down, 2: turned(up, "seq", size)}


def scratch_limit(*arrays):
    total = sum(v.size * v.dtype.itemsize for v in arrays)
    return total + total // 8 + 6 * 1024 * 1024


def project_kernel(layout, order, table, place_ref, *refs, rows, block_rows, window, first, final, accs):
    pieces, weights = layout
    groups = len(pieces)
    x_refs, refs = refs[: sum(pieces)], refs[sum(pieces) :]
    w_refs, refs = refs[: len(weights)], refs[len(weights) :]
    if first:
        acc_out, xs, ws, x_sem, w_sem = refs
    elif not final:
        *acc_in, acc_out, xs, ws, x_sem, w_sem = refs
    else:
        acc_in, refs = refs[: len(accs)], refs[len(accs) :]
        q_out, kv_out, halo_out, *homes, xs, ws, x_sem, w_sem = refs
    spots = [(ref, part) for ref, parts in zip(w_refs, weights) for part in range(parts)]

    def weight_copy(i, ref, part):
        at = pl.multiple_of(i * window + table[3 * order[i] + 2], 64)
        return pltpu.make_async_copy(
            ref.at[pl.ds(part * block_rows, block_rows), :],
            ws.at[pl.ds(at, block_rows), :],
            w_sem.at[i],
        )

    for i, (ref, part) in enumerate(spots):
        weight_copy(i, ref, part).start()
    for m in range(groups):
        for i in range(len(spots)):
            piece = table[3 * order[i]]
            start = pl.multiple_of(table[3 * order[i] + 1], LANES)
            for p in range(pieces[0]):

                @pl.when(piece == p)
                def _():
                    pltpu.make_async_copy(
                        x_refs[m * pieces[0] + p].at[:, pl.ds(start, window)],
                        xs.at[pl.ds(m * rows, rows), pl.ds(i * window, window)],
                        x_sem.at[m],
                    ).start()

    pad = window - block_rows
    for i, (ref, part) in enumerate(spots):
        weight_copy(i, ref, part).wait()
        spare = pl.multiple_of(i * window + jnp.where(table[3 * order[i] + 2] == 0, block_rows, 0), 64)
        ws[pl.ds(spare, pad), :] = jnp.zeros((pad, ws.shape[1]), ws.dtype)

    def one(m, carry, acc, before):
        at = pl.ds(pl.multiple_of(m * rows, rows), rows)
        pltpu.make_async_copy(xs.at[at, :], xs.at[at, :], x_sem.at[m]).wait()
        total = jnp.dot(xs[at, :], ws[...], preferred_element_type=jnp.float32)
        if not first:
            total = total + acc[pl.ds(pl.multiple_of((m - before) * rows, rows), rows), :]
        if not final:
            acc_out[at, :] = total
        else:
            width = q_out.shape[1]
            q_out[at, :] = (total[:, :width] * HD ** (-0.5)).astype(q_out.dtype)
            kv = total[:, width:].astype(kv_out.dtype)
            for other, home in enumerate(homes):

                @pl.when(m == other)
                def _():
                    home[...] = kv

            block = place_ref[0] ^ m
            kv_out[pl.ds(pl.multiple_of(block * rows, rows), rows), :] = kv
            skipped = groups - halo_out.shape[0] // rows

            @pl.when(block >= skipped)
            def _():
                halo_out[pl.ds(pl.multiple_of((block - skipped) * rows, rows), rows), :] = kv

        return carry

    if first:
        lax.fori_loop(0, groups, lambda m, carry: one(m, carry, None, 0), 0)
    else:
        low = 0
        for acc in acc_in:
            high = low + acc.shape[0] // rows
            lax.fori_loop(low, high, lambda m, carry: one(m, carry, acc, low), 0)
            low = high


def project(table, order, where, piece_rows, weights, accs, block_rows, head_width, name):
    groups, pieces = len(piece_rows), len(piece_rows[0])
    rows = piece_rows[0][0].shape[0]
    parts = [w.shape[0] // block_rows for w in weights]
    count, columns = sum(parts), weights[0].shape[1]
    window = -(-(block_rows + LANES // 2) // LANES) * LANES
    total = groups * rows
    first, final = not accs, name == "project_last"
    kernel = lambda table, place, *refs: project_kernel(
        ([pieces] * groups, parts),
        order,
        table,
        place,
        *refs,
        rows=rows,
        block_rows=block_rows,
        window=window,
        first=first,
        final=final,
        accs=accs,
    )
    scalar = pl.BlockSpec(memory_space=pltpu.SMEM)
    anywhere, local = pl.BlockSpec(memory_space=pltpu.HBM), pl.BlockSpec(memory_space=pltpu.VMEM)
    acc_shape = jax.ShapeDtypeStruct((total, columns), jnp.float32)
    x_shape = jax.ShapeDtypeStruct((total, count * window), jnp.bfloat16)
    w_shape = jax.ShapeDtypeStruct((count * window, columns), jnp.bfloat16)
    if not final:
        shapes, outs = acc_shape, local
    else:
        side = columns - head_width
        shapes = (
            jax.ShapeDtypeStruct((total, head_width), jnp.bfloat16),
            jax.ShapeDtypeStruct((total, side), jnp.bfloat16),
            jax.ShapeDtypeStruct(((WINDOW - 1) * TOK_DEV, side), jnp.bfloat16),
        ) + (jax.ShapeDtypeStruct((rows, side), jnp.bfloat16),) * groups
        outs = (local,) * (3 + groups)
    flops = 2 * total * count * window * columns
    moved = count * (total * window + block_rows * columns) * 2 + total * columns * 4
    return pl.pallas_call(
        kernel,
        out_shape=shapes,
        in_specs=[scalar, scalar]
        + [anywhere] * (groups * pieces + len(weights))
        + [local] * len(accs),
        out_specs=outs,
        scratch_shapes=[
            pltpu.VMEM(x_shape.shape, jnp.bfloat16),
            pltpu.VMEM(w_shape.shape, jnp.bfloat16),
            pltpu.SemaphoreType.DMA((groups,)),
            pltpu.SemaphoreType.DMA((count,)),
        ],
        cost_estimate=pl.CostEstimate(flops=flops, bytes_accessed=moved, transcendentals=0),
        compiler_params=pltpu.CompilerParams(
            vmem_limit_bytes=scratch_limit(x_shape, w_shape, acc_shape, acc_shape)
        ),
    )(table, where, *[v for row in piece_rows for v in row], *weights, *accs)


def attend_kernel(place_ref, starts_ref, q_ref, keys_ref, *refs, own):
    if own:
        stat_ref, acc_ref = refs
    else:
        stat_in, acc_in, out_ref = refs
    size = q_ref.shape[0] // TOK_DEV
    back = WINDOW - 1
    heads = q_ref.shape[1] // HD
    place, plane = place_ref[0], place_ref[1]

    def one(m, carry):
        block = place ^ m
        base = (plane * size + block) * TOK_DEV
        rows = pl.ds(pl.multiple_of(m * TOK_DEV, TOK_DEV), TOK_DEV)
        query_pos = base + lax.broadcasted_iota(jnp.int32, (1, TOK_DEV), 1)
        first_pos = jnp.zeros((1, TOK_DEV), jnp.int32)
        lowest = jnp.int32(0)
        for d in range(starts_ref.shape[0]):
            start = starts_ref[d]
            first_pos = jnp.where(start <= query_pos, jnp.maximum(first_pos, start), first_pos)
            lowest = jnp.where(start <= base, jnp.maximum(lowest, start), lowest)
        earliest = jnp.clip(lowest // TOK_DEV - (plane * size + block - back), 0, back)
        middle = jnp.maximum(back - block, 0)
        top = WINDOW - 1 if own else middle - 1

        def step(i, state):
            w = top - i
            at = (block + w) * TOK_DEV - (back * TOK_DEV if own else 0)
            at = pl.ds(pl.multiple_of(at, TOK_DEV), TOK_DEV)
            key_pos = base + (w - back) * TOK_DEV + lax.broadcasted_iota(
                jnp.int32, (TOK_DEV, 1), 0
            )
            allowed = (key_pos <= query_pos) & (key_pos >= first_pos)
            key_block, value_block = keys_ref[at, :HD], keys_ref[at, HD:]
            after = []
            for h in range(heads):
                best, norm, accum = state[h]
                scores = lax.dot_general(
                    key_block,
                    q_ref[rows, h * HD : (h + 1) * HD],
                    (((1,), (1,)), ((), ())),
                    preferred_element_type=jnp.float32,
                )
                masked = jnp.where(allowed, scores, NEG_LARGE)
                newest = jnp.maximum(best, jnp.max(masked, axis=0, keepdims=True))
                rescale = jnp.exp(best - newest)
                weights = jnp.exp(masked - newest)
                norm = norm * rescale + jnp.sum(weights, axis=0, keepdims=True)
                accum = accum * rescale + lax.dot_general(
                    value_block,
                    weights.astype(jnp.bfloat16),
                    (((0,), (0,)), ((), ())),
                    preferred_element_type=jnp.float32,
                )
                after.append((newest, norm, accum))
            return tuple(after)

        if own:
            count = WINDOW - jnp.maximum(earliest, middle)
            state = tuple(
                (
                    jnp.full((1, TOK_DEV), NEG_LARGE, jnp.float32),
                    jnp.zeros((1, TOK_DEV), jnp.float32),
                    jnp.zeros((HD, TOK_DEV), jnp.float32),
                )
                for _ in range(heads)
            )
        else:
            count = jnp.maximum(middle - earliest, 0)
            state = tuple(
                (
                    stat_in[2 * h : 2 * h + 1, rows],
                    stat_in[2 * h + 1 : 2 * h + 2, rows],
                    acc_in[h * HD : (h + 1) * HD, rows],
                )
                for h in range(heads)
            )
        state = lax.fori_loop(0, count, step, state)
        for h in range(heads):
            best, norm, accum = state[h]
            some = pl.ds(h * HD, HD)
            if own:
                stat_ref[2 * h : 2 * h + 1, rows] = best
                stat_ref[2 * h + 1 : 2 * h + 2, rows] = norm
                acc_ref[some, rows] = accum
            else:
                out_ref[some, rows] = (accum / norm).astype(out_ref.dtype)
        return carry

    lax.fori_loop(0, size, one, 0)


def attend(where, doc_starts, query_rows, keys, state):
    rows, width = query_rows.shape
    own = state is None
    scalar, local = pl.BlockSpec(memory_space=pltpu.SMEM), pl.BlockSpec(memory_space=pltpu.VMEM)
    stat = jax.ShapeDtypeStruct((2 * width // HD, rows), jnp.float32)
    accum = jax.ShapeDtypeStruct((width, rows), jnp.float32)
    out = jax.ShapeDtypeStruct((width, rows), jnp.bfloat16)
    blocks = WINDOW * WINDOW // 2
    return pl.pallas_call(
        lambda *refs: attend_kernel(*refs, own=own),
        out_shape=(stat, accum) if own else out,
        in_specs=[scalar, scalar, local, local] + ([] if own else [local, local]),
        out_specs=(local, local) if own else local,
        cost_estimate=pl.CostEstimate(
            flops=4 * blocks * TOK_DEV * width * TOK_DEV,
            bytes_accessed=8 * rows * width,
            transcendentals=blocks * TOK_DEV * TOK_DEV * width // HD,
        ),
        compiler_params=pltpu.CompilerParams(
            vmem_limit_bytes=scratch_limit(query_rows, keys, stat, accum, out, accum)
        ),
        name="attend_own" if own else "attend_halo",
    )(where, doc_starts, query_rows, keys, *([] if own else state))


def deliver_kernel(place_ref, *refs, size, steps, whole):
    if whole:
        (context_ref,), refs = refs[:1], refs[1:]
    else:
        contexts, refs = refs[:size], refs[size:]
    weights, refs = refs[:steps], refs[steps:]
    outs, refs = refs[:size], refs[size:]
    if whole:
        ws, w_sem = refs
    else:
        context_ref, ws, w_sem, c_sem = refs
    rows = weights[0].shape[0]
    copies = [
        pltpu.make_async_copy(weights[i], ws.at[pl.ds(i * rows, rows), :], w_sem.at[i])
        for i in range(steps)
    ]
    if not whole:
        width = contexts[0].shape[0]
        for m in range(size):
            for other in range(size):
                at = pl.multiple_of((place_ref[0] ^ other) * width, LANES)
                copies.append(
                    pltpu.make_async_copy(
                        contexts[other].at[:, pl.ds((m ^ other) * TOK_DEV, TOK_DEV)],
                        context_ref.at[pl.ds(at, width), pl.ds(m * TOK_DEV, TOK_DEV)],
                        c_sem.at[m * size + other],
                    )
                )
    for copy in copies:
        copy.start()
    for copy in copies:
        copy.wait()
    for m in range(size):
        outs[m][...] = jnp.dot(
            ws[...],
            context_ref[:, m * TOK_DEV : (m + 1) * TOK_DEV],
            preferred_element_type=jnp.float32,
        ).astype(outs[m].dtype)


def deliver(where, contexts, weights):
    steps, (rows, columns) = len(weights), weights[0].shape
    whole = len(contexts) == 1
    size = WINDOW
    total = contexts[0].shape[1]
    scalar = pl.BlockSpec(memory_space=pltpu.SMEM)
    anywhere, local = pl.BlockSpec(memory_space=pltpu.HBM), pl.BlockSpec(memory_space=pltpu.VMEM)
    part = jax.ShapeDtypeStruct((steps * rows, TOK_DEV), jnp.bfloat16)
    context = jax.ShapeDtypeStruct((columns, total), jnp.bfloat16)
    w_shape = jax.ShapeDtypeStruct((steps * rows, columns), jnp.bfloat16)
    scratch = [pltpu.VMEM(w_shape.shape, jnp.bfloat16), pltpu.SemaphoreType.DMA((steps,))]
    if not whole:
        scratch.append(pltpu.SemaphoreType.DMA((size * size,)))
    return pl.pallas_call(
        lambda *refs: deliver_kernel(*refs, size=size, steps=steps, whole=whole),
        out_shape=(part,) * size + (() if whole else (context,)),
        in_specs=[scalar] + [local if whole else anywhere] * len(contexts) + [anywhere] * steps,
        out_specs=(local,) * (size if whole else size + 1),
        scratch_shapes=scratch,
        cost_estimate=pl.CostEstimate(
            flops=2 * total * columns * steps * rows,
            bytes_accessed=2 * (total * columns + steps * rows * (columns + total)),
            transcendentals=0,
        ),
        compiler_params=pltpu.CompilerParams(
            vmem_limit_bytes=scratch_limit(context, w_shape, *[part] * (3 * size))
        ),
    )(where, *contexts, *weights)


def fetch(table, k, sources, target, sem):
    rows = target.shape[0]
    low = 0
    for group in sources:
        units = group[0].shape[0] // rows
        for m, ref in enumerate(group):
            inside = (table[2 * k] == m) & (table[2 * k + 1] >= low) & (table[2 * k + 1] < low + units)

            @pl.when(inside)
            def _():
                at = pl.multiple_of((table[2 * k + 1] - low) * rows, 32)
                pltpu.make_async_copy(ref.at[pl.ds(at, rows), :], target, sem).start()

        low += units


def choose(table, part, sources, rows):
    begin, end = part
    count = end - begin
    groups = [len(group) for group in sources]

    def kernel(table_ref, *refs):
        refs, (out, sem) = list(refs[:-2]), refs[-2:]
        split = [[refs.pop(0) for _ in range(n)] for n in groups]
        for k in range(count):
            fetch(table_ref, begin + k, split, out.at[k], sem.at[k])
        for k in range(count):
            pltpu.make_async_copy(out.at[k], out.at[k], sem.at[k]).wait()

    shape = jax.ShapeDtypeStruct((count, rows, TOK_DEV), jnp.bfloat16)
    flat = [v for group in sources for v in group]
    return pl.pallas_call(
        kernel,
        out_shape=shape,
        in_specs=[pl.BlockSpec(memory_space=pltpu.SMEM)]
        + [pl.BlockSpec(memory_space=pltpu.HBM)] * len(flat),
        out_specs=pl.BlockSpec(memory_space=pltpu.VMEM),
        scratch_shapes=[pltpu.SemaphoreType.DMA((count,))],
        cost_estimate=pl.CostEstimate(flops=0, bytes_accessed=4 * shape.size, transcendentals=0),
        compiler_params=pltpu.CompilerParams(vmem_limit_bytes=scratch_limit(shape, shape)),
    )(table, *flat)


def combine(ranks, mine, received):
    count, rows = mine.shape[:2]
    step = 640 // rows

    def kernel(rank_ref, mine_ref, *refs):
        theirs, sem = refs[-2:]
        out, refs = refs[-3], refs[:-3]
        low = 0
        copies = []
        for i, ref in enumerate(refs):
            units = ref.shape[0]
            copies.append(pltpu.make_async_copy(ref, theirs.at[pl.ds(low, units)], sem.at[i]))
            low += units
        for copy in copies:
            copy.start()
        for copy in copies:
            copy.wait()
        for k in range(0, count, step):
            some = [
                mine_ref[k + i].astype(jnp.float32) + theirs[rank_ref[k + i]].astype(jnp.float32)
                for i in range(step)
            ]
            total = jnp.concatenate(some, 0)
            out[:, k * rows : (k + step) * rows] = jnp.transpose(total).astype(out.dtype)

    shape = jax.ShapeDtypeStruct((TOK_DEV, count * rows), jnp.bfloat16)
    local = pl.BlockSpec(memory_space=pltpu.VMEM)
    return pl.pallas_call(
        kernel,
        out_shape=shape,
        in_specs=[pl.BlockSpec(memory_space=pltpu.SMEM), local]
        + [pl.BlockSpec(memory_space=pltpu.HBM)] * len(received),
        out_specs=local,
        scratch_shapes=[
            pltpu.VMEM((count, rows, TOK_DEV), jnp.bfloat16),
            pltpu.SemaphoreType.DMA((len(received),)),
        ],
        cost_estimate=pl.CostEstimate(
            flops=shape.size, bytes_accessed=6 * shape.size, transcendentals=0
        ),
        compiler_params=pltpu.CompilerParams(vmem_limit_bytes=scratch_limit(shape, shape, shape)),
        name="combine",
    )(ranks, mine, *received)


def settle(where, pieces):
    size, rows = len(pieces), pieces[0].shape[0]

    def kernel(place_ref, *refs):
        key_out, value_out = refs[-2:]
        for m, ref in enumerate(refs[:-2]):
            at = pl.ds(pl.multiple_of((place_ref[0] ^ m) * HD, HD), HD)
            key_out[:, at] = ref[:, :HD]
            value_out[:, at] = ref[:, HD:]

    shape = jax.ShapeDtypeStruct((rows, size * HD), jnp.bfloat16)
    local = pl.BlockSpec(memory_space=pltpu.VMEM)
    return pl.pallas_call(
        kernel,
        out_shape=(shape, shape),
        in_specs=[pl.BlockSpec(memory_space=pltpu.SMEM)] + [local] * size,
        out_specs=(local, local),
        cost_estimate=pl.CostEstimate(flops=0, bytes_accessed=8 * shape.size, transcendentals=0),
        compiler_params=pltpu.CompilerParams(vmem_limit_bytes=scratch_limit(*[shape] * 6)),
        name="settle",
    )(where, *pieces)


def plane_body(*args):
    return plane_steps(*args)


def plane_steps(rollout_rows, live_rows, doc_lengths, block_owner, norm_gain, qkv_weight, out_weight):
    seq_count, seq_index = lax.axis_size("seq"), lax.axis_index("seq")
    tp_index = lax.axis_index("tp")
    block_rows, columns = qkv_weight.shape
    local_features = rollout_rows.shape[1]
    group = HEADS // KV_HEADS
    size = columns // ((group + 2) * HD)
    planes = seq_count // size
    place, plane = seq_index % size, seq_index // size
    where = jnp.stack([place, plane]).astype(jnp.int32)
    head_width = group * HD
    half_rows = TOK_DEV // 2

    q_width = size * head_width

    def columns_of(k):
        cuts = ((k * head_width, head_width), (q_width + k * HD, HD), (q_width + (size + k) * HD, HD))
        return jnp.concatenate(
            [lax.dynamic_slice_in_dim(qkv_weight, at, wide, 1) for at, wide in cuts], 1
        )

    live = jnp.broadcast_to(live_rows[None], (8, LANES))
    lower = [turned(live, "seq", k * size) for k in range(1, planes)]
    below = sum(jnp.where(plane >= k, v, 0) for k, v in zip(range(1, planes), lower))
    chains = [three_away(columns_of(place), size)]
    pair = jnp.where(lax.broadcasted_iota(jnp.int32, live.shape, 0) == 0, below, live)
    plane_pairs = [pair] + [swapped(pair, "seq", m) for m in range(1, size)]
    for m in (2, 3, 1):
        chains.append(swapped(columns_of(place ^ m), "seq", m))
    chains = [chains[0]] + [three_away(chains[k], size) for k in (3, 1, 2)]
    last = 2
    top = out_weight.shape[0] // 2
    chain_o = [three_away(out_weight[:top], size), three_away(out_weight[top:], size)]

    before = sum(
        v[0, 0] + jnp.where((place ^ m) < place, v[1, 0], 0) for m, v in enumerate(plane_pairs)
    )
    spilled_in = before - seq_index * TOK_DEV
    tail_rows = lax.dynamic_slice_in_dim(rollout_rows, live_rows[0] - half_rows, half_rows, 0)
    arrived = shifted(tail_rows, "seq", 1)
    joined = jnp.concatenate([arrived, rollout_rows], 0)
    values_f = joined.astype(jnp.float32)
    squares = jnp.sum(values_f * values_f, axis=-1)
    squares = squares + swapped(squares, "tp", 1)
    scale = lax.rsqrt(squares[:, None] / D + EPSILON)
    gain = lax.dynamic_slice_in_dim(norm_gain, tp_index * local_features, local_features, 0)
    at = half_rows - spilled_in
    values_f = lax.dynamic_slice_in_dim(joined, at, TOK_DEV, 0).astype(jnp.float32)
    scale = lax.dynamic_slice_in_dim(scale, at, TOK_DEV, 0)
    normed = (values_f * scale * gain.astype(jnp.float32)).astype(jnp.bfloat16)

    cut = local_features // 2
    h1, h2 = normed[:, :cut], normed[:, cut:]
    x1, y2 = swapped(h1, "tp", 1), swapped(h2, "seq", 2)
    x2, y1 = swapped(h2, "tp", 1), swapped(h1, "seq", 2)
    yx2, xy1 = swapped(y2, "tp", 1), swapped(x1, "seq", 2)
    rows_a, rows_c = [h1, h2, x1, x2], [y1, y2, xy1, yx2]
    rows_b = [swapped(v, "seq", 1) for v in rows_a]
    rows_d = [swapped(v, "seq", 1) for v in rows_c]
    piece_rows = (rows_a, rows_b, rows_c, rows_d)

    numbers = jnp.arange(seq_count, dtype=jnp.int32)
    inverse = jnp.sum(
        jnp.where(block_owner[None, :] == numbers[:, None], numbers[None, :], 0), axis=1
    )
    half_blocks = local_features // block_rows

    def slot(blocks):
        source = inverse[blocks]
        step = (plane - source // size) % planes
        return step * size + ((source % size) ^ place)

    in_order = slot((numbers + tp_index * half_blocks) % seq_count)
    true_of = jnp.sum(
        jnp.where(in_order[None, :] == numbers[:, None], numbers[None, :], 0), axis=1
    )
    per_piece = cut // block_rows
    inside = (true_of % per_piece) * block_rows
    table = jnp.stack([true_of // per_piece, inside // LANES * LANES, inside % LANES], 1)
    doc_starts = (jnp.cumsum(doc_lengths) - doc_lengths).astype(jnp.int32)

    last = 2
    steps = [r for r in range(planes) if r != last]
    half = size // 2
    rows = block_rows // 2
    step, spot = in_order // size, in_order % size
    step = jnp.where(step == last, planes - 1, step - (step > last))
    units = jnp.stack([jnp.repeat(spot, 2), (2 * step[:, None] + jnp.arange(2)).reshape(-1)], 1)
    count = 2 * half_blocks
    here, there = units[:count], units[count:]
    among = jnp.arange(count, dtype=jnp.int32)
    early_units = 2 * (planes - 1)

    def ranks(part):
        key = jnp.maximum(part[:, 1] - early_units + 1, 0) * count + among
        return jnp.sum((key[None, :] < key[:, None]).astype(jnp.int32), axis=1)

    hit = ranks(there)[None, :] == among[:, None]
    going = jnp.sum(jnp.where(hit[:, :, None], there[None, :, :], 0), axis=1).astype(jnp.int32)
    where, table, doc_starts, going, here, here_ranks = lax.optimization_barrier(
        (
            where,
            table.astype(jnp.int32).reshape(-1),
            doc_starts,
            going.reshape(-1),
            here.astype(jnp.int32).reshape(-1),
            ranks(here),
        )
    )

    by_step = lambda some: [c[r] for r in some for c in chains]
    slots_of = lambda some: [r * size + m for r in some for m in range(size)]

    def projected(tokens, slots, weights, accs, name):
        return project(
            table, slots, where, tokens, weights, accs, block_rows, head_width, name
        )

    end = size - 1
    accs = [
        projected(piece_rows[k : k + half], slots_of(steps), by_step(steps), [], f"project_{k}")
        for k in (0, half)
    ]
    acc = projected(piece_rows, slots_of([last])[:end], by_step([last])[:end], accs, "project_mid")
    query_rows, kv_rows, kv_last, *kv_home = projected(
        piece_rows, slots_of([last])[end:], by_step([last])[end:], [acc], "project_last"
    )

    halo = shifted(kv_last, "seq", size)
    kv_home = [kv_home[0]] + [swapped(kv_home[m], "seq", m) for m in range(1, size)]
    key_out, value_out = settle(where, kv_home)

    state = attend(where, doc_starts, query_rows, kv_rows, None)
    context = attend(where, doc_starts, query_rows, halo, state)

    from_c = swapped(context, "seq", 2)
    from_b = swapped(context, "seq", 1)
    from_d = swapped(from_c, "seq", 1)
    contexts = (context, from_b, from_c, from_d)

    def delivered(given, weights):
        pieces = deliver(where, given, weights)
        home = [pieces[0]] + [swapped(pieces[m], "seq", m) for m in range(1, size)]
        return home, pieces[size:]

    near, whole = delivered(contexts, [c[r] for r in (0, 1) for c in chain_o])
    far, _ = delivered(whole, [c[3] for c in chain_o])
    mid, _ = delivered(whole, [chain_o[0][last]])
    late, _ = delivered(whole, [chain_o[1][last]])

    first, second = count - 2 * size, count - size
    cuts = (
        ((0, first), (near, far)),
        ((first, second), (near, far, mid)),
        ((second, count), (near, far, mid, late)),
    )
    received = [swapped(choose(going, part, sources, rows), "tp", 1) for part, sources in cuts]
    mine = choose(here, (0, count), (near, far, mid, late), rows)
    mixed = combine(here_ranks, mine, received)
    return (mixed, key_out, value_out)


def solution(mesh):
    in_specs = (P("seq", "tp"), P("seq"), P(), P(), P(), P("seq", "tp"), P("seq", "tp"))
    out_specs = (P("seq", "tp"), P("seq", "tp"), P("seq", "tp"))
    size = KV_HEADS // mesh.shape["tp"]
    by_planes = size == WINDOW and mesh.shape["tp"] == 2 and mesh.shape["seq"] == WINDOW * size
    body = plane_body if by_planes else gathered_body
    return jax.shard_map(body, mesh=mesh, in_specs=in_specs, out_specs=out_specs, check_vma=False)
```

```python
import jax
import jax.numpy as jnp
from jax import lax
from jax.experimental import pallas as pl
from jax.experimental.pallas import tpu as pltpu
from jax.sharding import PartitionSpec as P

D = 5120
KV_HEADS = 8
HD = 128
HEADS = 24
WINDOW = 4
TOK_DEV = 256


EPSILON = 1e-06
NEG_LARGE = -1e30


def carried_in(value, axis, join, neutral):
    count, mine = (lax.axis_size(axis), lax.axis_index(axis))
    pieces = lax.all_gather(value, axis)
    total = jnp.full_like(value, 0) + jnp.asarray(neutral, value.dtype)

    def turn(position, total):
        longer = join(total, pieces[position])
        return jnp.where(position < mine, longer, total)

    return lax.fori_loop(0, count - 1, turn, total)


def shifted(x, axis, by):
    count = lax.axis_size(axis)
    pairs = [(i, i + by) for i in range(count) if 0 <= i + by < count]
    return lax.ppermute(x, axis, pairs)


def gathered_body(rollout_rows, live_rows, doc_lengths, block_owner, norm_gain, qkv_weight, out_weight):
    half_rows = TOK_DEV // 2
    seq_index = lax.axis_index("seq")

    def combine(earlier, later):
        return earlier + later

    before = carried_in(live_rows, "seq", combine, jnp.zeros_like(live_rows))
    spilled_in = before[0] - seq_index * TOK_DEV
    tail_rows = lax.dynamic_slice_in_dim(rollout_rows, live_rows[0] - half_rows, half_rows, 0)
    arrived = shifted(tail_rows, "seq", 1)
    joined = jnp.concatenate([arrived, rollout_rows], 0)
    owned = lax.dynamic_slice_in_dim(joined, half_rows - spilled_in, TOK_DEV, 0)
    full_rows = lax.all_gather(owned, "tp", axis=1, tiled=True)
    values_f = full_rows.astype(jnp.float32)
    scale = lax.rsqrt(jnp.mean(values_f * values_f, axis=-1, keepdims=True) + EPSILON)
    normed = (values_f * scale * norm_gain.astype(jnp.float32)).astype(jnp.bfloat16)
    block_rows = qkv_weight.shape[0]
    block_count = D // block_rows
    permuted = normed.reshape(TOK_DEV, block_count, block_rows)[:, block_owner, :].reshape(
        TOK_DEV, D
    )
    positions = jnp.arange(block_count, dtype=jnp.int32)
    inverse = jnp.sum(
        jnp.where(block_owner[None, :] == positions[:, None], positions[None, :], 0), axis=1
    )
    projected = jnp.dot(
        permuted,
        lax.all_gather(qkv_weight, "seq", axis=0, tiled=True),
        preferred_element_type=jnp.float32,
    )
    group = HEADS // KV_HEADS
    kv_local = projected.shape[1] // ((group + 2) * HD)
    q_width = kv_local * group * HD
    query_rows = (projected[:, :q_width] * HD ** (-0.5)).astype(jnp.bfloat16)
    key_rows = projected[:, q_width : q_width + kv_local * HD].astype(jnp.bfloat16)
    value_rows = projected[:, q_width + kv_local * HD :].astype(jnp.bfloat16)
    queries = query_rows.reshape(TOK_DEV, kv_local, group, HD)
    query_pos = seq_index * TOK_DEV + jnp.arange(TOK_DEV, dtype=jnp.int32)
    doc_starts = jnp.cumsum(doc_lengths) - doc_lengths
    first_pos = jnp.max(
        jnp.where(doc_starts[None, :] <= query_pos[:, None], doc_starts[None, :], 0), axis=1
    )
    initial = (
        jnp.full((kv_local, group, TOK_DEV), NEG_LARGE, jnp.float32),
        jnp.zeros((kv_local, group, TOK_DEV), jnp.float32),
        jnp.zeros((kv_local, group, TOK_DEV, HD), jnp.float32),
    )
    keys_all, values_all = (key_rows, value_rows)
    for level in range(WINDOW.bit_length() - 1):
        got_keys, got_values = shifted((keys_all, values_all), "seq", 1 << level)
        keys_all = jnp.concatenate([got_keys, keys_all], 0)
        values_all = jnp.concatenate([got_values, values_all], 0)
    state = initial
    for block in range(WINDOW):
        keys_block = keys_all[block * TOK_DEV : (block + 1) * TOK_DEV]
        attend_best, attend_totals, attend_accum = state
        key_count = keys_block.shape[0]
        keys_three = keys_block.reshape(key_count, kv_local, HD)
        values_three = values_all[block * TOK_DEV : (block + 1) * TOK_DEV].reshape(
            key_count, kv_local, HD
        )
        scores = jnp.einsum(
            "tgjd,sgd->gjts", queries, keys_three, preferred_element_type=jnp.float32
        )
        key_pos = (seq_index - WINDOW + 1 + block) * TOK_DEV + jnp.arange(
            key_count, dtype=jnp.int32
        )
        allowed = (key_pos[None, :] <= query_pos[:, None]) & (
            key_pos[None, :] >= first_pos[:, None]
        )
        masked = jnp.where(allowed, scores, NEG_LARGE)
        newest = jnp.maximum(attend_best, jnp.max(masked, axis=-1))
        rescale = jnp.exp(attend_best - newest)
        weights = jnp.where(allowed, jnp.exp(masked - newest[..., None]), 0.0)
        attend_totals = attend_totals * rescale + jnp.sum(weights, axis=-1)
        update = jnp.einsum(
            "gjts,sgd->gjtd",
            weights.astype(jnp.bfloat16),
            values_three,
            preferred_element_type=jnp.float32,
        )
        attend_accum = attend_accum * rescale[..., None] + update
        state = (newest, attend_totals, attend_accum)
    _, totals, accum = state
    context = (
        jnp.transpose(accum / totals[..., None], (2, 0, 1, 3))
        .reshape(TOK_DEV, q_width)
        .astype(jnp.bfloat16)
    )
    delivered = lax.dot_general(
        context,
        lax.all_gather(out_weight, "seq", axis=0, tiled=True),
        (((1,), (1,)), ((), ())),
        preferred_element_type=jnp.float32,
    )
    partial_value = delivered.reshape(TOK_DEV, block_count, block_rows)[:, inverse, :].reshape(
        TOK_DEV, D
    )
    mixed = lax.psum_scatter(
        partial_value.astype(jnp.bfloat16).astype(jnp.float32).astype(jnp.bfloat16),
        "tp",
        scatter_dimension=1,
        tiled=True,
    )
    return (mixed, key_rows, value_rows)


LANES = 128


def swapped(x, axis, bit):
    count = lax.axis_size(axis)
    return lax.ppermute(x, axis, [(i, i ^ bit) for i in range(count)])


def turned(x, axis, by):
    count = lax.axis_size(axis)
    return lax.ppermute(x, axis, [(i, (i + by) % count) for i in range(count)])


def three_away(x, size):
    up = turned(x, "seq", size)
    down = turned(x, "seq", -size)
    return {0: x, 1: up, 3: down, 2: turned(up, "seq", size)}


def scratch_limit(*arrays):
    total = sum(v.size * v.dtype.itemsize for v in arrays)
    return total + total // 8 + 6 * 1024 * 1024


def project_kernel(layout, order, table, place_ref, *refs, rows, block_rows, window, first, final, accs):
    pieces, weights = layout
    groups = len(pieces)
    x_refs, refs = refs[: sum(pieces)], refs[sum(pieces) :]
    w_refs, refs = refs[: len(weights)], refs[len(weights) :]
    if first:
        acc_out, xs, ws, x_sem, w_sem = refs
    elif not final:
        *acc_in, acc_out, xs, ws, x_sem, w_sem = refs
    else:
        acc_in, refs = refs[: len(accs)], refs[len(accs) :]
        q_out, kv_out, halo_out, *homes, xs, ws, x_sem, w_sem = refs
    spots = [(ref, part) for ref, parts in zip(w_refs, weights) for part in range(parts)]

    def weight_copy(i, ref, part):
        at = pl.multiple_of(i * window + table[3 * order[i] + 2], 64)
        return pltpu.make_async_copy(
            ref.at[pl.ds(part * block_rows, block_rows), :],
            ws.at[pl.ds(at, block_rows), :],
            w_sem.at[i],
        )

    for i, (ref, part) in enumerate(spots):
        weight_copy(i, ref, part).start()
    for m in range(groups):
        for i in range(len(spots)):
            piece = table[3 * order[i]]
            start = pl.multiple_of(table[3 * order[i] + 1], LANES)
            for p in range(pieces[0]):

                @pl.when(piece == p)
                def _():
                    pltpu.make_async_copy(
                        x_refs[m * pieces[0] + p].at[:, pl.ds(start, window)],
                        xs.at[pl.ds(m * rows, rows), pl.ds(i * window, window)],
                        x_sem.at[m],
                    ).start()

    pad = window - block_rows
    for i, (ref, part) in enumerate(spots):
        weight_copy(i, ref, part).wait()
        spare = pl.multiple_of(i * window + jnp.where(table[3 * order[i] + 2] == 0, block_rows, 0), 64)
        ws[pl.ds(spare, pad), :] = jnp.zeros((pad, ws.shape[1]), ws.dtype)

    def one(m, carry, acc, before):
        at = pl.ds(pl.multiple_of(m * rows, rows), rows)
        pltpu.make_async_copy(xs.at[at, :], xs.at[at, :], x_sem.at[m]).wait()
        total = jnp.dot(xs[at, :], ws[...], preferred_element_type=jnp.float32)
        if not first:
            total = total + acc[pl.ds(pl.multiple_of((m - before) * rows, rows), rows), :]
        if not final:
            acc_out[at, :] = total
        else:
            width = q_out.shape[1]
            q_out[at, :] = (total[:, :width] * HD ** (-0.5)).astype(q_out.dtype)
            kv = total[:, width:].astype(kv_out.dtype)
            for other, home in enumerate(homes):

                @pl.when(m == other)
                def _():
                    home[...] = kv

            block = place_ref[0] ^ m
            kv_out[pl.ds(pl.multiple_of(block * rows, rows), rows), :] = kv
            skipped = groups - halo_out.shape[0] // rows

            @pl.when(block >= skipped)
            def _():
                halo_out[pl.ds(pl.multiple_of((block - skipped) * rows, rows), rows), :] = kv

        return carry

    if first:
        lax.fori_loop(0, groups, lambda m, carry: one(m, carry, None, 0), 0)
    else:
        low = 0
        for acc in acc_in:
            high = low + acc.shape[0] // rows
            lax.fori_loop(low, high, lambda m, carry: one(m, carry, acc, low), 0)
            low = high


def project(table, order, where, piece_rows, weights, accs, block_rows, head_width, name):
    groups, pieces = len(piece_rows), len(piece_rows[0])
    rows = piece_rows[0][0].shape[0]
    parts = [w.shape[0] // block_rows for w in weights]
    count, columns = sum(parts), weights[0].shape[1]
    window = -(-(block_rows + LANES // 2) // LANES) * LANES
    total = groups * rows
    first, final = not accs, name == "project_last"
    kernel = lambda table, place, *refs: project_kernel(
        ([pieces] * groups, parts),
        order,
        table,
        place,
        *refs,
        rows=rows,
        block_rows=block_rows,
        window=window,
        first=first,
        final=final,
        accs=accs,
    )
    scalar = pl.BlockSpec(memory_space=pltpu.SMEM)
    anywhere, local = pl.BlockSpec(memory_space=pltpu.HBM), pl.BlockSpec(memory_space=pltpu.VMEM)
    acc_shape = jax.ShapeDtypeStruct((total, columns), jnp.float32)
    x_shape = jax.ShapeDtypeStruct((total, count * window), jnp.bfloat16)
    w_shape = jax.ShapeDtypeStruct((count * window, columns), jnp.bfloat16)
    if not final:
        shapes, outs = acc_shape, local
    else:
        side = columns - head_width
        shapes = (
            jax.ShapeDtypeStruct((total, head_width), jnp.bfloat16),
            jax.ShapeDtypeStruct((total, side), jnp.bfloat16),
            jax.ShapeDtypeStruct(((WINDOW - 1) * TOK_DEV, side), jnp.bfloat16),
        ) + (jax.ShapeDtypeStruct((rows, side), jnp.bfloat16),) * groups
        outs = (local,) * (3 + groups)
    flops = 2 * total * count * window * columns
    moved = count * (total * window + block_rows * columns) * 2 + total * columns * 4
    return pl.pallas_call(
        kernel,
        out_shape=shapes,
        in_specs=[scalar, scalar]
        + [anywhere] * (groups * pieces + len(weights))
        + [local] * len(accs),
        out_specs=outs,
        scratch_shapes=[
            pltpu.VMEM(x_shape.shape, jnp.bfloat16),
            pltpu.VMEM(w_shape.shape, jnp.bfloat16),
            pltpu.SemaphoreType.DMA((groups,)),
            pltpu.SemaphoreType.DMA((count,)),
        ],
        cost_estimate=pl.CostEstimate(flops=flops, bytes_accessed=moved, transcendentals=0),
        compiler_params=pltpu.CompilerParams(
            vmem_limit_bytes=scratch_limit(x_shape, w_shape, acc_shape, acc_shape)
        ),
    )(table, where, *[v for row in piece_rows for v in row], *weights, *accs)


def attend_kernel(place_ref, starts_ref, q_ref, keys_ref, *refs, own):
    if own:
        stat_ref, acc_ref = refs
    else:
        stat_in, acc_in, out_ref = refs
    size = q_ref.shape[0] // TOK_DEV
    back = WINDOW - 1
    heads = q_ref.shape[1] // HD
    place, plane = place_ref[0], place_ref[1]

    def one(m, carry):
        block = place ^ m
        base = (plane * size + block) * TOK_DEV
        rows = pl.ds(pl.multiple_of(m * TOK_DEV, TOK_DEV), TOK_DEV)
        query_pos = base + lax.broadcasted_iota(jnp.int32, (1, TOK_DEV), 1)
        first_pos = jnp.zeros((1, TOK_DEV), jnp.int32)
        lowest = jnp.int32(0)
        for d in range(starts_ref.shape[0]):
            start = starts_ref[d]
            first_pos = jnp.where(start <= query_pos, jnp.maximum(first_pos, start), first_pos)
            lowest = jnp.where(start <= base, jnp.maximum(lowest, start), lowest)
        earliest = jnp.clip(lowest // TOK_DEV - (plane * size + block - back), 0, back)
        middle = jnp.maximum(back - block, 0)
        top = WINDOW - 1 if own else middle - 1

        def step(i, state):
            w = top - i
            at = (block + w) * TOK_DEV - (back * TOK_DEV if own else 0)
            at = pl.ds(pl.multiple_of(at, TOK_DEV), TOK_DEV)
            key_pos = base + (w - back) * TOK_DEV + lax.broadcasted_iota(
                jnp.int32, (TOK_DEV, 1), 0
            )
            allowed = (key_pos <= query_pos) & (key_pos >= first_pos)
            key_block, value_block = keys_ref[at, :HD], keys_ref[at, HD:]
            after = []
            for h in range(heads):
                best, norm, accum = state[h]
                scores = lax.dot_general(
                    key_block,
                    q_ref[rows, h * HD : (h + 1) * HD],
                    (((1,), (1,)), ((), ())),
                    preferred_element_type=jnp.float32,
                )
                masked = jnp.where(allowed, scores, NEG_LARGE)
                newest = jnp.maximum(best, jnp.max(masked, axis=0, keepdims=True))
                rescale = jnp.exp(best - newest)
                weights = jnp.exp(masked - newest)
                norm = norm * rescale + jnp.sum(weights, axis=0, keepdims=True)
                accum = accum * rescale + lax.dot_general(
                    value_block,
                    weights.astype(jnp.bfloat16),
                    (((0,), (0,)), ((), ())),
                    preferred_element_type=jnp.float32,
                )
                after.append((newest, norm, accum))
            return tuple(after)

        if own:
            count = WINDOW - jnp.maximum(earliest, middle)
            state = tuple(
                (
                    jnp.full((1, TOK_DEV), NEG_LARGE, jnp.float32),
                    jnp.zeros((1, TOK_DEV), jnp.float32),
                    jnp.zeros((HD, TOK_DEV), jnp.float32),
                )
                for _ in range(heads)
            )
        else:
            count = jnp.maximum(middle - earliest, 0)
            state = tuple(
                (
                    stat_in[2 * h : 2 * h + 1, rows],
                    stat_in[2 * h + 1 : 2 * h + 2, rows],
                    acc_in[h * HD : (h + 1) * HD, rows],
                )
                for h in range(heads)
            )
        state = lax.fori_loop(0, count, step, state)
        for h in range(heads):
            best, norm, accum = state[h]
            some = pl.ds(h * HD, HD)
            if own:
                stat_ref[2 * h : 2 * h + 1, rows] = best
                stat_ref[2 * h + 1 : 2 * h + 2, rows] = norm
                acc_ref[some, rows] = accum
            else:
                out_ref[some, rows] = (accum / norm).astype(out_ref.dtype)
        return carry

    lax.fori_loop(0, size, one, 0)


def attend(where, doc_starts, query_rows, keys, state):
    rows, width = query_rows.shape
    own = state is None
    scalar, local = pl.BlockSpec(memory_space=pltpu.SMEM), pl.BlockSpec(memory_space=pltpu.VMEM)
    stat = jax.ShapeDtypeStruct((2 * width // HD, rows), jnp.float32)
    accum = jax.ShapeDtypeStruct((width, rows), jnp.float32)
    out = jax.ShapeDtypeStruct((width, rows), jnp.bfloat16)
    blocks = WINDOW * WINDOW // 2
    return pl.pallas_call(
        lambda *refs: attend_kernel(*refs, own=own),
        out_shape=(stat, accum) if own else out,
        in_specs=[scalar, scalar, local, local] + ([] if own else [local, local]),
        out_specs=(local, local) if own else local,
        cost_estimate=pl.CostEstimate(
            flops=4 * blocks * TOK_DEV * width * TOK_DEV,
            bytes_accessed=8 * rows * width,
            transcendentals=blocks * TOK_DEV * TOK_DEV * width // HD,
        ),
        compiler_params=pltpu.CompilerParams(
            vmem_limit_bytes=scratch_limit(query_rows, keys, stat, accum, out, accum)
        ),
        name="attend_own" if own else "attend_halo",
    )(where, doc_starts, query_rows, keys, *([] if own else state))


def deliver_kernel(place_ref, *refs, size, steps, whole):
    if whole:
        (context_ref,), refs = refs[:1], refs[1:]
    else:
        contexts, refs = refs[:size], refs[size:]
    weights, refs = refs[:steps], refs[steps:]
    keep, send, *refs = refs
    if whole:
        ws, w_sem = refs
    else:
        context_ref, ws, w_sem, c_sem = refs
    rows = weights[0].shape[0]
    copies = [
        pltpu.make_async_copy(weights[i], ws.at[pl.ds(i * rows, rows), :], w_sem.at[i])
        for i in range(steps)
    ]
    if not whole:
        width = contexts[0].shape[0]
        for m in range(size):
            for other in range(size):
                at = pl.multiple_of((place_ref[0] ^ other) * width, LANES)
                copies.append(
                    pltpu.make_async_copy(
                        contexts[other].at[:, pl.ds((m ^ other) * TOK_DEV, TOK_DEV)],
                        context_ref.at[pl.ds(at, width), pl.ds(m * TOK_DEV, TOK_DEV)],
                        c_sem.at[m * size + other],
                    )
                )
    for copy in copies:
        copy.start()
    for copy in copies:
        copy.wait()
    for m in range(size):
        part = jnp.dot(
            ws[...],
            context_ref[:, m * TOK_DEV : (m + 1) * TOK_DEV],
            preferred_element_type=jnp.float32,
        ).astype(keep.dtype)
        half = TOK_DEV // 2
        at = pl.ds(m * half, half)

        @pl.when(place_ref[2] == 0)
        def _():
            keep[:, at], send[:, at] = part[:, :half], part[:, half:]

        @pl.when(place_ref[2] != 0)
        def _():
            keep[:, at], send[:, at] = part[:, half:], part[:, :half]


def deliver(where, contexts, weights):
    steps, (rows, columns) = len(weights), weights[0].shape
    whole = len(contexts) == 1
    size = WINDOW
    total = contexts[0].shape[1]
    scalar = pl.BlockSpec(memory_space=pltpu.SMEM)
    anywhere, local = pl.BlockSpec(memory_space=pltpu.HBM), pl.BlockSpec(memory_space=pltpu.VMEM)
    part = jax.ShapeDtypeStruct((steps * rows, total // 2), jnp.bfloat16)
    context = jax.ShapeDtypeStruct((columns, total), jnp.bfloat16)
    w_shape = jax.ShapeDtypeStruct((steps * rows, columns), jnp.bfloat16)
    scratch = [pltpu.VMEM(w_shape.shape, jnp.bfloat16), pltpu.SemaphoreType.DMA((steps,))]
    if not whole:
        scratch.append(pltpu.SemaphoreType.DMA((size * size,)))
    return pl.pallas_call(
        lambda *refs: deliver_kernel(*refs, size=size, steps=steps, whole=whole),
        out_shape=(part, part) + (() if whole else (context,)),
        in_specs=[scalar] + [local if whole else anywhere] * len(contexts) + [anywhere] * steps,
        out_specs=(local,) * (2 if whole else 3),
        scratch_shapes=scratch,
        cost_estimate=pl.CostEstimate(
            flops=2 * total * columns * steps * rows,
            bytes_accessed=2 * (total * columns + steps * rows * (columns + total)),
            transcendentals=0,
        ),
        compiler_params=pltpu.CompilerParams(
            vmem_limit_bytes=scratch_limit(context, w_shape, *[part] * 6)
        ),
    )(where, *contexts, *weights)


def merge(kept, received):
    rows, total = kept.shape
    size = WINDOW
    wide = total // size

    def kernel(kept_ref, received_ref, *outs):
        for m, out in enumerate(outs):
            at = pl.ds(m * wide, wide)
            total = kept_ref[:, at].astype(jnp.float32) + received_ref[:, at].astype(jnp.float32)
            out[...] = total.astype(out.dtype)

    local = pl.BlockSpec(memory_space=pltpu.VMEM)
    shape = jax.ShapeDtypeStruct((rows, wide), jnp.bfloat16)
    return pl.pallas_call(
        kernel,
        out_shape=(shape,) * size,
        in_specs=[local, local],
        out_specs=(local,) * size,
        cost_estimate=pl.CostEstimate(
            flops=rows * total, bytes_accessed=6 * rows * total, transcendentals=0
        ),
        compiler_params=pltpu.CompilerParams(vmem_limit_bytes=scratch_limit(kept, kept, kept)),
    )(kept, received)


def fetch(table, k, sources, target, sem):
    rows = target.shape[0]
    low = 0
    for group in sources:
        units = group[0].shape[0] // rows
        for m, ref in enumerate(group):
            inside = (table[2 * k] == m) & (table[2 * k + 1] >= low) & (table[2 * k + 1] < low + units)

            @pl.when(inside)
            def _():
                at = pl.multiple_of((table[2 * k + 1] - low) * rows, 32)
                pltpu.make_async_copy(ref.at[pl.ds(at, rows), :], target, sem).start()

        low += units


def choose(table, part, sources, rows):
    begin, end = part
    count = end - begin
    groups = [len(group) for group in sources]

    def kernel(table_ref, *refs):
        refs, (out, sem) = list(refs[:-2]), refs[-2:]
        split = [[refs.pop(0) for _ in range(n)] for n in groups]
        for k in range(count):
            fetch(table_ref, begin + k, split, out.at[k], sem.at[k])
        for k in range(count):
            pltpu.make_async_copy(out.at[k], out.at[k], sem.at[k]).wait()

    shape = jax.ShapeDtypeStruct((count, rows, sources[0][0].shape[1]), jnp.bfloat16)
    flat = [v for group in sources for v in group]
    return pl.pallas_call(
        kernel,
        out_shape=shape,
        in_specs=[pl.BlockSpec(memory_space=pltpu.SMEM)]
        + [pl.BlockSpec(memory_space=pltpu.HBM)] * len(flat),
        out_specs=pl.BlockSpec(memory_space=pltpu.VMEM),
        scratch_shapes=[pltpu.SemaphoreType.DMA((count,))],
        cost_estimate=pl.CostEstimate(flops=0, bytes_accessed=4 * shape.size, transcendentals=0),
        compiler_params=pltpu.CompilerParams(vmem_limit_bytes=scratch_limit(shape, shape)),
    )(table, *flat)


def combine(where, ranks, mine, received):
    count, rows, half = mine.shape
    step = 640 // rows

    def kernel(place_ref, rank_ref, mine_ref, *refs):
        theirs, sem = refs[-2:]
        out, refs = refs[-3], refs[:-3]
        low = 0
        copies = []
        for i, ref in enumerate(refs):
            units = ref.shape[0]
            copies.append(pltpu.make_async_copy(ref, theirs.at[pl.ds(low, units)], sem.at[i]))
            low += units
        for copy in copies:
            copy.start()
        for copy in copies:
            copy.wait()
        for k in range(0, count, step):
            some = [mine_ref[k + i] for i in range(step)]
            rest = [theirs[rank_ref[k + i]] for i in range(step)]
            for blocks, side in ((some, place_ref[2]), (rest, 1 - place_ref[2])):
                total = jnp.concatenate([v.astype(jnp.float32) for v in blocks], 0)
                at = pl.ds(pl.multiple_of(side * half, half), half)
                out[at, k * rows : (k + step) * rows] = jnp.transpose(total).astype(out.dtype)

    shape = jax.ShapeDtypeStruct((TOK_DEV, count * rows), jnp.bfloat16)
    local = pl.BlockSpec(memory_space=pltpu.VMEM)
    return pl.pallas_call(
        kernel,
        out_shape=shape,
        in_specs=[pl.BlockSpec(memory_space=pltpu.SMEM)] * 2
        + [local]
        + [pl.BlockSpec(memory_space=pltpu.HBM)] * len(received),
        out_specs=local,
        scratch_shapes=[
            pltpu.VMEM(mine.shape, jnp.bfloat16),
            pltpu.SemaphoreType.DMA((len(received),)),
        ],
        cost_estimate=pl.CostEstimate(
            flops=shape.size, bytes_accessed=6 * shape.size, transcendentals=0
        ),
        compiler_params=pltpu.CompilerParams(vmem_limit_bytes=scratch_limit(shape, shape, shape)),
        name="combine",
    )(where, ranks, mine, *received)


def settle(where, pieces):
    size, rows = len(pieces), pieces[0].shape[0]

    def kernel(place_ref, *refs):
        key_out, value_out = refs[-2:]
        for m, ref in enumerate(refs[:-2]):
            at = pl.ds(pl.multiple_of((place_ref[0] ^ m) * HD, HD), HD)
            key_out[:, at] = ref[:, :HD]
            value_out[:, at] = ref[:, HD:]

    shape = jax.ShapeDtypeStruct((rows, size * HD), jnp.bfloat16)
    local = pl.BlockSpec(memory_space=pltpu.VMEM)
    return pl.pallas_call(
        kernel,
        out_shape=(shape, shape),
        in_specs=[pl.BlockSpec(memory_space=pltpu.SMEM)] + [local] * size,
        out_specs=(local, local),
        cost_estimate=pl.CostEstimate(flops=0, bytes_accessed=8 * shape.size, transcendentals=0),
        compiler_params=pltpu.CompilerParams(vmem_limit_bytes=scratch_limit(*[shape] * 6)),
        name="settle",
    )(where, *pieces)


def plane_body(*args):
    return plane_steps(*args)


def plane_steps(rollout_rows, live_rows, doc_lengths, block_owner, norm_gain, qkv_weight, out_weight):
    seq_count, seq_index = lax.axis_size("seq"), lax.axis_index("seq")
    tp_index = lax.axis_index("tp")
    block_rows, columns = qkv_weight.shape
    local_features = rollout_rows.shape[1]
    group = HEADS // KV_HEADS
    size = columns // ((group + 2) * HD)
    planes = seq_count // size
    place, plane = seq_index % size, seq_index // size
    where = jnp.stack([place, plane, tp_index]).astype(jnp.int32)
    head_width = group * HD
    half_rows = TOK_DEV // 2

    q_width = size * head_width

    def columns_of(k):
        cuts = ((k * head_width, head_width), (q_width + k * HD, HD), (q_width + (size + k) * HD, HD))
        return jnp.concatenate(
            [lax.dynamic_slice_in_dim(qkv_weight, at, wide, 1) for at, wide in cuts], 1
        )

    live = jnp.broadcast_to(live_rows[None], (8, LANES))
    lower = [turned(live, "seq", k * size) for k in range(1, planes)]
    below = sum(jnp.where(plane >= k, v, 0) for k, v in zip(range(1, planes), lower))
    chains = [three_away(columns_of(place), size)]
    pair = jnp.where(lax.broadcasted_iota(jnp.int32, live.shape, 0) == 0, below, live)
    plane_pairs = [pair] + [swapped(pair, "seq", m) for m in range(1, size)]
    for m in (2, 3, 1):
        chains.append(swapped(columns_of(place ^ m), "seq", m))
    chains = [chains[0]] + [three_away(chains[k], size) for k in (3, 1, 2)]
    last = 2
    top = out_weight.shape[0] // 2
    chain_o = [three_away(out_weight[:top], size), three_away(out_weight[top:], size)]

    before = sum(
        v[0, 0] + jnp.where((place ^ m) < place, v[1, 0], 0) for m, v in enumerate(plane_pairs)
    )
    spilled_in = before - seq_index * TOK_DEV
    tail_rows = lax.dynamic_slice_in_dim(rollout_rows, live_rows[0] - half_rows, half_rows, 0)
    arrived = shifted(tail_rows, "seq", 1)
    joined = jnp.concatenate([arrived, rollout_rows], 0)
    values_f = joined.astype(jnp.float32)
    squares = jnp.sum(values_f * values_f, axis=-1)
    squares = squares + swapped(squares, "tp", 1)
    scale = lax.rsqrt(squares[:, None] / D + EPSILON)
    gain = lax.dynamic_slice_in_dim(norm_gain, tp_index * local_features, local_features, 0)
    at = half_rows - spilled_in
    values_f = lax.dynamic_slice_in_dim(joined, at, TOK_DEV, 0).astype(jnp.float32)
    scale = lax.dynamic_slice_in_dim(scale, at, TOK_DEV, 0)
    normed = (values_f * scale * gain.astype(jnp.float32)).astype(jnp.bfloat16)

    cut = local_features // 2
    h1, h2 = normed[:, :cut], normed[:, cut:]
    x1, y2 = swapped(h1, "tp", 1), swapped(h2, "seq", 2)
    x2, y1 = swapped(h2, "tp", 1), swapped(h1, "seq", 2)
    yx2, xy1 = swapped(y2, "tp", 1), swapped(x1, "seq", 2)
    rows_a, rows_c = [h1, h2, x1, x2], [y1, y2, xy1, yx2]
    rows_b = [swapped(v, "seq", 1) for v in rows_a]
    rows_d = [swapped(v, "seq", 1) for v in rows_c]
    piece_rows = (rows_a, rows_b, rows_c, rows_d)

    numbers = jnp.arange(seq_count, dtype=jnp.int32)
    inverse = jnp.sum(
        jnp.where(block_owner[None, :] == numbers[:, None], numbers[None, :], 0), axis=1
    )
    half_blocks = local_features // block_rows

    def slot(blocks):
        source = inverse[blocks]
        step = (plane - source // size) % planes
        return step * size + ((source % size) ^ place)

    in_order = slot((numbers + tp_index * half_blocks) % seq_count)
    true_of = jnp.sum(
        jnp.where(in_order[None, :] == numbers[:, None], numbers[None, :], 0), axis=1
    )
    per_piece = cut // block_rows
    inside = (true_of % per_piece) * block_rows
    table = jnp.stack([true_of // per_piece, inside // LANES * LANES, inside % LANES], 1)
    doc_starts = (jnp.cumsum(doc_lengths) - doc_lengths).astype(jnp.int32)

    last = 2
    steps = [r for r in range(planes) if r != last]
    rows = block_rows // 2
    step, spot = in_order // size, in_order % size
    step = jnp.where(step == last, planes - 1, step - (step > last))
    units = jnp.stack([jnp.repeat(spot, 2), (2 * step[:, None] + jnp.arange(2)).reshape(-1)], 1)
    count = 2 * half_blocks
    here, there = units[:count], units[count:]
    among = jnp.arange(count, dtype=jnp.int32)
    early_units = 2 * (planes - 1)

    def ranks(part):
        key = jnp.maximum(part[:, 1] - early_units + 1, 0) * count + among
        return jnp.sum((key[None, :] < key[:, None]).astype(jnp.int32), axis=1)

    hit = ranks(there)[None, :] == among[:, None]
    going = jnp.sum(jnp.where(hit[:, :, None], there[None, :, :], 0), axis=1).astype(jnp.int32)
    where, table, doc_starts, going, here, here_ranks = lax.optimization_barrier(
        (
            where,
            table.astype(jnp.int32).reshape(-1),
            doc_starts,
            going.reshape(-1),
            here.astype(jnp.int32).reshape(-1),
            ranks(here),
        )
    )

    by_step = lambda some: [c[r] for r in some for c in chains]
    slots_of = lambda some: [r * size + m for r in some for m in range(size)]

    def projected(tokens, slots, weights, accs, name):
        return project(
            table, slots, where, tokens, weights, accs, block_rows, head_width, name
        )

    end = size - 1
    acc = projected(piece_rows, slots_of(steps), by_step(steps), [], "project_first")
    acc = projected(piece_rows, slots_of([last])[:end], by_step([last])[:end], [acc], "project_mid")
    query_rows, kv_rows, kv_last, *kv_home = projected(
        piece_rows, slots_of([last])[end:], by_step([last])[end:], [acc], "project_last"
    )

    halo = shifted(kv_last, "seq", size)
    kv_home = [kv_home[0]] + [swapped(kv_home[m], "seq", m) for m in range(1, size)]
    key_out, value_out = settle(where, kv_home)

    state = attend(where, doc_starts, query_rows, kv_rows, None)
    context = attend(where, doc_starts, query_rows, halo, state)

    from_c = swapped(context, "seq", 2)
    from_b = swapped(context, "seq", 1)
    from_d = swapped(from_c, "seq", 1)
    contexts = (context, from_b, from_c, from_d)

    def delivered(given, weights):
        kept, going_over, *whole = deliver(where, given, weights)
        received = swapped(going_over, "tp", 1)
        pieces = merge(kept, received)
        home = [pieces[0]] + [swapped(pieces[m], "seq", m) for m in range(1, size)]
        return home, whole

    near, whole = delivered(contexts, [c[r] for r in (0, 1) for c in chain_o])
    far, _ = delivered(whole, [c[3] for c in chain_o])
    mid, _ = delivered(whole, [chain_o[0][last]])
    late, _ = delivered(whole, [chain_o[1][last]])

    first, second = count - 2 * size, count - size
    cuts = (
        ((0, first), (near, far)),
        ((first, second), (near, far, mid)),
        ((second, count), (near, far, mid, late)),
    )
    received = [swapped(choose(going, part, sources, rows), "tp", 1) for part, sources in cuts]
    mine = choose(here, (0, count), (near, far, mid, late), rows)
    mixed = combine(where, here_ranks, mine, received)
    return (mixed, key_out, value_out)


def solution(mesh):
    in_specs = (P("seq", "tp"), P("seq"), P(), P(), P(), P("seq", "tp"), P("seq", "tp"))
    out_specs = (P("seq", "tp"), P("seq", "tp"), P("seq", "tp"))
    size = KV_HEADS // mesh.shape["tp"]
    by_planes = size == WINDOW and mesh.shape["tp"] == 2 and mesh.shape["seq"] == WINDOW * size
    body = plane_body if by_planes else gathered_body
    return jax.shard_map(body, mesh=mesh, in_specs=in_specs, out_specs=out_specs, check_vma=False)
```

```python
import jax
import jax.numpy as jnp
from jax import lax
from jax.experimental import pallas as pl
from jax.experimental.pallas import tpu as pltpu
from jax.sharding import PartitionSpec as P

D = 5120
KV_HEADS = 8
HD = 128
HEADS = 24
WINDOW = 4
TOK_DEV = 256


EPSILON = 1e-06
NEG_LARGE = -1e30


def carried_in(value, axis, join, neutral):
    count, mine = (lax.axis_size(axis), lax.axis_index(axis))
    pieces = lax.all_gather(value, axis)
    total = jnp.full_like(value, 0) + jnp.asarray(neutral, value.dtype)

    def turn(position, total):
        longer = join(total, pieces[position])
        return jnp.where(position < mine, longer, total)

    return lax.fori_loop(0, count - 1, turn, total)


def shifted(x, axis, by):
    count = lax.axis_size(axis)
    pairs = [(i, i + by) for i in range(count) if 0 <= i + by < count]
    return lax.ppermute(x, axis, pairs)


def gathered_body(rollout_rows, live_rows, doc_lengths, block_owner, norm_gain, qkv_weight, out_weight):
    half_rows = TOK_DEV // 2
    seq_index = lax.axis_index("seq")

    def combine(earlier, later):
        return earlier + later

    before = carried_in(live_rows, "seq", combine, jnp.zeros_like(live_rows))
    spilled_in = before[0] - seq_index * TOK_DEV
    tail_rows = lax.dynamic_slice_in_dim(rollout_rows, live_rows[0] - half_rows, half_rows, 0)
    arrived = shifted(tail_rows, "seq", 1)
    joined = jnp.concatenate([arrived, rollout_rows], 0)
    owned = lax.dynamic_slice_in_dim(joined, half_rows - spilled_in, TOK_DEV, 0)
    full_rows = lax.all_gather(owned, "tp", axis=1, tiled=True)
    values_f = full_rows.astype(jnp.float32)
    scale = lax.rsqrt(jnp.mean(values_f * values_f, axis=-1, keepdims=True) + EPSILON)
    normed = (values_f * scale * norm_gain.astype(jnp.float32)).astype(jnp.bfloat16)
    block_rows = qkv_weight.shape[0]
    block_count = D // block_rows
    permuted = normed.reshape(TOK_DEV, block_count, block_rows)[:, block_owner, :].reshape(
        TOK_DEV, D
    )
    positions = jnp.arange(block_count, dtype=jnp.int32)
    inverse = jnp.sum(
        jnp.where(block_owner[None, :] == positions[:, None], positions[None, :], 0), axis=1
    )
    projected = jnp.dot(
        permuted,
        lax.all_gather(qkv_weight, "seq", axis=0, tiled=True),
        preferred_element_type=jnp.float32,
    )
    group = HEADS // KV_HEADS
    kv_local = projected.shape[1] // ((group + 2) * HD)
    q_width = kv_local * group * HD
    query_rows = (projected[:, :q_width] * HD ** (-0.5)).astype(jnp.bfloat16)
    key_rows = projected[:, q_width : q_width + kv_local * HD].astype(jnp.bfloat16)
    value_rows = projected[:, q_width + kv_local * HD :].astype(jnp.bfloat16)
    queries = query_rows.reshape(TOK_DEV, kv_local, group, HD)
    query_pos = seq_index * TOK_DEV + jnp.arange(TOK_DEV, dtype=jnp.int32)
    doc_starts = jnp.cumsum(doc_lengths) - doc_lengths
    first_pos = jnp.max(
        jnp.where(doc_starts[None, :] <= query_pos[:, None], doc_starts[None, :], 0), axis=1
    )
    initial = (
        jnp.full((kv_local, group, TOK_DEV), NEG_LARGE, jnp.float32),
        jnp.zeros((kv_local, group, TOK_DEV), jnp.float32),
        jnp.zeros((kv_local, group, TOK_DEV, HD), jnp.float32),
    )
    keys_all, values_all = (key_rows, value_rows)
    for level in range(WINDOW.bit_length() - 1):
        got_keys, got_values = shifted((keys_all, values_all), "seq", 1 << level)
        keys_all = jnp.concatenate([got_keys, keys_all], 0)
        values_all = jnp.concatenate([got_values, values_all], 0)
    state = initial
    for block in range(WINDOW):
        keys_block = keys_all[block * TOK_DEV : (block + 1) * TOK_DEV]
        attend_best, attend_totals, attend_accum = state
        key_count = keys_block.shape[0]
        keys_three = keys_block.reshape(key_count, kv_local, HD)
        values_three = values_all[block * TOK_DEV : (block + 1) * TOK_DEV].reshape(
            key_count, kv_local, HD
        )
        scores = jnp.einsum(
            "tgjd,sgd->gjts", queries, keys_three, preferred_element_type=jnp.float32
        )
        key_pos = (seq_index - WINDOW + 1 + block) * TOK_DEV + jnp.arange(
            key_count, dtype=jnp.int32
        )
        allowed = (key_pos[None, :] <= query_pos[:, None]) & (
            key_pos[None, :] >= first_pos[:, None]
        )
        masked = jnp.where(allowed, scores, NEG_LARGE)
        newest = jnp.maximum(attend_best, jnp.max(masked, axis=-1))
        rescale = jnp.exp(attend_best - newest)
        weights = jnp.where(allowed, jnp.exp(masked - newest[..., None]), 0.0)
        attend_totals = attend_totals * rescale + jnp.sum(weights, axis=-1)
        update = jnp.einsum(
            "gjts,sgd->gjtd",
            weights.astype(jnp.bfloat16),
            values_three,
            preferred_element_type=jnp.float32,
        )
        attend_accum = attend_accum * rescale[..., None] + update
        state = (newest, attend_totals, attend_accum)
    _, totals, accum = state
    context = (
        jnp.transpose(accum / totals[..., None], (2, 0, 1, 3))
        .reshape(TOK_DEV, q_width)
        .astype(jnp.bfloat16)
    )
    delivered = lax.dot_general(
        context,
        lax.all_gather(out_weight, "seq", axis=0, tiled=True),
        (((1,), (1,)), ((), ())),
        preferred_element_type=jnp.float32,
    )
    partial_value = delivered.reshape(TOK_DEV, block_count, block_rows)[:, inverse, :].reshape(
        TOK_DEV, D
    )
    mixed = lax.psum_scatter(
        partial_value.astype(jnp.bfloat16).astype(jnp.float32).astype(jnp.bfloat16),
        "tp",
        scatter_dimension=1,
        tiled=True,
    )
    return (mixed, key_rows, value_rows)


LANES = 128


def swapped(x, axis, bit):
    count = lax.axis_size(axis)
    return lax.ppermute(x, axis, [(i, i ^ bit) for i in range(count)])


def turned(x, axis, by):
    count = lax.axis_size(axis)
    return lax.ppermute(x, axis, [(i, (i + by) % count) for i in range(count)])


def three_away(x, size):
    up = turned(x, "seq", size)
    down = turned(x, "seq", -size)
    return {0: x, 1: up, 3: down, 2: turned(up, "seq", size)}


def scratch_limit(*arrays):
    total = sum(v.size * v.dtype.itemsize for v in arrays)
    return total + total // 8 + 6 * 1024 * 1024


def project_kernel(layout, order, table, place_ref, *refs, rows, block_rows, window, first, final, accs):
    pieces, weights = layout
    groups = len(pieces)
    x_refs, refs = refs[: sum(pieces)], refs[sum(pieces) :]
    w_refs, refs = refs[: len(weights)], refs[len(weights) :]
    if first:
        acc_out, xs, ws, x_sem, w_sem = refs
    elif not final:
        *acc_in, acc_out, xs, ws, x_sem, w_sem = refs
    else:
        acc_in, refs = refs[: len(accs)], refs[len(accs) :]
        q_out, kv_out, halo_out, *homes, xs, ws, x_sem, w_sem = refs
    spots = [(ref, part) for ref, parts in zip(w_refs, weights) for part in range(parts)]

    def weight_copy(i, ref, part):
        at = pl.multiple_of(i * window + table[3 * order[i] + 2], 64)
        return pltpu.make_async_copy(
            ref.at[pl.ds(part * block_rows, block_rows), :],
            ws.at[pl.ds(at, block_rows), :],
            w_sem.at[i],
        )

    for i, (ref, part) in enumerate(spots):
        weight_copy(i, ref, part).start()
    for m in range(groups):
        for i in range(len(spots)):
            piece = table[3 * order[i]]
            start = pl.multiple_of(table[3 * order[i] + 1], LANES)
            for p in range(pieces[0]):

                @pl.when(piece == p)
                def _():
                    pltpu.make_async_copy(
                        x_refs[m * pieces[0] + p].at[:, pl.ds(start, window)],
                        xs.at[pl.ds(m * rows, rows), pl.ds(i * window, window)],
                        x_sem.at[m],
                    ).start()

    pad = window - block_rows
    for i, (ref, part) in enumerate(spots):
        weight_copy(i, ref, part).wait()
        spare = pl.multiple_of(i * window + jnp.where(table[3 * order[i] + 2] == 0, block_rows, 0), 64)
        ws[pl.ds(spare, pad), :] = jnp.zeros((pad, ws.shape[1]), ws.dtype)

    def one(m, carry, acc, before):
        at = pl.ds(pl.multiple_of(m * rows, rows), rows)
        pltpu.make_async_copy(xs.at[at, :], xs.at[at, :], x_sem.at[m]).wait()
        total = jnp.dot(xs[at, :], ws[...], preferred_element_type=jnp.float32)
        if not first:
            total = total + acc[pl.ds(pl.multiple_of((m - before) * rows, rows), rows), :]
        if not final:
            acc_out[at, :] = total
        else:
            width = q_out.shape[1]
            q_out[at, :] = (total[:, :width] * HD ** (-0.5)).astype(q_out.dtype)
            kv = total[:, width:].astype(kv_out.dtype)
            for other, home in enumerate(homes):

                @pl.when(m == other)
                def _():
                    home[...] = kv

            block = place_ref[0] ^ m
            kv_out[pl.ds(pl.multiple_of(block * rows, rows), rows), :] = kv
            skipped = groups - halo_out.shape[0] // rows

            @pl.when(block >= skipped)
            def _():
                halo_out[pl.ds(pl.multiple_of((block - skipped) * rows, rows), rows), :] = kv

        return carry

    if first:
        lax.fori_loop(0, groups, lambda m, carry: one(m, carry, None, 0), 0)
    else:
        low = 0
        for acc in acc_in:
            high = low + acc.shape[0] // rows
            lax.fori_loop(low, high, lambda m, carry: one(m, carry, acc, low), 0)
            low = high


def project(table, order, where, piece_rows, weights, accs, block_rows, head_width, name):
    groups, pieces = len(piece_rows), len(piece_rows[0])
    rows = piece_rows[0][0].shape[0]
    parts = [w.shape[0] // block_rows for w in weights]
    count, columns = sum(parts), weights[0].shape[1]
    window = -(-(block_rows + LANES // 2) // LANES) * LANES
    total = groups * rows
    first, final = not accs, name == "project_last"
    kernel = lambda table, place, *refs: project_kernel(
        ([pieces] * groups, parts),
        order,
        table,
        place,
        *refs,
        rows=rows,
        block_rows=block_rows,
        window=window,
        first=first,
        final=final,
        accs=accs,
    )
    scalar = pl.BlockSpec(memory_space=pltpu.SMEM)
    anywhere, local = pl.BlockSpec(memory_space=pltpu.HBM), pl.BlockSpec(memory_space=pltpu.VMEM)
    acc_shape = jax.ShapeDtypeStruct((total, columns), jnp.float32)
    x_shape = jax.ShapeDtypeStruct((total, count * window), jnp.bfloat16)
    w_shape = jax.ShapeDtypeStruct((count * window, columns), jnp.bfloat16)
    if not final:
        shapes, outs = acc_shape, local
    else:
        side = columns - head_width
        shapes = (
            jax.ShapeDtypeStruct((total, head_width), jnp.bfloat16),
            jax.ShapeDtypeStruct((total, side), jnp.bfloat16),
            jax.ShapeDtypeStruct(((WINDOW - 1) * TOK_DEV, side), jnp.bfloat16),
        ) + (jax.ShapeDtypeStruct((rows, side), jnp.bfloat16),) * groups
        outs = (local,) * (3 + groups)
    flops = 2 * total * count * window * columns
    moved = count * (total * window + block_rows * columns) * 2 + total * columns * 4
    return pl.pallas_call(
        kernel,
        out_shape=shapes,
        in_specs=[scalar, scalar]
        + [anywhere] * (groups * pieces + len(weights))
        + [local] * len(accs),
        out_specs=outs,
        scratch_shapes=[
            pltpu.VMEM(x_shape.shape, jnp.bfloat16),
            pltpu.VMEM(w_shape.shape, jnp.bfloat16),
            pltpu.SemaphoreType.DMA((groups,)),
            pltpu.SemaphoreType.DMA((count,)),
        ],
        cost_estimate=pl.CostEstimate(flops=flops, bytes_accessed=moved, transcendentals=0),
        compiler_params=pltpu.CompilerParams(
            vmem_limit_bytes=scratch_limit(x_shape, w_shape, acc_shape, acc_shape)
        ),
    )(table, where, *[v for row in piece_rows for v in row], *weights, *accs)


def attend_kernel(place_ref, starts_ref, q_ref, keys_ref, *refs, own):
    if own:
        stat_ref, acc_ref = refs
    else:
        stat_in, acc_in, out_ref = refs
    size = q_ref.shape[0] // TOK_DEV
    back = WINDOW - 1
    heads = q_ref.shape[1] // HD
    place, plane = place_ref[0], place_ref[1]

    def one(m, carry):
        block = place ^ m
        base = (plane * size + block) * TOK_DEV
        rows = pl.ds(pl.multiple_of(m * TOK_DEV, TOK_DEV), TOK_DEV)
        query_pos = base + lax.broadcasted_iota(jnp.int32, (1, TOK_DEV), 1)
        first_pos = jnp.zeros((1, TOK_DEV), jnp.int32)
        lowest = jnp.int32(0)
        for d in range(starts_ref.shape[0]):
            start = starts_ref[d]
            first_pos = jnp.where(start <= query_pos, jnp.maximum(first_pos, start), first_pos)
            lowest = jnp.where(start <= base, jnp.maximum(lowest, start), lowest)
        earliest = jnp.clip(lowest // TOK_DEV - (plane * size + block - back), 0, back)
        middle = jnp.maximum(back - block, 0)
        top = WINDOW - 1 if own else middle - 1

        def step(i, state):
            w = top - i
            at = (block + w) * TOK_DEV - (back * TOK_DEV if own else 0)
            at = pl.ds(pl.multiple_of(at, TOK_DEV), TOK_DEV)
            key_pos = base + (w - back) * TOK_DEV + lax.broadcasted_iota(
                jnp.int32, (TOK_DEV, 1), 0
            )
            allowed = (key_pos <= query_pos) & (key_pos >= first_pos)
            key_block, value_block = keys_ref[at, :HD], keys_ref[at, HD:]
            after = []
            for h in range(heads):
                best, norm, accum = state[h]
                scores = lax.dot_general(
                    key_block,
                    q_ref[rows, h * HD : (h + 1) * HD],
                    (((1,), (1,)), ((), ())),
                    preferred_element_type=jnp.float32,
                )
                masked = jnp.where(allowed, scores, NEG_LARGE)
                newest = jnp.maximum(best, jnp.max(masked, axis=0, keepdims=True))
                rescale = jnp.exp(best - newest)
                weights = jnp.exp(masked - newest)
                norm = norm * rescale + jnp.sum(weights, axis=0, keepdims=True)
                accum = accum * rescale + lax.dot_general(
                    value_block,
                    weights.astype(jnp.bfloat16),
                    (((0,), (0,)), ((), ())),
                    preferred_element_type=jnp.float32,
                )
                after.append((newest, norm, accum))
            return tuple(after)

        if own:
            count = WINDOW - jnp.maximum(earliest, middle)
            state = tuple(
                (
                    jnp.full((1, TOK_DEV), NEG_LARGE, jnp.float32),
                    jnp.zeros((1, TOK_DEV), jnp.float32),
                    jnp.zeros((HD, TOK_DEV), jnp.float32),
                )
                for _ in range(heads)
            )
        else:
            count = jnp.maximum(middle - earliest, 0)
            state = tuple(
                (
                    stat_in[2 * h : 2 * h + 1, rows],
                    stat_in[2 * h + 1 : 2 * h + 2, rows],
                    acc_in[h * HD : (h + 1) * HD, rows],
                )
                for h in range(heads)
            )
        state = lax.fori_loop(0, count, step, state)
        for h in range(heads):
            best, norm, accum = state[h]
            some = pl.ds(h * HD, HD)
            if own:
                stat_ref[2 * h : 2 * h + 1, rows] = best
                stat_ref[2 * h + 1 : 2 * h + 2, rows] = norm
                acc_ref[some, rows] = accum
            else:
                out_ref[some, rows] = (accum / norm).astype(out_ref.dtype)
        return carry

    lax.fori_loop(0, size, one, 0)


def attend(where, doc_starts, query_rows, keys, state):
    rows, width = query_rows.shape
    own = state is None
    scalar, local = pl.BlockSpec(memory_space=pltpu.SMEM), pl.BlockSpec(memory_space=pltpu.VMEM)
    stat = jax.ShapeDtypeStruct((2 * width // HD, rows), jnp.float32)
    accum = jax.ShapeDtypeStruct((width, rows), jnp.float32)
    out = jax.ShapeDtypeStruct((width, rows), jnp.bfloat16)
    blocks = WINDOW * WINDOW // 2
    return pl.pallas_call(
        lambda *refs: attend_kernel(*refs, own=own),
        out_shape=(stat, accum) if own else out,
        in_specs=[scalar, scalar, local, local] + ([] if own else [local, local]),
        out_specs=(local, local) if own else local,
        cost_estimate=pl.CostEstimate(
            flops=4 * blocks * TOK_DEV * width * TOK_DEV,
            bytes_accessed=8 * rows * width,
            transcendentals=blocks * TOK_DEV * TOK_DEV * width // HD,
        ),
        compiler_params=pltpu.CompilerParams(
            vmem_limit_bytes=scratch_limit(query_rows, keys, stat, accum, out, accum)
        ),
        name="attend_own" if own else "attend_halo",
    )(where, doc_starts, query_rows, keys, *([] if own else state))


def deliver_kernel(place_ref, *refs, size, steps, whole):
    if whole:
        (context_ref,), refs = refs[:1], refs[1:]
    else:
        contexts, refs = refs[:size], refs[size:]
    weights, refs = refs[:steps], refs[steps:]
    keep, send, *refs = refs
    if whole:
        ws, w_sem = refs
    else:
        context_ref, ws, w_sem, c_sem = refs
    rows = weights[0].shape[0]
    copies = [
        pltpu.make_async_copy(weights[i], ws.at[pl.ds(i * rows, rows), :], w_sem.at[i])
        for i in range(steps)
    ]
    if not whole:
        width, half = contexts[0].shape[0], TOK_DEV // 2
        for m in range(size):
            for other in range(size):
                at = pl.multiple_of((place_ref[0] ^ other) * width, LANES)
                for side in range(2):
                    start = (m ^ other) * TOK_DEV + side * half
                    to = pl.multiple_of((side ^ place_ref[2]) * size * half + m * half, half)
                    copies.append(
                        pltpu.make_async_copy(
                            contexts[other].at[:, pl.ds(start, half)],
                            context_ref.at[pl.ds(at, width), pl.ds(to, half)],
                            c_sem.at[(m * size + other) * 2 + side],
                        )
                    )
    for copy in copies:
        copy.start()
    for copy in copies:
        copy.wait()
    mine = keep.shape[1]
    for side, out in enumerate((keep, send)):
        out[...] = jnp.dot(
            ws[...],
            context_ref[:, side * mine : (side + 1) * mine],
            preferred_element_type=jnp.float32,
        ).astype(out.dtype)


def deliver(where, contexts, weights):
    steps, (rows, columns) = len(weights), weights[0].shape
    whole = len(contexts) == 1
    size = WINDOW
    total = contexts[0].shape[1]
    scalar = pl.BlockSpec(memory_space=pltpu.SMEM)
    anywhere, local = pl.BlockSpec(memory_space=pltpu.HBM), pl.BlockSpec(memory_space=pltpu.VMEM)
    part = jax.ShapeDtypeStruct((steps * rows, total // 2), jnp.bfloat16)
    context = jax.ShapeDtypeStruct((columns, total), jnp.bfloat16)
    w_shape = jax.ShapeDtypeStruct((steps * rows, columns), jnp.bfloat16)
    scratch = [pltpu.VMEM(w_shape.shape, jnp.bfloat16), pltpu.SemaphoreType.DMA((steps,))]
    if not whole:
        scratch.append(pltpu.SemaphoreType.DMA((2 * size * size,)))
    return pl.pallas_call(
        lambda *refs: deliver_kernel(*refs, size=size, steps=steps, whole=whole),
        out_shape=(part, part) + (() if whole else (context,)),
        in_specs=[scalar] + [local if whole else anywhere] * len(contexts) + [anywhere] * steps,
        out_specs=(local,) * (2 if whole else 3),
        scratch_shapes=scratch,
        cost_estimate=pl.CostEstimate(
            flops=2 * total * columns * steps * rows,
            bytes_accessed=2 * (total * columns + steps * rows * (columns + total)),
            transcendentals=0,
        ),
        compiler_params=pltpu.CompilerParams(
            vmem_limit_bytes=scratch_limit(context, w_shape, *[part] * 6)
        ),
    )(where, *contexts, *weights)


def merge(kept, received):
    rows, total = kept.shape
    size = WINDOW
    wide = total // size

    def kernel(kept_ref, received_ref, *outs):
        for m, out in enumerate(outs):
            at = pl.ds(m * wide, wide)
            total = kept_ref[:, at].astype(jnp.float32) + received_ref[:, at].astype(jnp.float32)
            out[...] = total.astype(out.dtype)

    local = pl.BlockSpec(memory_space=pltpu.VMEM)
    shape = jax.ShapeDtypeStruct((rows, wide), jnp.bfloat16)
    return pl.pallas_call(
        kernel,
        out_shape=(shape,) * size,
        in_specs=[local, local],
        out_specs=(local,) * size,
        cost_estimate=pl.CostEstimate(
            flops=rows * total, bytes_accessed=6 * rows * total, transcendentals=0
        ),
        compiler_params=pltpu.CompilerParams(vmem_limit_bytes=scratch_limit(kept, kept, kept)),
    )(kept, received)


def fetch(table, k, sources, target, sem):
    rows = target.shape[0]
    low = 0
    for group in sources:
        units = group[0].shape[0] // rows
        for m, ref in enumerate(group):
            inside = (table[2 * k] == m) & (table[2 * k + 1] >= low) & (table[2 * k + 1] < low + units)

            @pl.when(inside)
            def _():
                at = pl.multiple_of((table[2 * k + 1] - low) * rows, 32)
                pltpu.make_async_copy(ref.at[pl.ds(at, rows), :], target, sem).start()

        low += units


def choose(table, part, sources, rows):
    begin, end = part
    count = end - begin
    groups = [len(group) for group in sources]

    def kernel(table_ref, *refs):
        refs, (out, sem) = list(refs[:-2]), refs[-2:]
        split = [[refs.pop(0) for _ in range(n)] for n in groups]
        for k in range(count):
            fetch(table_ref, begin + k, split, out.at[k], sem.at[k])
        for k in range(count):
            pltpu.make_async_copy(out.at[k], out.at[k], sem.at[k]).wait()

    shape = jax.ShapeDtypeStruct((count, rows, sources[0][0].shape[1]), jnp.bfloat16)
    flat = [v for group in sources for v in group]
    return pl.pallas_call(
        kernel,
        out_shape=shape,
        in_specs=[pl.BlockSpec(memory_space=pltpu.SMEM)]
        + [pl.BlockSpec(memory_space=pltpu.HBM)] * len(flat),
        out_specs=pl.BlockSpec(memory_space=pltpu.VMEM),
        scratch_shapes=[pltpu.SemaphoreType.DMA((count,))],
        cost_estimate=pl.CostEstimate(flops=0, bytes_accessed=4 * shape.size, transcendentals=0),
        compiler_params=pltpu.CompilerParams(vmem_limit_bytes=scratch_limit(shape, shape)),
    )(table, *flat)


def combine(where, ranks, mine, received):
    count, rows, half = mine.shape
    step = 640 // rows

    def kernel(place_ref, rank_ref, mine_ref, *refs):
        theirs, sem = refs[-2:]
        out, refs = refs[-3], refs[:-3]
        low = 0
        copies = []
        for i, ref in enumerate(refs):
            units = ref.shape[0]
            copies.append(pltpu.make_async_copy(ref, theirs.at[pl.ds(low, units)], sem.at[i]))
            low += units
        for copy in copies:
            copy.start()
        for copy in copies:
            copy.wait()
        for k in range(0, count, step):
            some = [mine_ref[k + i] for i in range(step)]
            rest = [theirs[rank_ref[k + i]] for i in range(step)]
            for blocks, side in ((some, place_ref[2]), (rest, 1 - place_ref[2])):
                total = jnp.concatenate([v.astype(jnp.float32) for v in blocks], 0)
                at = pl.ds(pl.multiple_of(side * half, half), half)
                out[at, k * rows : (k + step) * rows] = jnp.transpose(total).astype(out.dtype)

    shape = jax.ShapeDtypeStruct((TOK_DEV, count * rows), jnp.bfloat16)
    local = pl.BlockSpec(memory_space=pltpu.VMEM)
    return pl.pallas_call(
        kernel,
        out_shape=shape,
        in_specs=[pl.BlockSpec(memory_space=pltpu.SMEM)] * 2
        + [local]
        + [pl.BlockSpec(memory_space=pltpu.HBM)] * len(received),
        out_specs=local,
        scratch_shapes=[
            pltpu.VMEM(mine.shape, jnp.bfloat16),
            pltpu.SemaphoreType.DMA((len(received),)),
        ],
        cost_estimate=pl.CostEstimate(
            flops=shape.size, bytes_accessed=6 * shape.size, transcendentals=0
        ),
        compiler_params=pltpu.CompilerParams(vmem_limit_bytes=scratch_limit(shape, shape, shape)),
        name="combine",
    )(where, ranks, mine, *received)


def settle(where, pieces):
    size, rows = len(pieces), pieces[0].shape[0]

    def kernel(place_ref, *refs):
        key_out, value_out = refs[-2:]
        for m, ref in enumerate(refs[:-2]):
            at = pl.ds(pl.multiple_of((place_ref[0] ^ m) * HD, HD), HD)
            key_out[:, at] = ref[:, :HD]
            value_out[:, at] = ref[:, HD:]

    shape = jax.ShapeDtypeStruct((rows, size * HD), jnp.bfloat16)
    local = pl.BlockSpec(memory_space=pltpu.VMEM)
    return pl.pallas_call(
        kernel,
        out_shape=(shape, shape),
        in_specs=[pl.BlockSpec(memory_space=pltpu.SMEM)] + [local] * size,
        out_specs=(local, local),
        cost_estimate=pl.CostEstimate(flops=0, bytes_accessed=8 * shape.size, transcendentals=0),
        compiler_params=pltpu.CompilerParams(vmem_limit_bytes=scratch_limit(*[shape] * 6)),
        name="settle",
    )(where, *pieces)


def plane_body(*args):
    return plane_steps(*args)


def plane_steps(rollout_rows, live_rows, doc_lengths, block_owner, norm_gain, qkv_weight, out_weight):
    seq_count, seq_index = lax.axis_size("seq"), lax.axis_index("seq")
    tp_index = lax.axis_index("tp")
    block_rows, columns = qkv_weight.shape
    local_features = rollout_rows.shape[1]
    group = HEADS // KV_HEADS
    size = columns // ((group + 2) * HD)
    planes = seq_count // size
    place, plane = seq_index % size, seq_index // size
    where = jnp.stack([place, plane, tp_index]).astype(jnp.int32)
    head_width = group * HD
    half_rows = TOK_DEV // 2

    q_width = size * head_width

    def columns_of(k):
        cuts = ((k * head_width, head_width), (q_width + k * HD, HD), (q_width + (size + k) * HD, HD))
        return jnp.concatenate(
            [lax.dynamic_slice_in_dim(qkv_weight, at, wide, 1) for at, wide in cuts], 1
        )

    live = jnp.broadcast_to(live_rows[None], (8, LANES))
    lower = [turned(live, "seq", k * size) for k in range(1, planes)]
    below = sum(jnp.where(plane >= k, v, 0) for k, v in zip(range(1, planes), lower))
    chains = [three_away(columns_of(place), size)]
    pair = jnp.where(lax.broadcasted_iota(jnp.int32, live.shape, 0) == 0, below, live)
    plane_pairs = [pair] + [swapped(pair, "seq", m) for m in range(1, size)]
    for m in (2, 3, 1):
        chains.append(swapped(columns_of(place ^ m), "seq", m))
    chains = [chains[0]] + [three_away(chains[k], size) for k in (3, 1, 2)]
    last = 2
    top = out_weight.shape[0] // 2
    chain_o = [three_away(out_weight[:top], size), three_away(out_weight[top:], size)]

    before = sum(
        v[0, 0] + jnp.where((place ^ m) < place, v[1, 0], 0) for m, v in enumerate(plane_pairs)
    )
    spilled_in = before - seq_index * TOK_DEV
    tail_rows = lax.dynamic_slice_in_dim(rollout_rows, live_rows[0] - half_rows, half_rows, 0)
    arrived = shifted(tail_rows, "seq", 1)
    joined = jnp.concatenate([arrived, rollout_rows], 0)
    values_f = joined.astype(jnp.float32)
    squares = jnp.sum(values_f * values_f, axis=-1)
    squares = squares + swapped(squares, "tp", 1)
    scale = lax.rsqrt(squares[:, None] / D + EPSILON)
    gain = lax.dynamic_slice_in_dim(norm_gain, tp_index * local_features, local_features, 0)
    at = half_rows - spilled_in
    values_f = lax.dynamic_slice_in_dim(joined, at, TOK_DEV, 0).astype(jnp.float32)
    scale = lax.dynamic_slice_in_dim(scale, at, TOK_DEV, 0)
    normed = (values_f * scale * gain.astype(jnp.float32)).astype(jnp.bfloat16)

    cut = local_features // 2
    h1, h2 = normed[:, :cut], normed[:, cut:]
    x1, y2 = swapped(h1, "tp", 1), swapped(h2, "seq", 2)
    x2, y1 = swapped(h2, "tp", 1), swapped(h1, "seq", 2)
    yx2, xy1 = swapped(y2, "tp", 1), swapped(x1, "seq", 2)
    rows_a, rows_c = [h1, h2, x1, x2], [y1, y2, xy1, yx2]
    rows_b = [swapped(v, "seq", 1) for v in rows_a]
    rows_d = [swapped(v, "seq", 1) for v in rows_c]
    piece_rows = (rows_a, rows_b, rows_c, rows_d)

    numbers = jnp.arange(seq_count, dtype=jnp.int32)
    inverse = jnp.sum(
        jnp.where(block_owner[None, :] == numbers[:, None], numbers[None, :], 0), axis=1
    )
    half_blocks = local_features // block_rows

    def slot(blocks):
        source = inverse[blocks]
        step = (plane - source // size) % planes
        return step * size + ((source % size) ^ place)

    in_order = slot((numbers + tp_index * half_blocks) % seq_count)
    true_of = jnp.sum(
        jnp.where(in_order[None, :] == numbers[:, None], numbers[None, :], 0), axis=1
    )
    per_piece = cut // block_rows
    inside = (true_of % per_piece) * block_rows
    table = jnp.stack([true_of // per_piece, inside // LANES * LANES, inside % LANES], 1)
    doc_starts = (jnp.cumsum(doc_lengths) - doc_lengths).astype(jnp.int32)

    last = 2
    steps = [r for r in range(planes) if r != last]
    rows = block_rows // 2
    step, spot = in_order // size, in_order % size
    step = jnp.where(step == last, planes - 1, step - (step > last))
    units = jnp.stack([jnp.repeat(spot, 2), (2 * step[:, None] + jnp.arange(2)).reshape(-1)], 1)
    count = 2 * half_blocks
    here, there = units[:count], units[count:]
    among = jnp.arange(count, dtype=jnp.int32)
    early_units = 2 * (planes - 1)

    def ranks(part):
        key = jnp.maximum(part[:, 1] - early_units + 1, 0) * count + among
        return jnp.sum((key[None, :] < key[:, None]).astype(jnp.int32), axis=1)

    hit = ranks(there)[None, :] == among[:, None]
    going = jnp.sum(jnp.where(hit[:, :, None], there[None, :, :], 0), axis=1).astype(jnp.int32)
    where, table, doc_starts, going, here, here_ranks = lax.optimization_barrier(
        (
            where,
            table.astype(jnp.int32).reshape(-1),
            doc_starts,
            going.reshape(-1),
            here.astype(jnp.int32).reshape(-1),
            ranks(here),
        )
    )

    by_step = lambda some: [c[r] for r in some for c in chains]
    slots_of = lambda some: [r * size + m for r in some for m in range(size)]

    def projected(tokens, slots, weights, accs, name):
        return project(
            table, slots, where, tokens, weights, accs, block_rows, head_width, name
        )

    end = size - 1
    acc = projected(piece_rows, slots_of(steps), by_step(steps), [], "project_first")
    acc = projected(piece_rows, slots_of([last])[:end], by_step([last])[:end], [acc], "project_mid")
    query_rows, kv_rows, kv_last, *kv_home = projected(
        piece_rows, slots_of([last])[end:], by_step([last])[end:], [acc], "project_last"
    )

    halo = shifted(kv_last, "seq", size)
    kv_home = [kv_home[0]] + [swapped(kv_home[m], "seq", m) for m in range(1, size)]
    key_out, value_out = settle(where, kv_home)

    state = attend(where, doc_starts, query_rows, kv_rows, None)
    context = attend(where, doc_starts, query_rows, halo, state)

    from_c = swapped(context, "seq", 2)
    from_b = swapped(context, "seq", 1)
    from_d = swapped(from_c, "seq", 1)
    contexts = (context, from_b, from_c, from_d)

    def delivered(given, weights):
        kept, going_over, *whole = deliver(where, given, weights)
        received = swapped(going_over, "tp", 1)
        pieces = merge(kept, received)
        home = [pieces[0]] + [swapped(pieces[m], "seq", m) for m in range(1, size)]
        return home, whole

    near, whole = delivered(contexts, [c[r] for r in (0, 1) for c in chain_o])
    far, _ = delivered(whole, [c[3] for c in chain_o])
    mid, _ = delivered(whole, [chain_o[0][last]])
    late, _ = delivered(whole, [chain_o[1][last]])

    first, second = count - 2 * size, count - size
    cuts = (
        ((0, first), (near, far)),
        ((first, second), (near, far, mid)),
        ((second, count), (near, far, mid, late)),
    )
    received = [swapped(choose(going, part, sources, rows), "tp", 1) for part, sources in cuts]
    mine = choose(here, (0, count), (near, far, mid, late), rows)
    mixed = combine(where, here_ranks, mine, received)
    return (mixed, key_out, value_out)


def solution(mesh):
    in_specs = (P("seq", "tp"), P("seq"), P(), P(), P(), P("seq", "tp"), P("seq", "tp"))
    out_specs = (P("seq", "tp"), P("seq", "tp"), P("seq", "tp"))
    size = KV_HEADS // mesh.shape["tp"]
    by_planes = size == WINDOW and mesh.shape["tp"] == 2 and mesh.shape["seq"] == WINDOW * size
    body = plane_body if by_planes else gathered_body
    return jax.shard_map(body, mesh=mesh, in_specs=in_specs, out_specs=out_specs, check_vma=False)
```

```python
import jax
import jax.numpy as jnp
from jax import lax
from jax.experimental import pallas as pl
from jax.experimental.pallas import tpu as pltpu
from jax.sharding import PartitionSpec as P

D = 5120
KV_HEADS = 8
HD = 128
HEADS = 24
WINDOW = 4
TOK_DEV = 256


EPSILON = 1e-06
NEG_LARGE = -1e30


def carried_in(value, axis, join, neutral):
    count, mine = (lax.axis_size(axis), lax.axis_index(axis))
    pieces = lax.all_gather(value, axis)
    total = jnp.full_like(value, 0) + jnp.asarray(neutral, value.dtype)

    def turn(position, total):
        longer = join(total, pieces[position])
        return jnp.where(position < mine, longer, total)

    return lax.fori_loop(0, count - 1, turn, total)


def shifted(x, axis, by):
    count = lax.axis_size(axis)
    pairs = [(i, i + by) for i in range(count) if 0 <= i + by < count]
    return lax.ppermute(x, axis, pairs)


def gathered_body(rollout_rows, live_rows, doc_lengths, block_owner, norm_gain, qkv_weight, out_weight):
    half_rows = TOK_DEV // 2
    seq_index = lax.axis_index("seq")

    def combine(earlier, later):
        return earlier + later

    before = carried_in(live_rows, "seq", combine, jnp.zeros_like(live_rows))
    spilled_in = before[0] - seq_index * TOK_DEV
    tail_rows = lax.dynamic_slice_in_dim(rollout_rows, live_rows[0] - half_rows, half_rows, 0)
    arrived = shifted(tail_rows, "seq", 1)
    joined = jnp.concatenate([arrived, rollout_rows], 0)
    owned = lax.dynamic_slice_in_dim(joined, half_rows - spilled_in, TOK_DEV, 0)
    full_rows = lax.all_gather(owned, "tp", axis=1, tiled=True)
    values_f = full_rows.astype(jnp.float32)
    scale = lax.rsqrt(jnp.mean(values_f * values_f, axis=-1, keepdims=True) + EPSILON)
    normed = (values_f * scale * norm_gain.astype(jnp.float32)).astype(jnp.bfloat16)
    block_rows = qkv_weight.shape[0]
    block_count = D // block_rows
    permuted = normed.reshape(TOK_DEV, block_count, block_rows)[:, block_owner, :].reshape(
        TOK_DEV, D
    )
    positions = jnp.arange(block_count, dtype=jnp.int32)
    inverse = jnp.sum(
        jnp.where(block_owner[None, :] == positions[:, None], positions[None, :], 0), axis=1
    )
    projected = jnp.dot(
        permuted,
        lax.all_gather(qkv_weight, "seq", axis=0, tiled=True),
        preferred_element_type=jnp.float32,
    )
    group = HEADS // KV_HEADS
    kv_local = projected.shape[1] // ((group + 2) * HD)
    q_width = kv_local * group * HD
    query_rows = (projected[:, :q_width] * HD ** (-0.5)).astype(jnp.bfloat16)
    key_rows = projected[:, q_width : q_width + kv_local * HD].astype(jnp.bfloat16)
    value_rows = projected[:, q_width + kv_local * HD :].astype(jnp.bfloat16)
    queries = query_rows.reshape(TOK_DEV, kv_local, group, HD)
    query_pos = seq_index * TOK_DEV + jnp.arange(TOK_DEV, dtype=jnp.int32)
    doc_starts = jnp.cumsum(doc_lengths) - doc_lengths
    first_pos = jnp.max(
        jnp.where(doc_starts[None, :] <= query_pos[:, None], doc_starts[None, :], 0), axis=1
    )
    initial = (
        jnp.full((kv_local, group, TOK_DEV), NEG_LARGE, jnp.float32),
        jnp.zeros((kv_local, group, TOK_DEV), jnp.float32),
        jnp.zeros((kv_local, group, TOK_DEV, HD), jnp.float32),
    )
    keys_all, values_all = (key_rows, value_rows)
    for level in range(WINDOW.bit_length() - 1):
        got_keys, got_values = shifted((keys_all, values_all), "seq", 1 << level)
        keys_all = jnp.concatenate([got_keys, keys_all], 0)
        values_all = jnp.concatenate([got_values, values_all], 0)
    state = initial
    for block in range(WINDOW):
        keys_block = keys_all[block * TOK_DEV : (block + 1) * TOK_DEV]
        attend_best, attend_totals, attend_accum = state
        key_count = keys_block.shape[0]
        keys_three = keys_block.reshape(key_count, kv_local, HD)
        values_three = values_all[block * TOK_DEV : (block + 1) * TOK_DEV].reshape(
            key_count, kv_local, HD
        )
        scores = jnp.einsum(
            "tgjd,sgd->gjts", queries, keys_three, preferred_element_type=jnp.float32
        )
        key_pos = (seq_index - WINDOW + 1 + block) * TOK_DEV + jnp.arange(
            key_count, dtype=jnp.int32
        )
        allowed = (key_pos[None, :] <= query_pos[:, None]) & (
            key_pos[None, :] >= first_pos[:, None]
        )
        masked = jnp.where(allowed, scores, NEG_LARGE)
        newest = jnp.maximum(attend_best, jnp.max(masked, axis=-1))
        rescale = jnp.exp(attend_best - newest)
        weights = jnp.where(allowed, jnp.exp(masked - newest[..., None]), 0.0)
        attend_totals = attend_totals * rescale + jnp.sum(weights, axis=-1)
        update = jnp.einsum(
            "gjts,sgd->gjtd",
            weights.astype(jnp.bfloat16),
            values_three,
            preferred_element_type=jnp.float32,
        )
        attend_accum = attend_accum * rescale[..., None] + update
        state = (newest, attend_totals, attend_accum)
    _, totals, accum = state
    context = (
        jnp.transpose(accum / totals[..., None], (2, 0, 1, 3))
        .reshape(TOK_DEV, q_width)
        .astype(jnp.bfloat16)
    )
    delivered = lax.dot_general(
        context,
        lax.all_gather(out_weight, "seq", axis=0, tiled=True),
        (((1,), (1,)), ((), ())),
        preferred_element_type=jnp.float32,
    )
    partial_value = delivered.reshape(TOK_DEV, block_count, block_rows)[:, inverse, :].reshape(
        TOK_DEV, D
    )
    mixed = lax.psum_scatter(
        partial_value.astype(jnp.bfloat16).astype(jnp.float32).astype(jnp.bfloat16),
        "tp",
        scatter_dimension=1,
        tiled=True,
    )
    return (mixed, key_rows, value_rows)


LANES = 128


def swapped(x, axis, bit):
    count = lax.axis_size(axis)
    return lax.ppermute(x, axis, [(i, i ^ bit) for i in range(count)])


def turned(x, axis, by):
    count = lax.axis_size(axis)
    return lax.ppermute(x, axis, [(i, (i + by) % count) for i in range(count)])


def three_away(x, size):
    up = turned(x, "seq", size)
    down = turned(x, "seq", -size)
    return {0: x, 1: up, 3: down, 2: turned(up, "seq", size)}


def scratch_limit(*arrays):
    total = sum(v.size * v.dtype.itemsize for v in arrays)
    return total + total // 8 + 6 * 1024 * 1024


def project_kernel(layout, order, table, place_ref, *refs, rows, block_rows, window, first, final, accs):
    pieces, weights = layout
    groups = len(pieces)
    x_refs, refs = refs[: sum(pieces)], refs[sum(pieces) :]
    w_refs, refs = refs[: len(weights)], refs[len(weights) :]
    if first:
        acc_out, xs, ws, x_sem, w_sem = refs
    elif not final:
        *acc_in, acc_out, xs, ws, x_sem, w_sem = refs
    else:
        acc_in, refs = refs[: len(accs)], refs[len(accs) :]
        q_out, kv_out, halo_out, *homes, xs, ws, x_sem, w_sem = refs
    spots = [(ref, part) for ref, parts in zip(w_refs, weights) for part in range(parts)]

    def weight_copy(i, ref, part):
        at = pl.multiple_of(i * window + table[3 * order[i] + 2], 64)
        return pltpu.make_async_copy(
            ref.at[pl.ds(part * block_rows, block_rows), :],
            ws.at[pl.ds(at, block_rows), :],
            w_sem.at[i],
        )

    for i, (ref, part) in enumerate(spots):
        weight_copy(i, ref, part).start()
    for m in range(groups):
        for i in range(len(spots)):
            piece = table[3 * order[i]]
            start = pl.multiple_of(table[3 * order[i] + 1], LANES)
            for p in range(pieces[0]):

                @pl.when(piece == p)
                def _():
                    pltpu.make_async_copy(
                        x_refs[m * pieces[0] + p].at[:, pl.ds(start, window)],
                        xs.at[pl.ds(m * rows, rows), pl.ds(i * window, window)],
                        x_sem.at[m],
                    ).start()

    pad = window - block_rows
    for i, (ref, part) in enumerate(spots):
        weight_copy(i, ref, part).wait()
        spare = pl.multiple_of(i * window + jnp.where(table[3 * order[i] + 2] == 0, block_rows, 0), 64)
        ws[pl.ds(spare, pad), :] = jnp.zeros((pad, ws.shape[1]), ws.dtype)

    def one(m, carry, acc, before):
        at = pl.ds(pl.multiple_of(m * rows, rows), rows)
        pltpu.make_async_copy(xs.at[at, :], xs.at[at, :], x_sem.at[m]).wait()
        total = jnp.dot(xs[at, :], ws[...], preferred_element_type=jnp.float32)
        if not first:
            total = total + acc[pl.ds(pl.multiple_of((m - before) * rows, rows), rows), :]
        if not final:
            acc_out[at, :] = total
        else:
            width = q_out.shape[1]
            q_out[at, :] = (total[:, :width] * HD ** (-0.5)).astype(q_out.dtype)
            kv = total[:, width:].astype(kv_out.dtype)
            for other, home in enumerate(homes):

                @pl.when(m == other)
                def _():
                    home[...] = kv

            block = place_ref[0] ^ m
            kv_out[pl.ds(pl.multiple_of(block * rows, rows), rows), :] = kv
            skipped = groups - halo_out.shape[0] // rows

            @pl.when(block >= skipped)
            def _():
                halo_out[pl.ds(pl.multiple_of((block - skipped) * rows, rows), rows), :] = kv

        return carry

    if first:
        lax.fori_loop(0, groups, lambda m, carry: one(m, carry, None, 0), 0)
    else:
        low = 0
        for acc in acc_in:
            high = low + acc.shape[0] // rows
            lax.fori_loop(low, high, lambda m, carry: one(m, carry, acc, low), 0)
            low = high


def project(table, order, where, piece_rows, weights, accs, block_rows, head_width, name):
    groups, pieces = len(piece_rows), len(piece_rows[0])
    rows = piece_rows[0][0].shape[0]
    parts = [w.shape[0] // block_rows for w in weights]
    count, columns = sum(parts), weights[0].shape[1]
    window = -(-(block_rows + LANES // 2) // LANES) * LANES
    total = groups * rows
    first, final = not accs, name == "project_last"
    kernel = lambda table, place, *refs: project_kernel(
        ([pieces] * groups, parts),
        order,
        table,
        place,
        *refs,
        rows=rows,
        block_rows=block_rows,
        window=window,
        first=first,
        final=final,
        accs=accs,
    )
    scalar = pl.BlockSpec(memory_space=pltpu.SMEM)
    anywhere, local = pl.BlockSpec(memory_space=pltpu.HBM), pl.BlockSpec(memory_space=pltpu.VMEM)
    acc_shape = jax.ShapeDtypeStruct((total, columns), jnp.float32)
    x_shape = jax.ShapeDtypeStruct((total, count * window), jnp.bfloat16)
    w_shape = jax.ShapeDtypeStruct((count * window, columns), jnp.bfloat16)
    if not final:
        shapes, outs = acc_shape, local
    else:
        side = columns - head_width
        shapes = (
            jax.ShapeDtypeStruct((total, head_width), jnp.bfloat16),
            jax.ShapeDtypeStruct((total, side), jnp.bfloat16),
            jax.ShapeDtypeStruct(((WINDOW - 1) * TOK_DEV, side), jnp.bfloat16),
        ) + (jax.ShapeDtypeStruct((rows, side), jnp.bfloat16),) * groups
        outs = (local,) * (3 + groups)
    flops = 2 * total * count * window * columns
    moved = count * (total * window + block_rows * columns) * 2 + total * columns * 4
    return pl.pallas_call(
        kernel,
        out_shape=shapes,
        in_specs=[scalar, scalar]
        + [anywhere] * (groups * pieces + len(weights))
        + [local] * len(accs),
        out_specs=outs,
        scratch_shapes=[
            pltpu.VMEM(x_shape.shape, jnp.bfloat16),
            pltpu.VMEM(w_shape.shape, jnp.bfloat16),
            pltpu.SemaphoreType.DMA((groups,)),
            pltpu.SemaphoreType.DMA((count,)),
        ],
        cost_estimate=pl.CostEstimate(flops=flops, bytes_accessed=moved, transcendentals=0),
        compiler_params=pltpu.CompilerParams(
            vmem_limit_bytes=scratch_limit(x_shape, w_shape, acc_shape, acc_shape)
        ),
    )(table, where, *[v for row in piece_rows for v in row], *weights, *accs)


def attend_kernel(place_ref, starts_ref, q_ref, keys_ref, *refs, own):
    if own:
        stat_ref, acc_ref = refs
    else:
        stat_in, acc_in, out_ref = refs
    size = q_ref.shape[0] // TOK_DEV
    back = WINDOW - 1
    heads = q_ref.shape[1] // HD
    place, plane = place_ref[0], place_ref[1]

    def one(m, carry):
        block = place ^ m
        base = (plane * size + block) * TOK_DEV
        rows = pl.ds(pl.multiple_of(m * TOK_DEV, TOK_DEV), TOK_DEV)
        query_pos = base + lax.broadcasted_iota(jnp.int32, (1, TOK_DEV), 1)
        first_pos = jnp.zeros((1, TOK_DEV), jnp.int32)
        lowest = jnp.int32(0)
        for d in range(starts_ref.shape[0]):
            start = starts_ref[d]
            first_pos = jnp.where(start <= query_pos, jnp.maximum(first_pos, start), first_pos)
            lowest = jnp.where(start <= base, jnp.maximum(lowest, start), lowest)
        earliest = jnp.clip(lowest // TOK_DEV - (plane * size + block - back), 0, back)
        middle = jnp.maximum(back - block, 0)
        top = WINDOW - 1 if own else middle - 1

        def step(i, state):
            w = top - i
            at = (block + w) * TOK_DEV - (back * TOK_DEV if own else 0)
            at = pl.ds(pl.multiple_of(at, TOK_DEV), TOK_DEV)
            key_pos = base + (w - back) * TOK_DEV + lax.broadcasted_iota(
                jnp.int32, (TOK_DEV, 1), 0
            )
            allowed = (key_pos <= query_pos) & (key_pos >= first_pos)
            key_block, value_block = keys_ref[at, :HD], keys_ref[at, HD:]
            after = []
            for h in range(heads):
                best, norm, accum = state[h]
                scores = lax.dot_general(
                    key_block,
                    q_ref[rows, h * HD : (h + 1) * HD],
                    (((1,), (1,)), ((), ())),
                    preferred_element_type=jnp.float32,
                )
                masked = jnp.where(allowed, scores, NEG_LARGE)
                newest = jnp.maximum(best, jnp.max(masked, axis=0, keepdims=True))
                rescale = jnp.exp(best - newest)
                weights = jnp.exp(masked - newest)
                norm = norm * rescale + jnp.sum(weights, axis=0, keepdims=True)
                accum = accum * rescale + lax.dot_general(
                    value_block,
                    weights.astype(jnp.bfloat16),
                    (((0,), (0,)), ((), ())),
                    preferred_element_type=jnp.float32,
                )
                after.append((newest, norm, accum))
            return tuple(after)

        if own:
            count = WINDOW - jnp.maximum(earliest, middle)
            state = tuple(
                (
                    jnp.full((1, TOK_DEV), NEG_LARGE, jnp.float32),
                    jnp.zeros((1, TOK_DEV), jnp.float32),
                    jnp.zeros((HD, TOK_DEV), jnp.float32),
                )
                for _ in range(heads)
            )
        else:
            count = jnp.maximum(middle - earliest, 0)
            state = tuple(
                (
                    stat_in[2 * h : 2 * h + 1, rows],
                    stat_in[2 * h + 1 : 2 * h + 2, rows],
                    acc_in[h * HD : (h + 1) * HD, rows],
                )
                for h in range(heads)
            )
        state = lax.fori_loop(0, count, step, state)
        for h in range(heads):
            best, norm, accum = state[h]
            some = pl.ds(h * HD, HD)
            if own:
                stat_ref[2 * h : 2 * h + 1, rows] = best
                stat_ref[2 * h + 1 : 2 * h + 2, rows] = norm
                acc_ref[some, rows] = accum
            else:
                out_ref[some, rows] = (accum / norm).astype(out_ref.dtype)
        return carry

    lax.fori_loop(0, size, one, 0)


def attend(where, doc_starts, query_rows, keys, state):
    rows, width = query_rows.shape
    own = state is None
    scalar, local = pl.BlockSpec(memory_space=pltpu.SMEM), pl.BlockSpec(memory_space=pltpu.VMEM)
    stat = jax.ShapeDtypeStruct((2 * width // HD, rows), jnp.float32)
    accum = jax.ShapeDtypeStruct((width, rows), jnp.float32)
    out = jax.ShapeDtypeStruct((width, rows), jnp.bfloat16)
    blocks = WINDOW * WINDOW // 2
    return pl.pallas_call(
        lambda *refs: attend_kernel(*refs, own=own),
        out_shape=(stat, accum) if own else out,
        in_specs=[scalar, scalar, local, local] + ([] if own else [local, local]),
        out_specs=(local, local) if own else local,
        cost_estimate=pl.CostEstimate(
            flops=4 * blocks * TOK_DEV * width * TOK_DEV,
            bytes_accessed=8 * rows * width,
            transcendentals=blocks * TOK_DEV * TOK_DEV * width // HD,
        ),
        compiler_params=pltpu.CompilerParams(
            vmem_limit_bytes=scratch_limit(query_rows, keys, stat, accum, out, accum)
        ),
        name="attend_own" if own else "attend_halo",
    )(where, doc_starts, query_rows, keys, *([] if own else state))


def deliver_kernel(place_ref, *refs, size, spans, whole):
    if whole:
        (context_ref,), refs = refs[:1], refs[1:]
    else:
        contexts, refs = refs[:size], refs[size:]
    steps = len(spans)
    weights, refs = refs[:steps], refs[steps:]
    keep, send, *refs = refs
    if whole:
        ws, w_sem = refs
    else:
        context_ref, ws, w_sem, c_sem = refs
    copies, to = [], 0
    for i, (start, rows) in enumerate(spans):
        copies.append(
            pltpu.make_async_copy(
                weights[i].at[pl.ds(start, rows), :], ws.at[pl.ds(to, rows), :], w_sem.at[i]
            )
        )
        to += rows
    if not whole:
        width, half = contexts[0].shape[0], TOK_DEV // 2
        for m in range(size):
            for other in range(size):
                at = pl.multiple_of((place_ref[0] ^ other) * width, LANES)
                for side in range(2):
                    start = (m ^ other) * TOK_DEV + side * half
                    to = pl.multiple_of((side ^ place_ref[2]) * size * half + m * half, half)
                    copies.append(
                        pltpu.make_async_copy(
                            contexts[other].at[:, pl.ds(start, half)],
                            context_ref.at[pl.ds(at, width), pl.ds(to, half)],
                            c_sem.at[(m * size + other) * 2 + side],
                        )
                    )
    for copy in copies:
        copy.start()
    for copy in copies:
        copy.wait()
    mine = keep.shape[1]
    for side, out in enumerate((keep, send)):
        out[...] = jnp.dot(
            ws[...],
            context_ref[:, side * mine : (side + 1) * mine],
            preferred_element_type=jnp.float32,
        ).astype(out.dtype)


def deliver(where, contexts, weights):
    spans = [(start, rows) for _, start, rows in weights]
    weights = [v for v, _, _ in weights]
    steps, columns = len(weights), weights[0].shape[1]
    rows = sum(v for _, v in spans)
    whole = len(contexts) == 1
    size = WINDOW
    total = contexts[0].shape[1]
    scalar = pl.BlockSpec(memory_space=pltpu.SMEM)
    anywhere, local = pl.BlockSpec(memory_space=pltpu.HBM), pl.BlockSpec(memory_space=pltpu.VMEM)
    part = jax.ShapeDtypeStruct((rows, total // 2), jnp.bfloat16)
    context = jax.ShapeDtypeStruct((columns, total), jnp.bfloat16)
    w_shape = jax.ShapeDtypeStruct((rows, columns), jnp.bfloat16)
    scratch = [pltpu.VMEM(w_shape.shape, jnp.bfloat16), pltpu.SemaphoreType.DMA((steps,))]
    if not whole:
        scratch.append(pltpu.SemaphoreType.DMA((2 * size * size,)))
    return pl.pallas_call(
        lambda *refs: deliver_kernel(*refs, size=size, spans=spans, whole=whole),
        out_shape=(part, part) + (() if whole else (context,)),
        in_specs=[scalar] + [local if whole else anywhere] * len(contexts) + [anywhere] * steps,
        out_specs=(local,) * (2 if whole else 3),
        scratch_shapes=scratch,
        cost_estimate=pl.CostEstimate(
            flops=2 * total * columns * rows,
            bytes_accessed=2 * (total * columns + rows * (columns + total)),
            transcendentals=0,
        ),
        compiler_params=pltpu.CompilerParams(
            vmem_limit_bytes=scratch_limit(context, w_shape, *[part] * 6)
        ),
    )(where, *contexts, *weights)


def merge(kept, received):
    rows, total = kept.shape
    size = WINDOW
    wide = total // size

    def kernel(kept_ref, received_ref, *outs):
        for m, out in enumerate(outs):
            at = pl.ds(m * wide, wide)
            total = kept_ref[:, at].astype(jnp.float32) + received_ref[:, at].astype(jnp.float32)
            out[...] = total.astype(out.dtype)

    local = pl.BlockSpec(memory_space=pltpu.VMEM)
    shape = jax.ShapeDtypeStruct((rows, wide), jnp.bfloat16)
    return pl.pallas_call(
        kernel,
        out_shape=(shape,) * size,
        in_specs=[local, local],
        out_specs=(local,) * size,
        cost_estimate=pl.CostEstimate(
            flops=rows * total, bytes_accessed=6 * rows * total, transcendentals=0
        ),
        compiler_params=pltpu.CompilerParams(vmem_limit_bytes=scratch_limit(kept, kept, kept)),
    )(kept, received)


def fetch(table, k, sources, target, sem):
    rows = target.shape[0]
    low = 0
    for group in sources:
        units = group[0].shape[0] // rows
        for m, ref in enumerate(group):
            inside = (table[2 * k] == m) & (table[2 * k + 1] >= low) & (table[2 * k + 1] < low + units)

            @pl.when(inside)
            def _():
                at = pl.multiple_of((table[2 * k + 1] - low) * rows, 32)
                pltpu.make_async_copy(ref.at[pl.ds(at, rows), :], target, sem).start()

        low += units


def choose(table, part, sources, rows):
    begin, end = part
    count = end - begin
    groups = [len(group) for group in sources]

    def kernel(table_ref, *refs):
        refs, (out, sem) = list(refs[:-2]), refs[-2:]
        split = [[refs.pop(0) for _ in range(n)] for n in groups]
        for k in range(count):
            fetch(table_ref, begin + k, split, out.at[k], sem.at[k])
        for k in range(count):
            pltpu.make_async_copy(out.at[k], out.at[k], sem.at[k]).wait()

    shape = jax.ShapeDtypeStruct((count, rows, sources[0][0].shape[1]), jnp.bfloat16)
    flat = [v for group in sources for v in group]
    return pl.pallas_call(
        kernel,
        out_shape=shape,
        in_specs=[pl.BlockSpec(memory_space=pltpu.SMEM)]
        + [pl.BlockSpec(memory_space=pltpu.HBM)] * len(flat),
        out_specs=pl.BlockSpec(memory_space=pltpu.VMEM),
        scratch_shapes=[pltpu.SemaphoreType.DMA((count,))],
        cost_estimate=pl.CostEstimate(flops=0, bytes_accessed=4 * shape.size, transcendentals=0),
        compiler_params=pltpu.CompilerParams(vmem_limit_bytes=scratch_limit(shape, shape)),
    )(table, *flat)


def combine(where, ranks, mine, received):
    count, rows, half = mine.shape
    step = 640 // rows

    def kernel(place_ref, rank_ref, mine_ref, *refs):
        theirs, sem = refs[-2:]
        out, refs = refs[-3], refs[:-3]
        low = 0
        copies = []
        for i, ref in enumerate(refs):
            units = ref.shape[0]
            copies.append(pltpu.make_async_copy(ref, theirs.at[pl.ds(low, units)], sem.at[i]))
            low += units
        for copy in copies:
            copy.start()
        for copy in copies:
            copy.wait()
        for k in range(0, count, step):
            some = [mine_ref[k + i] for i in range(step)]
            rest = [theirs[rank_ref[k + i]] for i in range(step)]
            for blocks, side in ((some, place_ref[2]), (rest, 1 - place_ref[2])):
                total = jnp.concatenate([v.astype(jnp.float32) for v in blocks], 0)
                at = pl.ds(pl.multiple_of(side * half, half), half)
                out[at, k * rows : (k + step) * rows] = jnp.transpose(total).astype(out.dtype)

    shape = jax.ShapeDtypeStruct((TOK_DEV, count * rows), jnp.bfloat16)
    local = pl.BlockSpec(memory_space=pltpu.VMEM)
    return pl.pallas_call(
        kernel,
        out_shape=shape,
        in_specs=[pl.BlockSpec(memory_space=pltpu.SMEM)] * 2
        + [local]
        + [pl.BlockSpec(memory_space=pltpu.HBM)] * len(received),
        out_specs=local,
        scratch_shapes=[
            pltpu.VMEM(mine.shape, jnp.bfloat16),
            pltpu.SemaphoreType.DMA((len(received),)),
        ],
        cost_estimate=pl.CostEstimate(
            flops=shape.size, bytes_accessed=6 * shape.size, transcendentals=0
        ),
        compiler_params=pltpu.CompilerParams(vmem_limit_bytes=scratch_limit(shape, shape, shape)),
        name="combine",
    )(where, ranks, mine, *received)


def settle(where, pieces):
    size, rows = len(pieces), pieces[0].shape[0]

    def kernel(place_ref, *refs):
        key_out, value_out = refs[-2:]
        for m, ref in enumerate(refs[:-2]):
            at = pl.ds(pl.multiple_of((place_ref[0] ^ m) * HD, HD), HD)
            key_out[:, at] = ref[:, :HD]
            value_out[:, at] = ref[:, HD:]

    shape = jax.ShapeDtypeStruct((rows, size * HD), jnp.bfloat16)
    local = pl.BlockSpec(memory_space=pltpu.VMEM)
    return pl.pallas_call(
        kernel,
        out_shape=(shape, shape),
        in_specs=[pl.BlockSpec(memory_space=pltpu.SMEM)] + [local] * size,
        out_specs=(local, local),
        cost_estimate=pl.CostEstimate(flops=0, bytes_accessed=8 * shape.size, transcendentals=0),
        compiler_params=pltpu.CompilerParams(vmem_limit_bytes=scratch_limit(*[shape] * 6)),
        name="settle",
    )(where, *pieces)


def plane_body(*args):
    return plane_steps(*args)


def plane_steps(rollout_rows, live_rows, doc_lengths, block_owner, norm_gain, qkv_weight, out_weight):
    seq_count, seq_index = lax.axis_size("seq"), lax.axis_index("seq")
    tp_index = lax.axis_index("tp")
    block_rows, columns = qkv_weight.shape
    local_features = rollout_rows.shape[1]
    group = HEADS // KV_HEADS
    size = columns // ((group + 2) * HD)
    planes = seq_count // size
    place, plane = seq_index % size, seq_index // size
    where = jnp.stack([place, plane, tp_index]).astype(jnp.int32)
    head_width = group * HD
    half_rows = TOK_DEV // 2

    q_width = size * head_width

    def columns_of(k):
        cuts = ((k * head_width, head_width), (q_width + k * HD, HD), (q_width + (size + k) * HD, HD))
        return jnp.concatenate(
            [lax.dynamic_slice_in_dim(qkv_weight, at, wide, 1) for at, wide in cuts], 1
        )

    live = jnp.broadcast_to(live_rows[None], (8, LANES))
    lower = [turned(live, "seq", k * size) for k in range(1, planes)]
    below = sum(jnp.where(plane >= k, v, 0) for k, v in zip(range(1, planes), lower))
    chains = [three_away(columns_of(place), size)]
    pair = jnp.where(lax.broadcasted_iota(jnp.int32, live.shape, 0) == 0, below, live)
    plane_pairs = [pair] + [swapped(pair, "seq", m) for m in range(1, size)]
    for m in (2, 3, 1):
        chains.append(swapped(columns_of(place ^ m), "seq", m))
    chains = [chains[0]] + [three_away(chains[k], size) for k in (3, 1, 2)]
    head = block_rows * 3 // 10 // 32 * 32
    up_head = turned(out_weight[:head], "seq", size)
    up_rest = turned(out_weight[head:], "seq", size)
    down = turned(out_weight, "seq", -size)
    on_rest = turned(up_rest, "seq", size)
    on_head = turned(up_head, "seq", size)

    before = sum(
        v[0, 0] + jnp.where((place ^ m) < place, v[1, 0], 0) for m, v in enumerate(plane_pairs)
    )
    spilled_in = before - seq_index * TOK_DEV
    tail_rows = lax.dynamic_slice_in_dim(rollout_rows, live_rows[0] - half_rows, half_rows, 0)
    arrived = shifted(tail_rows, "seq", 1)
    joined = jnp.concatenate([arrived, rollout_rows], 0)
    values_f = joined.astype(jnp.float32)
    squares = jnp.sum(values_f * values_f, axis=-1)
    squares = squares + swapped(squares, "tp", 1)
    scale = lax.rsqrt(squares[:, None] / D + EPSILON)
    gain = lax.dynamic_slice_in_dim(norm_gain, tp_index * local_features, local_features, 0)
    at = half_rows - spilled_in
    values_f = lax.dynamic_slice_in_dim(joined, at, TOK_DEV, 0).astype(jnp.float32)
    scale = lax.dynamic_slice_in_dim(scale, at, TOK_DEV, 0)
    normed = (values_f * scale * gain.astype(jnp.float32)).astype(jnp.bfloat16)

    cut = local_features // 2
    h1, h2 = normed[:, :cut], normed[:, cut:]
    x1, y2 = swapped(h1, "tp", 1), swapped(h2, "seq", 2)
    x2, y1 = swapped(h2, "tp", 1), swapped(h1, "seq", 2)
    yx2, xy1 = swapped(y2, "tp", 1), swapped(x1, "seq", 2)
    rows_a, rows_c = [h1, h2, x1, x2], [y1, y2, xy1, yx2]
    rows_b = [swapped(v, "seq", 1) for v in rows_a]
    rows_d = [swapped(v, "seq", 1) for v in rows_c]
    piece_rows = (rows_a, rows_b, rows_c, rows_d)

    numbers = jnp.arange(seq_count, dtype=jnp.int32)
    inverse = jnp.sum(
        jnp.where(block_owner[None, :] == numbers[:, None], numbers[None, :], 0), axis=1
    )
    half_blocks = local_features // block_rows

    def slot(blocks):
        source = inverse[blocks]
        step = (plane - source // size) % planes
        return step * size + ((source % size) ^ place)

    in_order = slot((numbers + tp_index * half_blocks) % seq_count)
    true_of = jnp.sum(
        jnp.where(in_order[None, :] == numbers[:, None], numbers[None, :], 0), axis=1
    )
    per_piece = cut // block_rows
    inside = (true_of % per_piece) * block_rows
    table = jnp.stack([true_of // per_piece, inside // LANES * LANES, inside % LANES], 1)
    doc_starts = (jnp.cumsum(doc_lengths) - doc_lengths).astype(jnp.int32)

    last = 2
    steps = [r for r in range(planes) if r != last]
    rows = block_rows // 2
    step, spot = in_order // size, in_order % size
    step = jnp.where(step == last, planes - 1, step - (step > last))
    order_in = jnp.where((step == planes - 1)[:, None], jnp.array([[1, 0]]), jnp.array([[0, 1]]))
    units = jnp.stack([jnp.repeat(spot, 2), (2 * step[:, None] + order_in).reshape(-1)], 1)
    count = 2 * half_blocks
    here, there = units[:count], units[count:]
    among = jnp.arange(count, dtype=jnp.int32)
    early_units = 2 * (planes - 1)

    def ranks(part):
        key = jnp.maximum(part[:, 1] - early_units + 1, 0) * count + among
        return jnp.sum((key[None, :] < key[:, None]).astype(jnp.int32), axis=1)

    hit = ranks(there)[None, :] == among[:, None]
    going = jnp.sum(jnp.where(hit[:, :, None], there[None, :, :], 0), axis=1).astype(jnp.int32)
    where, table, doc_starts, going, here, here_ranks = lax.optimization_barrier(
        (
            where,
            table.astype(jnp.int32).reshape(-1),
            doc_starts,
            going.reshape(-1),
            here.astype(jnp.int32).reshape(-1),
            ranks(here),
        )
    )

    by_step = lambda some: [c[r] for r in some for c in chains]
    slots_of = lambda some: [r * size + m for r in some for m in range(size)]

    def projected(tokens, slots, weights, accs, name):
        return project(
            table, slots, where, tokens, weights, accs, block_rows, head_width, name
        )

    end = size - 1
    acc = projected(piece_rows, slots_of(steps), by_step(steps), [], "project_first")
    acc = projected(piece_rows, slots_of([last])[:end], by_step([last])[:end], [acc], "project_mid")
    query_rows, kv_rows, kv_last, *kv_home = projected(
        piece_rows, slots_of([last])[end:], by_step([last])[end:], [acc], "project_last"
    )

    halo = shifted(kv_last, "seq", size)
    kv_home = [kv_home[0]] + [swapped(kv_home[m], "seq", m) for m in range(1, size)]
    key_out, value_out = settle(where, kv_home)

    state = attend(where, doc_starts, query_rows, kv_rows, None)
    context = attend(where, doc_starts, query_rows, halo, state)

    from_c = swapped(context, "seq", 2)
    from_b = swapped(context, "seq", 1)
    from_d = swapped(from_c, "seq", 1)
    contexts = (context, from_b, from_c, from_d)

    def delivered(given, weights):
        kept, going_over, *whole = deliver(where, given, weights)
        received = swapped(going_over, "tp", 1)
        pieces = merge(kept, received)
        home = [pieces[0]] + [swapped(pieces[m], "seq", m) for m in range(1, size)]
        return home, whole

    middle = block_rows // 2
    near, whole = delivered(
        contexts, [(out_weight, 0, block_rows), (up_head, 0, head), (up_rest, 0, block_rows - head)]
    )
    far, _ = delivered(whole, [(down, 0, block_rows)])
    mid, _ = delivered(whole, [(on_rest, middle - head, block_rows - middle)])
    late, _ = delivered(whole, [(on_head, 0, head), (on_rest, 0, middle - head)])

    first, second = count - 2 * size, count - size
    cuts = (
        ((0, first), (near, far)),
        ((first, second), (near, far, mid)),
        ((second, count), (near, far, mid, late)),
    )
    received = [swapped(choose(going, part, sources, rows), "tp", 1) for part, sources in cuts]
    mine = choose(here, (0, count), (near, far, mid, late), rows)
    mixed = combine(where, here_ranks, mine, received)
    return (mixed, key_out, value_out)


def solution(mesh):
    in_specs = (P("seq", "tp"), P("seq"), P(), P(), P(), P("seq", "tp"), P("seq", "tp"))
    out_specs = (P("seq", "tp"), P("seq", "tp"), P("seq", "tp"))
    size = KV_HEADS // mesh.shape["tp"]
    by_planes = size == WINDOW and mesh.shape["tp"] == 2 and mesh.shape["seq"] == WINDOW * size
    body = plane_body if by_planes else gathered_body
    return jax.shard_map(body, mesh=mesh, in_specs=in_specs, out_specs=out_specs, check_vma=False)
```

```python
import jax
import jax.numpy as jnp
from jax import lax
from jax.experimental import pallas as pl
from jax.experimental.pallas import tpu as pltpu
from jax.sharding import PartitionSpec as P

D = 5120
KV_HEADS = 8
HD = 128
HEADS = 24
WINDOW = 4
TOK_DEV = 256


EPSILON = 1e-06
NEG_LARGE = -1e30


def carried_in(value, axis, join, neutral):
    count, mine = (lax.axis_size(axis), lax.axis_index(axis))
    pieces = lax.all_gather(value, axis)
    total = jnp.full_like(value, 0) + jnp.asarray(neutral, value.dtype)

    def turn(position, total):
        longer = join(total, pieces[position])
        return jnp.where(position < mine, longer, total)

    return lax.fori_loop(0, count - 1, turn, total)


def shifted(x, axis, by):
    count = lax.axis_size(axis)
    pairs = [(i, i + by) for i in range(count) if 0 <= i + by < count]
    return lax.ppermute(x, axis, pairs)


def gathered_body(rollout_rows, live_rows, doc_lengths, block_owner, norm_gain, qkv_weight, out_weight):
    half_rows = TOK_DEV // 2
    seq_index = lax.axis_index("seq")

    def combine(earlier, later):
        return earlier + later

    before = carried_in(live_rows, "seq", combine, jnp.zeros_like(live_rows))
    spilled_in = before[0] - seq_index * TOK_DEV
    tail_rows = lax.dynamic_slice_in_dim(rollout_rows, live_rows[0] - half_rows, half_rows, 0)
    arrived = shifted(tail_rows, "seq", 1)
    joined = jnp.concatenate([arrived, rollout_rows], 0)
    owned = lax.dynamic_slice_in_dim(joined, half_rows - spilled_in, TOK_DEV, 0)
    full_rows = lax.all_gather(owned, "tp", axis=1, tiled=True)
    values_f = full_rows.astype(jnp.float32)
    scale = lax.rsqrt(jnp.mean(values_f * values_f, axis=-1, keepdims=True) + EPSILON)
    normed = (values_f * scale * norm_gain.astype(jnp.float32)).astype(jnp.bfloat16)
    block_rows = qkv_weight.shape[0]
    block_count = D // block_rows
    permuted = normed.reshape(TOK_DEV, block_count, block_rows)[:, block_owner, :].reshape(
        TOK_DEV, D
    )
    positions = jnp.arange(block_count, dtype=jnp.int32)
    inverse = jnp.sum(
        jnp.where(block_owner[None, :] == positions[:, None], positions[None, :], 0), axis=1
    )
    projected = jnp.dot(
        permuted,
        lax.all_gather(qkv_weight, "seq", axis=0, tiled=True),
        preferred_element_type=jnp.float32,
    )
    group = HEADS // KV_HEADS
    kv_local = projected.shape[1] // ((group + 2) * HD)
    q_width = kv_local * group * HD
    query_rows = (projected[:, :q_width] * HD ** (-0.5)).astype(jnp.bfloat16)
    key_rows = projected[:, q_width : q_width + kv_local * HD].astype(jnp.bfloat16)
    value_rows = projected[:, q_width + kv_local * HD :].astype(jnp.bfloat16)
    queries = query_rows.reshape(TOK_DEV, kv_local, group, HD)
    query_pos = seq_index * TOK_DEV + jnp.arange(TOK_DEV, dtype=jnp.int32)
    doc_starts = jnp.cumsum(doc_lengths) - doc_lengths
    first_pos = jnp.max(
        jnp.where(doc_starts[None, :] <= query_pos[:, None], doc_starts[None, :], 0), axis=1
    )
    initial = (
        jnp.full((kv_local, group, TOK_DEV), NEG_LARGE, jnp.float32),
        jnp.zeros((kv_local, group, TOK_DEV), jnp.float32),
        jnp.zeros((kv_local, group, TOK_DEV, HD), jnp.float32),
    )
    keys_all, values_all = (key_rows, value_rows)
    for level in range(WINDOW.bit_length() - 1):
        got_keys, got_values = shifted((keys_all, values_all), "seq", 1 << level)
        keys_all = jnp.concatenate([got_keys, keys_all], 0)
        values_all = jnp.concatenate([got_values, values_all], 0)
    state = initial
    for block in range(WINDOW):
        keys_block = keys_all[block * TOK_DEV : (block + 1) * TOK_DEV]
        attend_best, attend_totals, attend_accum = state
        key_count = keys_block.shape[0]
        keys_three = keys_block.reshape(key_count, kv_local, HD)
        values_three = values_all[block * TOK_DEV : (block + 1) * TOK_DEV].reshape(
            key_count, kv_local, HD
        )
        scores = jnp.einsum(
            "tgjd,sgd->gjts", queries, keys_three, preferred_element_type=jnp.float32
        )
        key_pos = (seq_index - WINDOW + 1 + block) * TOK_DEV + jnp.arange(
            key_count, dtype=jnp.int32
        )
        allowed = (key_pos[None, :] <= query_pos[:, None]) & (
            key_pos[None, :] >= first_pos[:, None]
        )
        masked = jnp.where(allowed, scores, NEG_LARGE)
        newest = jnp.maximum(attend_best, jnp.max(masked, axis=-1))
        rescale = jnp.exp(attend_best - newest)
        weights = jnp.where(allowed, jnp.exp(masked - newest[..., None]), 0.0)
        attend_totals = attend_totals * rescale + jnp.sum(weights, axis=-1)
        update = jnp.einsum(
            "gjts,sgd->gjtd",
            weights.astype(jnp.bfloat16),
            values_three,
            preferred_element_type=jnp.float32,
        )
        attend_accum = attend_accum * rescale[..., None] + update
        state = (newest, attend_totals, attend_accum)
    _, totals, accum = state
    context = (
        jnp.transpose(accum / totals[..., None], (2, 0, 1, 3))
        .reshape(TOK_DEV, q_width)
        .astype(jnp.bfloat16)
    )
    delivered = lax.dot_general(
        context,
        lax.all_gather(out_weight, "seq", axis=0, tiled=True),
        (((1,), (1,)), ((), ())),
        preferred_element_type=jnp.float32,
    )
    partial_value = delivered.reshape(TOK_DEV, block_count, block_rows)[:, inverse, :].reshape(
        TOK_DEV, D
    )
    mixed = lax.psum_scatter(
        partial_value.astype(jnp.bfloat16).astype(jnp.float32).astype(jnp.bfloat16),
        "tp",
        scatter_dimension=1,
        tiled=True,
    )
    return (mixed, key_rows, value_rows)


LANES = 128


def swapped(x, axis, bit):
    count = lax.axis_size(axis)
    return lax.ppermute(x, axis, [(i, i ^ bit) for i in range(count)])


def turned(x, axis, by):
    count = lax.axis_size(axis)
    return lax.ppermute(x, axis, [(i, (i + by) % count) for i in range(count)])


def three_away(x, size):
    up = turned(x, "seq", size)
    down = turned(x, "seq", -size)
    return {0: x, 1: up, 3: down, 2: turned(up, "seq", size)}


def scratch_limit(*arrays):
    total = sum(v.size * v.dtype.itemsize for v in arrays)
    return total + total // 8 + 6 * 1024 * 1024


def project_kernel(layout, order, table, place_ref, *refs, rows, block_rows, window, first, final, accs):
    pieces, weights = layout
    groups = len(pieces)
    x_refs, refs = refs[: sum(pieces)], refs[sum(pieces) :]
    w_refs, refs = refs[: len(weights)], refs[len(weights) :]
    if first:
        acc_out, xs, ws, x_sem, w_sem = refs
    elif not final:
        *acc_in, acc_out, xs, ws, x_sem, w_sem = refs
    else:
        acc_in, refs = refs[: len(accs)], refs[len(accs) :]
        q_out, kv_out, halo_out, *homes, xs, ws, x_sem, w_sem = refs
    spots = [(ref, part) for ref, parts in zip(w_refs, weights) for part in range(parts)]

    def weight_copy(i, ref, part):
        at = pl.multiple_of(i * window + table[3 * order[i] + 2], 64)
        return pltpu.make_async_copy(
            ref.at[pl.ds(part * block_rows, block_rows), :],
            ws.at[pl.ds(at, block_rows), :],
            w_sem.at[i],
        )

    for i, (ref, part) in enumerate(spots):
        weight_copy(i, ref, part).start()
    for m in range(groups):
        for i in range(len(spots)):
            piece = table[3 * order[i]]
            start = pl.multiple_of(table[3 * order[i] + 1], LANES)
            for p in range(pieces[0]):

                @pl.when(piece == p)
                def _():
                    pltpu.make_async_copy(
                        x_refs[m * pieces[0] + p].at[:, pl.ds(start, window)],
                        xs.at[pl.ds(m * rows, rows), pl.ds(i * window, window)],
                        x_sem.at[m],
                    ).start()

    pad = window - block_rows
    for i, (ref, part) in enumerate(spots):
        weight_copy(i, ref, part).wait()
        spare = pl.multiple_of(i * window + jnp.where(table[3 * order[i] + 2] == 0, block_rows, 0), 64)
        ws[pl.ds(spare, pad), :] = jnp.zeros((pad, ws.shape[1]), ws.dtype)

    def one(m, carry, acc, before):
        at = pl.ds(pl.multiple_of(m * rows, rows), rows)
        pltpu.make_async_copy(xs.at[at, :], xs.at[at, :], x_sem.at[m]).wait()
        total = jnp.dot(xs[at, :], ws[...], preferred_element_type=jnp.float32)
        if not first:
            total = total + acc[pl.ds(pl.multiple_of((m - before) * rows, rows), rows), :]
        if not final:
            acc_out[at, :] = total
        else:
            width = q_out.shape[1]
            q_out[at, :] = (total[:, :width] * HD ** (-0.5)).astype(q_out.dtype)
            kv = total[:, width:].astype(kv_out.dtype)
            for other, home in enumerate(homes):

                @pl.when(m == other)
                def _():
                    home[...] = kv

            block = place_ref[0] ^ m
            kv_out[pl.ds(pl.multiple_of(block * rows, rows), rows), :] = kv
            skipped = groups - halo_out.shape[0] // rows

            @pl.when(block >= skipped)
            def _():
                halo_out[pl.ds(pl.multiple_of((block - skipped) * rows, rows), rows), :] = kv

        return carry

    if first:
        lax.fori_loop(0, groups, lambda m, carry: one(m, carry, None, 0), 0)
    else:
        low = 0
        for acc in acc_in:
            high = low + acc.shape[0] // rows
            lax.fori_loop(low, high, lambda m, carry: one(m, carry, acc, low), 0)
            low = high


def project(table, order, where, piece_rows, weights, accs, block_rows, head_width, name):
    groups, pieces = len(piece_rows), len(piece_rows[0])
    rows = piece_rows[0][0].shape[0]
    parts = [w.shape[0] // block_rows for w in weights]
    count, columns = sum(parts), weights[0].shape[1]
    window = -(-(block_rows + LANES // 2) // LANES) * LANES
    total = groups * rows
    first, final = not accs, name == "project_last"
    kernel = lambda table, place, *refs: project_kernel(
        ([pieces] * groups, parts),
        order,
        table,
        place,
        *refs,
        rows=rows,
        block_rows=block_rows,
        window=window,
        first=first,
        final=final,
        accs=accs,
    )
    scalar = pl.BlockSpec(memory_space=pltpu.SMEM)
    anywhere, local = pl.BlockSpec(memory_space=pltpu.HBM), pl.BlockSpec(memory_space=pltpu.VMEM)
    acc_shape = jax.ShapeDtypeStruct((total, columns), jnp.float32)
    x_shape = jax.ShapeDtypeStruct((total, count * window), jnp.bfloat16)
    w_shape = jax.ShapeDtypeStruct((count * window, columns), jnp.bfloat16)
    if not final:
        shapes, outs = acc_shape, local
    else:
        side = columns - head_width
        shapes = (
            jax.ShapeDtypeStruct((total, head_width), jnp.bfloat16),
            jax.ShapeDtypeStruct((total, side), jnp.bfloat16),
            jax.ShapeDtypeStruct(((WINDOW - 1) * TOK_DEV, side), jnp.bfloat16),
        ) + (jax.ShapeDtypeStruct((rows, side), jnp.bfloat16),) * groups
        outs = (local,) * (3 + groups)
    flops = 2 * total * count * window * columns
    moved = count * (total * window + block_rows * columns) * 2 + total * columns * 4
    return pl.pallas_call(
        kernel,
        out_shape=shapes,
        in_specs=[scalar, scalar]
        + [anywhere] * (groups * pieces + len(weights))
        + [local] * len(accs),
        out_specs=outs,
        scratch_shapes=[
            pltpu.VMEM(x_shape.shape, jnp.bfloat16),
            pltpu.VMEM(w_shape.shape, jnp.bfloat16),
            pltpu.SemaphoreType.DMA((groups,)),
            pltpu.SemaphoreType.DMA((count,)),
        ],
        cost_estimate=pl.CostEstimate(flops=flops, bytes_accessed=moved, transcendentals=0),
        compiler_params=pltpu.CompilerParams(
            vmem_limit_bytes=scratch_limit(x_shape, w_shape, acc_shape, acc_shape)
        ),
    )(table, where, *[v for row in piece_rows for v in row], *weights, *accs)


def attend_kernel(place_ref, starts_ref, q_ref, keys_ref, *refs, own):
    if own:
        stat_ref, acc_ref = refs
    else:
        stat_in, acc_in, out_ref = refs
    size = q_ref.shape[0] // TOK_DEV
    back = WINDOW - 1
    heads = q_ref.shape[1] // HD
    place, plane = place_ref[0], place_ref[1]

    def one(m, carry):
        block = place ^ m
        base = (plane * size + block) * TOK_DEV
        rows = pl.ds(pl.multiple_of(m * TOK_DEV, TOK_DEV), TOK_DEV)
        query_pos = base + lax.broadcasted_iota(jnp.int32, (1, TOK_DEV), 1)
        first_pos = jnp.zeros((1, TOK_DEV), jnp.int32)
        lowest = jnp.int32(0)
        for d in range(starts_ref.shape[0]):
            start = starts_ref[d]
            first_pos = jnp.where(start <= query_pos, jnp.maximum(first_pos, start), first_pos)
            lowest = jnp.where(start <= base, jnp.maximum(lowest, start), lowest)
        earliest = jnp.clip(lowest // TOK_DEV - (plane * size + block - back), 0, back)
        middle = jnp.maximum(back - block, 0)
        top = WINDOW - 1 if own else middle - 1

        def step(i, state):
            w = top - i
            at = (block + w) * TOK_DEV - (back * TOK_DEV if own else 0)
            at = pl.ds(pl.multiple_of(at, TOK_DEV), TOK_DEV)
            key_pos = base + (w - back) * TOK_DEV + lax.broadcasted_iota(
                jnp.int32, (TOK_DEV, 1), 0
            )
            allowed = (key_pos <= query_pos) & (key_pos >= first_pos)
            key_block, value_block = keys_ref[at, :HD], keys_ref[at, HD:]
            after = []
            for h in range(heads):
                best, norm, accum = state[h]
                scores = lax.dot_general(
                    key_block,
                    q_ref[rows, h * HD : (h + 1) * HD],
                    (((1,), (1,)), ((), ())),
                    preferred_element_type=jnp.float32,
                )
                masked = jnp.where(allowed, scores, NEG_LARGE)
                newest = jnp.maximum(best, jnp.max(masked, axis=0, keepdims=True))
                rescale = jnp.exp(best - newest)
                weights = jnp.exp(masked - newest)
                norm = norm * rescale + jnp.sum(weights, axis=0, keepdims=True)
                accum = accum * rescale + lax.dot_general(
                    value_block,
                    weights.astype(jnp.bfloat16),
                    (((0,), (0,)), ((), ())),
                    preferred_element_type=jnp.float32,
                )
                after.append((newest, norm, accum))
            return tuple(after)

        if own:
            count = WINDOW - jnp.maximum(earliest, middle)
            state = tuple(
                (
                    jnp.full((1, TOK_DEV), NEG_LARGE, jnp.float32),
                    jnp.zeros((1, TOK_DEV), jnp.float32),
                    jnp.zeros((HD, TOK_DEV), jnp.float32),
                )
                for _ in range(heads)
            )
        else:
            count = jnp.maximum(middle - earliest, 0)
            state = tuple(
                (
                    stat_in[2 * h : 2 * h + 1, rows],
                    stat_in[2 * h + 1 : 2 * h + 2, rows],
                    acc_in[h * HD : (h + 1) * HD, rows],
                )
                for h in range(heads)
            )
        state = lax.fori_loop(0, count, step, state)
        for h in range(heads):
            best, norm, accum = state[h]
            some = pl.ds(h * HD, HD)
            if own:
                stat_ref[2 * h : 2 * h + 1, rows] = best
                stat_ref[2 * h + 1 : 2 * h + 2, rows] = norm
                acc_ref[some, rows] = accum
            else:
                out_ref[some, rows] = (accum / norm).astype(out_ref.dtype)
        return carry

    lax.fori_loop(0, size, one, 0)


def attend(where, doc_starts, query_rows, keys, state):
    rows, width = query_rows.shape
    own = state is None
    scalar, local = pl.BlockSpec(memory_space=pltpu.SMEM), pl.BlockSpec(memory_space=pltpu.VMEM)
    stat = jax.ShapeDtypeStruct((2 * width // HD, rows), jnp.float32)
    accum = jax.ShapeDtypeStruct((width, rows), jnp.float32)
    out = jax.ShapeDtypeStruct((width, rows), jnp.bfloat16)
    blocks = WINDOW * WINDOW // 2
    return pl.pallas_call(
        lambda *refs: attend_kernel(*refs, own=own),
        out_shape=(stat, accum) if own else out,
        in_specs=[scalar, scalar, local, local] + ([] if own else [local, local]),
        out_specs=(local, local) if own else local,
        cost_estimate=pl.CostEstimate(
            flops=4 * blocks * TOK_DEV * width * TOK_DEV,
            bytes_accessed=8 * rows * width,
            transcendentals=blocks * TOK_DEV * TOK_DEV * width // HD,
        ),
        compiler_params=pltpu.CompilerParams(
            vmem_limit_bytes=scratch_limit(query_rows, keys, stat, accum, out, accum)
        ),
        name="attend_own" if own else "attend_halo",
    )(where, doc_starts, query_rows, keys, *([] if own else state))


def deliver_kernel(place_ref, *refs, size, spans, whole):
    if whole:
        (context_ref,), refs = refs[:1], refs[1:]
    else:
        contexts, refs = refs[:size], refs[size:]
    steps = len(spans)
    weights, refs = refs[:steps], refs[steps:]
    keep, send, *refs = refs
    if whole:
        ws, w_sem = refs
    else:
        context_ref, ws, w_sem, c_sem = refs
    copies, to = [], 0
    for i, (start, rows) in enumerate(spans):
        copies.append(
            pltpu.make_async_copy(
                weights[i].at[pl.ds(start, rows), :], ws.at[pl.ds(to, rows), :], w_sem.at[i]
            )
        )
        to += rows
    if not whole:
        width, half = contexts[0].shape[0], TOK_DEV // 2
        for m in range(size):
            for other in range(size):
                at = pl.multiple_of((place_ref[0] ^ other) * width, LANES)
                for side in range(2):
                    start = (m ^ other) * TOK_DEV + side * half
                    to = pl.multiple_of((side ^ place_ref[2]) * size * half + m * half, half)
                    copies.append(
                        pltpu.make_async_copy(
                            contexts[other].at[:, pl.ds(start, half)],
                            context_ref.at[pl.ds(at, width), pl.ds(to, half)],
                            c_sem.at[(m * size + other) * 2 + side],
                        )
                    )
    for copy in copies:
        copy.start()
    for copy in copies:
        copy.wait()
    mine = keep.shape[1]
    for side, out in enumerate((keep, send)):
        out[...] = jnp.dot(
            ws[...],
            context_ref[:, side * mine : (side + 1) * mine],
            preferred_element_type=jnp.float32,
        ).astype(out.dtype)


def deliver(where, contexts, weights):
    spans = [(start, rows) for _, start, rows in weights]
    weights = [v for v, _, _ in weights]
    steps, columns = len(weights), weights[0].shape[1]
    rows = sum(v for _, v in spans)
    whole = len(contexts) == 1
    size = WINDOW
    total = contexts[0].shape[1]
    scalar = pl.BlockSpec(memory_space=pltpu.SMEM)
    anywhere, local = pl.BlockSpec(memory_space=pltpu.HBM), pl.BlockSpec(memory_space=pltpu.VMEM)
    part = jax.ShapeDtypeStruct((rows, total // 2), jnp.bfloat16)
    context = jax.ShapeDtypeStruct((columns, total), jnp.bfloat16)
    w_shape = jax.ShapeDtypeStruct((rows, columns), jnp.bfloat16)
    scratch = [pltpu.VMEM(w_shape.shape, jnp.bfloat16), pltpu.SemaphoreType.DMA((steps,))]
    if not whole:
        scratch.append(pltpu.SemaphoreType.DMA((2 * size * size,)))
    return pl.pallas_call(
        lambda *refs: deliver_kernel(*refs, size=size, spans=spans, whole=whole),
        out_shape=(part, part) + (() if whole else (context,)),
        in_specs=[scalar] + [local if whole else anywhere] * len(contexts) + [anywhere] * steps,
        out_specs=(local,) * (2 if whole else 3),
        scratch_shapes=scratch,
        cost_estimate=pl.CostEstimate(
            flops=2 * total * columns * rows,
            bytes_accessed=2 * (total * columns + rows * (columns + total)),
            transcendentals=0,
        ),
        compiler_params=pltpu.CompilerParams(
            vmem_limit_bytes=scratch_limit(context, w_shape, *[part] * 6)
        ),
    )(where, *contexts, *weights)


def merge(kept, received):
    rows, total = kept.shape
    size = WINDOW
    wide = total // size

    def kernel(kept_ref, received_ref, *outs):
        for m, out in enumerate(outs):
            at = pl.ds(m * wide, wide)
            total = kept_ref[:, at].astype(jnp.float32) + received_ref[:, at].astype(jnp.float32)
            out[...] = total.astype(out.dtype)

    local = pl.BlockSpec(memory_space=pltpu.VMEM)
    shape = jax.ShapeDtypeStruct((rows, wide), jnp.bfloat16)
    return pl.pallas_call(
        kernel,
        out_shape=(shape,) * size,
        in_specs=[local, local],
        out_specs=(local,) * size,
        cost_estimate=pl.CostEstimate(
            flops=rows * total, bytes_accessed=6 * rows * total, transcendentals=0
        ),
        compiler_params=pltpu.CompilerParams(vmem_limit_bytes=scratch_limit(kept, kept, kept)),
    )(kept, received)


def fetch(table, k, sources, target, sem):
    rows = target.shape[0]
    low = 0
    for group in sources:
        units = group[0].shape[0] // rows
        for m, ref in enumerate(group):
            inside = (table[2 * k] == m) & (table[2 * k + 1] >= low) & (table[2 * k + 1] < low + units)

            @pl.when(inside)
            def _():
                at = pl.multiple_of((table[2 * k + 1] - low) * rows, 32)
                pltpu.make_async_copy(ref.at[pl.ds(at, rows), :], target, sem).start()

        low += units


def choose(table, part, sources, rows):
    begin, end = part
    count = end - begin
    groups = [len(group) for group in sources]

    def kernel(table_ref, *refs):
        refs, (out, sem) = list(refs[:-2]), refs[-2:]
        split = [[refs.pop(0) for _ in range(n)] for n in groups]
        for k in range(count):
            fetch(table_ref, begin + k, split, out.at[k], sem.at[k])
        for k in range(count):
            pltpu.make_async_copy(out.at[k], out.at[k], sem.at[k]).wait()

    shape = jax.ShapeDtypeStruct((count, rows, sources[0][0].shape[1]), jnp.bfloat16)
    flat = [v for group in sources for v in group]
    return pl.pallas_call(
        kernel,
        out_shape=shape,
        in_specs=[pl.BlockSpec(memory_space=pltpu.SMEM)]
        + [pl.BlockSpec(memory_space=pltpu.HBM)] * len(flat),
        out_specs=pl.BlockSpec(memory_space=pltpu.VMEM),
        scratch_shapes=[pltpu.SemaphoreType.DMA((count,))],
        cost_estimate=pl.CostEstimate(flops=0, bytes_accessed=4 * shape.size, transcendentals=0),
        compiler_params=pltpu.CompilerParams(vmem_limit_bytes=scratch_limit(shape, shape)),
    )(table, *flat)


def combine(where, ranks, mine, received):
    count, rows, half = mine.shape
    step = 640 // rows

    def kernel(place_ref, rank_ref, mine_ref, *refs):
        theirs, sem = refs[-2:]
        out, refs = refs[-3], refs[:-3]
        low = 0
        copies = []
        for i, ref in enumerate(refs):
            units = ref.shape[0]
            copies.append(pltpu.make_async_copy(ref, theirs.at[pl.ds(low, units)], sem.at[i]))
            low += units
        for copy in copies:
            copy.start()
        for copy in copies:
            copy.wait()
        for k in range(0, count, step):
            some = [mine_ref[k + i] for i in range(step)]
            rest = [theirs[rank_ref[k + i]] for i in range(step)]
            for blocks, side in ((some, place_ref[2]), (rest, 1 - place_ref[2])):
                total = jnp.concatenate([v.astype(jnp.float32) for v in blocks], 0)
                at = pl.ds(pl.multiple_of(side * half, half), half)
                out[at, k * rows : (k + step) * rows] = jnp.transpose(total).astype(out.dtype)

    shape = jax.ShapeDtypeStruct((TOK_DEV, count * rows), jnp.bfloat16)
    local = pl.BlockSpec(memory_space=pltpu.VMEM)
    return pl.pallas_call(
        kernel,
        out_shape=shape,
        in_specs=[pl.BlockSpec(memory_space=pltpu.SMEM)] * 2
        + [local]
        + [pl.BlockSpec(memory_space=pltpu.HBM)] * len(received),
        out_specs=local,
        scratch_shapes=[
            pltpu.VMEM(mine.shape, jnp.bfloat16),
            pltpu.SemaphoreType.DMA((len(received),)),
        ],
        cost_estimate=pl.CostEstimate(
            flops=shape.size, bytes_accessed=6 * shape.size, transcendentals=0
        ),
        compiler_params=pltpu.CompilerParams(vmem_limit_bytes=scratch_limit(shape, shape, shape)),
        name="combine",
    )(where, ranks, mine, *received)


def settle(where, pieces):
    size, rows = len(pieces), pieces[0].shape[0]

    def kernel(place_ref, *refs):
        key_out, value_out = refs[-2:]
        for m, ref in enumerate(refs[:-2]):
            at = pl.ds(pl.multiple_of((place_ref[0] ^ m) * HD, HD), HD)
            key_out[:, at] = ref[:, :HD]
            value_out[:, at] = ref[:, HD:]

    shape = jax.ShapeDtypeStruct((rows, size * HD), jnp.bfloat16)
    local = pl.BlockSpec(memory_space=pltpu.VMEM)
    return pl.pallas_call(
        kernel,
        out_shape=(shape, shape),
        in_specs=[pl.BlockSpec(memory_space=pltpu.SMEM)] + [local] * size,
        out_specs=(local, local),
        cost_estimate=pl.CostEstimate(flops=0, bytes_accessed=8 * shape.size, transcendentals=0),
        compiler_params=pltpu.CompilerParams(vmem_limit_bytes=scratch_limit(*[shape] * 6)),
        name="settle",
    )(where, *pieces)


def plane_body(*args):
    return plane_steps(*args)


def plane_steps(rollout_rows, live_rows, doc_lengths, block_owner, norm_gain, qkv_weight, out_weight):
    seq_count, seq_index = lax.axis_size("seq"), lax.axis_index("seq")
    tp_index = lax.axis_index("tp")
    block_rows, columns = qkv_weight.shape
    local_features = rollout_rows.shape[1]
    group = HEADS // KV_HEADS
    size = columns // ((group + 2) * HD)
    planes = seq_count // size
    place, plane = seq_index % size, seq_index // size
    where = jnp.stack([place, plane, tp_index]).astype(jnp.int32)
    head_width = group * HD
    half_rows = TOK_DEV // 2

    q_width = size * head_width

    def columns_of(k):
        cuts = ((k * head_width, head_width), (q_width + k * HD, HD), (q_width + (size + k) * HD, HD))
        return jnp.concatenate(
            [lax.dynamic_slice_in_dim(qkv_weight, at, wide, 1) for at, wide in cuts], 1
        )

    live = jnp.broadcast_to(live_rows[None], (8, LANES))
    lower = [turned(live, "seq", k * size) for k in range(1, planes)]
    below = sum(jnp.where(plane >= k, v, 0) for k, v in zip(range(1, planes), lower))
    chains = [three_away(columns_of(place), size)]
    pair = jnp.where(lax.broadcasted_iota(jnp.int32, live.shape, 0) == 0, below, live)
    plane_pairs = [pair] + [swapped(pair, "seq", m) for m in range(1, size)]
    for m in (2, 3, 1):
        chains.append(swapped(columns_of(place ^ m), "seq", m))
    chains = [chains[0]] + [three_away(chains[k], size) for k in (3, 1, 2)]
    head = block_rows * 3 // 10 // 32 * 32
    up_head = turned(out_weight[:head], "seq", size)
    up_rest = turned(out_weight[head:], "seq", size)
    down = turned(out_weight, "seq", -size)
    on_rest = turned(up_rest, "seq", size)
    on_head = turned(up_head, "seq", size)

    before = sum(
        v[0, 0] + jnp.where((place ^ m) < place, v[1, 0], 0) for m, v in enumerate(plane_pairs)
    )
    spilled_in = before - seq_index * TOK_DEV
    tail_rows = lax.dynamic_slice_in_dim(rollout_rows, live_rows[0] - half_rows, half_rows, 0)
    arrived = shifted(tail_rows, "seq", 1)
    joined = jnp.concatenate([arrived, rollout_rows], 0)
    values_f = joined.astype(jnp.float32)
    squares = jnp.sum(values_f * values_f, axis=-1)
    squares = squares + swapped(squares, "tp", 1)
    scale = lax.rsqrt(squares[:, None] / D + EPSILON)
    gain = lax.dynamic_slice_in_dim(norm_gain, tp_index * local_features, local_features, 0)
    at = half_rows - spilled_in
    values_f = lax.dynamic_slice_in_dim(joined, at, TOK_DEV, 0).astype(jnp.float32)
    scale = lax.dynamic_slice_in_dim(scale, at, TOK_DEV, 0)
    normed = (values_f * scale * gain.astype(jnp.float32)).astype(jnp.bfloat16)

    cut = local_features // 2
    h1, h2 = normed[:, :cut], normed[:, cut:]
    x1, y2 = swapped(h1, "tp", 1), swapped(h2, "seq", 2)
    x2, y1 = swapped(h2, "tp", 1), swapped(h1, "seq", 2)
    yx2, xy1 = swapped(y2, "tp", 1), swapped(x1, "seq", 2)
    rows_a, rows_c = [h1, h2, x1, x2], [y1, y2, xy1, yx2]
    rows_b = [swapped(v, "seq", 1) for v in rows_a]
    rows_d = [swapped(v, "seq", 1) for v in rows_c]
    piece_rows = (rows_a, rows_b, rows_c, rows_d)

    numbers = jnp.arange(seq_count, dtype=jnp.int32)
    inverse = jnp.sum(
        jnp.where(block_owner[None, :] == numbers[:, None], numbers[None, :], 0), axis=1
    )
    half_blocks = local_features // block_rows

    def slot(blocks):
        source = inverse[blocks]
        step = (plane - source // size) % planes
        return step * size + ((source % size) ^ place)

    in_order = slot((numbers + tp_index * half_blocks) % seq_count)
    true_of = jnp.sum(
        jnp.where(in_order[None, :] == numbers[:, None], numbers[None, :], 0), axis=1
    )
    per_piece = cut // block_rows
    inside = (true_of % per_piece) * block_rows
    table = jnp.stack([true_of // per_piece, inside // LANES * LANES, inside % LANES], 1)
    doc_starts = (jnp.cumsum(doc_lengths) - doc_lengths).astype(jnp.int32)

    last = 2
    steps = [r for r in range(planes) if r != last]
    half = size // 2
    rows = block_rows // 2
    step, spot = in_order // size, in_order % size
    step = jnp.where(step == last, planes - 1, step - (step > last))
    order_in = jnp.where((step == planes - 1)[:, None], jnp.array([[1, 0]]), jnp.array([[0, 1]]))
    units = jnp.stack([jnp.repeat(spot, 2), (2 * step[:, None] + order_in).reshape(-1)], 1)
    count = 2 * half_blocks
    here, there = units[:count], units[count:]
    among = jnp.arange(count, dtype=jnp.int32)
    early_units = 2 * (planes - 1)

    def ranks(part):
        key = jnp.maximum(part[:, 1] - early_units + 1, 0) * count + among
        return jnp.sum((key[None, :] < key[:, None]).astype(jnp.int32), axis=1)

    hit = ranks(there)[None, :] == among[:, None]
    going = jnp.sum(jnp.where(hit[:, :, None], there[None, :, :], 0), axis=1).astype(jnp.int32)
    where, table, doc_starts, going, here, here_ranks = lax.optimization_barrier(
        (
            where,
            table.astype(jnp.int32).reshape(-1),
            doc_starts,
            going.reshape(-1),
            here.astype(jnp.int32).reshape(-1),
            ranks(here),
        )
    )

    by_step = lambda some: [c[r] for r in some for c in chains]
    slots_of = lambda some: [r * size + m for r in some for m in range(size)]

    def projected(tokens, slots, weights, accs, name):
        return project(
            table, slots, where, tokens, weights, accs, block_rows, head_width, name
        )

    end = size - 1
    accs = [
        projected(piece_rows[k : k + half], slots_of(steps), by_step(steps), [], f"project_{k}")
        for k in (0, half)
    ]
    acc = projected(piece_rows, slots_of([last])[:end], by_step([last])[:end], accs, "project_mid")
    query_rows, kv_rows, kv_last, *kv_home = projected(
        piece_rows, slots_of([last])[end:], by_step([last])[end:], [acc], "project_last"
    )

    halo = shifted(kv_last, "seq", size)
    kv_home = [kv_home[0]] + [swapped(kv_home[m], "seq", m) for m in range(1, size)]
    key_out, value_out = settle(where, kv_home)

    state = attend(where, doc_starts, query_rows, kv_rows, None)
    context = attend(where, doc_starts, query_rows, halo, state)

    from_c = swapped(context, "seq", 2)
    from_b = swapped(context, "seq", 1)
    from_d = swapped(from_c, "seq", 1)
    contexts = (context, from_b, from_c, from_d)

    def delivered(given, weights):
        kept, going_over, *whole = deliver(where, given, weights)
        received = swapped(going_over, "tp", 1)
        pieces = merge(kept, received)
        home = [pieces[0]] + [swapped(pieces[m], "seq", m) for m in range(1, size)]
        return home, whole

    middle = block_rows // 2
    near, whole = delivered(
        contexts, [(out_weight, 0, block_rows), (up_head, 0, head), (up_rest, 0, block_rows - head)]
    )
    far, _ = delivered(whole, [(down, 0, block_rows)])
    mid, _ = delivered(whole, [(on_rest, middle - head, block_rows - middle)])
    late, _ = delivered(whole, [(on_head, 0, head), (on_rest, 0, middle - head)])

    first, second = count - 2 * size, count - size
    cuts = (
        ((0, first), (near, far)),
        ((first, second), (near, far, mid)),
        ((second, count), (near, far, mid, late)),
    )
    received = [swapped(choose(going, part, sources, rows), "tp", 1) for part, sources in cuts]
    mine = choose(here, (0, count), (near, far, mid, late), rows)
    mixed = combine(where, here_ranks, mine, received)
    return (mixed, key_out, value_out)


def solution(mesh):
    in_specs = (P("seq", "tp"), P("seq"), P(), P(), P(), P("seq", "tp"), P("seq", "tp"))
    out_specs = (P("seq", "tp"), P("seq", "tp"), P("seq", "tp"))
    size = KV_HEADS // mesh.shape["tp"]
    by_planes = size == WINDOW and mesh.shape["tp"] == 2 and mesh.shape["seq"] == WINDOW * size
    body = plane_body if by_planes else gathered_body
    return jax.shard_map(body, mesh=mesh, in_specs=in_specs, out_specs=out_specs, check_vma=False)
```

```python
import jax
import jax.numpy as jnp
from jax import lax
from jax.experimental import pallas as pl
from jax.experimental.pallas import tpu as pltpu
from jax.sharding import PartitionSpec as P

D = 5120
KV_HEADS = 8
HD = 128
HEADS = 24
WINDOW = 4
TOK_DEV = 256


EPSILON = 1e-06
NEG_LARGE = -1e30


def carried_in(value, axis, join, neutral):
    count, mine = (lax.axis_size(axis), lax.axis_index(axis))
    pieces = lax.all_gather(value, axis)
    total = jnp.full_like(value, 0) + jnp.asarray(neutral, value.dtype)

    def turn(position, total):
        longer = join(total, pieces[position])
        return jnp.where(position < mine, longer, total)

    return lax.fori_loop(0, count - 1, turn, total)


def shifted(x, axis, by):
    count = lax.axis_size(axis)
    pairs = [(i, i + by) for i in range(count) if 0 <= i + by < count]
    return lax.ppermute(x, axis, pairs)


def gathered_body(rollout_rows, live_rows, doc_lengths, block_owner, norm_gain, qkv_weight, out_weight):
    half_rows = TOK_DEV // 2
    seq_index = lax.axis_index("seq")

    def combine(earlier, later):
        return earlier + later

    before = carried_in(live_rows, "seq", combine, jnp.zeros_like(live_rows))
    spilled_in = before[0] - seq_index * TOK_DEV
    tail_rows = lax.dynamic_slice_in_dim(rollout_rows, live_rows[0] - half_rows, half_rows, 0)
    arrived = shifted(tail_rows, "seq", 1)
    joined = jnp.concatenate([arrived, rollout_rows], 0)
    owned = lax.dynamic_slice_in_dim(joined, half_rows - spilled_in, TOK_DEV, 0)
    full_rows = lax.all_gather(owned, "tp", axis=1, tiled=True)
    values_f = full_rows.astype(jnp.float32)
    scale = lax.rsqrt(jnp.mean(values_f * values_f, axis=-1, keepdims=True) + EPSILON)
    normed = (values_f * scale * norm_gain.astype(jnp.float32)).astype(jnp.bfloat16)
    block_rows = qkv_weight.shape[0]
    block_count = D // block_rows
    permuted = normed.reshape(TOK_DEV, block_count, block_rows)[:, block_owner, :].reshape(
        TOK_DEV, D
    )
    positions = jnp.arange(block_count, dtype=jnp.int32)
    inverse = jnp.sum(
        jnp.where(block_owner[None, :] == positions[:, None], positions[None, :], 0), axis=1
    )
    projected = jnp.dot(
        permuted,
        lax.all_gather(qkv_weight, "seq", axis=0, tiled=True),
        preferred_element_type=jnp.float32,
    )
    group = HEADS // KV_HEADS
    kv_local = projected.shape[1] // ((group + 2) * HD)
    q_width = kv_local * group * HD
    query_rows = (projected[:, :q_width] * HD ** (-0.5)).astype(jnp.bfloat16)
    key_rows = projected[:, q_width : q_width + kv_local * HD].astype(jnp.bfloat16)
    value_rows = projected[:, q_width + kv_local * HD :].astype(jnp.bfloat16)
    queries = query_rows.reshape(TOK_DEV, kv_local, group, HD)
    query_pos = seq_index * TOK_DEV + jnp.arange(TOK_DEV, dtype=jnp.int32)
    doc_starts = jnp.cumsum(doc_lengths) - doc_lengths
    first_pos = jnp.max(
        jnp.where(doc_starts[None, :] <= query_pos[:, None], doc_starts[None, :], 0), axis=1
    )
    initial = (
        jnp.full((kv_local, group, TOK_DEV), NEG_LARGE, jnp.float32),
        jnp.zeros((kv_local, group, TOK_DEV), jnp.float32),
        jnp.zeros((kv_local, group, TOK_DEV, HD), jnp.float32),
    )
    keys_all, values_all = (key_rows, value_rows)
    for level in range(WINDOW.bit_length() - 1):
        got_keys, got_values = shifted((keys_all, values_all), "seq", 1 << level)
        keys_all = jnp.concatenate([got_keys, keys_all], 0)
        values_all = jnp.concatenate([got_values, values_all], 0)
    state = initial
    for block in range(WINDOW):
        keys_block = keys_all[block * TOK_DEV : (block + 1) * TOK_DEV]
        attend_best, attend_totals, attend_accum = state
        key_count = keys_block.shape[0]
        keys_three = keys_block.reshape(key_count, kv_local, HD)
        values_three = values_all[block * TOK_DEV : (block + 1) * TOK_DEV].reshape(
            key_count, kv_local, HD
        )
        scores = jnp.einsum(
            "tgjd,sgd->gjts", queries, keys_three, preferred_element_type=jnp.float32
        )
        key_pos = (seq_index - WINDOW + 1 + block) * TOK_DEV + jnp.arange(
            key_count, dtype=jnp.int32
        )
        allowed = (key_pos[None, :] <= query_pos[:, None]) & (
            key_pos[None, :] >= first_pos[:, None]
        )
        masked = jnp.where(allowed, scores, NEG_LARGE)
        newest = jnp.maximum(attend_best, jnp.max(masked, axis=-1))
        rescale = jnp.exp(attend_best - newest)
        weights = jnp.where(allowed, jnp.exp(masked - newest[..., None]), 0.0)
        attend_totals = attend_totals * rescale + jnp.sum(weights, axis=-1)
        update = jnp.einsum(
            "gjts,sgd->gjtd",
            weights.astype(jnp.bfloat16),
            values_three,
            preferred_element_type=jnp.float32,
        )
        attend_accum = attend_accum * rescale[..., None] + update
        state = (newest, attend_totals, attend_accum)
    _, totals, accum = state
    context = (
        jnp.transpose(accum / totals[..., None], (2, 0, 1, 3))
        .reshape(TOK_DEV, q_width)
        .astype(jnp.bfloat16)
    )
    delivered = lax.dot_general(
        context,
        lax.all_gather(out_weight, "seq", axis=0, tiled=True),
        (((1,), (1,)), ((), ())),
        preferred_element_type=jnp.float32,
    )
    partial_value = delivered.reshape(TOK_DEV, block_count, block_rows)[:, inverse, :].reshape(
        TOK_DEV, D
    )
    mixed = lax.psum_scatter(
        partial_value.astype(jnp.bfloat16).astype(jnp.float32).astype(jnp.bfloat16),
        "tp",
        scatter_dimension=1,
        tiled=True,
    )
    return (mixed, key_rows, value_rows)


LANES = 128


def swapped(x, axis, bit):
    count = lax.axis_size(axis)
    return lax.ppermute(x, axis, [(i, i ^ bit) for i in range(count)])


def turned(x, axis, by):
    count = lax.axis_size(axis)
    return lax.ppermute(x, axis, [(i, (i + by) % count) for i in range(count)])


def three_away(x, size):
    up = turned(x, "seq", size)
    down = turned(x, "seq", -size)
    return {0: x, 1: up, 3: down, 2: turned(up, "seq", size)}


def scratch_limit(*arrays):
    total = sum(v.size * v.dtype.itemsize for v in arrays)
    return total + total // 8 + 6 * 1024 * 1024


def project_kernel(layout, order, table, place_ref, *refs, rows, block_rows, window, first, final, accs):
    pieces, weights = layout
    groups = len(pieces)
    x_refs, refs = refs[: sum(pieces)], refs[sum(pieces) :]
    w_refs, refs = refs[: len(weights)], refs[len(weights) :]
    if first:
        acc_out, xs, ws, x_sem, w_sem = refs
    elif not final:
        *acc_in, acc_out, xs, ws, x_sem, w_sem = refs
    else:
        acc_in, refs = refs[: len(accs)], refs[len(accs) :]
        q_out, kv_out, halo_out, *homes, xs, ws, x_sem, w_sem = refs
    spots = [(ref, part) for ref, parts in zip(w_refs, weights) for part in range(parts)]

    def weight_copy(i, ref, part):
        at = pl.multiple_of(i * window + table[3 * order[i] + 2], 64)
        return pltpu.make_async_copy(
            ref.at[pl.ds(part * block_rows, block_rows), :],
            ws.at[pl.ds(at, block_rows), :],
            w_sem.at[i],
        )

    for i, (ref, part) in enumerate(spots):
        weight_copy(i, ref, part).start()
    for m in range(groups):
        for i in range(len(spots)):
            piece = table[3 * order[i]]
            start = pl.multiple_of(table[3 * order[i] + 1], LANES)
            for p in range(pieces[0]):

                @pl.when(piece == p)
                def _():
                    pltpu.make_async_copy(
                        x_refs[m * pieces[0] + p].at[:, pl.ds(start, window)],
                        xs.at[pl.ds(m * rows, rows), pl.ds(i * window, window)],
                        x_sem.at[m],
                    ).start()

    pad = window - block_rows
    for i, (ref, part) in enumerate(spots):
        weight_copy(i, ref, part).wait()
        spare = pl.multiple_of(i * window + jnp.where(table[3 * order[i] + 2] == 0, block_rows, 0), 64)
        ws[pl.ds(spare, pad), :] = jnp.zeros((pad, ws.shape[1]), ws.dtype)

    def one(m, carry, acc, before):
        at = pl.ds(pl.multiple_of(m * rows, rows), rows)
        pltpu.make_async_copy(xs.at[at, :], xs.at[at, :], x_sem.at[m]).wait()
        total = jnp.dot(xs[at, :], ws[...], preferred_element_type=jnp.float32)
        if not first:
            total = total + acc[pl.ds(pl.multiple_of((m - before) * rows, rows), rows), :]
        if not final:
            acc_out[at, :] = total
        else:
            width = q_out.shape[1]
            q_out[at, :] = (total[:, :width] * HD ** (-0.5)).astype(q_out.dtype)
            kv = total[:, width:].astype(kv_out.dtype)
            for other, home in enumerate(homes):

                @pl.when(m == other)
                def _():
                    home[...] = kv

            block = place_ref[0] ^ m
            kv_out[pl.ds(pl.multiple_of(block * rows, rows), rows), :] = kv
            skipped = groups - halo_out.shape[0] // rows

            @pl.when(block >= skipped)
            def _():
                halo_out[pl.ds(pl.multiple_of((block - skipped) * rows, rows), rows), :] = kv

        return carry

    if first:
        lax.fori_loop(0, groups, lambda m, carry: one(m, carry, None, 0), 0)
    else:
        low = 0
        for acc in acc_in:
            high = low + acc.shape[0] // rows
            lax.fori_loop(low, high, lambda m, carry: one(m, carry, acc, low), 0)
            low = high


def project(table, order, where, piece_rows, weights, accs, block_rows, head_width, name):
    groups, pieces = len(piece_rows), len(piece_rows[0])
    rows = piece_rows[0][0].shape[0]
    parts = [w.shape[0] // block_rows for w in weights]
    count, columns = sum(parts), weights[0].shape[1]
    window = -(-(block_rows + LANES // 2) // LANES) * LANES
    total = groups * rows
    first, final = not accs, name == "project_last"
    kernel = lambda table, place, *refs: project_kernel(
        ([pieces] * groups, parts),
        order,
        table,
        place,
        *refs,
        rows=rows,
        block_rows=block_rows,
        window=window,
        first=first,
        final=final,
        accs=accs,
    )
    scalar = pl.BlockSpec(memory_space=pltpu.SMEM)
    anywhere, local = pl.BlockSpec(memory_space=pltpu.HBM), pl.BlockSpec(memory_space=pltpu.VMEM)
    acc_shape = jax.ShapeDtypeStruct((total, columns), jnp.float32)
    x_shape = jax.ShapeDtypeStruct((total, count * window), jnp.bfloat16)
    w_shape = jax.ShapeDtypeStruct((count * window, columns), jnp.bfloat16)
    if not final:
        shapes, outs = acc_shape, local
    else:
        side = columns - head_width
        shapes = (
            jax.ShapeDtypeStruct((total, head_width), jnp.bfloat16),
            jax.ShapeDtypeStruct((total, side), jnp.bfloat16),
            jax.ShapeDtypeStruct(((WINDOW - 1) * TOK_DEV, side), jnp.bfloat16),
        ) + (jax.ShapeDtypeStruct((rows, side), jnp.bfloat16),) * groups
        outs = (local,) * (3 + groups)
    flops = 2 * total * count * window * columns
    moved = count * (total * window + block_rows * columns) * 2 + total * columns * 4
    return pl.pallas_call(
        kernel,
        out_shape=shapes,
        in_specs=[scalar, scalar]
        + [anywhere] * (groups * pieces + len(weights))
        + [local] * len(accs),
        out_specs=outs,
        scratch_shapes=[
            pltpu.VMEM(x_shape.shape, jnp.bfloat16),
            pltpu.VMEM(w_shape.shape, jnp.bfloat16),
            pltpu.SemaphoreType.DMA((groups,)),
            pltpu.SemaphoreType.DMA((count,)),
        ],
        cost_estimate=pl.CostEstimate(flops=flops, bytes_accessed=moved, transcendentals=0),
        compiler_params=pltpu.CompilerParams(
            vmem_limit_bytes=scratch_limit(x_shape, w_shape, acc_shape, acc_shape)
        ),
    )(table, where, *[v for row in piece_rows for v in row], *weights, *accs)


def attend_kernel(place_ref, starts_ref, q_ref, keys_ref, *refs, own):
    if own:
        stat_ref, acc_ref = refs
    else:
        stat_in, acc_in, out_ref = refs
    size = q_ref.shape[0] // TOK_DEV
    back = WINDOW - 1
    heads = q_ref.shape[1] // HD
    place, plane = place_ref[0], place_ref[1]

    def one(m, carry):
        block = place ^ m
        base = (plane * size + block) * TOK_DEV
        rows = pl.ds(pl.multiple_of(m * TOK_DEV, TOK_DEV), TOK_DEV)
        query_pos = base + lax.broadcasted_iota(jnp.int32, (1, TOK_DEV), 1)
        first_pos = jnp.zeros((1, TOK_DEV), jnp.int32)
        lowest = jnp.int32(0)
        for d in range(starts_ref.shape[0]):
            start = starts_ref[d]
            first_pos = jnp.where(start <= query_pos, jnp.maximum(first_pos, start), first_pos)
            lowest = jnp.where(start <= base, jnp.maximum(lowest, start), lowest)
        earliest = jnp.clip(lowest // TOK_DEV - (plane * size + block - back), 0, back)
        middle = jnp.maximum(back - block, 0)
        top = WINDOW - 1 if own else middle - 1

        def step(i, state):
            w = top - i
            at = (block + w) * TOK_DEV - (back * TOK_DEV if own else 0)
            at = pl.ds(pl.multiple_of(at, TOK_DEV), TOK_DEV)
            key_pos = base + (w - back) * TOK_DEV + lax.broadcasted_iota(
                jnp.int32, (TOK_DEV, 1), 0
            )
            allowed = (key_pos <= query_pos) & (key_pos >= first_pos)
            key_block, value_block = keys_ref[at, :HD], keys_ref[at, HD:]
            after = []
            for h in range(heads):
                best, norm, accum = state[h]
                scores = lax.dot_general(
                    key_block,
                    q_ref[rows, h * HD : (h + 1) * HD],
                    (((1,), (1,)), ((), ())),
                    preferred_element_type=jnp.float32,
                )
                masked = jnp.where(allowed, scores, NEG_LARGE)
                newest = jnp.maximum(best, jnp.max(masked, axis=0, keepdims=True))
                rescale = jnp.exp(best - newest)
                weights = jnp.exp(masked - newest)
                norm = norm * rescale + jnp.sum(weights, axis=0, keepdims=True)
                accum = accum * rescale + lax.dot_general(
                    value_block,
                    weights.astype(jnp.bfloat16),
                    (((0,), (0,)), ((), ())),
                    preferred_element_type=jnp.float32,
                )
                after.append((newest, norm, accum))
            return tuple(after)

        if own:
            count = WINDOW - jnp.maximum(earliest, middle)
            state = tuple(
                (
                    jnp.full((1, TOK_DEV), NEG_LARGE, jnp.float32),
                    jnp.zeros((1, TOK_DEV), jnp.float32),
                    jnp.zeros((HD, TOK_DEV), jnp.float32),
                )
                for _ in range(heads)
            )
        else:
            count = jnp.maximum(middle - earliest, 0)
            state = tuple(
                (
                    stat_in[2 * h : 2 * h + 1, rows],
                    stat_in[2 * h + 1 : 2 * h + 2, rows],
                    acc_in[h * HD : (h + 1) * HD, rows],
                )
                for h in range(heads)
            )
        state = lax.fori_loop(0, count, step, state)
        for h in range(heads):
            best, norm, accum = state[h]
            some = pl.ds(h * HD, HD)
            if own:
                stat_ref[2 * h : 2 * h + 1, rows] = best
                stat_ref[2 * h + 1 : 2 * h + 2, rows] = norm
                acc_ref[some, rows] = accum
            else:
                out_ref[some, rows] = (accum / norm).astype(out_ref.dtype)
        return carry

    lax.fori_loop(0, size, one, 0)


def attend(where, doc_starts, query_rows, keys, state):
    rows, width = query_rows.shape
    own = state is None
    scalar, local = pl.BlockSpec(memory_space=pltpu.SMEM), pl.BlockSpec(memory_space=pltpu.VMEM)
    stat = jax.ShapeDtypeStruct((2 * width // HD, rows), jnp.float32)
    accum = jax.ShapeDtypeStruct((width, rows), jnp.float32)
    out = jax.ShapeDtypeStruct((width, rows), jnp.bfloat16)
    blocks = WINDOW * WINDOW // 2
    return pl.pallas_call(
        lambda *refs: attend_kernel(*refs, own=own),
        out_shape=(stat, accum) if own else out,
        in_specs=[scalar, scalar, local, local] + ([] if own else [local, local]),
        out_specs=(local, local) if own else local,
        cost_estimate=pl.CostEstimate(
            flops=4 * blocks * TOK_DEV * width * TOK_DEV,
            bytes_accessed=8 * rows * width,
            transcendentals=blocks * TOK_DEV * TOK_DEV * width // HD,
        ),
        compiler_params=pltpu.CompilerParams(
            vmem_limit_bytes=scratch_limit(query_rows, keys, stat, accum, out, accum)
        ),
        name="attend_own" if own else "attend_halo",
    )(where, doc_starts, query_rows, keys, *([] if own else state))


def deliver_kernel(place_ref, *refs, size, spans, whole):
    if whole:
        (context_ref,), refs = refs[:1], refs[1:]
    else:
        contexts, refs = refs[:size], refs[size:]
    steps = len(spans)
    weights, refs = refs[:steps], refs[steps:]
    keep, send, *refs = refs
    if whole:
        ws, w_sem = refs
    else:
        context_ref, ws, w_sem, c_sem = refs
    copies, to = [], 0
    for i, (start, rows) in enumerate(spans):
        copies.append(
            pltpu.make_async_copy(
                weights[i].at[pl.ds(start, rows), :], ws.at[pl.ds(to, rows), :], w_sem.at[i]
            )
        )
        to += rows
    if not whole:
        width, half = contexts[0].shape[0], TOK_DEV // 2
        for m in range(size):
            for other in range(size):
                at = pl.multiple_of((place_ref[0] ^ other) * width, LANES)
                for side in range(2):
                    start = (m ^ other) * TOK_DEV + side * half
                    to = pl.multiple_of((side ^ place_ref[2]) * size * half + m * half, half)
                    copies.append(
                        pltpu.make_async_copy(
                            contexts[other].at[:, pl.ds(start, half)],
                            context_ref.at[pl.ds(at, width), pl.ds(to, half)],
                            c_sem.at[(m * size + other) * 2 + side],
                        )
                    )
    for copy in copies:
        copy.start()
    for copy in copies:
        copy.wait()
    mine = keep.shape[1]
    for side, out in enumerate((keep, send)):
        out[...] = jnp.dot(
            ws[...],
            context_ref[:, side * mine : (side + 1) * mine],
            preferred_element_type=jnp.float32,
        ).astype(out.dtype)


def deliver(where, contexts, weights):
    spans = [(start, rows) for _, start, rows in weights]
    weights = [v for v, _, _ in weights]
    steps, columns = len(weights), weights[0].shape[1]
    rows = sum(v for _, v in spans)
    whole = len(contexts) == 1
    size = WINDOW
    total = contexts[0].shape[1]
    scalar = pl.BlockSpec(memory_space=pltpu.SMEM)
    anywhere, local = pl.BlockSpec(memory_space=pltpu.HBM), pl.BlockSpec(memory_space=pltpu.VMEM)
    part = jax.ShapeDtypeStruct((rows, total // 2), jnp.bfloat16)
    context = jax.ShapeDtypeStruct((columns, total), jnp.bfloat16)
    w_shape = jax.ShapeDtypeStruct((rows, columns), jnp.bfloat16)
    scratch = [pltpu.VMEM(w_shape.shape, jnp.bfloat16), pltpu.SemaphoreType.DMA((steps,))]
    if not whole:
        scratch.append(pltpu.SemaphoreType.DMA((2 * size * size,)))
    return pl.pallas_call(
        lambda *refs: deliver_kernel(*refs, size=size, spans=spans, whole=whole),
        out_shape=(part, part) + (() if whole else (context,)),
        in_specs=[scalar] + [local if whole else anywhere] * len(contexts) + [anywhere] * steps,
        out_specs=(local,) * (2 if whole else 3),
        scratch_shapes=scratch,
        cost_estimate=pl.CostEstimate(
            flops=2 * total * columns * rows,
            bytes_accessed=2 * (total * columns + rows * (columns + total)),
            transcendentals=0,
        ),
        compiler_params=pltpu.CompilerParams(
            vmem_limit_bytes=scratch_limit(context, w_shape, *[part] * 6)
        ),
    )(where, *contexts, *weights)


def merge(kept, received):
    rows, total = kept.shape
    size = WINDOW
    wide = total // size

    def kernel(kept_ref, received_ref, *outs):
        for m, out in enumerate(outs):
            at = pl.ds(m * wide, wide)
            total = kept_ref[:, at].astype(jnp.float32) + received_ref[:, at].astype(jnp.float32)
            out[...] = total.astype(out.dtype)

    local = pl.BlockSpec(memory_space=pltpu.VMEM)
    shape = jax.ShapeDtypeStruct((rows, wide), jnp.bfloat16)
    return pl.pallas_call(
        kernel,
        out_shape=(shape,) * size,
        in_specs=[local, local],
        out_specs=(local,) * size,
        cost_estimate=pl.CostEstimate(
            flops=rows * total, bytes_accessed=6 * rows * total, transcendentals=0
        ),
        compiler_params=pltpu.CompilerParams(vmem_limit_bytes=scratch_limit(kept, kept, kept)),
    )(kept, received)


def fetch(table, k, sources, target, sem):
    rows = target.shape[0]
    low = 0
    for group in sources:
        units = group[0].shape[0] // rows

        @pl.when((table[2 * k + 1] >= low) & (table[2 * k + 1] < low + units))
        def _():
            at = pl.multiple_of((table[2 * k + 1] - low) * rows, 32)
            for m, ref in enumerate(group):

                @pl.when(table[2 * k] == m)
                def _():
                    pltpu.make_async_copy(ref.at[pl.ds(at, rows), :], target, sem).start()

        low += units


def choose(table, part, sources, rows):
    begin, end = part
    count = end - begin
    groups = [len(group) for group in sources]

    def kernel(table_ref, *refs):
        refs, (out, sem) = list(refs[:-2]), refs[-2:]
        split = [[refs.pop(0) for _ in range(n)] for n in groups]
        for k in range(count):
            fetch(table_ref, begin + k, split, out.at[k], sem.at[k])
        for k in range(count):
            pltpu.make_async_copy(out.at[k], out.at[k], sem.at[k]).wait()

    shape = jax.ShapeDtypeStruct((count, rows, sources[0][0].shape[1]), jnp.bfloat16)
    flat = [v for group in sources for v in group]
    return pl.pallas_call(
        kernel,
        out_shape=shape,
        in_specs=[pl.BlockSpec(memory_space=pltpu.SMEM)]
        + [pl.BlockSpec(memory_space=pltpu.HBM)] * len(flat),
        out_specs=pl.BlockSpec(memory_space=pltpu.VMEM),
        scratch_shapes=[pltpu.SemaphoreType.DMA((count,))],
        cost_estimate=pl.CostEstimate(flops=0, bytes_accessed=4 * shape.size, transcendentals=0),
        compiler_params=pltpu.CompilerParams(vmem_limit_bytes=scratch_limit(shape, shape)),
    )(table, *flat)


def combine(where, ranks, mine, received):
    count, rows, half = mine.shape
    step = 640 // rows

    def kernel(place_ref, rank_ref, mine_ref, *refs):
        theirs, sem = refs[-2:]
        out, refs = refs[-3], refs[:-3]
        low = 0
        copies = []
        for i, ref in enumerate(refs):
            units = ref.shape[0]
            copies.append(pltpu.make_async_copy(ref, theirs.at[pl.ds(low, units)], sem.at[i]))
            low += units
        for copy in copies:
            copy.start()
        for copy in copies:
            copy.wait()
        for k in range(0, count, step):
            some = [mine_ref[k + i] for i in range(step)]
            rest = [theirs[rank_ref[k + i]] for i in range(step)]
            for blocks, side in ((some, place_ref[2]), (rest, 1 - place_ref[2])):
                total = jnp.concatenate([v.astype(jnp.float32) for v in blocks], 0)
                at = pl.ds(pl.multiple_of(side * half, half), half)
                out[at, k * rows : (k + step) * rows] = jnp.transpose(total).astype(out.dtype)

    shape = jax.ShapeDtypeStruct((TOK_DEV, count * rows), jnp.bfloat16)
    local = pl.BlockSpec(memory_space=pltpu.VMEM)
    return pl.pallas_call(
        kernel,
        out_shape=shape,
        in_specs=[pl.BlockSpec(memory_space=pltpu.SMEM)] * 2
        + [local]
        + [pl.BlockSpec(memory_space=pltpu.HBM)] * len(received),
        out_specs=local,
        scratch_shapes=[
            pltpu.VMEM(mine.shape, jnp.bfloat16),
            pltpu.SemaphoreType.DMA((len(received),)),
        ],
        cost_estimate=pl.CostEstimate(
            flops=shape.size, bytes_accessed=6 * shape.size, transcendentals=0
        ),
        compiler_params=pltpu.CompilerParams(vmem_limit_bytes=scratch_limit(shape, shape, shape)),
        name="combine",
    )(where, ranks, mine, *received)


def settle(where, pieces):
    size, rows = len(pieces), pieces[0].shape[0]

    def kernel(place_ref, *refs):
        key_out, value_out = refs[-2:]
        for m, ref in enumerate(refs[:-2]):
            at = pl.ds(pl.multiple_of((place_ref[0] ^ m) * HD, HD), HD)
            key_out[:, at] = ref[:, :HD]
            value_out[:, at] = ref[:, HD:]

    shape = jax.ShapeDtypeStruct((rows, size * HD), jnp.bfloat16)
    local = pl.BlockSpec(memory_space=pltpu.VMEM)
    return pl.pallas_call(
        kernel,
        out_shape=(shape, shape),
        in_specs=[pl.BlockSpec(memory_space=pltpu.SMEM)] + [local] * size,
        out_specs=(local, local),
        cost_estimate=pl.CostEstimate(flops=0, bytes_accessed=8 * shape.size, transcendentals=0),
        compiler_params=pltpu.CompilerParams(vmem_limit_bytes=scratch_limit(*[shape] * 6)),
        name="settle",
    )(where, *pieces)


def plane_body(*args):
    return plane_steps(*args)


def plane_steps(rollout_rows, live_rows, doc_lengths, block_owner, norm_gain, qkv_weight, out_weight):
    seq_count, seq_index = lax.axis_size("seq"), lax.axis_index("seq")
    tp_index = lax.axis_index("tp")
    block_rows, columns = qkv_weight.shape
    local_features = rollout_rows.shape[1]
    group = HEADS // KV_HEADS
    size = columns // ((group + 2) * HD)
    planes = seq_count // size
    place, plane = seq_index % size, seq_index // size
    where = jnp.stack([place, plane, tp_index]).astype(jnp.int32)
    head_width = group * HD
    half_rows = TOK_DEV // 2

    q_width = size * head_width

    def columns_of(k):
        cuts = ((k * head_width, head_width), (q_width + k * HD, HD), (q_width + (size + k) * HD, HD))
        return jnp.concatenate(
            [lax.dynamic_slice_in_dim(qkv_weight, at, wide, 1) for at, wide in cuts], 1
        )

    live = jnp.broadcast_to(live_rows[None], (8, LANES))
    lower = [turned(live, "seq", k * size) for k in range(1, planes)]
    below = sum(jnp.where(plane >= k, v, 0) for k, v in zip(range(1, planes), lower))
    chains = [three_away(columns_of(place), size)]
    pair = jnp.where(lax.broadcasted_iota(jnp.int32, live.shape, 0) == 0, below, live)
    plane_pairs = [pair] + [swapped(pair, "seq", m) for m in range(1, size)]
    for m in (2, 3, 1):
        chains.append(swapped(columns_of(place ^ m), "seq", m))
    chains = [chains[0]] + [three_away(chains[k], size) for k in (3, 1, 2)]
    head = block_rows * 3 // 10 // 32 * 32
    up_head = turned(out_weight[:head], "seq", size)
    up_rest = turned(out_weight[head:], "seq", size)
    down = turned(out_weight, "seq", -size)
    on_rest = turned(up_rest, "seq", size)
    on_head = turned(up_head, "seq", size)

    before = sum(
        v[0, 0] + jnp.where((place ^ m) < place, v[1, 0], 0) for m, v in enumerate(plane_pairs)
    )
    spilled_in = before - seq_index * TOK_DEV
    tail_rows = lax.dynamic_slice_in_dim(rollout_rows, live_rows[0] - half_rows, half_rows, 0)
    arrived = shifted(tail_rows, "seq", 1)
    joined = jnp.concatenate([arrived, rollout_rows], 0)
    values_f = joined.astype(jnp.float32)
    squares = jnp.sum(values_f * values_f, axis=-1)
    squares = squares + swapped(squares, "tp", 1)
    scale = lax.rsqrt(squares[:, None] / D + EPSILON)
    gain = lax.dynamic_slice_in_dim(norm_gain, tp_index * local_features, local_features, 0)
    at = half_rows - spilled_in
    values_f = lax.dynamic_slice_in_dim(joined, at, TOK_DEV, 0).astype(jnp.float32)
    scale = lax.dynamic_slice_in_dim(scale, at, TOK_DEV, 0)
    normed = (values_f * scale * gain.astype(jnp.float32)).astype(jnp.bfloat16)

    cut = local_features // 2
    h1, h2 = normed[:, :cut], normed[:, cut:]
    x1, y2 = swapped(h1, "tp", 1), swapped(h2, "seq", 2)
    x2, y1 = swapped(h2, "tp", 1), swapped(h1, "seq", 2)
    yx2, xy1 = swapped(y2, "tp", 1), swapped(x1, "seq", 2)
    rows_a, rows_c = [h1, h2, x1, x2], [y1, y2, xy1, yx2]
    rows_b = [swapped(v, "seq", 1) for v in rows_a]
    rows_d = [swapped(v, "seq", 1) for v in rows_c]
    piece_rows = (rows_a, rows_b, rows_c, rows_d)

    numbers = jnp.arange(seq_count, dtype=jnp.int32)
    inverse = jnp.sum(
        jnp.where(block_owner[None, :] == numbers[:, None], numbers[None, :], 0), axis=1
    )
    half_blocks = local_features // block_rows

    def slot(blocks):
        source = inverse[blocks]
        step = (plane - source // size) % planes
        return step * size + ((source % size) ^ place)

    in_order = slot((numbers + tp_index * half_blocks) % seq_count)
    true_of = jnp.sum(
        jnp.where(in_order[None, :] == numbers[:, None], numbers[None, :], 0), axis=1
    )
    per_piece = cut // block_rows
    inside = (true_of % per_piece) * block_rows
    table = jnp.stack([true_of // per_piece, inside // LANES * LANES, inside % LANES], 1)
    doc_starts = (jnp.cumsum(doc_lengths) - doc_lengths).astype(jnp.int32)

    last = 2
    steps = [r for r in range(planes) if r != last]
    half = size // 2
    rows = block_rows // 2
    step, spot = in_order // size, in_order % size
    step = jnp.where(step == last, planes - 1, step - (step > last))
    order_in = jnp.where((step == planes - 1)[:, None], jnp.array([[1, 0]]), jnp.array([[0, 1]]))
    units = jnp.stack([jnp.repeat(spot, 2), (2 * step[:, None] + order_in).reshape(-1)], 1)
    count = 2 * half_blocks
    here, there = units[:count], units[count:]
    among = jnp.arange(count, dtype=jnp.int32)
    early_units = 2 * (planes - 1)

    def ranks(part):
        key = jnp.maximum(part[:, 1] - early_units + 1, 0) * count + among
        return jnp.sum((key[None, :] < key[:, None]).astype(jnp.int32), axis=1)

    hit = ranks(there)[None, :] == among[:, None]
    going = jnp.sum(jnp.where(hit[:, :, None], there[None, :, :], 0), axis=1).astype(jnp.int32)
    where, table, doc_starts, going, here, here_ranks = lax.optimization_barrier(
        (
            where,
            table.astype(jnp.int32).reshape(-1),
            doc_starts,
            going.reshape(-1),
            here.astype(jnp.int32).reshape(-1),
            ranks(here),
        )
    )

    by_step = lambda some: [c[r] for r in some for c in chains]
    slots_of = lambda some: [r * size + m for r in some for m in range(size)]

    def projected(tokens, slots, weights, accs, name):
        return project(
            table, slots, where, tokens, weights, accs, block_rows, head_width, name
        )

    end = size - 1
    accs = [
        projected(piece_rows[k : k + half], slots_of(steps), by_step(steps), [], f"project_{k}")
        for k in (0, half)
    ]
    acc = projected(piece_rows, slots_of([last])[:end], by_step([last])[:end], accs, "project_mid")
    query_rows, kv_rows, kv_last, *kv_home = projected(
        piece_rows, slots_of([last])[end:], by_step([last])[end:], [acc], "project_last"
    )

    halo = shifted(kv_last, "seq", size)
    kv_home = [kv_home[0]] + [swapped(kv_home[m], "seq", m) for m in range(1, size)]
    key_out, value_out = settle(where, kv_home)

    state = attend(where, doc_starts, query_rows, kv_rows, None)
    context = attend(where, doc_starts, query_rows, halo, state)

    from_c = swapped(context, "seq", 2)
    from_b = swapped(context, "seq", 1)
    from_d = swapped(from_c, "seq", 1)
    contexts = (context, from_b, from_c, from_d)

    def delivered(given, weights):
        kept, going_over, *whole = deliver(where, given, weights)
        received = swapped(going_over, "tp", 1)
        pieces = merge(kept, received)
        home = [pieces[0]] + [swapped(pieces[m], "seq", m) for m in range(1, size)]
        return home, whole

    middle = block_rows // 2
    near, whole = delivered(
        contexts, [(out_weight, 0, block_rows), (up_head, 0, head), (up_rest, 0, block_rows - head)]
    )
    far, _ = delivered(whole, [(down, 0, block_rows)])
    mid, _ = delivered(whole, [(on_rest, middle - head, block_rows - middle)])
    late, _ = delivered(whole, [(on_head, 0, head), (on_rest, 0, middle - head)])

    first, second = count - 2 * size, count - size
    cuts = (
        ((0, first), (near, far)),
        ((first, second), (near, far, mid)),
        ((second, count), (near, far, mid, late)),
    )
    received = [swapped(choose(going, part, sources, rows), "tp", 1) for part, sources in cuts]
    mine = choose(here, (0, count), (near, far, mid, late), rows)
    mixed = combine(where, here_ranks, mine, received)
    return (mixed, key_out, value_out)


def solution(mesh):
    in_specs = (P("seq", "tp"), P("seq"), P(), P(), P(), P("seq", "tp"), P("seq", "tp"))
    out_specs = (P("seq", "tp"), P("seq", "tp"), P("seq", "tp"))
    size = KV_HEADS // mesh.shape["tp"]
    by_planes = size == WINDOW and mesh.shape["tp"] == 2 and mesh.shape["seq"] == WINDOW * size
    body = plane_body if by_planes else gathered_body
    return jax.shard_map(body, mesh=mesh, in_specs=in_specs, out_specs=out_specs, check_vma=False)
```

```python
import jax
import jax.numpy as jnp
from jax import lax
from jax.experimental import pallas as pl
from jax.experimental.pallas import tpu as pltpu
from jax.sharding import PartitionSpec as P

D = 5120
KV_HEADS = 8
HD = 128
HEADS = 24
WINDOW = 4
TOK_DEV = 256


EPSILON = 1e-06
NEG_LARGE = -1e30


def carried_in(value, axis, join, neutral):
    count, mine = (lax.axis_size(axis), lax.axis_index(axis))
    pieces = lax.all_gather(value, axis)
    total = jnp.full_like(value, 0) + jnp.asarray(neutral, value.dtype)

    def turn(position, total):
        longer = join(total, pieces[position])
        return jnp.where(position < mine, longer, total)

    return lax.fori_loop(0, count - 1, turn, total)


def shifted(x, axis, by):
    count = lax.axis_size(axis)
    pairs = [(i, i + by) for i in range(count) if 0 <= i + by < count]
    return lax.ppermute(x, axis, pairs)


def gathered_body(rollout_rows, live_rows, doc_lengths, block_owner, norm_gain, qkv_weight, out_weight):
    half_rows = TOK_DEV // 2
    seq_index = lax.axis_index("seq")

    def combine(earlier, later):
        return earlier + later

    before = carried_in(live_rows, "seq", combine, jnp.zeros_like(live_rows))
    spilled_in = before[0] - seq_index * TOK_DEV
    tail_rows = lax.dynamic_slice_in_dim(rollout_rows, live_rows[0] - half_rows, half_rows, 0)
    arrived = shifted(tail_rows, "seq", 1)
    joined = jnp.concatenate([arrived, rollout_rows], 0)
    owned = lax.dynamic_slice_in_dim(joined, half_rows - spilled_in, TOK_DEV, 0)
    full_rows = lax.all_gather(owned, "tp", axis=1, tiled=True)
    values_f = full_rows.astype(jnp.float32)
    scale = lax.rsqrt(jnp.mean(values_f * values_f, axis=-1, keepdims=True) + EPSILON)
    normed = (values_f * scale * norm_gain.astype(jnp.float32)).astype(jnp.bfloat16)
    block_rows = qkv_weight.shape[0]
    block_count = D // block_rows
    permuted = normed.reshape(TOK_DEV, block_count, block_rows)[:, block_owner, :].reshape(
        TOK_DEV, D
    )
    positions = jnp.arange(block_count, dtype=jnp.int32)
    inverse = jnp.sum(
        jnp.where(block_owner[None, :] == positions[:, None], positions[None, :], 0), axis=1
    )
    projected = jnp.dot(
        permuted,
        lax.all_gather(qkv_weight, "seq", axis=0, tiled=True),
        preferred_element_type=jnp.float32,
    )
    group = HEADS // KV_HEADS
    kv_local = projected.shape[1] // ((group + 2) * HD)
    q_width = kv_local * group * HD
    query_rows = (projected[:, :q_width] * HD ** (-0.5)).astype(jnp.bfloat16)
    key_rows = projected[:, q_width : q_width + kv_local * HD].astype(jnp.bfloat16)
    value_rows = projected[:, q_width + kv_local * HD :].astype(jnp.bfloat16)
    queries = query_rows.reshape(TOK_DEV, kv_local, group, HD)
    query_pos = seq_index * TOK_DEV + jnp.arange(TOK_DEV, dtype=jnp.int32)
    doc_starts = jnp.cumsum(doc_lengths) - doc_lengths
    first_pos = jnp.max(
        jnp.where(doc_starts[None, :] <= query_pos[:, None], doc_starts[None, :], 0), axis=1
    )
    initial = (
        jnp.full((kv_local, group, TOK_DEV), NEG_LARGE, jnp.float32),
        jnp.zeros((kv_local, group, TOK_DEV), jnp.float32),
        jnp.zeros((kv_local, group, TOK_DEV, HD), jnp.float32),
    )
    keys_all, values_all = (key_rows, value_rows)
    for level in range(WINDOW.bit_length() - 1):
        got_keys, got_values = shifted((keys_all, values_all), "seq", 1 << level)
        keys_all = jnp.concatenate([got_keys, keys_all], 0)
        values_all = jnp.concatenate([got_values, values_all], 0)
    state = initial
    for block in range(WINDOW):
        keys_block = keys_all[block * TOK_DEV : (block + 1) * TOK_DEV]
        attend_best, attend_totals, attend_accum = state
        key_count = keys_block.shape[0]
        keys_three = keys_block.reshape(key_count, kv_local, HD)
        values_three = values_all[block * TOK_DEV : (block + 1) * TOK_DEV].reshape(
            key_count, kv_local, HD
        )
        scores = jnp.einsum(
            "tgjd,sgd->gjts", queries, keys_three, preferred_element_type=jnp.float32
        )
        key_pos = (seq_index - WINDOW + 1 + block) * TOK_DEV + jnp.arange(
            key_count, dtype=jnp.int32
        )
        allowed = (key_pos[None, :] <= query_pos[:, None]) & (
            key_pos[None, :] >= first_pos[:, None]
        )
        masked = jnp.where(allowed, scores, NEG_LARGE)
        newest = jnp.maximum(attend_best, jnp.max(masked, axis=-1))
        rescale = jnp.exp(attend_best - newest)
        weights = jnp.where(allowed, jnp.exp(masked - newest[..., None]), 0.0)
        attend_totals = attend_totals * rescale + jnp.sum(weights, axis=-1)
        update = jnp.einsum(
            "gjts,sgd->gjtd",
            weights.astype(jnp.bfloat16),
            values_three,
            preferred_element_type=jnp.float32,
        )
        attend_accum = attend_accum * rescale[..., None] + update
        state = (newest, attend_totals, attend_accum)
    _, totals, accum = state
    context = (
        jnp.transpose(accum / totals[..., None], (2, 0, 1, 3))
        .reshape(TOK_DEV, q_width)
        .astype(jnp.bfloat16)
    )
    delivered = lax.dot_general(
        context,
        lax.all_gather(out_weight, "seq", axis=0, tiled=True),
        (((1,), (1,)), ((), ())),
        preferred_element_type=jnp.float32,
    )
    partial_value = delivered.reshape(TOK_DEV, block_count, block_rows)[:, inverse, :].reshape(
        TOK_DEV, D
    )
    mixed = lax.psum_scatter(
        partial_value.astype(jnp.bfloat16).astype(jnp.float32).astype(jnp.bfloat16),
        "tp",
        scatter_dimension=1,
        tiled=True,
    )
    return (mixed, key_rows, value_rows)


LANES = 128


def swapped(x, axis, bit):
    count = lax.axis_size(axis)
    return lax.ppermute(x, axis, [(i, i ^ bit) for i in range(count)])


def turned(x, axis, by):
    count = lax.axis_size(axis)
    return lax.ppermute(x, axis, [(i, (i + by) % count) for i in range(count)])


def three_away(x, size):
    up = turned(x, "seq", size)
    down = turned(x, "seq", -size)
    return {0: x, 1: up, 3: down, 2: turned(up, "seq", size)}


def scratch_limit(*arrays):
    total = sum(v.size * v.dtype.itemsize for v in arrays)
    return total + total // 8 + 6 * 1024 * 1024


def project_kernel(layout, order, table, place_ref, *refs, rows, block_rows, window, first, final, accs):
    pieces, weights = layout
    groups = len(pieces)
    x_refs, refs = refs[: sum(pieces)], refs[sum(pieces) :]
    w_refs, refs = refs[: len(weights)], refs[len(weights) :]
    if first:
        acc_out, xs, ws, x_sem, w_sem = refs
    elif not final:
        *acc_in, acc_out, xs, ws, x_sem, w_sem = refs
    else:
        acc_in, refs = refs[: len(accs)], refs[len(accs) :]
        q_out, kv_out, halo_out, *homes, xs, ws, x_sem, w_sem = refs
    spots = [(ref, part) for ref, parts in zip(w_refs, weights) for part in range(parts)]

    def weight_copy(i, ref, part):
        at = pl.multiple_of(i * window + table[3 * order[i] + 2], 64)
        return pltpu.make_async_copy(
            ref.at[pl.ds(part * block_rows, block_rows), :],
            ws.at[pl.ds(at, block_rows), :],
            w_sem.at[i],
        )

    for i, (ref, part) in enumerate(spots):
        weight_copy(i, ref, part).start()
    for m in range(groups):
        for i in range(len(spots)):
            piece = table[3 * order[i]]
            start = pl.multiple_of(table[3 * order[i] + 1], LANES)
            for p in range(pieces[0]):

                @pl.when(piece == p)
                def _():
                    pltpu.make_async_copy(
                        x_refs[m * pieces[0] + p].at[:, pl.ds(start, window)],
                        xs.at[pl.ds(m * rows, rows), pl.ds(i * window, window)],
                        x_sem.at[m],
                    ).start()

    pad = window - block_rows
    for i, (ref, part) in enumerate(spots):
        weight_copy(i, ref, part).wait()
        spare = pl.multiple_of(i * window + jnp.where(table[3 * order[i] + 2] == 0, block_rows, 0), 64)
        ws[pl.ds(spare, pad), :] = jnp.zeros((pad, ws.shape[1]), ws.dtype)

    def one(m, carry, acc, before):
        at = pl.ds(pl.multiple_of(m * rows, rows), rows)
        pltpu.make_async_copy(xs.at[at, :], xs.at[at, :], x_sem.at[m]).wait()
        total = jnp.dot(xs[at, :], ws[...], preferred_element_type=jnp.float32)
        if not first:
            total = total + acc[pl.ds(pl.multiple_of((m - before) * rows, rows), rows), :]
        if not final:
            acc_out[at, :] = total
        else:
            width = q_out.shape[1]
            q_out[at, :] = (total[:, :width] * HD ** (-0.5)).astype(q_out.dtype)
            kv = total[:, width:].astype(kv_out.dtype)
            for other, home in enumerate(homes):

                @pl.when(m == other)
                def _():
                    home[...] = kv

            block = place_ref[0] ^ m
            kv_out[pl.ds(pl.multiple_of(block * rows, rows), rows), :] = kv
            skipped = groups - halo_out.shape[0] // rows

            @pl.when(block >= skipped)
            def _():
                halo_out[pl.ds(pl.multiple_of((block - skipped) * rows, rows), rows), :] = kv

        return carry

    if first:
        lax.fori_loop(0, groups, lambda m, carry: one(m, carry, None, 0), 0)
    else:
        low = 0
        for acc in acc_in:
            high = low + acc.shape[0] // rows
            lax.fori_loop(low, high, lambda m, carry: one(m, carry, acc, low), 0)
            low = high


def project(table, order, where, piece_rows, weights, accs, block_rows, head_width, name):
    groups, pieces = len(piece_rows), len(piece_rows[0])
    rows = piece_rows[0][0].shape[0]
    parts = [w.shape[0] // block_rows for w in weights]
    count, columns = sum(parts), weights[0].shape[1]
    window = -(-(block_rows + LANES // 2) // LANES) * LANES
    total = groups * rows
    first, final = not accs, name == "project_last"
    kernel = lambda table, place, *refs: project_kernel(
        ([pieces] * groups, parts),
        order,
        table,
        place,
        *refs,
        rows=rows,
        block_rows=block_rows,
        window=window,
        first=first,
        final=final,
        accs=accs,
    )
    scalar = pl.BlockSpec(memory_space=pltpu.SMEM)
    anywhere, local = pl.BlockSpec(memory_space=pltpu.HBM), pl.BlockSpec(memory_space=pltpu.VMEM)
    acc_shape = jax.ShapeDtypeStruct((total, columns), jnp.float32)
    x_shape = jax.ShapeDtypeStruct((total, count * window), jnp.bfloat16)
    w_shape = jax.ShapeDtypeStruct((count * window, columns), jnp.bfloat16)
    if not final:
        shapes, outs = acc_shape, local
    else:
        side = columns - head_width
        shapes = (
            jax.ShapeDtypeStruct((total, head_width), jnp.bfloat16),
            jax.ShapeDtypeStruct((total, side), jnp.bfloat16),
            jax.ShapeDtypeStruct(((WINDOW - 1) * TOK_DEV, side), jnp.bfloat16),
        ) + (jax.ShapeDtypeStruct((rows, side), jnp.bfloat16),) * groups
        outs = (local,) * (3 + groups)
    flops = 2 * total * count * window * columns
    moved = count * (total * window + block_rows * columns) * 2 + total * columns * 4
    return pl.pallas_call(
        kernel,
        out_shape=shapes,
        in_specs=[scalar, scalar]
        + [anywhere] * (groups * pieces + len(weights))
        + [local] * len(accs),
        out_specs=outs,
        scratch_shapes=[
            pltpu.VMEM(x_shape.shape, jnp.bfloat16),
            pltpu.VMEM(w_shape.shape, jnp.bfloat16),
            pltpu.SemaphoreType.DMA((groups,)),
            pltpu.SemaphoreType.DMA((count,)),
        ],
        cost_estimate=pl.CostEstimate(flops=flops, bytes_accessed=moved, transcendentals=0),
        compiler_params=pltpu.CompilerParams(
            vmem_limit_bytes=scratch_limit(x_shape, w_shape, acc_shape, acc_shape)
        ),
    )(table, where, *[v for row in piece_rows for v in row], *weights, *accs)


def attend_kernel(place_ref, starts_ref, q_ref, keys_ref, *refs, own):
    if own:
        stat_ref, acc_ref = refs
    else:
        stat_in, acc_in, out_ref = refs
    size = q_ref.shape[0] // TOK_DEV
    back = WINDOW - 1
    heads = q_ref.shape[1] // HD
    place, plane = place_ref[0], place_ref[1]

    def one(m, carry):
        block = place ^ m
        base = (plane * size + block) * TOK_DEV
        rows = pl.ds(pl.multiple_of(m * TOK_DEV, TOK_DEV), TOK_DEV)
        query_pos = base + lax.broadcasted_iota(jnp.int32, (1, TOK_DEV), 1)
        first_pos = jnp.zeros((1, TOK_DEV), jnp.int32)
        lowest = jnp.int32(0)
        for d in range(starts_ref.shape[0]):
            start = starts_ref[d]
            first_pos = jnp.where(start <= query_pos, jnp.maximum(first_pos, start), first_pos)
            lowest = jnp.where(start <= base, jnp.maximum(lowest, start), lowest)
        earliest = jnp.clip(lowest // TOK_DEV - (plane * size + block - back), 0, back)
        middle = jnp.maximum(back - block, 0)
        top = WINDOW - 1 if own else middle - 1

        def step(i, state):
            w = top - i
            at = (block + w) * TOK_DEV - (back * TOK_DEV if own else 0)
            at = pl.ds(pl.multiple_of(at, TOK_DEV), TOK_DEV)
            key_pos = base + (w - back) * TOK_DEV + lax.broadcasted_iota(
                jnp.int32, (TOK_DEV, 1), 0
            )
            allowed = (key_pos <= query_pos) & (key_pos >= first_pos)
            key_block, value_block = keys_ref[at, :HD], keys_ref[at, HD:]
            after = []
            for h in range(heads):
                best, norm, accum = state[h]
                scores = lax.dot_general(
                    key_block,
                    q_ref[rows, h * HD : (h + 1) * HD],
                    (((1,), (1,)), ((), ())),
                    preferred_element_type=jnp.float32,
                )
                masked = jnp.where(allowed, scores, NEG_LARGE)
                newest = jnp.maximum(best, jnp.max(masked, axis=0, keepdims=True))
                rescale = jnp.exp(best - newest)
                weights = jnp.exp(masked - newest)
                norm = norm * rescale + jnp.sum(weights, axis=0, keepdims=True)
                accum = accum * rescale + lax.dot_general(
                    value_block,
                    weights.astype(jnp.bfloat16),
                    (((0,), (0,)), ((), ())),
                    preferred_element_type=jnp.float32,
                )
                after.append((newest, norm, accum))
            return tuple(after)

        if own:
            count = WINDOW - jnp.maximum(earliest, middle)
            state = tuple(
                (
                    jnp.full((1, TOK_DEV), NEG_LARGE, jnp.float32),
                    jnp.zeros((1, TOK_DEV), jnp.float32),
                    jnp.zeros((HD, TOK_DEV), jnp.float32),
                )
                for _ in range(heads)
            )
        else:
            count = jnp.maximum(middle - earliest, 0)
            state = tuple(
                (
                    stat_in[2 * h : 2 * h + 1, rows],
                    stat_in[2 * h + 1 : 2 * h + 2, rows],
                    acc_in[h * HD : (h + 1) * HD, rows],
                )
                for h in range(heads)
            )
        state = lax.fori_loop(0, count, step, state)
        for h in range(heads):
            best, norm, accum = state[h]
            some = pl.ds(h * HD, HD)
            if own:
                stat_ref[2 * h : 2 * h + 1, rows] = best
                stat_ref[2 * h + 1 : 2 * h + 2, rows] = norm
                acc_ref[some, rows] = accum
            else:
                out_ref[some, rows] = (accum / norm).astype(out_ref.dtype)
        return carry

    lax.fori_loop(0, size, one, 0)


def attend(where, doc_starts, query_rows, keys, state):
    rows, width = query_rows.shape
    own = state is None
    scalar, local = pl.BlockSpec(memory_space=pltpu.SMEM), pl.BlockSpec(memory_space=pltpu.VMEM)
    stat = jax.ShapeDtypeStruct((2 * width // HD, rows), jnp.float32)
    accum = jax.ShapeDtypeStruct((width, rows), jnp.float32)
    out = jax.ShapeDtypeStruct((width, rows), jnp.bfloat16)
    blocks = WINDOW * WINDOW // 2
    return pl.pallas_call(
        lambda *refs: attend_kernel(*refs, own=own),
        out_shape=(stat, accum) if own else out,
        in_specs=[scalar, scalar, local, local] + ([] if own else [local, local]),
        out_specs=(local, local) if own else local,
        cost_estimate=pl.CostEstimate(
            flops=4 * blocks * TOK_DEV * width * TOK_DEV,
            bytes_accessed=8 * rows * width,
            transcendentals=blocks * TOK_DEV * TOK_DEV * width // HD,
        ),
        compiler_params=pltpu.CompilerParams(
            vmem_limit_bytes=scratch_limit(query_rows, keys, stat, accum, out, accum)
        ),
        name="attend_own" if own else "attend_halo",
    )(where, doc_starts, query_rows, keys, *([] if own else state))


def deliver_kernel(place_ref, *refs, size, spans, whole):
    if whole:
        (context_ref,), refs = refs[:1], refs[1:]
    else:
        contexts, refs = refs[:size], refs[size:]
    steps = len(spans)
    weights, refs = refs[:steps], refs[steps:]
    keep, send, *refs = refs
    if whole:
        ws, w_sem = refs
    else:
        context_ref, ws, w_sem, c_sem = refs
    copies, to = [], 0
    for i, (start, rows) in enumerate(spans):
        copies.append(
            pltpu.make_async_copy(
                weights[i].at[pl.ds(start, rows), :], ws.at[pl.ds(to, rows), :], w_sem.at[i]
            )
        )
        to += rows
    if not whole:
        width, half = contexts[0].shape[0], TOK_DEV // 2
        for m in range(size):
            for other in range(size):
                at = pl.multiple_of((place_ref[0] ^ other) * width, LANES)
                for side in range(2):
                    start = (m ^ other) * TOK_DEV + side * half
                    to = pl.multiple_of((side ^ place_ref[2]) * size * half + m * half, half)
                    copies.append(
                        pltpu.make_async_copy(
                            contexts[other].at[:, pl.ds(start, half)],
                            context_ref.at[pl.ds(at, width), pl.ds(to, half)],
                            c_sem.at[(m * size + other) * 2 + side],
                        )
                    )
    for copy in copies:
        copy.start()
    for copy in copies:
        copy.wait()
    mine = keep.shape[1]
    for side, out in enumerate((keep, send)):
        out[...] = jnp.dot(
            ws[...],
            context_ref[:, side * mine : (side + 1) * mine],
            preferred_element_type=jnp.float32,
        ).astype(out.dtype)


def deliver(where, contexts, weights):
    spans = [(start, rows) for _, start, rows in weights]
    weights = [v for v, _, _ in weights]
    steps, columns = len(weights), weights[0].shape[1]
    rows = sum(v for _, v in spans)
    whole = len(contexts) == 1
    size = WINDOW
    total = contexts[0].shape[1]
    scalar = pl.BlockSpec(memory_space=pltpu.SMEM)
    anywhere, local = pl.BlockSpec(memory_space=pltpu.HBM), pl.BlockSpec(memory_space=pltpu.VMEM)
    part = jax.ShapeDtypeStruct((rows, total // 2), jnp.bfloat16)
    context = jax.ShapeDtypeStruct((columns, total), jnp.bfloat16)
    w_shape = jax.ShapeDtypeStruct((rows, columns), jnp.bfloat16)
    scratch = [pltpu.VMEM(w_shape.shape, jnp.bfloat16), pltpu.SemaphoreType.DMA((steps,))]
    if not whole:
        scratch.append(pltpu.SemaphoreType.DMA((2 * size * size,)))
    return pl.pallas_call(
        lambda *refs: deliver_kernel(*refs, size=size, spans=spans, whole=whole),
        out_shape=(part, part) + (() if whole else (context,)),
        in_specs=[scalar] + [local if whole else anywhere] * len(contexts) + [anywhere] * steps,
        out_specs=(local,) * (2 if whole else 3),
        scratch_shapes=scratch,
        cost_estimate=pl.CostEstimate(
            flops=2 * total * columns * rows,
            bytes_accessed=2 * (total * columns + rows * (columns + total)),
            transcendentals=0,
        ),
        compiler_params=pltpu.CompilerParams(
            vmem_limit_bytes=scratch_limit(context, w_shape, *[part] * 6)
        ),
    )(where, *contexts, *weights)


def merge(kept, received):
    rows, total = kept.shape
    size = WINDOW
    wide = total // size

    def kernel(kept_ref, received_ref, *outs):
        for m, out in enumerate(outs):
            at = pl.ds(m * wide, wide)
            total = kept_ref[:, at].astype(jnp.float32) + received_ref[:, at].astype(jnp.float32)
            out[...] = total.astype(out.dtype)

    local = pl.BlockSpec(memory_space=pltpu.VMEM)
    shape = jax.ShapeDtypeStruct((rows, wide), jnp.bfloat16)
    return pl.pallas_call(
        kernel,
        out_shape=(shape,) * size,
        in_specs=[local, local],
        out_specs=(local,) * size,
        cost_estimate=pl.CostEstimate(
            flops=rows * total, bytes_accessed=6 * rows * total, transcendentals=0
        ),
        compiler_params=pltpu.CompilerParams(vmem_limit_bytes=scratch_limit(kept, kept, kept)),
    )(kept, received)


def fetch(table, k, sources, target, sem):
    rows = target.shape[0]
    low = 0
    for group in sources:
        units = group[0].shape[0] // rows

        @pl.when((table[2 * k + 1] >= low) & (table[2 * k + 1] < low + units))
        def _():
            at = pl.multiple_of((table[2 * k + 1] - low) * rows, 32)
            for m, ref in enumerate(group):

                @pl.when(table[2 * k] == m)
                def _():
                    pltpu.make_async_copy(ref.at[pl.ds(at, rows), :], target, sem).start()

        low += units


def choose(table, part, sources, rows):
    begin, end = part
    count = end - begin
    groups = [len(group) for group in sources]

    def kernel(table_ref, *refs):
        refs, (out, sem) = list(refs[:-2]), refs[-2:]
        split = [[refs.pop(0) for _ in range(n)] for n in groups]
        for k in range(count):
            fetch(table_ref, begin + k, split, out.at[k], sem.at[k])
        for k in range(count):
            pltpu.make_async_copy(out.at[k], out.at[k], sem.at[k]).wait()

    shape = jax.ShapeDtypeStruct((count, rows, sources[0][0].shape[1]), jnp.bfloat16)
    flat = [v for group in sources for v in group]
    return pl.pallas_call(
        kernel,
        out_shape=shape,
        in_specs=[pl.BlockSpec(memory_space=pltpu.SMEM)]
        + [pl.BlockSpec(memory_space=pltpu.HBM)] * len(flat),
        out_specs=pl.BlockSpec(memory_space=pltpu.VMEM),
        scratch_shapes=[pltpu.SemaphoreType.DMA((count,))],
        cost_estimate=pl.CostEstimate(flops=0, bytes_accessed=4 * shape.size, transcendentals=0),
        compiler_params=pltpu.CompilerParams(vmem_limit_bytes=scratch_limit(shape, shape)),
    )(table, *flat)


def combine(where, ranks, mine, received):
    count, rows, half = mine.shape
    step = 640 // rows

    def kernel(place_ref, rank_ref, mine_ref, *refs):
        theirs, sem = refs[-2:]
        out, refs = refs[-3], refs[:-3]
        low = 0
        copies = []
        for i, ref in enumerate(refs):
            units = ref.shape[0]
            copies.append(pltpu.make_async_copy(ref, theirs.at[pl.ds(low, units)], sem.at[i]))
            low += units
        for copy in copies:
            copy.start()
        for copy in copies:
            copy.wait()
        for k in range(0, count, step):
            some = [mine_ref[k + i] for i in range(step)]
            rest = [theirs[rank_ref[k + i]] for i in range(step)]
            for blocks, side in ((some, place_ref[2]), (rest, 1 - place_ref[2])):
                total = jnp.concatenate([v.astype(jnp.float32) for v in blocks], 0)
                at = pl.ds(pl.multiple_of(side * half, half), half)
                out[at, k * rows : (k + step) * rows] = jnp.transpose(total).astype(out.dtype)

    shape = jax.ShapeDtypeStruct((TOK_DEV, count * rows), jnp.bfloat16)
    local = pl.BlockSpec(memory_space=pltpu.VMEM)
    return pl.pallas_call(
        kernel,
        out_shape=shape,
        in_specs=[pl.BlockSpec(memory_space=pltpu.SMEM)] * 2
        + [local]
        + [pl.BlockSpec(memory_space=pltpu.HBM)] * len(received),
        out_specs=local,
        scratch_shapes=[
            pltpu.VMEM(mine.shape, jnp.bfloat16),
            pltpu.SemaphoreType.DMA((len(received),)),
        ],
        cost_estimate=pl.CostEstimate(
            flops=shape.size, bytes_accessed=6 * shape.size, transcendentals=0
        ),
        compiler_params=pltpu.CompilerParams(vmem_limit_bytes=scratch_limit(shape, shape, shape)),
        name="combine",
    )(where, ranks, mine, *received)


def settle(where, pieces):
    size, rows = len(pieces), pieces[0].shape[0]

    def kernel(place_ref, *refs):
        key_out, value_out = refs[-2:]
        for m, ref in enumerate(refs[:-2]):
            at = pl.ds(pl.multiple_of((place_ref[0] ^ m) * HD, HD), HD)
            key_out[:, at] = ref[:, :HD]
            value_out[:, at] = ref[:, HD:]

    shape = jax.ShapeDtypeStruct((rows, size * HD), jnp.bfloat16)
    local = pl.BlockSpec(memory_space=pltpu.VMEM)
    return pl.pallas_call(
        kernel,
        out_shape=(shape, shape),
        in_specs=[pl.BlockSpec(memory_space=pltpu.SMEM)] + [local] * size,
        out_specs=(local, local),
        cost_estimate=pl.CostEstimate(flops=0, bytes_accessed=8 * shape.size, transcendentals=0),
        compiler_params=pltpu.CompilerParams(vmem_limit_bytes=scratch_limit(*[shape] * 6)),
        name="settle",
    )(where, *pieces)


def plane_body(*args):
    return plane_steps(*args)


def plane_steps(rollout_rows, live_rows, doc_lengths, block_owner, norm_gain, qkv_weight, out_weight):
    seq_count, seq_index = lax.axis_size("seq"), lax.axis_index("seq")
    tp_index = lax.axis_index("tp")
    block_rows, columns = qkv_weight.shape
    local_features = rollout_rows.shape[1]
    group = HEADS // KV_HEADS
    size = columns // ((group + 2) * HD)
    planes = seq_count // size
    place, plane = seq_index % size, seq_index // size
    where = jnp.stack([place, plane, tp_index]).astype(jnp.int32)
    head_width = group * HD
    half_rows = TOK_DEV // 2

    q_width = size * head_width

    def columns_of(k):
        cuts = ((k * head_width, head_width), (q_width + k * HD, HD), (q_width + (size + k) * HD, HD))
        return jnp.concatenate(
            [lax.dynamic_slice_in_dim(qkv_weight, at, wide, 1) for at, wide in cuts], 1
        )

    live = jnp.broadcast_to(live_rows[None], (8, LANES))
    lower = [turned(live, "seq", k * size) for k in range(1, planes)]
    below = sum(jnp.where(plane >= k, v, 0) for k, v in zip(range(1, planes), lower))
    chains = [three_away(columns_of(place), size)]
    pair = jnp.where(lax.broadcasted_iota(jnp.int32, live.shape, 0) == 0, below, live)
    plane_pairs = [pair] + [swapped(pair, "seq", m) for m in range(1, size)]
    for m in (2, 3, 1):
        chains.append(swapped(columns_of(place ^ m), "seq", m))
    chains = [chains[0]] + [three_away(chains[k], size) for k in (3, 1, 2)]
    head = block_rows * 3 // 10 // 32 * 32
    up_head = turned(out_weight[:head], "seq", size)
    up_rest = turned(out_weight[head:], "seq", size)
    down = turned(out_weight, "seq", -size)
    on_rest = turned(up_rest, "seq", size)
    on_head = turned(up_head, "seq", size)

    before = sum(
        v[0, 0] + jnp.where((place ^ m) < place, v[1, 0], 0) for m, v in enumerate(plane_pairs)
    )
    spilled_in = before - seq_index * TOK_DEV
    tail_rows = lax.dynamic_slice_in_dim(rollout_rows, live_rows[0] - half_rows, half_rows, 0)
    arrived = shifted(tail_rows, "seq", 1)
    joined = jnp.concatenate([arrived, rollout_rows], 0)
    values_f = joined.astype(jnp.float32)
    squares = jnp.sum(values_f * values_f, axis=-1)
    squares = squares + swapped(squares, "tp", 1)
    scale = lax.rsqrt(squares[:, None] / D + EPSILON)
    gain = lax.dynamic_slice_in_dim(norm_gain, tp_index * local_features, local_features, 0)
    at = half_rows - spilled_in
    values_f = lax.dynamic_slice_in_dim(joined, at, TOK_DEV, 0).astype(jnp.float32)
    scale = lax.dynamic_slice_in_dim(scale, at, TOK_DEV, 0)
    normed = (values_f * scale * gain.astype(jnp.float32)).astype(jnp.bfloat16)

    cut = local_features // 2
    h1, h2 = normed[:, :cut], normed[:, cut:]
    x1, y2 = swapped(h1, "tp", 1), swapped(h2, "seq", 2)
    x2, y1 = swapped(h2, "tp", 1), swapped(h1, "seq", 2)
    yx2, xy1 = swapped(y2, "tp", 1), swapped(x1, "seq", 2)
    rows_a, rows_c = [h1, h2, x1, x2], [y1, y2, xy1, yx2]
    rows_b = [swapped(v, "seq", 1) for v in rows_a]
    rows_d = [swapped(v, "seq", 1) for v in rows_c]
    piece_rows = (rows_a, rows_b, rows_c, rows_d)

    numbers = jnp.arange(seq_count, dtype=jnp.int32)
    inverse = jnp.sum(
        jnp.where(block_owner[None, :] == numbers[:, None], numbers[None, :], 0), axis=1
    )
    half_blocks = local_features // block_rows

    def slot(blocks):
        source = inverse[blocks]
        step = (plane - source // size) % planes
        return step * size + ((source % size) ^ place)

    in_order = slot((numbers + tp_index * half_blocks) % seq_count)
    true_of = jnp.sum(
        jnp.where(in_order[None, :] == numbers[:, None], numbers[None, :], 0), axis=1
    )
    per_piece = cut // block_rows
    inside = (true_of % per_piece) * block_rows
    table = jnp.stack([true_of // per_piece, inside // LANES * LANES, inside % LANES], 1)
    doc_starts = (jnp.cumsum(doc_lengths) - doc_lengths).astype(jnp.int32)

    last = 2
    steps = [r for r in range(planes) if r != last]
    rows = block_rows // 2
    step, spot = in_order // size, in_order % size
    step = jnp.where(step == last, planes - 1, step - (step > last))
    order_in = jnp.where((step == planes - 1)[:, None], jnp.array([[1, 0]]), jnp.array([[0, 1]]))
    units = jnp.stack([jnp.repeat(spot, 2), (2 * step[:, None] + order_in).reshape(-1)], 1)
    count = 2 * half_blocks
    here, there = units[:count], units[count:]
    among = jnp.arange(count, dtype=jnp.int32)
    early_units = 2 * (planes - 1)

    def ranks(part):
        key = jnp.maximum(part[:, 1] - early_units + 1, 0) * count + among
        return jnp.sum((key[None, :] < key[:, None]).astype(jnp.int32), axis=1)

    hit = ranks(there)[None, :] == among[:, None]
    going = jnp.sum(jnp.where(hit[:, :, None], there[None, :, :], 0), axis=1).astype(jnp.int32)
    where, table, doc_starts, going, here, here_ranks = lax.optimization_barrier(
        (
            where,
            table.astype(jnp.int32).reshape(-1),
            doc_starts,
            going.reshape(-1),
            here.astype(jnp.int32).reshape(-1),
            ranks(here),
        )
    )

    by_step = lambda some: [c[r] for r in some for c in chains]
    slots_of = lambda some: [r * size + m for r in some for m in range(size)]

    def projected(tokens, slots, weights, accs, name):
        return project(
            table, slots, where, tokens, weights, accs, block_rows, head_width, name
        )

    end = size - 1
    acc = projected(piece_rows, slots_of(steps), by_step(steps), [], "project_first")
    acc = projected(piece_rows, slots_of([last])[:end], by_step([last])[:end], [acc], "project_mid")
    query_rows, kv_rows, kv_last, *kv_home = projected(
        piece_rows, slots_of([last])[end:], by_step([last])[end:], [acc], "project_last"
    )

    halo = shifted(kv_last, "seq", size)
    kv_home = [kv_home[0]] + [swapped(kv_home[m], "seq", m) for m in range(1, size)]
    key_out, value_out = settle(where, kv_home)

    state = attend(where, doc_starts, query_rows, kv_rows, None)
    context = attend(where, doc_starts, query_rows, halo, state)

    from_c = swapped(context, "seq", 2)
    from_b = swapped(context, "seq", 1)
    from_d = swapped(from_c, "seq", 1)
    contexts = (context, from_b, from_c, from_d)

    def delivered(given, weights):
        kept, going_over, *whole = deliver(where, given, weights)
        received = swapped(going_over, "tp", 1)
        pieces = merge(kept, received)
        home = [pieces[0]] + [swapped(pieces[m], "seq", m) for m in range(1, size)]
        return home, whole

    middle = block_rows // 2
    near, whole = delivered(
        contexts, [(out_weight, 0, block_rows), (up_head, 0, head), (up_rest, 0, block_rows - head)]
    )
    far, _ = delivered(whole, [(down, 0, block_rows)])
    mid, _ = delivered(whole, [(on_rest, middle - head, block_rows - middle)])
    late, _ = delivered(whole, [(on_head, 0, head), (on_rest, 0, middle - head)])

    first, second = count - 2 * size, count - size
    cuts = (
        ((0, first), (near, far)),
        ((first, second), (near, far, mid)),
        ((second, count), (near, far, mid, late)),
    )
    received = [swapped(choose(going, part, sources, rows), "tp", 1) for part, sources in cuts]
    mine = choose(here, (0, count), (near, far, mid, late), rows)
    mixed = combine(where, here_ranks, mine, received)
    return (mixed, key_out, value_out)


def solution(mesh):
    in_specs = (P("seq", "tp"), P("seq"), P(), P(), P(), P("seq", "tp"), P("seq", "tp"))
    out_specs = (P("seq", "tp"), P("seq", "tp"), P("seq", "tp"))
    size = KV_HEADS // mesh.shape["tp"]
    by_planes = size == WINDOW and mesh.shape["tp"] == 2 and mesh.shape["seq"] == WINDOW * size
    body = plane_body if by_planes else gathered_body
    return jax.shard_map(body, mesh=mesh, in_specs=in_specs, out_specs=out_specs, check_vma=False)
```
